32 devices in a mesh: dp: 16 (over z, y, core), tensor: 2 (over x).
Axes of the slice: x: 2, y: 2, z: 4, core: 2. Of those that a mesh axis runs over, the one named last changes fastest.
Arguments:
- tokens: bfloat16 [16384, 1536], P(('dp', 'tensor')), may hold values from -6 to 6
- parents: int32 [16, 8], P('dp'), may hold values from -1 to 6, as said below
- attn_gain: float32 [1536], replicated, may hold values from 0.5 to 1.5
- ffn_gain: float32 [1536], replicated, may hold values from 0.5 to 1.5
- query_weight: bfloat16 [1536, 1536], P('dp', 'tensor'), may hold values from -0.21875 to 0.21875
- key_weight: bfloat16 [1536, 1536], P('dp', 'tensor'), may hold values from -0.21875 to 0.21875
- value_weight: bfloat16 [1536, 1536], P('dp', 'tensor'), may hold values from -0.15625 to 0.15625
- output_weight: bfloat16 [1536, 1536], P('tensor', 'dp'), may hold values from -0.4375 to 0.4375
- gate_weight: bfloat16 [1536, 4096], P('dp', 'tensor'), may hold values from -0.15625 to 0.15625
- up_weight: bfloat16 [1536, 4096], P('dp', 'tensor'), may hold values from -0.15625 to 0.15625
- down_weight: bfloat16 [4096, 1536], P('tensor', 'dp'), may hold values from -0.09375 to 0.09375
- cotangent: bfloat16 [16384, 1536], P(('dp', 'tensor')), may hold values from -6 to 6
Outputs:
- block_out: bfloat16 [16384, 1536], P(('dp', 'tensor'))
- token_grad: bfloat16 [16384, 1536], P(('dp', 'tensor'))
- query_grad: float32 [1536, 1536], P('dp', 'tensor')
- key_grad: float32 [1536, 1536], P('dp', 'tensor')
- value_grad: float32 [1536, 1536], P('dp', 'tensor')
- output_grad: float32 [1536, 1536], P('tensor', 'dp')
- gate_grad: float32 [1536, 4096], P('dp', 'tensor')
- up_grad: float32 [1536, 4096], P('dp', 'tensor')
- down_grad: float32 [4096, 1536], P('tensor', 'dp')
- attn_gain_grad: float32 [1536], P(('dp', 'tensor'))
- ffn_gain_grad: float32 [1536], P(('dp', 'tensor'))
The draws below stay inside these ranges and needn't reach their ends.
Inputs may be any that keep to these rules, and one draw needn't show every extreme that they name: parents[t, 0] is -1 (the root segment of tree t); for s >= 1, parents[t, s] is a segment before s of the same tree; in tree 0 the parent of the last segment is the segment before it.
All inputs are finite; a program needn't handle non-finite values.
Results may differ from the reference program's by a relative error of at most 0.02.
Values may be sent and summed in bfloat16 or wider, within the bound.
A program may use at most 256 MiB of HBM per device.

```python
import math
import jax
import jax.numpy as jnp
from jax import lax

D = 1536
HEADS = 24
HD = 64
FF = 4096
SEG = 128
NSEG = 8
TREE_LEN = 1024
TREES = 16
ROWS = 16384


def draw_parents(key, part):
    raw_draw = jax.random.randint(key, (TREES, NSEG), 0, 1 << 20, dtype=jnp.int32)
    seg_index = jnp.arange(NSEG, dtype=jnp.int32)
    tree_index = jnp.arange(TREES, dtype=jnp.int32)
    picked = raw_draw % jnp.maximum(seg_index, 1)[None, :]
    forced = (tree_index[:, None] == 0) & (seg_index[None, :] == NSEG - 1)
    picked = jnp.where(forced, NSEG - 2, picked)
    return jnp.where(seg_index[None, :] == 0, -1, picked).astype(jnp.int32)


def raised(values, stream_key, source, target, shards_of, factor):
    def block_of(position):
        return (jnp.arange(values.shape[position]) // (values.shape[position] // shards_of)).reshape((-1,) + (1,) * (values.ndim - 1 - position))

    one_side = jax.random.permutation(stream_key, shards_of)[block_of(target)]
    other_side = (block_of(target) + shards_of // 2) % shards_of
    return jnp.where((block_of(source) == one_side) | (block_of(source) == other_side), factor * values, values)


def block_levels(own_key, dims, cuts, smallest, top_value):
    factor_of = 1.0
    for dim, shards_of in cuts:
        draws = jax.random.uniform(jax.random.fold_in(jax.random.fold_in(own_key, 6), dim), (shards_of,), jnp.float32, smallest / len(cuts), top_value / len(cuts))
        factor_of = factor_of * jnp.repeat(jnp.exp(draws), dims[dim] // shards_of).reshape((-1,) + (1,) * (len(dims) - 1 - dim))
    return factor_of


def bell_draw(key, dims, width, most, pieces=(), kind=jnp.bfloat16):
    level = block_levels(key, dims, pieces, -0.22, 0.18) if pieces else 1.0
    array = jax.random.normal(key, dims, jnp.float32) * width * level
    return jnp.minimum(jnp.maximum(array, -most), most).astype(kind)


def heavy_noise(key, extent, scale, bound, pieces, heavy, kind=jnp.bfloat16):
    values = scale * jax.random.normal(key, extent, jnp.float32)
    if pieces:
        values = values * block_levels(key, extent, pieces, -0.22, 0.18)
    return jnp.clip(raised(values, jax.random.fold_in(key, 3), *heavy), -bound, bound).astype(kind)


def setup_inputs(seed: int = 0) -> dict:
    arg_keys = jax.random.split(jax.random.key(seed), 13)
    tokens = bell_draw(arg_keys[0], (ROWS, D), 1.0, 6.0, ((0, 32),))
    parents = draw_parents(jax.random.fold_in(arg_keys[12], 71), 0)
    attn_gain = jnp.clip(1.0 + 0.1 * jax.random.normal(arg_keys[2], (D,), jnp.float32), 0.5, 1.5)
    ffn_gain = jnp.clip(1.0 + 0.1 * jax.random.normal(arg_keys[3], (D,), jnp.float32), 0.5, 1.5)
    query_weight = bell_draw(arg_keys[4], (D, HEADS * HD), (D // 2) ** -0.5, 0.21875, ((0, 16), (1, 2)))
    key_weight = bell_draw(arg_keys[5], (D, HEADS * HD), (D // 2) ** -0.5, 0.21875, ((0, 16), (1, 2)))
    value_weight = bell_draw(arg_keys[6], (D, HEADS * HD), D ** -0.5, 0.15625, ((0, 16), (1, 2)))
    output_weight = bell_draw(arg_keys[7], (HEADS * HD, D), (HEADS * HD // 8) ** -0.5, 0.4375, ((0, 2), (1, 16)))
    gate_weight = bell_draw(arg_keys[8], (D, FF), D ** -0.5, 0.15625, ((0, 16), (1, 2)))
    up_weight = bell_draw(arg_keys[9], (D, FF), D ** -0.5, 0.15625, ((0, 16), (1, 2)))
    down_weight = bell_draw(arg_keys[10], (FF, D), FF ** -0.5, 0.09375, ((0, 2), (1, 16)))
    cotangent = heavy_noise(arg_keys[11], (ROWS, D), 1.0, 6.0, ((0, 32),), (0, 1, 32, 2.75))
    return dict(tokens=tokens, parents=parents, attn_gain=attn_gain, ffn_gain=ffn_gain, query_weight=query_weight, key_weight=key_weight, value_weight=value_weight, output_weight=output_weight, gate_weight=gate_weight, up_weight=up_weight, down_weight=down_weight, cotangent=cotangent)


@jax.custom_vjp
def low(v):
    return lax.optimization_barrier(v.astype(jnp.bfloat16)).astype(jnp.float32)

@jax.custom_vjp
def low_back(v):
    return v

def low_keep(v):
    return (low(v), None)

def low_pass(kept, grad):
    return (grad,)

def back_keep(v):
    return (v, None)

def back_low(kept, grad):
    return (low(grad),)
low.defvjp(low_keep, low_pass)
low_back.defvjp(back_keep, back_low)
epsilon = 1e-05
highest = lax.Precision.HIGHEST

def matmul(left, right):
    return jnp.dot(left, right, precision=highest, preferred_element_type=jnp.float32)

def tree_layout(parent_row):
    seg_count = parent_row.shape[0]
    seg_index = jnp.arange(seg_count, dtype=jnp.int32)
    step_up = (parent_row[:, None] == seg_index[None, :]).astype(jnp.int32)
    eye_ints = (seg_index[:, None] == seg_index[None, :]).astype(jnp.int32)
    reachable = eye_ints
    for sweep in range(seg_count):
        reachable = jnp.minimum(eye_ints + jnp.dot(step_up, reachable), 1)
    depths = lax.optimization_barrier(jnp.sum(reachable, axis=1)) - 1
    return (reachable, depths)

def row_tables(parent_row, seg_rows):
    reachable, depths = tree_layout(parent_row)
    seg_count = parent_row.shape[0]
    length = seg_count * seg_rows
    wide_mask = jnp.broadcast_to(reachable[:, None, :, None], (seg_count, seg_rows, seg_count, seg_rows)).reshape(length, length)
    row_ids = jnp.arange(length, dtype=jnp.int32)
    allowed = (wide_mask > 0) & (row_ids[None, :] <= row_ids[:, None])
    positions = jnp.broadcast_to((depths * seg_rows)[:, None], (seg_count, seg_rows)).reshape(length) + row_ids % seg_rows
    return (allowed, positions.astype(jnp.float32))

def rotate(values, positions, direction):
    head_width = values.shape[-1]
    middle = head_width // 2
    freq_rates = jnp.exp(jnp.arange(middle, dtype=jnp.float32) * (-2.0 * math.log(10000.0) / head_width))
    angles = positions[:, None, None] * freq_rates[None, None, :]
    cosine = jnp.cos(angles)
    sine_part = direction * jnp.sin(angles)
    first_half = values[..., :middle]
    second_half = values[..., middle:]
    return jnp.concatenate([first_half * cosine - second_half * sine_part, second_half * cosine + first_half * sine_part], axis=-1)

def rms_scale(values, gain_vec):
    inverse = lax.rsqrt(lax.optimization_barrier(jnp.mean(values * values, axis=-1, keepdims=True)) + epsilon)
    return values * inverse * gain_vec

def reference(tokens, parents, attn_gain, ffn_gain, query_weight, key_weight, value_weight, output_weight, gate_weight, up_weight, down_weight, cotangent):
    score_scale = 1.0 / math.sqrt(HD)

    def forward(token_rows, attn_vec, ffn_vec, query_mat, key_mat, value_mat, output_mat, gate_mat, up_mat, down_mat):

        def one_tree(tree_rows, parent_row):
            allowed, positions = row_tables(parent_row, SEG)
            length = tree_rows.shape[0]
            normed_one = low(rms_scale(tree_rows, attn_vec))
            queries = low(rotate(low_back(matmul(normed_one, query_mat)).reshape(length, HEADS, HD), positions, 1.0))
            keys_rot = low(rotate(low_back(matmul(normed_one, key_mat)).reshape(length, HEADS, HD), positions, 1.0))
            values_low = low_back(low(matmul(normed_one, value_mat))).reshape(length, HEADS, HD)
            scores = low_back(jnp.einsum('qhd,khd->hqk', queries, keys_rot, precision=highest) * score_scale)
            scores = jnp.where(allowed[None], scores, -1e+30)
            peak_score = lax.optimization_barrier(jnp.max(scores, axis=-1, keepdims=True))
            exponent = jnp.exp(scores - peak_score)
            attn_probs = exponent / lax.optimization_barrier(jnp.sum(exponent, axis=-1, keepdims=True))
            probs_low = low(attn_probs)
            attended = jnp.einsum('hqk,khd->qhd', probs_low, values_low, precision=highest).reshape(length, HEADS * HD)
            attended = low_back(low(attended))
            middle = low_back(low(tree_rows + matmul(attended, output_mat)))
            normed_two = low(rms_scale(middle, ffn_vec))
            gate_pre = low_back(matmul(normed_two, gate_mat))
            up_pre = low_back(matmul(normed_two, up_mat))
            hidden = low(gate_pre * jax.nn.sigmoid(gate_pre) * up_pre)
            return low(middle + matmul(hidden, down_mat))

        def tree_step(tree_pair):
            return jax.checkpoint(one_tree)(tree_pair[0], tree_pair[1])
        stacked = lax.map(tree_step, (token_rows.reshape(TREES, TREE_LEN, D), parents))
        return stacked.reshape(TREES * TREE_LEN, D)
    primals = (tokens.astype(jnp.float32), attn_gain.astype(jnp.float32), ffn_gain.astype(jnp.float32), query_weight.astype(jnp.float32), key_weight.astype(jnp.float32), value_weight.astype(jnp.float32), output_weight.astype(jnp.float32), gate_weight.astype(jnp.float32), up_weight.astype(jnp.float32), down_weight.astype(jnp.float32))
    result, pullback = jax.vjp(forward, *primals)
    grads = pullback(cotangent.astype(jnp.float32))
    return (result.astype(jnp.bfloat16), grads[0].astype(jnp.bfloat16), grads[3], grads[4], grads[5], grads[6], grads[7], grads[8], grads[9], grads[1], grads[2])
```

```python
import functools
import math

import jax
import jax.numpy as jnp
from jax import lax
from jax.experimental import pallas as pl
from jax.experimental.pallas import tpu as pltpu
from jax.sharding import PartitionSpec as P

HD = 64
EPS = 1e-05
BF = jnp.bfloat16
F32 = jnp.float32
COLS = 256
LANES = 128
MASKED = -1e30


def settings(mib=48):
    return pltpu.CompilerParams(
        dimension_semantics=("arbitrary",), vmem_limit_bytes=mib * 1024 * 1024
    )


def cost(flops, bytes_accessed, transcendentals=0):
    return pl.CostEstimate(
        flops=int(flops), bytes_accessed=int(bytes_accessed), transcendentals=int(transcendentals)
    )


def nn(a, b):
    return jnp.dot(a, b, preferred_element_type=F32)


def nt(a, b):
    return lax.dot_general(a, b, (((1,), (1,)), ((), ())), preferred_element_type=F32)


def tree_tables(parent_row, seg_rows):
    segs = parent_row.shape[0]
    index = jnp.arange(segs, dtype=jnp.int32)
    step_up = (parent_row[:, None] == index[None, :]).astype(jnp.int32)
    eye = (index[:, None] == index[None, :]).astype(jnp.int32)
    reach = eye
    for _ in range(segs):
        up = jnp.sum(step_up[:, :, None] * reach[None, :, :], axis=1)
        reach = jnp.minimum(eye + up, 1)
    depths = jnp.sum(reach, axis=1) - 1
    bias = jnp.where(reach.T > 0, 0.0, MASKED).astype(F32)
    bias = jnp.repeat(bias, seg_rows, axis=1)
    rows = jnp.arange(segs * seg_rows, dtype=jnp.int32)
    positions = jnp.repeat(depths * seg_rows, seg_rows) + rows % seg_rows
    return bias, positions.astype(F32)


def turn_tables(positions, width):
    half = HD // 2
    rates = jnp.exp(jnp.arange(half, dtype=F32) * (-2.0 * math.log(10000.0) / HD))
    angles = positions[:, None] * rates[None, :]
    cosine, sine = jnp.cos(angles), jnp.sin(angles)
    heads = width // HD
    return (
        jnp.tile(jnp.concatenate([cosine, cosine], axis=1), (1, heads)),
        jnp.tile(jnp.concatenate([-sine, sine], axis=1), (1, heads)),
    )


def turn(x, cosine, sine):
    width = x.shape[1]
    lane = lax.broadcasted_iota(jnp.int32, x.shape, 1)
    first = (lane % HD) < HD // 2
    other = jnp.where(
        first, pltpu.roll(x, width - HD // 2, 1), pltpu.roll(x, HD // 2, 1)
    )
    return x * cosine + other * sine


def inverse_rms(x):
    return lax.rsqrt(jnp.mean(x * x, axis=1, keepdims=True) + EPS)


def project_kernel(parts, x_ref, gain_ref, cos_ref, sin_ref, w_ref, out_ref, normed_ref):
    j = pl.program_id(0)
    rows = x_ref.shape[0]
    chunk = 256

    @pl.when(j == 0)
    def _():
        for r in range(0, rows, chunk):
            x = x_ref[r : r + chunk, :].astype(F32)
            normed_ref[r : r + chunk, :] = (x * inverse_rms(x) * gain_ref[...]).astype(BF)

    @pl.when(j < 2 * parts)
    def _():
        scale = jnp.where(j < parts, 1.0 / math.sqrt(HD), 1.0).astype(F32)
        for r in range(0, rows, chunk):
            pre = nn(normed_ref[r : r + chunk, :], w_ref[...])
            rotated = turn(pre, cos_ref[r : r + chunk, :], sin_ref[r : r + chunk, :])
            out_ref[r : r + chunk, :] = rotated.astype(BF) * scale.astype(BF)

    @pl.when(j >= 2 * parts)
    def _():
        for r in range(0, rows, chunk):
            out_ref[r : r + chunk, :] = nn(normed_ref[r : r + chunk, :], w_ref[...]).astype(BF)


def project(x, gain, cosine, sine, w, width):
    rows, d = x.shape
    parts = width // COLS
    whole = lambda j: (0, 0)
    return pl.pallas_call(
        functools.partial(project_kernel, parts),
        grid=(3 * parts,),
        in_specs=[
            pl.BlockSpec((rows, d), whole),
            pl.BlockSpec((1, d), whole),
            pl.BlockSpec((rows, COLS), whole),
            pl.BlockSpec((rows, COLS), whole),
            pl.BlockSpec((d, COLS), lambda j: (0, j)),
        ],
        out_specs=[
            pl.BlockSpec((rows, COLS), lambda j: (0, j)),
            pl.BlockSpec((rows, d), whole),
        ],
        out_shape=[
            jax.ShapeDtypeStruct((rows, 3 * width), BF),
            jax.ShapeDtypeStruct((rows, d), BF),
        ],
        compiler_params=settings(),
        cost_estimate=cost(6 * rows * d * width, 2 * (2 * rows * d + 3 * d * width)),
        name="project",
    )(x, gain, cosine, sine, w)


def mask_block(block, seg_rows, bias_ref, m, u):
    cols = slice(m * block, (m + 1) * block)
    per = block // seg_rows
    return jnp.concatenate(
        [
            jnp.broadcast_to(bias_ref[u * per + i : u * per + i + 1, cols], (seg_rows, block))
            for i in range(per)
        ],
        axis=0,
    )


def causal(block):
    key = lax.broadcasted_iota(jnp.int32, (block, block), 0)
    query = lax.broadcasted_iota(jnp.int32, (block, block), 1)
    return key <= query


def attend_kernel(block, seg_rows, q_ref, k_ref, v_ref, bias_ref, out_ref, lse_ref):
    length = q_ref.shape[0]
    heads = q_ref.shape[1] // HD
    v_turned = v_ref[...].T
    for m in range(length // block):
        cols = slice(m * block, (m + 1) * block)
        outs = []
        for h in range(heads):
            lanes = slice(h * HD, (h + 1) * HD)
            q = q_ref[cols, lanes]
            scores = []
            for u in range(m + 1):
                s = nt(k_ref[u * block : (u + 1) * block, lanes], q)
                s = s + mask_block(block, seg_rows, bias_ref, m, u)
                if u == m:
                    s = jnp.where(causal(block), s, MASKED)
                scores.append(s)
            peak = scores[0].max(axis=0, keepdims=True)
            for s in scores[1:]:
                peak = jnp.maximum(peak, s.max(axis=0, keepdims=True))
            total = jnp.zeros_like(peak)
            acc = jnp.zeros((HD, block), F32)
            for u, s in enumerate(scores):
                e = jnp.exp(s - peak)
                total = total + e.sum(axis=0, keepdims=True)
                acc = acc + nn(v_turned[lanes, u * block : (u + 1) * block], e.astype(BF))
            outs.append(acc / total)
            lse_ref[0, h : h + 1, cols] = peak + jnp.log(total)
        out_ref[cols, :] = jnp.concatenate(outs, axis=0).T.astype(BF)


def attend(qkv, bias, width, seg_rows):
    length = qkv.shape[0]
    groups = width // LANES
    heads = LANES // HD
    block = 2 * seg_rows
    live = length * length // 2
    return pl.pallas_call(
        functools.partial(attend_kernel, block, seg_rows),
        grid=(groups,),
        in_specs=[
            pl.BlockSpec((length, LANES), lambda i: (0, i)),
            pl.BlockSpec((length, LANES), lambda i: (0, groups + i)),
            pl.BlockSpec((length, LANES), lambda i: (0, 2 * groups + i)),
            pl.BlockSpec(bias.shape, lambda i: (0, 0)),
        ],
        out_specs=[
            pl.BlockSpec((length, LANES), lambda i: (0, i)),
            pl.BlockSpec((1, heads, length), lambda i: (i, 0, 0)),
        ],
        out_shape=[
            jax.ShapeDtypeStruct((length, width), BF),
            jax.ShapeDtypeStruct((groups, heads, length), F32),
        ],
        compiler_params=settings(),
        cost_estimate=cost(16 * live * width, 8 * length * width, live * width // HD),
        name="attend",
    )(qkv, qkv, qkv, bias)


def attend_back_kernel(
    block,
    seg_rows,
    q_ref,
    k_ref,
    v_ref,
    o_ref,
    do_ref,
    lse_ref,
    bias_ref,
    cos_ref,
    sin_ref,
    out_ref,
    dk_ref,
    dv_ref,
):
    length = q_ref.shape[0]
    heads = q_ref.shape[1] // HD
    k_turned = k_ref[...].T
    product = (do_ref[...].astype(F32) * o_ref[...].astype(F32)).T
    deltas = [product[h * HD : (h + 1) * HD].sum(axis=0, keepdims=True) for h in range(heads)]
    for m in range(length // block):
        cols = slice(m * block, (m + 1) * block)
        grads = []
        for h in range(heads):
            lanes = slice(h * HD, (h + 1) * HD)
            q, do = q_ref[cols, lanes], do_ref[cols, lanes]
            lse = lse_ref[0, h : h + 1, cols]
            delta = deltas[h][:, cols]
            acc = jnp.zeros((HD, block), F32)
            for u in range(m + 1):
                keys = slice(u * block, (u + 1) * block)
                s = nt(k_ref[keys, lanes], q)
                p = jnp.exp(s + (mask_block(block, seg_rows, bias_ref, m, u) - lse))
                if u == m:
                    p = jnp.where(causal(block), p, 0.0)
                dp = nt(v_ref[keys, lanes], do)
                ds = (p * (dp - delta)).astype(BF)
                dv = nn(p.astype(BF), do)
                dk = nn(ds, q)
                if u == m:
                    dv_ref[h, keys, :] = dv
                    dk_ref[h, keys, :] = dk
                else:
                    dv_ref[h, keys, :] += dv
                    dk_ref[h, keys, :] += dk
                acc = acc + nn(k_turned[lanes, keys], ds)
            grads.append(acc)
        dq = jnp.concatenate(grads, axis=0).T * (1.0 / math.sqrt(HD))
        out_ref[0, cols, :] = turn(dq, cos_ref[cols, :], -sin_ref[cols, :]).astype(BF)
    for m in range(length // block):
        cols = slice(m * block, (m + 1) * block)
        dk = jnp.concatenate([dk_ref[h, cols, :] for h in range(heads)], axis=1)
        out_ref[1, cols, :] = turn(dk, cos_ref[cols, :], -sin_ref[cols, :]).astype(BF)
        out_ref[2, cols, :] = jnp.concatenate(
            [dv_ref[h, cols, :] for h in range(heads)], axis=1
        ).astype(BF)


def attend_back(qkv, attended, grad_attended, lse, bias, cosine, sine, seg_rows):
    length, width = attended.shape
    groups = width // LANES
    heads = LANES // HD
    block = 2 * seg_rows
    live = length * length // 2
    return pl.pallas_call(
        functools.partial(attend_back_kernel, block, seg_rows),
        grid=(groups,),
        in_specs=[
            pl.BlockSpec((length, LANES), lambda i: (0, i)),
            pl.BlockSpec((length, LANES), lambda i: (0, groups + i)),
            pl.BlockSpec((length, LANES), lambda i: (0, 2 * groups + i)),
            pl.BlockSpec((length, LANES), lambda i: (0, i)),
            pl.BlockSpec((length, LANES), lambda i: (0, i)),
            pl.BlockSpec((1, heads, length), lambda i: (i, 0, 0)),
            pl.BlockSpec(bias.shape, lambda i: (0, 0)),
            pl.BlockSpec((length, LANES), lambda i: (0, 0)),
            pl.BlockSpec((length, LANES), lambda i: (0, 0)),
        ],
        out_specs=pl.BlockSpec((3, length, LANES), lambda i: (0, 0, i)),
        out_shape=jax.ShapeDtypeStruct((3, length, width), BF),
        scratch_shapes=[
            pltpu.VMEM((heads, length, HD), F32),
            pltpu.VMEM((heads, length, HD), F32),
        ],
        compiler_params=settings(),
        cost_estimate=cost(40 * live * width, 16 * length * width, live * width // HD),
        name="attend_back",
    )(qkv, qkv, qkv, attended, grad_attended, lse, bias, cosine, sine)


def rms_back(grad, x, gain):
    inverse = inverse_rms(x)
    unit = x * inverse
    scaled = grad * gain
    inner = jnp.mean(scaled * unit, axis=1, keepdims=True)
    return inverse * (scaled - unit * inner), jnp.sum(grad * unit, axis=0, keepdims=True)


def ffn_kernel(
    x_ref,
    cot_ref,
    gain_ref,
    wg_ref,
    wu_ref,
    wd_ref,
    hidden_ref,
    grads_ref,
    normed_ref,
    part_ref,
    gain_part_ref,
    acc_ref,
):
    j = pl.program_id(0)
    rows = x_ref.shape[0]
    chunk = 256

    @pl.when(j == 0)
    def _():
        for r in range(0, rows, chunk):
            x = x_ref[r : r + chunk, :].astype(F32)
            normed_ref[r : r + chunk, :] = (x * inverse_rms(x) * gain_ref[...]).astype(BF)
        acc_ref[...] = jnp.zeros_like(acc_ref)

    for r in range(0, rows, chunk):
        span = slice(r, r + chunk)
        gate = nn(normed_ref[span, :], wg_ref[...])
        up = nn(normed_ref[span, :], wu_ref[...])
        grad_hidden = nn(cot_ref[span, :], wd_ref[...])
        sig = jax.nn.sigmoid(gate)
        silu = gate * sig
        hidden_ref[span, :] = (silu * up).astype(BF)
        grad_gate = (grad_hidden * up * sig * (1.0 + gate * (1.0 - sig))).astype(BF)
        grad_up = (grad_hidden * silu).astype(BF)
        grads_ref[0, span, :] = grad_gate
        grads_ref[1, span, :] = grad_up
        acc_ref[span, :] += nt(grad_gate, wg_ref[...]) + nt(grad_up, wu_ref[...])

    @pl.when(j == pl.num_programs(0) - 1)
    def _():
        gain_part = jnp.zeros_like(gain_part_ref)
        for r in range(0, rows, chunk):
            span = slice(r, r + chunk)
            part, piece = rms_back(acc_ref[span, :], x_ref[span, :].astype(F32), gain_ref[...])
            part_ref[span, :] = part.astype(BF)
            gain_part = gain_part + piece
        gain_part_ref[...] = gain_part


def ffn(x, cot, gain, w, start, hidden_width):
    rows, d = x.shape
    steps = hidden_width // COLS
    first = start // COLS
    whole = lambda j: (0, 0)
    return pl.pallas_call(
        ffn_kernel,
        grid=(steps,),
        in_specs=[
            pl.BlockSpec((rows, d), whole),
            pl.BlockSpec((rows, d), whole),
            pl.BlockSpec((1, d), whole),
            pl.BlockSpec((d, COLS), lambda j: (0, first + j)),
            pl.BlockSpec((d, COLS), lambda j: (0, first + steps + j)),
            pl.BlockSpec((d, COLS), lambda j: (0, first + 2 * steps + j)),
        ],
        out_specs=[
            pl.BlockSpec((rows, COLS), lambda j: (0, j)),
            pl.BlockSpec((2, rows, COLS), lambda j: (0, 0, j)),
            pl.BlockSpec((rows, d), whole),
            pl.BlockSpec((rows, d), whole),
            pl.BlockSpec((1, d), whole),
        ],
        out_shape=[
            jax.ShapeDtypeStruct((rows, hidden_width), BF),
            jax.ShapeDtypeStruct((2, rows, hidden_width), BF),
            jax.ShapeDtypeStruct((rows, d), BF),
            jax.ShapeDtypeStruct((rows, d), BF),
            jax.ShapeDtypeStruct((1, d), F32),
        ],
        scratch_shapes=[pltpu.VMEM((rows, d), F32)],
        compiler_params=settings(),
        cost_estimate=cost(
            10 * rows * d * hidden_width,
            6 * d * hidden_width + 8 * rows * d + 6 * rows * hidden_width,
            rows * hidden_width,
        ),
        name="ffn",
    )(x, cot, gain, w, w, w)


def input_grad_kernel(x_ref, gain_ref, g_ref, w_ref, part_ref, gain_part_ref, acc_ref):
    j = pl.program_id(0)
    rows = x_ref.shape[0]
    chunk = 256

    @pl.when(j == 0)
    def _():
        acc_ref[...] = jnp.zeros_like(acc_ref)

    for r in range(0, rows, chunk):
        acc_ref[r : r + chunk, :] += nt(g_ref[0, r : r + chunk, :], w_ref[...])

    @pl.when(j == pl.num_programs(0) - 1)
    def _():
        gain_part = jnp.zeros_like(gain_part_ref)
        for r in range(0, rows, chunk):
            span = slice(r, r + chunk)
            part, piece = rms_back(acc_ref[span, :], x_ref[span, :].astype(F32), gain_ref[...])
            part_ref[span, :] = part.astype(BF)
            gain_part = gain_part + piece
        gain_part_ref[...] = gain_part


def input_grad(x, gain, grads, w):
    rows, d = x.shape
    kinds, _, width = grads.shape
    per = width // COLS
    whole = lambda j: (0, 0)
    return pl.pallas_call(
        input_grad_kernel,
        grid=(kinds * per,),
        in_specs=[
            pl.BlockSpec((rows, d), whole),
            pl.BlockSpec((1, d), whole),
            pl.BlockSpec((1, rows, COLS), lambda j: (j // per, 0, j % per)),
            pl.BlockSpec((d, COLS), lambda j: (0, j)),
        ],
        out_specs=[pl.BlockSpec((rows, d), whole), pl.BlockSpec((1, d), whole)],
        out_shape=[jax.ShapeDtypeStruct((rows, d), BF), jax.ShapeDtypeStruct((1, d), F32)],
        scratch_shapes=[pltpu.VMEM((rows, d), F32)],
        compiler_params=settings(),
        cost_estimate=cost(2 * rows * d * kinds * width, 2 * kinds * width * (rows + d)),
        name="input_grad",
    )(x, gain, grads, w)


def weight_grad_kernel(count, *refs):
    lefts, rights = refs[:count], refs[count : 2 * count]
    out_ref, turned_ref = refs[-2], refs[-1]
    j = pl.program_id(0)
    chunk = 256

    @pl.when(j == 0)
    def _():
        start = 0
        for left in lefts:
            for r in range(0, left.shape[0], chunk):
                turned_ref[:, start + r : start + r + chunk] = left[r : r + chunk, :].T
            start += left.shape[0]

    d = out_ref.shape[0]
    for c in range(0, d, chunk):
        total, start = None, 0
        for right in rights:
            rows = right.shape[1]
            piece = nn(turned_ref[c : c + chunk, start : start + rows], right[0])
            total = piece if total is None else total + piece
            start += rows
        out_ref[c : c + chunk, :] = total.astype(BF)


def weight_grad(lefts, rights):
    d = lefts[0].shape[1]
    kinds, _, width = rights[0].shape
    rows = sum(left.shape[0] for left in lefts)
    per = width // COLS
    return pl.pallas_call(
        functools.partial(weight_grad_kernel, len(lefts)),
        grid=(kinds * per,),
        in_specs=[pl.BlockSpec(left.shape, lambda j: (0, 0)) for left in lefts]
        + [
            pl.BlockSpec((1, right.shape[1], COLS), lambda j: (j // per, 0, j % per))
            for right in rights
        ],
        out_specs=pl.BlockSpec((d, COLS), lambda j: (0, j)),
        out_shape=jax.ShapeDtypeStruct((d, kinds * width), BF),
        scratch_shapes=[pltpu.VMEM((d, rows), BF)],
        compiler_params=settings(),
        cost_estimate=cost(2 * rows * d * kinds * width, 2 * kinds * width * (rows + d)),
        name="weight_grad",
    )(*lefts, *rights)


def swap(x):
    return lax.ppermute(x, "tensor", [(0, 1), (1, 0)])


def body(
    tokens,
    parents,
    attn_gain,
    ffn_gain,
    query_weight,
    key_weight,
    value_weight,
    output_weight,
    gate_weight,
    up_weight,
    down_weight,
    cotangent,
):
    half, d = tokens.shape
    length = 2 * half
    width = query_weight.shape[1]
    hidden_width = gate_weight.shape[1]
    seg_rows = length // parents.shape[1]
    mine = lax.axis_index("tensor")
    own_start = mine * half
    other_start = (1 - mine) * half

    def place(own, other):
        full = jnp.zeros((length, own.shape[1]), own.dtype)
        full = lax.dynamic_update_slice(full, own, (own_start, 0))
        return lax.dynamic_update_slice(full, other, (other_start, 0))

    def own_rows(full):
        return lax.dynamic_slice_in_dim(full, own_start, half, 0)

    def other_rows(full):
        return lax.dynamic_slice_in_dim(full, other_start, half, 0)

    def gather(shard):
        return lax.all_gather(shard, "dp", axis=0, tiled=True)

    attn_row = attn_gain[None, :]
    ffn_row = ffn_gain[None, :]

    wqkv = gather(jnp.concatenate([query_weight, key_weight, value_weight], axis=1))
    wrest = gather(
        jnp.concatenate([output_weight.T, gate_weight, up_weight, down_weight.T], axis=1)
    )

    bias, positions = tree_tables(parents[0], seg_rows)
    cosine, sine = turn_tables(positions, COLS)
    rows_all = place(tokens, swap(tokens))
    cot_other = swap(cotangent)

    qkv, normed_one = project(rows_all, attn_row, cosine, sine, wqkv, width)
    attended, lse = attend(qkv, bias, width, seg_rows)
    out_turned = wrest[:, :width]
    send = nt(other_rows(attended), out_turned).astype(BF)
    received = swap(send)
    middle = (
        tokens.astype(F32) + nt(own_rows(attended), out_turned) + received.astype(F32)
    ).astype(BF)
    middle_other = swap(middle)

    hid_own, gg_own, normed_own, part_own, gp_own = ffn(
        middle, cotangent, ffn_row, wrest, width, hidden_width
    )
    hid_other, gg_other, normed_other, part_other, gp_other = ffn(
        middle_other, cot_other, ffn_row, wrest, width, hidden_width
    )
    gp = gp_own + gp_other
    part_received = swap(part_other)
    gp_received = swap(gp)
    down_turned_grad = weight_grad([cotangent, cot_other], [hid_own[None], hid_other[None]])
    gate_up_grad = weight_grad([normed_own, normed_other], [gg_own, gg_other])
    grad_middle = (
        cotangent.astype(F32) + part_own.astype(F32) + part_received.astype(F32)
    ).astype(BF)
    grad_middle_other = swap(grad_middle)

    down_turned = wrest[:, width + 2 * hidden_width :]
    out_received = swap(nt(hid_other, down_turned).astype(BF))
    block_out = (
        middle.astype(F32) + nt(hid_own, down_turned) + out_received.astype(F32)
    ).astype(BF)

    def scatter(grad):
        return lax.psum_scatter(grad, "dp", scatter_dimension=0, tiled=True).astype(F32)

    def gain_block(gain_sum):
        return jnp.broadcast_to(gain_sum.astype(BF).T, (d, LANES))

    down_grad = scatter(down_turned_grad).T
    gate_up = scatter(jnp.concatenate([gate_up_grad, gain_block(gp + gp_received)], axis=1))
    gate_grad = gate_up[:, :hidden_width]
    up_grad = gate_up[:, hidden_width : 2 * hidden_width]

    grad_attended = place(
        nn(grad_middle, out_turned).astype(BF), nn(grad_middle_other, out_turned).astype(BF)
    )
    grads = attend_back(
        qkv, attended, grad_attended, lse, bias, cosine[:, :LANES], sine[:, :LANES], seg_rows
    )
    part, gain_part = input_grad(rows_all, attn_row, grads, wqkv)
    tokens_received = swap(other_rows(part))
    gain_received = swap(gain_part)
    qkv_grad = weight_grad([normed_one], [grads])
    out_turned_grad = weight_grad(
        [grad_middle, grad_middle_other], [own_rows(attended)[None], other_rows(attended)[None]]
    )
    token_grad = (
        grad_middle.astype(F32) + own_rows(part).astype(F32) + tokens_received.astype(F32)
    ).astype(BF)
    last = scatter(
        jnp.concatenate(
            [qkv_grad, out_turned_grad, gain_block(gain_part + gain_received)], axis=1
        )
    )
    gain_rows = d // lax.axis_size("dp") // 2

    def gain_piece(column):
        return lax.dynamic_slice_in_dim(column[:, 0], mine * gain_rows, gain_rows, 0)

    return (
        block_out,
        token_grad,
        last[:, :width],
        last[:, width : 2 * width],
        last[:, 2 * width : 3 * width],
        last[:, 3 * width : 4 * width].T,
        gate_grad,
        up_grad,
        down_grad,
        gain_piece(last[:, 4 * width :]),
        gain_piece(gate_up[:, 2 * hidden_width :]),
    )


def solution(mesh):
    rows = P(("dp", "tensor"), None)
    tall = P("dp", "tensor")
    wide = P("tensor", "dp")
    return jax.shard_map(
        body,
        mesh=mesh,
        in_specs=(
            rows, P("dp", None), P(), P(), tall, tall, tall, wide, tall, tall, wide, rows,
        ),
        out_specs=(
            rows, rows, tall, tall, tall, wide, tall, tall, wide,
            P(("dp", "tensor")), P(("dp", "tensor")),
        ),
        check_vma=False,
    )
```

```python
import functools
import math

import jax
import jax.numpy as jnp
from jax import lax
from jax.experimental import pallas as pl
from jax.experimental.pallas import tpu as pltpu
from jax.sharding import PartitionSpec as P

HD = 64
EPS = 1e-05
BF = jnp.bfloat16
F32 = jnp.float32
COLS = 256
LANES = 128
MASKED = -1e30


def settings(mib=48):
    return pltpu.CompilerParams(
        dimension_semantics=("arbitrary",), vmem_limit_bytes=mib * 1024 * 1024
    )


def cost(flops, bytes_accessed, transcendentals=0):
    return pl.CostEstimate(
        flops=int(flops), bytes_accessed=int(bytes_accessed), transcendentals=int(transcendentals)
    )


def nn(a, b):
    return jnp.dot(a, b, preferred_element_type=F32)


def nt(a, b):
    return lax.dot_general(a, b, (((1,), (1,)), ((), ())), preferred_element_type=F32)


def tree_tables(parent_row, seg_rows):
    segs = parent_row.shape[0]
    index = jnp.arange(segs, dtype=jnp.int32)
    step_up = (parent_row[:, None] == index[None, :]).astype(jnp.int32)
    eye = (index[:, None] == index[None, :]).astype(jnp.int32)
    reach = eye
    for _ in range(segs):
        up = jnp.sum(step_up[:, :, None] * reach[None, :, :], axis=1)
        reach = jnp.minimum(eye + up, 1)
    depths = jnp.sum(reach, axis=1) - 1
    bias = jnp.where(reach.T > 0, 0.0, MASKED).astype(F32)
    bias = jnp.repeat(bias, seg_rows, axis=1)
    rows = jnp.arange(segs * seg_rows, dtype=jnp.int32)
    positions = jnp.repeat(depths * seg_rows, seg_rows) + rows % seg_rows
    return bias, positions.astype(F32)


def turn_tables(positions, width):
    half = HD // 2
    rates = jnp.exp(jnp.arange(half, dtype=F32) * (-2.0 * math.log(10000.0) / HD))
    angles = positions[:, None] * rates[None, :]
    cosine, sine = jnp.cos(angles), jnp.sin(angles)
    heads = width // HD
    return (
        jnp.tile(jnp.concatenate([cosine, cosine], axis=1), (1, heads)),
        jnp.tile(jnp.concatenate([-sine, sine], axis=1), (1, heads)),
    )


def turn(x, cosine, sine):
    width = x.shape[1]
    lane = lax.broadcasted_iota(jnp.int32, x.shape, 1)
    first = (lane % HD) < HD // 2
    other = jnp.where(
        first, pltpu.roll(x, width - HD // 2, 1), pltpu.roll(x, HD // 2, 1)
    )
    return x * cosine + other * sine


def inverse_rms(x):
    return lax.rsqrt(jnp.mean(x * x, axis=1, keepdims=True) + EPS)


def project_kernel(parts, x_ref, gain_ref, cos_ref, sin_ref, w_ref, out_ref, normed_ref):
    j = pl.program_id(0)
    rows = x_ref.shape[0]
    chunk = 256

    @pl.when(j == 0)
    def _():
        for r in range(0, rows, chunk):
            x = x_ref[r : r + chunk, :].astype(F32)
            normed_ref[r : r + chunk, :] = (x * inverse_rms(x) * gain_ref[...]).astype(BF)

    @pl.when(j < 2 * parts)
    def _():
        scale = jnp.where(j < parts, 1.0 / math.sqrt(HD), 1.0).astype(F32)
        for r in range(0, rows, chunk):
            pre = nn(normed_ref[r : r + chunk, :], w_ref[...])
            rotated = turn(pre, cos_ref[r : r + chunk, :], sin_ref[r : r + chunk, :])
            out_ref[r : r + chunk, :] = rotated.astype(BF) * scale.astype(BF)

    @pl.when(j >= 2 * parts)
    def _():
        for r in range(0, rows, chunk):
            out_ref[r : r + chunk, :] = nn(normed_ref[r : r + chunk, :], w_ref[...]).astype(BF)


def project(x, gain, cosine, sine, w, width):
    rows, d = x.shape
    parts = width // COLS
    whole = lambda j: (0, 0)
    return pl.pallas_call(
        functools.partial(project_kernel, parts),
        grid=(3 * parts,),
        in_specs=[
            pl.BlockSpec((rows, d), whole),
            pl.BlockSpec((1, d), whole),
            pl.BlockSpec((rows, COLS), whole),
            pl.BlockSpec((rows, COLS), whole),
            pl.BlockSpec((d, COLS), lambda j: (0, j)),
        ],
        out_specs=[
            pl.BlockSpec((rows, COLS), lambda j: (0, j)),
            pl.BlockSpec((rows, d), whole),
        ],
        out_shape=[
            jax.ShapeDtypeStruct((rows, 3 * width), BF),
            jax.ShapeDtypeStruct((rows, d), BF),
        ],
        compiler_params=settings(),
        cost_estimate=cost(6 * rows * d * width, 2 * (2 * rows * d + 3 * d * width)),
        name="project",
    )(x, gain, cosine, sine, w)


def mask_block(block, seg_rows, bias_ref, m, u):
    cols = slice(m * block, (m + 1) * block)
    per = block // seg_rows
    return jnp.concatenate(
        [
            jnp.broadcast_to(bias_ref[u * per + i : u * per + i + 1, cols], (seg_rows, block))
            for i in range(per)
        ],
        axis=0,
    )


def causal(block):
    key = lax.broadcasted_iota(jnp.int32, (block, block), 0)
    query = lax.broadcasted_iota(jnp.int32, (block, block), 1)
    return key <= query


def attend_kernel(block, seg_rows, q_ref, k_ref, v_ref, bias_ref, out_ref, lse_ref):
    length = q_ref.shape[0]
    heads = q_ref.shape[1] // HD
    v_turned = v_ref[...].T
    for m in range(length // block):
        cols = slice(m * block, (m + 1) * block)
        outs = []
        for h in range(heads):
            lanes = slice(h * HD, (h + 1) * HD)
            q = q_ref[cols, lanes]
            scores = []
            for u in range(m + 1):
                s = nt(k_ref[u * block : (u + 1) * block, lanes], q)
                s = s + mask_block(block, seg_rows, bias_ref, m, u)
                if u == m:
                    s = jnp.where(causal(block), s, MASKED)
                scores.append(s)
            peak = scores[0].max(axis=0, keepdims=True)
            for s in scores[1:]:
                peak = jnp.maximum(peak, s.max(axis=0, keepdims=True))
            total = jnp.zeros_like(peak)
            acc = jnp.zeros((HD, block), F32)
            for u, s in enumerate(scores):
                e = jnp.exp(s - peak)
                total = total + e.sum(axis=0, keepdims=True)
                acc = acc + nn(v_turned[lanes, u * block : (u + 1) * block], e.astype(BF))
            outs.append(acc / total)
            lse_ref[0, h : h + 1, cols] = peak + jnp.log(total)
        out_ref[cols, :] = jnp.concatenate(outs, axis=0).T.astype(BF)


def attend(qkv, bias, width, seg_rows):
    length = qkv.shape[0]
    groups = width // LANES
    heads = LANES // HD
    block = 2 * seg_rows
    live = length * length // 2
    return pl.pallas_call(
        functools.partial(attend_kernel, block, seg_rows),
        grid=(groups,),
        in_specs=[
            pl.BlockSpec((length, LANES), lambda i: (0, i)),
            pl.BlockSpec((length, LANES), lambda i: (0, groups + i)),
            pl.BlockSpec((length, LANES), lambda i: (0, 2 * groups + i)),
            pl.BlockSpec(bias.shape, lambda i: (0, 0)),
        ],
        out_specs=[
            pl.BlockSpec((length, LANES), lambda i: (0, i)),
            pl.BlockSpec((1, heads, length), lambda i: (i, 0, 0)),
        ],
        out_shape=[
            jax.ShapeDtypeStruct((length, width), BF),
            jax.ShapeDtypeStruct((groups, heads, length), F32),
        ],
        compiler_params=settings(),
        cost_estimate=cost(16 * live * width, 8 * length * width, live * width // HD),
        name="attend",
    )(qkv, qkv, qkv, bias)


def attend_back_kernel(
    block,
    seg_rows,
    q_ref,
    k_ref,
    v_ref,
    o_ref,
    do_ref,
    lse_ref,
    bias_ref,
    cos_ref,
    sin_ref,
    out_ref,
    dk_ref,
    dv_ref,
):
    length = q_ref.shape[0]
    heads = q_ref.shape[1] // HD
    k_turned = k_ref[...].T
    product = (do_ref[...].astype(F32) * o_ref[...].astype(F32)).T
    deltas = [product[h * HD : (h + 1) * HD].sum(axis=0, keepdims=True) for h in range(heads)]
    for m in range(length // block):
        cols = slice(m * block, (m + 1) * block)
        grads = []
        for h in range(heads):
            lanes = slice(h * HD, (h + 1) * HD)
            q, do = q_ref[cols, lanes], do_ref[cols, lanes]
            lse = lse_ref[0, h : h + 1, cols]
            delta = deltas[h][:, cols]
            acc = jnp.zeros((HD, block), F32)
            for u in range(m + 1):
                keys = slice(u * block, (u + 1) * block)
                s = nt(k_ref[keys, lanes], q)
                p = jnp.exp(s + (mask_block(block, seg_rows, bias_ref, m, u) - lse))
                if u == m:
                    p = jnp.where(causal(block), p, 0.0)
                dp = nt(v_ref[keys, lanes], do)
                ds = (p * (dp - delta)).astype(BF)
                dv = nn(p.astype(BF), do)
                dk = nn(ds, q)
                if u == m:
                    dv_ref[h, keys, :] = dv
                    dk_ref[h, keys, :] = dk
                else:
                    dv_ref[h, keys, :] += dv
                    dk_ref[h, keys, :] += dk
                acc = acc + nn(k_turned[lanes, keys], ds)
            grads.append(acc)
        dq = jnp.concatenate(grads, axis=0).T * (1.0 / math.sqrt(HD))
        out_ref[0, cols, :] = turn(dq, cos_ref[cols, :], -sin_ref[cols, :]).astype(BF)
    for m in range(length // block):
        cols = slice(m * block, (m + 1) * block)
        dk = jnp.concatenate([dk_ref[h, cols, :] for h in range(heads)], axis=1)
        out_ref[1, cols, :] = turn(dk, cos_ref[cols, :], -sin_ref[cols, :]).astype(BF)
        out_ref[2, cols, :] = jnp.concatenate(
            [dv_ref[h, cols, :] for h in range(heads)], axis=1
        ).astype(BF)


def attend_back(qkv, attended, grad_attended, lse, bias, cosine, sine, seg_rows):
    length, width = attended.shape
    groups = width // LANES
    heads = LANES // HD
    block = 2 * seg_rows
    live = length * length // 2
    return pl.pallas_call(
        functools.partial(attend_back_kernel, block, seg_rows),
        grid=(groups,),
        in_specs=[
            pl.BlockSpec((length, LANES), lambda i: (0, i)),
            pl.BlockSpec((length, LANES), lambda i: (0, groups + i)),
            pl.BlockSpec((length, LANES), lambda i: (0, 2 * groups + i)),
            pl.BlockSpec((length, LANES), lambda i: (0, i)),
            pl.BlockSpec((length, LANES), lambda i: (0, i)),
            pl.BlockSpec((1, heads, length), lambda i: (i, 0, 0)),
            pl.BlockSpec(bias.shape, lambda i: (0, 0)),
            pl.BlockSpec((length, LANES), lambda i: (0, 0)),
            pl.BlockSpec((length, LANES), lambda i: (0, 0)),
        ],
        out_specs=pl.BlockSpec((3, length, LANES), lambda i: (0, 0, i)),
        out_shape=jax.ShapeDtypeStruct((3, length, width), BF),
        scratch_shapes=[
            pltpu.VMEM((heads, length, HD), F32),
            pltpu.VMEM((heads, length, HD), F32),
        ],
        compiler_params=settings(),
        cost_estimate=cost(40 * live * width, 16 * length * width, live * width // HD),
        name="attend_back",
    )(qkv, qkv, qkv, attended, grad_attended, lse, bias, cosine, sine)


def rms_back(grad, x, gain):
    inverse = inverse_rms(x)
    unit = x * inverse
    scaled = grad * gain
    inner = jnp.mean(scaled * unit, axis=1, keepdims=True)
    return inverse * (scaled - unit * inner), jnp.sum(grad * unit, axis=0, keepdims=True)


def ffn_kernel(
    x_ref,
    cot_ref,
    gain_ref,
    wg_ref,
    wu_ref,
    wd_ref,
    grads_ref,
    normed_ref,
    part_ref,
    gain_part_ref,
    acc_ref,
):
    j = pl.program_id(0)
    rows = x_ref.shape[0]
    chunk = rows

    @pl.when(j == 0)
    def _():
        for r in range(0, rows, chunk):
            x = x_ref[r : r + chunk, :].astype(F32)
            normed_ref[r : r + chunk, :] = (x * inverse_rms(x) * gain_ref[...]).astype(BF)
        acc_ref[...] = jnp.zeros_like(acc_ref)

    for r in range(0, rows, chunk):
        span = slice(r, r + chunk)
        gate = nn(normed_ref[span, :], wg_ref[...])
        up = nn(normed_ref[span, :], wu_ref[...])
        grad_hidden = nn(cot_ref[span, :], wd_ref[...])
        sig = jax.nn.sigmoid(gate)
        silu = gate * sig
        grads_ref[2, span, :] = (silu * up).astype(BF)
        grad_gate = (grad_hidden * up * sig * (1.0 + gate * (1.0 - sig))).astype(BF)
        grad_up = (grad_hidden * silu).astype(BF)
        grads_ref[0, span, :] = grad_gate
        grads_ref[1, span, :] = grad_up
        acc_ref[span, :] += nt(grad_gate, wg_ref[...]) + nt(grad_up, wu_ref[...])

    @pl.when(j == pl.num_programs(0) - 1)
    def _():
        gain_part = jnp.zeros_like(gain_part_ref)
        for r in range(0, rows, chunk):
            span = slice(r, r + chunk)
            part, piece = rms_back(acc_ref[span, :], x_ref[span, :].astype(F32), gain_ref[...])
            part_ref[span, :] = part.astype(BF)
            gain_part = gain_part + piece
        gain_part_ref[...] = gain_part


def ffn(x, cot, gain, w, start, hidden_width):
    rows, d = x.shape
    steps = hidden_width // COLS
    first = start // COLS
    whole = lambda j: (0, 0)
    return pl.pallas_call(
        ffn_kernel,
        grid=(steps,),
        in_specs=[
            pl.BlockSpec((rows, d), whole),
            pl.BlockSpec((rows, d), whole),
            pl.BlockSpec((1, d), whole),
            pl.BlockSpec((d, COLS), lambda j: (0, first + j)),
            pl.BlockSpec((d, COLS), lambda j: (0, first + steps + j)),
            pl.BlockSpec((d, COLS), lambda j: (0, first + 2 * steps + j)),
        ],
        out_specs=[
            pl.BlockSpec((3, rows, COLS), lambda j: (0, 0, j)),
            pl.BlockSpec((rows, d), whole),
            pl.BlockSpec((rows, d), whole),
            pl.BlockSpec((1, d), whole),
        ],
        out_shape=[
            jax.ShapeDtypeStruct((3, rows, hidden_width), BF),
            jax.ShapeDtypeStruct((rows, d), BF),
            jax.ShapeDtypeStruct((rows, d), BF),
            jax.ShapeDtypeStruct((1, d), F32),
        ],
        scratch_shapes=[pltpu.VMEM((rows, d), F32)],
        compiler_params=settings(),
        cost_estimate=cost(
            10 * rows * d * hidden_width,
            6 * d * hidden_width + 8 * rows * d + 6 * rows * hidden_width,
            rows * hidden_width,
        ),
        name="ffn",
    )(x, cot, gain, w, w, w)


def input_grad_kernel(x_ref, gain_ref, g_ref, w_ref, part_ref, gain_part_ref, acc_ref):
    j = pl.program_id(0)
    rows = x_ref.shape[0]
    chunk = 256

    @pl.when(j == 0)
    def _():
        acc_ref[...] = jnp.zeros_like(acc_ref)

    for r in range(0, rows, chunk):
        acc_ref[r : r + chunk, :] += nt(g_ref[0, r : r + chunk, :], w_ref[...])

    @pl.when(j == pl.num_programs(0) - 1)
    def _():
        gain_part = jnp.zeros_like(gain_part_ref)
        for r in range(0, rows, chunk):
            span = slice(r, r + chunk)
            part, piece = rms_back(acc_ref[span, :], x_ref[span, :].astype(F32), gain_ref[...])
            half = part_ref.shape[1]
            part_ref[r // half, r % half : r % half + chunk, :] = part.astype(BF)
            gain_part = gain_part + piece
        gain_part_ref[...] = gain_part


def input_grad(x, gain, grads, w):
    rows, d = x.shape
    kinds, _, width = grads.shape
    per = width // COLS
    whole = lambda j: (0, 0)
    return pl.pallas_call(
        input_grad_kernel,
        grid=(kinds * per,),
        in_specs=[
            pl.BlockSpec((rows, d), whole),
            pl.BlockSpec((1, d), whole),
            pl.BlockSpec((1, rows, COLS), lambda j: (j // per, 0, j % per)),
            pl.BlockSpec((d, COLS), lambda j: (0, j)),
        ],
        out_specs=[pl.BlockSpec((2, rows // 2, d), lambda j: (0, 0, 0)), pl.BlockSpec((1, d), whole)],
        out_shape=[
            jax.ShapeDtypeStruct((2, rows // 2, d), BF),
            jax.ShapeDtypeStruct((1, d), F32),
        ],
        scratch_shapes=[pltpu.VMEM((rows, d), F32)],
        compiler_params=settings(),
        cost_estimate=cost(2 * rows * d * kinds * width, 2 * kinds * width * (rows + d)),
        name="input_grad",
    )(x, gain, grads, w)


MESH = pl.DeviceIdType.MESH
QUARTERS = 4


class Scatter:
    def __init__(self, devices, rows, count):
        self.devices, self.rows, self.count = devices, rows, count
        self.stages = devices.bit_length() - 1
        self.lags = [2 if s == 1 else 1 for s in range(self.stages)]
        self.starts = [sum(self.lags[:s]) for s in range(self.stages + 1)]
        self.steps = count + self.starts[-1]

    def scratch(self):
        shapes = []
        for s in range(self.stages):
            slots, left = 2 * self.lags[s], self.devices >> (s + 1)
            shapes.append(pltpu.VMEM((slots, 2, left, self.rows, COLS), BF))
            shapes.append(pltpu.VMEM((slots, left, self.rows, COLS), BF))
            shapes.append(pltpu.SemaphoreType.DMA((slots,)))
            shapes.append(pltpu.SemaphoreType.DMA((slots,)))
        return shapes

    def bind(self, refs):
        self.held, self.got = refs[0::4], refs[1::4]
        self.sent_sem, self.got_sem = refs[2::4], refs[3::4]
        self.me, self.side = lax.axis_index("dp"), lax.axis_index("tensor")

    def bit(self, s):
        return (self.me // (1 << s)) % 2

    def partner(self, s):
        return (self.me + (1 - 2 * self.bit(s)) * (1 << s), self.side)

    def barrier(self):
        arrived = pltpu.get_barrier_semaphore()
        for s in range(self.stages):
            pl.semaphore_signal(arrived, inc=1, device_id=self.partner(s), device_id_type=MESH)
        pl.semaphore_signal(
            arrived, inc=1, device_id=(self.me, 1 - self.side), device_id_type=MESH
        )
        pl.semaphore_wait(arrived, self.stages + 1)

    def copy(self, s, slot):
        return pltpu.make_async_remote_copy(
            src_ref=self.held[s].at[slot, 1 - self.bit(s)],
            dst_ref=self.got[s].at[slot],
            send_sem=self.sent_sem[s].at[slot],
            recv_sem=self.got_sem[s].at[slot],
            device_id=self.partner(s),
            device_id_type=MESH,
        )

    def advance(self, step, out_ref):
        for s in range(self.stages, 0, -1):
            block = step - self.starts[s]

            @pl.when((block >= 0) & (block < self.count))
            def _():
                slot = block % (2 * self.lags[s - 1])
                keep = self.bit(s - 1)
                self.copy(s - 1, slot).wait()
                held, got = self.held[s - 1], self.got[s - 1]
                if s == self.stages:
                    out_ref[...] = held[slot, keep, 0].astype(F32) + got[slot, 0].astype(F32)
                else:
                    later = block % (2 * self.lags[s])
                    for k in range(self.devices >> s):
                        total = held[slot, keep, k].astype(F32) + got[slot, k].astype(F32)
                        self.held[s][later, k % 2, k // 2] = total.astype(BF)
                    self.copy(s, later).start()

    def put(self, slot, start, piece):
        for r in range(0, piece.shape[0], self.rows):
            k = (start + r) // self.rows
            self.held[0][slot, k % 2, k // 2] = piece[r : r + self.rows].astype(BF)

    def put_gain(self, slot, mine_ref, other_ref):
        for k in range(self.devices):
            span = slice(k * self.rows, (k + 1) * self.rows)
            total = mine_ref[span, :].astype(F32) + other_ref[span, :].astype(F32)
            total = jnp.concatenate([total] * (COLS // LANES), axis=1)
            self.held[0][slot, k % 2, k // 2] = total.astype(BF)


def turn_into(turned_ref, lefts):
    start = 0
    for left in lefts:
        for r in range(0, left.shape[0], 256):
            turned_ref[:, start + r : start + r + 256] = left[r : r + 256, :].T
        start += left.shape[0]


def gain_copy(scatter, gain_ref, got_ref, sems):
    return pltpu.make_async_remote_copy(
        src_ref=gain_ref,
        dst_ref=got_ref,
        send_sem=sems.at[0],
        recv_sem=sems.at[1],
        device_id=(scatter.me, 1 - scatter.side),
        device_id_type=MESH,
    )


def ffn_scatter_kernel(scatter, per, *refs):
    (
        norm_own, norm_other, cot_own, cot_other, right_own, right_other,
        part_own, part_other, gain_ref,
    ) = refs[:9]
    out_ref, gm_ref = refs[9:11]
    turned_ref, got_part, gm_own, gain_got, gain_sems, x_sems, local_sem = refs[11:18]
    scatter.bind(refs[18:])
    step = pl.program_id(0)
    side = scatter.side
    quarter = part_own.shape[0] // QUARTERS

    def part_copy(r):
        span = pl.ds(r * quarter, quarter)
        return pltpu.make_async_remote_copy(
            src_ref=part_other.at[span],
            dst_ref=got_part.at[span],
            send_sem=x_sems.at[0, r],
            recv_sem=x_sems.at[1, r],
            device_id=(scatter.me, 1 - side),
            device_id_type=MESH,
        )

    def gm_copy(r):
        span = pl.ds(r * quarter, quarter)
        return pltpu.make_async_remote_copy(
            src_ref=gm_own.at[span],
            dst_ref=gm_ref.at[side, span],
            send_sem=x_sems.at[2, r],
            recv_sem=x_sems.at[3, r],
            device_id=(scatter.me, 1 - side),
            device_id_type=MESH,
        )

    def gm_keep():
        return pltpu.make_async_copy(gm_own, gm_ref.at[side], local_sem)

    @pl.when(step == 0)
    def _():
        scatter.barrier()
        for r in range(QUARTERS):
            part_copy(r).start()
        gain_copy(scatter, gain_ref, gain_got, gain_sems).start()
        turn_into(turned_ref, [norm_own, norm_other])

    @pl.when(step == 2 * per)
    def _():
        turn_into(turned_ref, [cot_own, cot_other])

    scatter.advance(step, out_ref)

    @pl.when(step < 3 * per)
    def _():
        slot = step % 2
        piece_rows = 384
        half = right_own.shape[1]
        for r in range(0, turned_ref.shape[0], piece_rows):
            span = slice(r, r + piece_rows)
            piece = nn(turned_ref[span, :half], right_own[0])
            piece = piece + nn(turned_ref[span, half:], right_other[0])
            scatter.put(slot, r, piece)
        scatter.copy(0, slot).start()

    @pl.when(step == 3 * per)
    def _():
        slot = step % 2
        gain_copy(scatter, gain_ref, gain_got, gain_sems).wait()
        scatter.put_gain(slot, gain_ref, gain_got)
        scatter.copy(0, slot).start()

    for r in range(QUARTERS):

        @pl.when(step == 3 + 2 * r)
        def _():
            span = slice(r * quarter, (r + 1) * quarter)
            part_copy(r).wait()
            total = cot_own[span, :].astype(F32) + part_own[span, :].astype(F32)
            gm_own[span, :] = (total + got_part[span, :].astype(F32)).astype(BF)
            gm_copy(r).start()
            if r == QUARTERS - 1:
                gm_keep().start()

    @pl.when(step == scatter.steps - 1)
    def _():
        for r in range(QUARTERS):
            gm_copy(r).wait()
        gm_keep().wait()


def resident(shape):
    zeros = (0,) * len(shape)
    return pl.BlockSpec(shape, lambda j: zeros, pipeline_mode=pl.Buffered(1))


def remote_settings(identity, mib=56):
    return pltpu.CompilerParams(
        dimension_semantics=("arbitrary",),
        vmem_limit_bytes=mib * 1024 * 1024,
        collective_id=identity,
        has_side_effects=True,
    )


def ffn_scatter(devices, normed, cots, rights, parts, gain_block):
    half, d = normed[0].shape
    per = rights[0].shape[2] // COLS
    scatter = Scatter(devices, d // devices, 3 * per + 1)
    last = 3 * per - 1

    def right_map(j):
        c = jnp.minimum(j, last)
        return (c // per, 0, c % per)

    first = scatter.starts[-1]
    return pl.pallas_call(
        functools.partial(ffn_scatter_kernel, scatter, per),
        grid=(scatter.steps,),
        in_specs=[resident((half, d))] * 4
        + [pl.BlockSpec((1, half, COLS), right_map)] * 2
        + [
            resident((half, d)),
            pl.BlockSpec(memory_space=pl.ANY),
            resident((d, LANES)),
        ],
        out_specs=[
            pl.BlockSpec((scatter.rows, COLS), lambda j: (0, jnp.maximum(j - first, 0))),
            pl.BlockSpec(memory_space=pl.ANY),
        ],
        out_shape=[
            jax.ShapeDtypeStruct((scatter.rows, scatter.count * COLS), F32),
            jax.ShapeDtypeStruct((2, half, d), BF),
        ],
        scratch_shapes=[
            pltpu.VMEM((d, 2 * half), BF),
            pltpu.VMEM((half, d), BF),
            pltpu.VMEM((half, d), BF),
            pltpu.VMEM((d, LANES), BF),
            pltpu.SemaphoreType.DMA((2,)),
            pltpu.SemaphoreType.DMA((4, QUARTERS)),
            pltpu.SemaphoreType.DMA,
        ]
        + scatter.scratch(),
        compiler_params=remote_settings(0),
        cost_estimate=cost(12 * half * d * per * COLS, 20 * half * d),
        name="ffn_scatter",
    )(*normed, *cots, *rights, *parts, gain_block)


def attention_scatter_kernel(scatter, per, *refs):
    normed_ref, gm_ref, right_ref, attended_ref, part_ref, gain_ref = refs[:6]
    out_ref, got_part = refs[6:8]
    turned_ref, gain_got, gain_sems, x_sems = refs[8:12]
    scatter.bind(refs[12:])
    step = pl.program_id(0)
    side = scatter.side
    piece_rows = 384

    def part_copy():
        return pltpu.make_async_remote_copy(
            src_ref=part_ref.at[1 - side],
            dst_ref=got_part,
            send_sem=x_sems.at[0],
            recv_sem=x_sems.at[1],
            device_id=(scatter.me, 1 - side),
            device_id_type=MESH,
        )

    @pl.when(step == 0)
    def _():
        scatter.barrier()
        part_copy().start()
        gain_copy(scatter, gain_ref, gain_got, gain_sems).start()
        turn_into(turned_ref, [normed_ref])

    @pl.when(step == 3 * per)
    def _():
        turn_into(turned_ref, [gm_ref])

    scatter.advance(step, out_ref)
    slot = step % 2

    @pl.when(step < 3 * per)
    def _():
        for r in range(0, turned_ref.shape[0], piece_rows):
            scatter.put(slot, r, nn(turned_ref[r : r + piece_rows, :], right_ref[0]))
        scatter.copy(0, slot).start()

    @pl.when((step >= 3 * per) & (step < 4 * per))
    def _():
        for r in range(0, turned_ref.shape[0], piece_rows):
            scatter.put(slot, r, nn(turned_ref[r : r + piece_rows, :], attended_ref[...]))
        scatter.copy(0, slot).start()

    @pl.when(step == 4 * per)
    def _():
        gain_copy(scatter, gain_ref, gain_got, gain_sems).wait()
        scatter.put_gain(slot, gain_ref, gain_got)
        scatter.copy(0, slot).start()

    @pl.when(step == scatter.steps - 1)
    def _():
        part_copy().wait()


def attention_scatter(devices, normed, gm, grads, attended, part, gain_block):
    length, d = normed.shape
    per = grads.shape[2] // COLS
    scatter = Scatter(devices, d // devices, 4 * per + 1)

    def right_map(j):
        c = jnp.minimum(j, 3 * per - 1)
        return (c // per, 0, c % per)

    def attended_map(j):
        return (0, jnp.clip(j - 3 * per, 0, per - 1))

    first = scatter.starts[-1]
    return pl.pallas_call(
        functools.partial(attention_scatter_kernel, scatter, per),
        grid=(scatter.steps,),
        in_specs=[
            resident((length, d)),
            resident((length, d)),
            pl.BlockSpec((1, length, COLS), right_map),
            pl.BlockSpec((length, COLS), attended_map),
            pl.BlockSpec(memory_space=pl.ANY),
            resident((d, LANES)),
        ],
        out_specs=[
            pl.BlockSpec((scatter.rows, COLS), lambda j: (0, jnp.maximum(j - first, 0))),
            pl.BlockSpec(memory_space=pl.ANY),
        ],
        out_shape=[
            jax.ShapeDtypeStruct((scatter.rows, scatter.count * COLS), F32),
            jax.ShapeDtypeStruct((length // 2, d), BF),
        ],
        scratch_shapes=[
            pltpu.VMEM((d, length), BF),
            pltpu.VMEM((d, LANES), BF),
            pltpu.SemaphoreType.DMA((2,)),
            pltpu.SemaphoreType.DMA((2,)),
        ]
        + scatter.scratch(),
        compiler_params=remote_settings(1),
        cost_estimate=cost(8 * length * d * per * COLS, 20 * length * d),
        name="attention_scatter",
    )(normed, gm, grads, attended, part, gain_block)


def swap(x):
    return lax.ppermute(x, "tensor", [(0, 1), (1, 0)])


def body(
    tokens,
    parents,
    attn_gain,
    ffn_gain,
    query_weight,
    key_weight,
    value_weight,
    output_weight,
    gate_weight,
    up_weight,
    down_weight,
    cotangent,
):
    half, d = tokens.shape
    length = 2 * half
    width = query_weight.shape[1]
    hidden_width = gate_weight.shape[1]
    seg_rows = length // parents.shape[1]
    mine = lax.axis_index("tensor")
    own_start = mine * half
    other_start = (1 - mine) * half

    def place(own, other):
        full = jnp.zeros((length, own.shape[1]), own.dtype)
        full = lax.dynamic_update_slice(full, own, (own_start, 0))
        return lax.dynamic_update_slice(full, other, (other_start, 0))

    def own_rows(full):
        return lax.dynamic_slice_in_dim(full, own_start, half, 0)

    def other_rows(full):
        return lax.dynamic_slice_in_dim(full, other_start, half, 0)

    def gather(shard):
        return lax.all_gather(shard, "dp", axis=0, tiled=True)

    attn_row = attn_gain[None, :]
    ffn_row = ffn_gain[None, :]

    first = gather(
        jnp.concatenate([query_weight, key_weight, value_weight, output_weight.T], axis=1)
    )
    second = gather(jnp.concatenate([gate_weight, up_weight, down_weight.T], axis=1))
    devices = lax.axis_size("dp")

    bias, positions = tree_tables(parents[0], seg_rows)
    cosine, sine = turn_tables(positions, COLS)
    rows_all = place(tokens, swap(tokens))
    cot_other = swap(cotangent)

    qkv, normed_one = project(rows_all, attn_row, cosine, sine, first, width)
    attended, lse = attend(qkv, bias, width, seg_rows)
    out_turned = first[:, 3 * width :]
    send = nt(other_rows(attended), out_turned).astype(BF)
    received = swap(send)
    middle = (
        tokens.astype(F32) + nt(own_rows(attended), out_turned) + received.astype(F32)
    ).astype(BF)
    middle_other = swap(middle)

    gg_own, normed_own, part_own, gp_own = ffn(
        middle, cotangent, ffn_row, second, 0, hidden_width
    )
    gg_other, normed_other, part_other, gp_other = ffn(
        middle_other, cot_other, ffn_row, second, 0, hidden_width
    )

    def gain_block(gain_sum):
        return jnp.broadcast_to(gain_sum.astype(BF).T, (d, LANES))

    ffn_grads, grad_middle = ffn_scatter(
        devices,
        (normed_own, normed_other),
        (cotangent, cot_other),
        (gg_own, gg_other),
        (part_own, part_other),
        gain_block(gp_own + gp_other),
    )
    grad_middle_all = grad_middle.reshape(length, d)

    down_turned = second[:, 2 * hidden_width :]
    out_received = swap(nt(gg_other[2], down_turned).astype(BF))
    block_out = (
        middle.astype(F32) + nt(gg_own[2], down_turned) + out_received.astype(F32)
    ).astype(BF)

    grad_attended = nn(grad_middle_all, out_turned).astype(BF)
    grads = attend_back(
        qkv, attended, grad_attended, lse, bias, cosine[:, :LANES], sine[:, :LANES], seg_rows
    )
    part, gain_part = input_grad(rows_all, attn_row, grads, first)
    attn_grads, tokens_received = attention_scatter(
        devices, normed_one, grad_middle_all, grads, attended, part, gain_block(gain_part)
    )
    token_grad = (
        lax.dynamic_index_in_dim(grad_middle, mine, 0, False).astype(F32)
        + lax.dynamic_index_in_dim(part, mine, 0, False).astype(F32)
        + tokens_received.astype(F32)
    ).astype(BF)
    gain_rows = d // devices // 2

    def gain_piece(columns):
        return lax.dynamic_slice_in_dim(columns[:, 0], mine * gain_rows, gain_rows, 0)

    def column(grads_out, kind, size):
        return grads_out[:, kind * size : (kind + 1) * size]

    return (
        block_out,
        token_grad,
        column(attn_grads, 0, width),
        column(attn_grads, 1, width),
        column(attn_grads, 2, width),
        column(attn_grads, 3, width).T,
        column(ffn_grads, 0, hidden_width),
        column(ffn_grads, 1, hidden_width),
        column(ffn_grads, 2, hidden_width).T,
        gain_piece(attn_grads[:, 4 * width :]),
        gain_piece(ffn_grads[:, 3 * hidden_width :]),
    )


def solution(mesh):
    rows = P(("dp", "tensor"), None)
    tall = P("dp", "tensor")
    wide = P("tensor", "dp")
    return jax.shard_map(
        body,
        mesh=mesh,
        in_specs=(
            rows, P("dp", None), P(), P(), tall, tall, tall, wide, tall, tall, wide, rows,
        ),
        out_specs=(
            rows, rows, tall, tall, tall, wide, tall, tall, wide,
            P(("dp", "tensor")), P(("dp", "tensor")),
        ),
        check_vma=False,
    )
```

```python
import functools
import math

import jax
import jax.numpy as jnp
from jax import lax
from jax.experimental import pallas as pl
from jax.experimental.pallas import tpu as pltpu
from jax.sharding import PartitionSpec as P

HD = 64
EPS = 1e-05
BF = jnp.bfloat16
F32 = jnp.float32
COLS = 256
LANES = 128
MASKED = -1e30


def settings(mib=48):
    return pltpu.CompilerParams(
        dimension_semantics=("arbitrary",), vmem_limit_bytes=mib * 1024 * 1024
    )


def cost(flops, bytes_accessed, transcendentals=0):
    return pl.CostEstimate(
        flops=int(flops), bytes_accessed=int(bytes_accessed), transcendentals=int(transcendentals)
    )


def nn(a, b):
    return jnp.dot(a, b, preferred_element_type=F32)


def nt(a, b):
    return lax.dot_general(a, b, (((1,), (1,)), ((), ())), preferred_element_type=F32)


def tree_tables(parent_row, seg_rows):
    segs = parent_row.shape[0]
    index = jnp.arange(segs, dtype=jnp.int32)
    step_up = (parent_row[:, None] == index[None, :]).astype(jnp.int32)
    eye = (index[:, None] == index[None, :]).astype(jnp.int32)
    reach = eye
    for _ in range(segs):
        up = jnp.sum(step_up[:, :, None] * reach[None, :, :], axis=1)
        reach = jnp.minimum(eye + up, 1)
    depths = jnp.sum(reach, axis=1) - 1
    bias = jnp.where(reach.T > 0, 0.0, MASKED).astype(F32)
    bias = jnp.repeat(bias, seg_rows, axis=1)
    rows = jnp.arange(segs * seg_rows, dtype=jnp.int32)
    positions = jnp.repeat(depths * seg_rows, seg_rows) + rows % seg_rows
    return bias, positions.astype(F32)


def turn_tables(positions, width):
    half = HD // 2
    rates = jnp.exp(jnp.arange(half, dtype=F32) * (-2.0 * math.log(10000.0) / HD))
    angles = positions[:, None] * rates[None, :]
    cosine, sine = jnp.cos(angles), jnp.sin(angles)
    heads = width // HD
    return (
        jnp.tile(jnp.concatenate([cosine, cosine], axis=1), (1, heads)),
        jnp.tile(jnp.concatenate([-sine, sine], axis=1), (1, heads)),
    )


def turn(x, cosine, sine):
    width = x.shape[1]
    lane = lax.broadcasted_iota(jnp.int32, x.shape, 1)
    first = (lane % HD) < HD // 2
    other = jnp.where(
        first, pltpu.roll(x, width - HD // 2, 1), pltpu.roll(x, HD // 2, 1)
    )
    return x * cosine + other * sine


def inverse_rms(x):
    return lax.rsqrt(jnp.mean(x * x, axis=1, keepdims=True) + EPS)


def norm_rows(x_ref, gain_ref, normed_ref):
    chunk = 128

    @pl.loop(0, x_ref.shape[0] // chunk)
    def _(i):
        span = pl.ds(i * chunk, chunk)
        x = x_ref[span, :].astype(F32)
        normed_ref[span, :] = (x * inverse_rms(x) * gain_ref[...]).astype(BF)


def project_kernel(parts, x_ref, gain_ref, cos_ref, sin_ref, w_ref, out_ref, normed_ref):
    j = pl.program_id(0)
    rows = x_ref.shape[0]
    chunk = 256

    @pl.when(j == 0)
    def _():
        norm_rows(x_ref, gain_ref, normed_ref)

    @pl.when(j < 2 * parts)
    def _():
        scale = jnp.where(j < parts, 1.0 / math.sqrt(HD), 1.0).astype(BF)
        for r in range(0, rows, chunk):
            pre = nn(normed_ref[r : r + chunk, :], w_ref[...])
            rotated = turn(pre, cos_ref[r : r + chunk, :], sin_ref[r : r + chunk, :])
            out_ref[r : r + chunk, :] = rotated.astype(BF) * scale

    @pl.when(j >= 2 * parts)
    def _():
        for r in range(0, rows, chunk):
            out_ref[r : r + chunk, :] = nn(normed_ref[r : r + chunk, :], w_ref[...]).astype(BF)


def project(x, gain, cosine, sine, w, width):
    rows, d = x.shape
    parts = width // COLS
    whole = lambda j: (0, 0)
    return pl.pallas_call(
        functools.partial(project_kernel, parts),
        grid=(3 * parts,),
        in_specs=[
            pl.BlockSpec((rows, d), whole),
            pl.BlockSpec((1, d), whole),
            pl.BlockSpec((rows, COLS), whole),
            pl.BlockSpec((rows, COLS), whole),
            pl.BlockSpec((d, COLS), lambda j: (0, j)),
        ],
        out_specs=[
            pl.BlockSpec((rows, COLS), lambda j: (0, j)),
            pl.BlockSpec((rows, d), whole),
        ],
        out_shape=[
            jax.ShapeDtypeStruct((rows, 3 * width), BF),
            jax.ShapeDtypeStruct((rows, d), BF),
        ],
        compiler_params=settings(),
        cost_estimate=cost(6 * rows * d * width, 2 * (2 * rows * d + 3 * d * width)),
        name="project",
    )(x, gain, cosine, sine, w)


def mask_block(block, seg_rows, bias_ref, m, u):
    cols = slice(m * block, (m + 1) * block)
    per = block // seg_rows
    return jnp.concatenate(
        [
            jnp.broadcast_to(bias_ref[u * per + i : u * per + i + 1, cols], (seg_rows, block))
            for i in range(per)
        ],
        axis=0,
    )


def causal(block):
    key = lax.broadcasted_iota(jnp.int32, (block, block), 0)
    query = lax.broadcasted_iota(jnp.int32, (block, block), 1)
    return key <= query


def attend_kernel(block, seg_rows, q_ref, k_ref, v_ref, bias_ref, out_ref, lse_ref):
    length = q_ref.shape[0]
    heads = q_ref.shape[1] // HD
    v_turned = v_ref[...].T
    for m in range(length // block):
        cols = slice(m * block, (m + 1) * block)
        outs = []
        for h in range(heads):
            lanes = slice(h * HD, (h + 1) * HD)
            q = q_ref[cols, lanes]
            scores = []
            for u in range(m + 1):
                s = nt(k_ref[u * block : (u + 1) * block, lanes], q)
                s = s + mask_block(block, seg_rows, bias_ref, m, u)
                if u == m:
                    s = jnp.where(causal(block), s, MASKED)
                scores.append(s)
            peak = scores[0].max(axis=0, keepdims=True)
            for s in scores[1:]:
                peak = jnp.maximum(peak, s.max(axis=0, keepdims=True))
            total = jnp.zeros_like(peak)
            acc = jnp.zeros((HD, block), F32)
            for u, s in enumerate(scores):
                e = jnp.exp(s - peak)
                total = total + e.sum(axis=0, keepdims=True)
                acc = acc + nn(v_turned[lanes, u * block : (u + 1) * block], e.astype(BF))
            outs.append(acc / total)
            lse_ref[0, h : h + 1, cols] = peak + jnp.log(total)
        out_ref[cols, :] = jnp.concatenate(outs, axis=0).T.astype(BF)


def attend(qkv, bias, width, seg_rows):
    length = qkv.shape[0]
    groups = width // LANES
    heads = LANES // HD
    block = 2 * seg_rows
    live = length * length // 2
    return pl.pallas_call(
        functools.partial(attend_kernel, block, seg_rows),
        grid=(groups,),
        in_specs=[
            pl.BlockSpec((length, LANES), lambda i: (0, i)),
            pl.BlockSpec((length, LANES), lambda i: (0, groups + i)),
            pl.BlockSpec((length, LANES), lambda i: (0, 2 * groups + i)),
            pl.BlockSpec(bias.shape, lambda i: (0, 0)),
        ],
        out_specs=[
            pl.BlockSpec((length, LANES), lambda i: (0, i)),
            pl.BlockSpec((1, heads, length), lambda i: (i, 0, 0)),
        ],
        out_shape=[
            jax.ShapeDtypeStruct((length, width), BF),
            jax.ShapeDtypeStruct((groups, heads, length), F32),
        ],
        compiler_params=settings(),
        cost_estimate=cost(16 * live * width, 8 * length * width, live * width // HD),
        name="attend",
    )(qkv, qkv, qkv, bias)


def attend_back_kernel(
    block,
    seg_rows,
    q_ref,
    k_ref,
    v_ref,
    o_ref,
    do_ref,
    lse_ref,
    bias_ref,
    cos_ref,
    sin_ref,
    out_ref,
    dk_ref,
    dv_ref,
):
    length = q_ref.shape[0]
    heads = q_ref.shape[1] // HD
    k_turned = k_ref[...].T
    product = (do_ref[...].astype(F32) * o_ref[...].astype(F32)).T
    deltas = [product[h * HD : (h + 1) * HD].sum(axis=0, keepdims=True) for h in range(heads)]
    for m in range(length // block):
        cols = slice(m * block, (m + 1) * block)
        grads = []
        for h in range(heads):
            lanes = slice(h * HD, (h + 1) * HD)
            q, do = q_ref[cols, lanes], do_ref[cols, lanes]
            lse = lse_ref[0, h : h + 1, cols]
            delta = deltas[h][:, cols]
            acc = jnp.zeros((HD, block), F32)
            for u in range(m + 1):
                keys = slice(u * block, (u + 1) * block)
                s = nt(k_ref[keys, lanes], q)
                p = jnp.exp(s + (mask_block(block, seg_rows, bias_ref, m, u) - lse))
                if u == m:
                    p = jnp.where(causal(block), p, 0.0)
                dp = nt(v_ref[keys, lanes], do)
                ds = (p * (dp - delta)).astype(BF)
                dv = nn(p.astype(BF), do)
                dk = nn(ds, q)
                if u == m:
                    dv_ref[h, keys, :] = dv
                    dk_ref[h, keys, :] = dk
                else:
                    dv_ref[h, keys, :] += dv
                    dk_ref[h, keys, :] += dk
                acc = acc + nn(k_turned[lanes, keys], ds)
            grads.append(acc)
        dq = jnp.concatenate(grads, axis=0).T * (1.0 / math.sqrt(HD))
        out_ref[0, cols, :] = turn(dq, cos_ref[cols, :], -sin_ref[cols, :]).astype(BF)
    for m in range(length // block):
        cols = slice(m * block, (m + 1) * block)
        dk = jnp.concatenate([dk_ref[h, cols, :] for h in range(heads)], axis=1)
        out_ref[1, cols, :] = turn(dk, cos_ref[cols, :], -sin_ref[cols, :]).astype(BF)
        out_ref[2, cols, :] = jnp.concatenate(
            [dv_ref[h, cols, :] for h in range(heads)], axis=1
        ).astype(BF)


def attend_back(qkv, attended, grad_attended, lse, bias, cosine, sine, seg_rows):
    length, width = attended.shape
    groups = width // LANES
    heads = LANES // HD
    block = 2 * seg_rows
    live = length * length // 2
    return pl.pallas_call(
        functools.partial(attend_back_kernel, block, seg_rows),
        grid=(groups,),
        in_specs=[
            pl.BlockSpec((length, LANES), lambda i: (0, i)),
            pl.BlockSpec((length, LANES), lambda i: (0, groups + i)),
            pl.BlockSpec((length, LANES), lambda i: (0, 2 * groups + i)),
            pl.BlockSpec((length, LANES), lambda i: (0, i)),
            pl.BlockSpec((length, LANES), lambda i: (0, i)),
            pl.BlockSpec((1, heads, length), lambda i: (i, 0, 0)),
            pl.BlockSpec(bias.shape, lambda i: (0, 0)),
            pl.BlockSpec((length, LANES), lambda i: (0, 0)),
            pl.BlockSpec((length, LANES), lambda i: (0, 0)),
        ],
        out_specs=pl.BlockSpec((3, length, LANES), lambda i: (0, 0, i)),
        out_shape=jax.ShapeDtypeStruct((3, length, width), BF),
        scratch_shapes=[
            pltpu.VMEM((heads, length, HD), F32),
            pltpu.VMEM((heads, length, HD), F32),
        ],
        compiler_params=settings(),
        cost_estimate=cost(40 * live * width, 16 * length * width, live * width // HD),
        name="attend_back",
    )(qkv, qkv, qkv, attended, grad_attended, lse, bias, cosine, sine)


def rms_back(grad, x, gain):
    inverse = inverse_rms(x)
    unit = x * inverse
    scaled = grad * gain
    inner = jnp.mean(scaled * unit, axis=1, keepdims=True)
    return inverse * (scaled - unit * inner), jnp.sum(grad * unit, axis=0, keepdims=True)


def back_rows(acc_ref, x_ref, gain_ref, gain_part_ref, part_ref):
    chunk = 128
    gain_part_ref[...] = jnp.zeros_like(gain_part_ref)

    @pl.loop(0, x_ref.shape[0] // chunk)
    def _(i):
        span = pl.ds(i * chunk, chunk)
        part, piece = rms_back(acc_ref[span, :], x_ref[span, :].astype(F32), gain_ref[...])
        part_ref[span, :] = part.astype(BF)
        gain_part_ref[...] += piece


def ffn_kernel(
    x_ref,
    cot_ref,
    gain_ref,
    wg_ref,
    wu_ref,
    wd_ref,
    grads_ref,
    normed_ref,
    part_ref,
    gain_part_ref,
    acc_ref,
):
    j = pl.program_id(0)
    rows = x_ref.shape[0]
    chunk = 256

    @pl.when(j == 0)
    def _():
        norm_rows(x_ref, gain_ref, normed_ref)
        acc_ref[...] = jnp.zeros_like(acc_ref)

    @pl.loop(0, rows // chunk)
    def _(i):
        span = pl.ds(i * chunk, chunk)
        gate = nn(normed_ref[span, :], wg_ref[...])
        up = nn(normed_ref[span, :], wu_ref[...])
        grad_hidden = nn(cot_ref[span, :], wd_ref[...])
        sig = jax.nn.sigmoid(gate)
        silu = gate * sig
        grads_ref[2, span, :] = (silu * up).astype(BF)
        grad_gate = (grad_hidden * up * sig * (1.0 + gate * (1.0 - sig))).astype(BF)
        grad_up = (grad_hidden * silu).astype(BF)
        grads_ref[0, span, :] = grad_gate
        grads_ref[1, span, :] = grad_up
        acc_ref[span, :] += nt(grad_gate, wg_ref[...]) + nt(grad_up, wu_ref[...])

    @pl.when(j == pl.num_programs(0) - 1)
    def _():
        back_rows(acc_ref, x_ref, gain_ref, gain_part_ref, part_ref)


def ffn(x, cot, gain, w, start, hidden_width):
    rows, d = x.shape
    steps = hidden_width // COLS
    first = start // COLS
    whole = lambda j: (0, 0)
    return pl.pallas_call(
        ffn_kernel,
        grid=(steps,),
        in_specs=[
            pl.BlockSpec((rows, d), whole),
            pl.BlockSpec((rows, d), whole),
            pl.BlockSpec((1, d), whole),
            pl.BlockSpec((d, COLS), lambda j: (0, first + j)),
            pl.BlockSpec((d, COLS), lambda j: (0, first + steps + j)),
            pl.BlockSpec((d, COLS), lambda j: (0, first + 2 * steps + j)),
        ],
        out_specs=[
            pl.BlockSpec((3, rows, COLS), lambda j: (0, 0, j)),
            pl.BlockSpec((rows, d), whole),
            pl.BlockSpec((rows, d), whole),
            pl.BlockSpec((1, d), whole),
        ],
        out_shape=[
            jax.ShapeDtypeStruct((3, rows, hidden_width), BF),
            jax.ShapeDtypeStruct((rows, d), BF),
            jax.ShapeDtypeStruct((rows, d), BF),
            jax.ShapeDtypeStruct((1, d), F32),
        ],
        scratch_shapes=[pltpu.VMEM((rows, d), F32)],
        compiler_params=settings(),
        cost_estimate=cost(
            10 * rows * d * hidden_width,
            6 * d * hidden_width + 8 * rows * d + 6 * rows * hidden_width,
            rows * hidden_width,
        ),
        name="ffn",
    )(x, cot, gain, w, w, w)


def input_grad_kernel(x_ref, gain_ref, g_ref, w_ref, part_ref, gain_part_ref, acc_ref):
    j = pl.program_id(0)
    chunk = 256

    @pl.when(j == 0)
    def _():
        acc_ref[...] = jnp.zeros_like(acc_ref)

    @pl.loop(0, x_ref.shape[0] // chunk)
    def _(i):
        span = pl.ds(i * chunk, chunk)
        acc_ref[span, :] += nt(g_ref[0, span, :], w_ref[...])

    @pl.when(j == pl.num_programs(0) - 1)
    def _():
        back_rows(acc_ref, x_ref, gain_ref, gain_part_ref, part_ref)


def input_grad(x, gain, grads, w):
    rows, d = x.shape
    kinds, _, width = grads.shape
    per = width // COLS
    whole = lambda j: (0, 0)
    return pl.pallas_call(
        input_grad_kernel,
        grid=(kinds * per,),
        in_specs=[
            pl.BlockSpec((rows, d), whole),
            pl.BlockSpec((1, d), whole),
            pl.BlockSpec((1, rows, COLS), lambda j: (j // per, 0, j % per)),
            pl.BlockSpec((d, COLS), lambda j: (0, j)),
        ],
        out_specs=[pl.BlockSpec((rows, d), whole), pl.BlockSpec((1, d), whole)],
        out_shape=[
            jax.ShapeDtypeStruct((rows, d), BF),
            jax.ShapeDtypeStruct((1, d), F32),
        ],
        scratch_shapes=[pltpu.VMEM((rows, d), F32)],
        compiler_params=settings(),
        cost_estimate=cost(2 * rows * d * kinds * width, 2 * kinds * width * (rows + d)),
        name="input_grad",
    )(x, gain, grads, w)


MESH = pl.DeviceIdType.MESH
QUARTERS = 4


class Scatter:
    def __init__(self, devices, rows, count):
        self.devices, self.rows, self.count = devices, rows, count
        self.stages = devices.bit_length() - 1
        self.lags = [min(s + 1, 2) for s in range(self.stages)]
        self.slots = [2 * lag for lag in self.lags]
        if self.stages >= 3:
            self.slots[1] = self.slots[2] = 8
        self.starts = [sum(self.lags[:s]) for s in range(self.stages + 1)]
        self.steps = count + self.starts[-1]

    def scratch(self):
        shapes = []
        for s in range(self.stages):
            slots, left = self.slots[s], self.devices >> (s + 1)
            shapes.append(pltpu.VMEM((slots, 2, left, self.rows, COLS), BF))
            shapes.append(pltpu.VMEM((slots, left, self.rows, COLS), BF))
            shapes.append(pltpu.SemaphoreType.DMA((slots,)))
            shapes.append(pltpu.SemaphoreType.DMA((slots,)))
        return shapes

    def bind(self, refs):
        self.held, self.got = refs[0::4], refs[1::4]
        self.sent_sem, self.got_sem = refs[2::4], refs[3::4]
        self.me, self.side = lax.axis_index("dp"), lax.axis_index("tensor")

    def late(self, block):
        return (block % 4) // 3

    def own_bit(self, b):
        return (self.me // (1 << b)) % 2

    def partner(self, b):
        return self.me + (1 - 2 * self.own_bit(b)) * (1 << b)

    def turned(self, s, block):
        if s not in (1, 2) or self.stages < 3:
            return self.own_bit(s), self.partner(s)
        late = self.late(block)
        return (
            self.own_bit(s) * (1 - late) + self.own_bit(3 - s) * late,
            self.partner(s) * (1 - late) + self.partner(3 - s) * late,
        )

    def barrier(self):
        arrived = pltpu.get_barrier_semaphore()
        for b in range(self.stages):
            pl.semaphore_signal(
                arrived, inc=1, device_id=(self.partner(b), self.side), device_id_type=MESH
            )
        pl.semaphore_signal(
            arrived, inc=1, device_id=(self.me, 1 - self.side), device_id_type=MESH
        )
        pl.semaphore_wait(arrived, self.stages + 1)

    def copy(self, s, block):
        slot = block % self.slots[s]
        bit, partner = self.turned(s, block)
        return pltpu.make_async_remote_copy(
            src_ref=self.held[s].at[slot, 1 - bit],
            dst_ref=self.got[s].at[slot],
            send_sem=self.sent_sem[s].at[slot],
            recv_sem=self.got_sem[s].at[slot],
            device_id=(partner, self.side),
            device_id_type=MESH,
        )

    def advance(self, step, emit):
        for s in range(self.stages, 0, -1):
            block = step - self.starts[s]

            @pl.when((block >= 0) & (block < self.count))
            def _():
                slot = block % self.slots[s - 1]
                self.copy(s - 1, block).wait()
                keep, _ = self.turned(s - 1, block)
                held, got = self.held[s - 1], self.got[s - 1]
                if s == self.stages:
                    emit(block, held[slot, keep, 0].astype(F32) + got[slot, 0].astype(F32))
                else:
                    later = block % self.slots[s]
                    late = self.late(block)

                    def add(k, carry):
                        total = held[slot, keep, k].astype(F32) + got[slot, k].astype(F32)
                        bit, rest = k % 2, k // 2
                        if s == 1 and self.stages >= 3:
                            bit = bit * (1 - late) + (k // 2) % 2 * late
                            rest = rest * (1 - late) + (k // 4 * 2 + k % 2) * late
                        self.held[s][later, bit, rest] = total.astype(BF)
                        return carry

                    lax.fori_loop(0, self.devices >> s, add, 0)
                    self.copy(s, block).start()

    def multiply(self, block, turned_ref, rights):
        slot = block % self.slots[0]
        pieces = 4
        size = self.devices // pieces

        def piece(i, carry):
            span = pl.ds(i * size * self.rows, size * self.rows)
            total, start = None, 0
            for right in rights:
                part = nn(turned_ref[span, start : start + right.shape[0]], right)
                total = part if total is None else total + part
                start += right.shape[0]
            for r in range(size):
                block_rows = total[r * self.rows : (r + 1) * self.rows].astype(BF)
                self.held[0][slot, r % 2, i * (size // 2) + r // 2] = block_rows
            return carry

        lax.fori_loop(0, pieces, piece, 0)
        self.copy(0, block).start()

    def put_gain(self, block, mine_ref, other_ref):
        slot = block % self.slots[0]
        for k in range(self.devices):
            span = slice(k * self.rows, (k + 1) * self.rows)
            total = mine_ref[span, :].astype(F32) + other_ref[span, :].astype(F32)
            total = jnp.concatenate([total] * (COLS // LANES), axis=1)
            self.held[0][slot, k % 2, k // 2] = total.astype(BF)
        self.copy(0, block).start()


def turn_into(turned_ref, lefts):
    start = 0
    for left in lefts:
        for r in range(0, left.shape[0], 256):

            @pl.loop(0, left.shape[1] // 256)
            def _(i):
                span = pl.ds(pl.multiple_of(i * 256, 256), 256)
                turned_ref[span, start + r : start + r + 256] = left[r : r + 256, span].T

        start += left.shape[0]


def gain_copy(scatter, gain_ref, got_ref, sems):
    return pltpu.make_async_remote_copy(
        src_ref=gain_ref,
        dst_ref=got_ref,
        send_sem=sems.at[0],
        recv_sem=sems.at[1],
        device_id=(scatter.me, 1 - scatter.side),
        device_id_type=MESH,
    )


def emit_into(outs, per, turned, block, value):
    for kind, out in enumerate(outs):
        first, last = kind * per, (kind + 1) * per

        @pl.when((block >= first) & (block < last))
        def _():
            out[...] = value.T if kind in turned else value


def emit_specs(scatter, kinds, per, width, turned):
    lead = scatter.starts[-1]
    specs, shapes = [], []
    for kind in range(kinds + 1):
        most = per - 1 if kind < kinds else 0

        def where(j, kind=kind, most=most):
            return jnp.clip(j - lead - kind * per, 0, most)

        if kind in turned:
            specs.append(pl.BlockSpec((COLS, scatter.rows), lambda j, f=where: (f(j), 0)))
            shapes.append(jax.ShapeDtypeStruct((width, scatter.rows), F32))
        else:
            specs.append(pl.BlockSpec((scatter.rows, COLS), lambda j, f=where: (0, f(j))))
            size = width if kind < kinds else COLS
            shapes.append(jax.ShapeDtypeStruct((scatter.rows, size), F32))
    return specs, shapes


def ffn_scatter_kernel(scatter, per, *refs):
    (
        norm_own, norm_other, cot_own, cot_other, right_own, right_other,
        part_own, part_other, gain_ref, middle_own, wd_ref,
    ) = refs[:11]
    outs, gm_ref, block_out_ref = refs[11:15], refs[15], refs[16]
    (
        turned_ref, got_part, gm_own, gain_got, acc_own, acc_other, block_send, block_got,
        gain_sems, x_sems, block_sems, local_sem,
    ) = refs[17:29]
    scatter.bind(refs[29:])
    step = pl.program_id(0)
    side = scatter.side
    half = part_own.shape[0]
    quarter = half // QUARTERS
    row_chunk = 128

    def part_copy(r):
        span = pl.ds(r * quarter, quarter)
        return pltpu.make_async_remote_copy(
            src_ref=part_other.at[span],
            dst_ref=got_part.at[span],
            send_sem=x_sems.at[0, r],
            recv_sem=x_sems.at[1, r],
            device_id=(scatter.me, 1 - side),
            device_id_type=MESH,
        )

    def gm_copy(r):
        span = pl.ds(r * quarter, quarter)
        return pltpu.make_async_remote_copy(
            src_ref=gm_own.at[span],
            dst_ref=gm_ref.at[side, span],
            send_sem=x_sems.at[2, r],
            recv_sem=x_sems.at[3, r],
            device_id=(scatter.me, 1 - side),
            device_id_type=MESH,
        )

    def block_copy():
        return pltpu.make_async_remote_copy(
            src_ref=block_send,
            dst_ref=block_got,
            send_sem=block_sems.at[0],
            recv_sem=block_sems.at[1],
            device_id=(scatter.me, 1 - side),
            device_id_type=MESH,
        )

    def gm_keep():
        return pltpu.make_async_copy(gm_own, gm_ref.at[side], local_sem)

    @pl.when(step == 0)
    def _():
        scatter.barrier()
        for r in range(QUARTERS):
            part_copy(r).start()
        gain_copy(scatter, gain_ref, gain_got, gain_sems).start()
        turn_into(turned_ref, [cot_own, cot_other])
        acc_own[...] = jnp.zeros_like(acc_own)
        acc_other[...] = jnp.zeros_like(acc_other)

    @pl.when(step == per)
    def _():
        turn_into(turned_ref, [norm_own, norm_other])

    scatter.advance(step, functools.partial(emit_into, outs, per, (0,)))

    @pl.when(step < 3 * per)
    def _():
        scatter.multiply(step, turned_ref, (right_own[0], right_other[0]))

    @pl.when(step == 3 * per)
    def _():
        gain_copy(scatter, gain_ref, gain_got, gain_sems).wait()
        scatter.put_gain(step, gain_ref, gain_got)

    @pl.when(step < per)
    def _():
        @pl.loop(0, half // 256)
        def _(i):
            span = pl.ds(i * 256, 256)
            acc_own[span, :] += nt(right_own[0, span, :], wd_ref[...])
            acc_other[span, :] += nt(right_other[0, span, :], wd_ref[...])

    for r in range(QUARTERS):

        @pl.when(step == 3 + 2 * r)
        def _():
            part_copy(r).wait()

            @pl.loop(r * quarter // row_chunk, (r + 1) * quarter // row_chunk)
            def _(i):
                span = pl.ds(i * row_chunk, row_chunk)
                total = cot_own[span, :].astype(F32) + part_own[span, :].astype(F32)
                gm_own[span, :] = (total + got_part[span, :].astype(F32)).astype(BF)

            gm_copy(r).start()
            if r == QUARTERS - 1:
                gm_keep().start()

    @pl.when(step == 3 + 2 * QUARTERS)
    def _():
        block_send[...] = acc_other[...].astype(BF)
        block_copy().start()

    @pl.when(step == scatter.steps - 1)
    def _():
        for r in range(QUARTERS):
            gm_copy(r).wait()
        gm_keep().wait()
        block_copy().wait()

        @pl.loop(0, half // row_chunk)
        def _(i):
            span = pl.ds(i * row_chunk, row_chunk)
            total = middle_own[span, :].astype(F32) + acc_own[span, :]
            block_out_ref[span, :] = (total + block_got[span, :].astype(F32)).astype(BF)


def resident(shape):
    zeros = (0,) * len(shape)
    return pl.BlockSpec(shape, lambda j: zeros, pipeline_mode=pl.Buffered(1))


def remote_settings(identity, mib=56):
    return pltpu.CompilerParams(
        dimension_semantics=("arbitrary",),
        vmem_limit_bytes=mib * 1024 * 1024,
        collective_id=identity,
        has_side_effects=True,
    )


def ffn_scatter(devices, normed, cots, rights, parts, gain_block, middle, w):
    half, d = middle.shape
    width = rights[0].shape[2]
    per = width // COLS
    scatter = Scatter(devices, d // devices, 3 * per + 1)
    assert per >= 3 + 2 * QUARTERS - 3 and scatter.rows * devices == d

    def right_map(j):
        c = jnp.minimum(j, 3 * per - 1)
        return ((c // per + 2) % 3, 0, c % per)

    specs, shapes = emit_specs(scatter, 3, per, width, (0,))
    whole = lambda j: (0, 0)
    return pl.pallas_call(
        functools.partial(ffn_scatter_kernel, scatter, per),
        grid=(scatter.steps,),
        in_specs=[resident((half, d))] * 4
        + [pl.BlockSpec((1, half, COLS), right_map)] * 2
        + [
            resident((half, d)),
            pl.BlockSpec(memory_space=pl.ANY),
            resident((d, LANES)),
            resident((half, d)),
            pl.BlockSpec((d, COLS), lambda j: (0, 2 * per + jnp.minimum(j, per - 1))),
        ],
        out_specs=specs + [pl.BlockSpec(memory_space=pl.ANY), pl.BlockSpec((half, d), whole)],
        out_shape=shapes
        + [jax.ShapeDtypeStruct((2, half, d), BF), jax.ShapeDtypeStruct((half, d), BF)],
        scratch_shapes=[
            pltpu.VMEM((d, 2 * half), BF),
            pltpu.VMEM((half, d), BF),
            pltpu.VMEM((half, d), BF),
            pltpu.VMEM((d, LANES), BF),
            pltpu.VMEM((half, d), F32),
            pltpu.VMEM((half, d), F32),
            pltpu.VMEM((half, d), BF),
            pltpu.VMEM((half, d), BF),
            pltpu.SemaphoreType.DMA((2,)),
            pltpu.SemaphoreType.DMA((4, QUARTERS)),
            pltpu.SemaphoreType.DMA((2,)),
            pltpu.SemaphoreType.DMA,
        ]
        + scatter.scratch(),
        compiler_params=remote_settings(0),
        cost_estimate=cost(16 * half * d * per * COLS, 20 * half * d),
        name="ffn_scatter",
    )(*normed, *cots, *rights, *parts, gain_block, middle, w)


def attention_scatter_kernel(scatter, per, *refs):
    normed_ref, gm_ref, right_ref, attended_ref, part_ref, gain_ref = refs[:6]
    outs, got_part = refs[6:11], refs[11]
    turned_ref, gain_got, gain_sems, x_sems = refs[12:16]
    scatter.bind(refs[16:])
    step = pl.program_id(0)
    side = scatter.side

    def part_copy():
        return pltpu.make_async_remote_copy(
            src_ref=part_ref.at[1 - side],
            dst_ref=got_part,
            send_sem=x_sems.at[0],
            recv_sem=x_sems.at[1],
            device_id=(scatter.me, 1 - side),
            device_id_type=MESH,
        )

    @pl.when(step == 0)
    def _():
        scatter.barrier()
        part_copy().start()
        gain_copy(scatter, gain_ref, gain_got, gain_sems).start()
        turn_into(turned_ref, [normed_ref])

    @pl.when(step == 3 * per)
    def _():
        turn_into(turned_ref, [gm_ref])

    scatter.advance(step, functools.partial(emit_into, outs, per, (3,)))

    @pl.when(step < 3 * per)
    def _():
        scatter.multiply(step, turned_ref, (right_ref[0],))

    @pl.when((step >= 3 * per) & (step < 4 * per))
    def _():
        scatter.multiply(step, turned_ref, (attended_ref[...],))

    @pl.when(step == 4 * per)
    def _():
        gain_copy(scatter, gain_ref, gain_got, gain_sems).wait()
        scatter.put_gain(step, gain_ref, gain_got)

    @pl.when(step == scatter.steps - 1)
    def _():
        part_copy().wait()


def attention_scatter(devices, normed, gm, grads, attended, part, gain_block):
    length, d = normed.shape
    width = grads.shape[2]
    per = width // COLS
    scatter = Scatter(devices, d // devices, 4 * per + 1)

    def right_map(j):
        c = jnp.minimum(j, 3 * per - 1)
        return (c // per, 0, c % per)

    def attended_map(j):
        return (0, jnp.clip(j - 3 * per, 0, per - 1))

    specs, shapes = emit_specs(scatter, 4, per, width, (3,))
    return pl.pallas_call(
        functools.partial(attention_scatter_kernel, scatter, per),
        grid=(scatter.steps,),
        in_specs=[
            resident((length, d)),
            resident((length, d)),
            pl.BlockSpec((1, length, COLS), right_map),
            pl.BlockSpec((length, COLS), attended_map),
            pl.BlockSpec(memory_space=pl.ANY),
            resident((d, LANES)),
        ],
        out_specs=specs + [pl.BlockSpec(memory_space=pl.ANY)],
        out_shape=shapes + [jax.ShapeDtypeStruct((length // 2, d), BF)],
        scratch_shapes=[
            pltpu.VMEM((d, length), BF),
            pltpu.VMEM((d, LANES), BF),
            pltpu.SemaphoreType.DMA((2,)),
            pltpu.SemaphoreType.DMA((2,)),
        ]
        + scatter.scratch(),
        compiler_params=remote_settings(1),
        cost_estimate=cost(8 * length * d * per * COLS, 20 * length * d),
        name="attention_scatter",
    )(normed, gm, grads, attended, part, gain_block)


def swap(x):
    return lax.ppermute(x, "tensor", [(0, 1), (1, 0)])


def body(
    tokens,
    parents,
    attn_gain,
    ffn_gain,
    query_weight,
    key_weight,
    value_weight,
    output_weight,
    gate_weight,
    up_weight,
    down_weight,
    cotangent,
):
    half, d = tokens.shape
    length = 2 * half
    width = query_weight.shape[1]
    hidden_width = gate_weight.shape[1]
    seg_rows = length // parents.shape[1]
    mine = lax.axis_index("tensor")
    own_start = mine * half
    other_start = (1 - mine) * half

    def place(own, other):
        full = jnp.zeros((length, own.shape[1]), own.dtype)
        full = lax.dynamic_update_slice(full, own, (own_start, 0))
        return lax.dynamic_update_slice(full, other, (other_start, 0))

    def own_rows(full):
        return lax.dynamic_slice_in_dim(full, own_start, half, 0)

    def other_rows(full):
        return lax.dynamic_slice_in_dim(full, other_start, half, 0)

    def gather(shard):
        return lax.all_gather(shard, "dp", axis=0, tiled=True)

    attn_row = attn_gain[None, :]
    ffn_row = ffn_gain[None, :]

    first = gather(
        jnp.concatenate([query_weight, key_weight, value_weight, output_weight.T], axis=1)
    )
    second = gather(jnp.concatenate([gate_weight, up_weight, down_weight.T], axis=1))
    devices = lax.axis_size("dp")

    bias, positions = tree_tables(parents[0], seg_rows)
    cosine, sine = turn_tables(positions, COLS)
    rows_all, cot_other = lax.optimization_barrier(
        (place(tokens, swap(tokens)), swap(cotangent))
    )

    qkv, normed_one = project(rows_all, attn_row, cosine, sine, first, width)
    attended, lse = attend(qkv, bias, width, seg_rows)
    out_turned = first[:, 3 * width :]
    send = nt(other_rows(attended), out_turned).astype(BF)
    received = swap(send)
    middle = (
        tokens.astype(F32) + nt(own_rows(attended), out_turned) + received.astype(F32)
    ).astype(BF)
    middle_other = swap(middle)

    gg_own, normed_own, part_own, gp_own = ffn(
        middle, cotangent, ffn_row, second, 0, hidden_width
    )
    gg_other, normed_other, part_other, gp_other = ffn(
        middle_other, cot_other, ffn_row, second, 0, hidden_width
    )

    def gain_block(gain_sum):
        return jnp.broadcast_to(gain_sum.astype(BF).T, (d, LANES))

    down_grad, gate_grad, up_grad, ffn_gain_grad, grad_middle, block_out = ffn_scatter(
        devices,
        (normed_own, normed_other),
        (cotangent, cot_other),
        (gg_own, gg_other),
        (part_own, part_other),
        gain_block(gp_own + gp_other),
        middle,
        second,
    )
    grad_middle_all = grad_middle.reshape(length, d)

    grad_attended = nn(grad_middle_all, out_turned).astype(BF)
    grads = attend_back(
        qkv, attended, grad_attended, lse, bias, cosine[:, :LANES], sine[:, :LANES], seg_rows
    )
    part, gain_part = input_grad(rows_all, attn_row, grads, first)
    part = part.reshape(2, half, d)
    query_grad, key_grad, value_grad, output_grad, attn_gain_grad, received = attention_scatter(
        devices, normed_one, grad_middle_all, grads, attended, part, gain_block(gain_part)
    )
    token_grad = (
        lax.dynamic_index_in_dim(grad_middle, mine, 0, False).astype(F32)
        + lax.dynamic_index_in_dim(part, mine, 0, False).astype(F32)
        + received.astype(F32)
    ).astype(BF)
    gain_rows = d // devices // 2

    def gain_piece(columns):
        return lax.dynamic_slice_in_dim(columns[:, 0], mine * gain_rows, gain_rows, 0)

    return (
        block_out,
        token_grad,
        query_grad,
        key_grad,
        value_grad,
        output_grad,
        gate_grad,
        up_grad,
        down_grad,
        gain_piece(attn_gain_grad),
        gain_piece(ffn_gain_grad),
    )


def solution(mesh):
    rows = P(("dp", "tensor"), None)
    tall = P("dp", "tensor")
    wide = P("tensor", "dp")
    return jax.shard_map(
        body,
        mesh=mesh,
        in_specs=(
            rows, P("dp", None), P(), P(), tall, tall, tall, wide, tall, tall, wide, rows,
        ),
        out_specs=(
            rows, rows, tall, tall, tall, wide, tall, tall, wide,
            P(("dp", "tensor")), P(("dp", "tensor")),
        ),
        check_vma=False,
    )
```

```python
import functools
import math

import jax
import jax.numpy as jnp
from jax import lax
from jax.experimental import pallas as pl
from jax.experimental.pallas import tpu as pltpu
from jax.sharding import PartitionSpec as P

HD = 64
EPS = 1e-05
BF = jnp.bfloat16
F32 = jnp.float32
COLS = 256
LANES = 128
MASKED = -1e30


def settings(mib=48):
    return pltpu.CompilerParams(
        dimension_semantics=("arbitrary",), vmem_limit_bytes=mib * 1024 * 1024
    )


def cost(flops, bytes_accessed, transcendentals=0):
    return pl.CostEstimate(
        flops=int(flops), bytes_accessed=int(bytes_accessed), transcendentals=int(transcendentals)
    )


def nn(a, b):
    return jnp.dot(a, b, preferred_element_type=F32)


def nt(a, b):
    return lax.dot_general(a, b, (((1,), (1,)), ((), ())), preferred_element_type=F32)


def tree_tables(parent_row, seg_rows):
    segs = parent_row.shape[0]
    index = jnp.arange(segs, dtype=jnp.int32)
    step_up = (parent_row[:, None] == index[None, :]).astype(jnp.int32)
    eye = (index[:, None] == index[None, :]).astype(jnp.int32)
    reach = eye
    for _ in range(segs):
        up = jnp.sum(step_up[:, :, None] * reach[None, :, :], axis=1)
        reach = jnp.minimum(eye + up, 1)
    depths = jnp.sum(reach, axis=1) - 1
    bias = jnp.where(reach.T > 0, 0.0, MASKED).astype(F32)
    bias = jnp.repeat(bias, seg_rows, axis=1)
    rows = jnp.arange(segs * seg_rows, dtype=jnp.int32)
    positions = jnp.repeat(depths * seg_rows, seg_rows) + rows % seg_rows
    return bias, positions.astype(F32)


def turn_tables(positions, width):
    half = HD // 2
    rates = jnp.exp(jnp.arange(half, dtype=F32) * (-2.0 * math.log(10000.0) / HD))
    angles = positions[:, None] * rates[None, :]
    cosine, sine = jnp.cos(angles), jnp.sin(angles)
    heads = width // HD
    return (
        jnp.tile(jnp.concatenate([cosine, cosine], axis=1), (1, heads)),
        jnp.tile(jnp.concatenate([-sine, sine], axis=1), (1, heads)),
    )


def turn(x, cosine, sine):
    width = x.shape[1]
    lane = lax.broadcasted_iota(jnp.int32, x.shape, 1)
    first = (lane % HD) < HD // 2
    other = jnp.where(
        first, pltpu.roll(x, width - HD // 2, 1), pltpu.roll(x, HD // 2, 1)
    )
    return x * cosine + other * sine


def inverse_rms(x):
    return lax.rsqrt(jnp.mean(x * x, axis=1, keepdims=True) + EPS)


def norm_rows(x_ref, gain_ref, normed_ref):
    chunk = 128

    @pl.loop(0, x_ref.shape[0] // chunk)
    def _(i):
        span = pl.ds(i * chunk, chunk)
        x = x_ref[span, :].astype(F32)
        normed_ref[span, :] = (x * inverse_rms(x) * gain_ref[...]).astype(BF)


def project_kernel(parts, x_ref, gain_ref, cos_ref, sin_ref, w_ref, out_ref, normed_ref):
    j = pl.program_id(0)
    rows = x_ref.shape[0]
    chunk = 256

    @pl.when(j == 0)
    def _():
        norm_rows(x_ref, gain_ref, normed_ref)

    @pl.when(j < 2 * parts)
    def _():
        scale = jnp.where(j < parts, 1.0 / math.sqrt(HD), 1.0).astype(BF)
        for r in range(0, rows, chunk):
            pre = nn(normed_ref[r : r + chunk, :], w_ref[...])
            rotated = turn(pre, cos_ref[r : r + chunk, :], sin_ref[r : r + chunk, :])
            out_ref[r : r + chunk, :] = rotated.astype(BF) * scale

    @pl.when(j >= 2 * parts)
    def _():
        for r in range(0, rows, chunk):
            out_ref[r : r + chunk, :] = nn(normed_ref[r : r + chunk, :], w_ref[...]).astype(BF)


def project(x, gain, cosine, sine, w, width):
    rows, d = x.shape
    parts = width // COLS
    whole = lambda j: (0, 0)
    return pl.pallas_call(
        functools.partial(project_kernel, parts),
        grid=(3 * parts,),
        in_specs=[
            pl.BlockSpec((rows, d), whole),
            pl.BlockSpec((1, d), whole),
            pl.BlockSpec((rows, COLS), whole),
            pl.BlockSpec((rows, COLS), whole),
            pl.BlockSpec((d, COLS), lambda j: (0, j)),
        ],
        out_specs=[
            pl.BlockSpec((rows, COLS), lambda j: (0, j)),
            pl.BlockSpec((rows, d), whole),
        ],
        out_shape=[
            jax.ShapeDtypeStruct((rows, 3 * width), BF),
            jax.ShapeDtypeStruct((rows, d), BF),
        ],
        compiler_params=settings(),
        cost_estimate=cost(6 * rows * d * width, 2 * (2 * rows * d + 3 * d * width)),
        name="project",
    )(x, gain, cosine, sine, w)


def mask_block(block, seg_rows, bias_ref, m, u):
    cols = slice(m * block, (m + 1) * block)
    per = block // seg_rows
    return jnp.concatenate(
        [
            jnp.broadcast_to(bias_ref[u * per + i : u * per + i + 1, cols], (seg_rows, block))
            for i in range(per)
        ],
        axis=0,
    )


def causal(block):
    key = lax.broadcasted_iota(jnp.int32, (block, block), 0)
    query = lax.broadcasted_iota(jnp.int32, (block, block), 1)
    return key <= query


def attend_kernel(block, seg_rows, q_ref, k_ref, v_ref, bias_ref, out_ref, lse_ref):
    length = q_ref.shape[0]
    heads = q_ref.shape[1] // HD
    v_turned = v_ref[...].T
    for m in range(length // block):
        cols = slice(m * block, (m + 1) * block)
        outs = []
        for h in range(heads):
            lanes = slice(h * HD, (h + 1) * HD)
            q = q_ref[cols, lanes]
            scores = []
            for u in range(m + 1):
                s = nt(k_ref[u * block : (u + 1) * block, lanes], q)
                s = s + mask_block(block, seg_rows, bias_ref, m, u)
                if u == m:
                    s = jnp.where(causal(block), s, MASKED)
                scores.append(s)
            peak = scores[0].max(axis=0, keepdims=True)
            for s in scores[1:]:
                peak = jnp.maximum(peak, s.max(axis=0, keepdims=True))
            total = jnp.zeros_like(peak)
            acc = jnp.zeros((HD, block), F32)
            for u, s in enumerate(scores):
                e = jnp.exp(s - peak)
                total = total + e.sum(axis=0, keepdims=True)
                acc = acc + nn(v_turned[lanes, u * block : (u + 1) * block], e.astype(BF))
            outs.append(acc / total)
            lse_ref[0, h : h + 1, cols] = peak + jnp.log(total)
        out_ref[cols, :] = jnp.concatenate(outs, axis=0).T.astype(BF)


def attend(qkv, bias, width, seg_rows):
    length = qkv.shape[0]
    groups = width // LANES
    heads = LANES // HD
    block = 2 * seg_rows
    live = length * length // 2
    return pl.pallas_call(
        functools.partial(attend_kernel, block, seg_rows),
        grid=(groups,),
        in_specs=[
            pl.BlockSpec((length, LANES), lambda i: (0, i)),
            pl.BlockSpec((length, LANES), lambda i: (0, groups + i)),
            pl.BlockSpec((length, LANES), lambda i: (0, 2 * groups + i)),
            pl.BlockSpec(bias.shape, lambda i: (0, 0)),
        ],
        out_specs=[
            pl.BlockSpec((length, LANES), lambda i: (0, i)),
            pl.BlockSpec((1, heads, length), lambda i: (i, 0, 0)),
        ],
        out_shape=[
            jax.ShapeDtypeStruct((length, width), BF),
            jax.ShapeDtypeStruct((groups, heads, length), F32),
        ],
        compiler_params=settings(),
        cost_estimate=cost(16 * live * width, 8 * length * width, live * width // HD),
        name="attend",
    )(qkv, qkv, qkv, bias)


def attend_back_kernel(
    block,
    seg_rows,
    q_ref,
    k_ref,
    v_ref,
    o_ref,
    do_ref,
    lse_ref,
    bias_ref,
    cos_ref,
    sin_ref,
    out_ref,
    dk_ref,
    dv_ref,
):
    length = q_ref.shape[0]
    heads = q_ref.shape[1] // HD
    k_turned = k_ref[...].T
    product = (do_ref[...].astype(F32) * o_ref[...].astype(F32)).T
    deltas = [product[h * HD : (h + 1) * HD].sum(axis=0, keepdims=True) for h in range(heads)]
    for m in range(length // block):
        cols = slice(m * block, (m + 1) * block)
        grads = []
        for h in range(heads):
            lanes = slice(h * HD, (h + 1) * HD)
            q, do = q_ref[cols, lanes], do_ref[cols, lanes]
            lse = lse_ref[0, h : h + 1, cols]
            delta = deltas[h][:, cols]
            acc = jnp.zeros((HD, block), F32)
            for u in range(m + 1):
                keys = slice(u * block, (u + 1) * block)
                s = nt(k_ref[keys, lanes], q)
                p = jnp.exp(s + (mask_block(block, seg_rows, bias_ref, m, u) - lse))
                if u == m:
                    p = jnp.where(causal(block), p, 0.0)
                dp = nt(v_ref[keys, lanes], do)
                ds = (p * (dp - delta)).astype(BF)
                dv = nn(p.astype(BF), do)
                dk = nn(ds, q)
                if u == m:
                    dv_ref[h, keys, :] = dv
                    dk_ref[h, keys, :] = dk
                else:
                    dv_ref[h, keys, :] += dv
                    dk_ref[h, keys, :] += dk
                acc = acc + nn(k_turned[lanes, keys], ds)
            grads.append(acc)
        dq = jnp.concatenate(grads, axis=0).T * (1.0 / math.sqrt(HD))
        out_ref[0, cols, :] = turn(dq, cos_ref[cols, :], -sin_ref[cols, :]).astype(BF)
    for m in range(length // block):
        cols = slice(m * block, (m + 1) * block)
        dk = jnp.concatenate([dk_ref[h, cols, :] for h in range(heads)], axis=1)
        out_ref[1, cols, :] = turn(dk, cos_ref[cols, :], -sin_ref[cols, :]).astype(BF)
        out_ref[2, cols, :] = jnp.concatenate(
            [dv_ref[h, cols, :] for h in range(heads)], axis=1
        ).astype(BF)


def attend_back(qkv, attended, grad_attended, lse, bias, cosine, sine, seg_rows):
    length, width = attended.shape
    groups = width // LANES
    heads = LANES // HD
    block = 2 * seg_rows
    live = length * length // 2
    return pl.pallas_call(
        functools.partial(attend_back_kernel, block, seg_rows),
        grid=(groups,),
        in_specs=[
            pl.BlockSpec((length, LANES), lambda i: (0, i)),
            pl.BlockSpec((length, LANES), lambda i: (0, groups + i)),
            pl.BlockSpec((length, LANES), lambda i: (0, 2 * groups + i)),
            pl.BlockSpec((length, LANES), lambda i: (0, i)),
            pl.BlockSpec((length, LANES), lambda i: (0, i)),
            pl.BlockSpec((1, heads, length), lambda i: (i, 0, 0)),
            pl.BlockSpec(bias.shape, lambda i: (0, 0)),
            pl.BlockSpec((length, LANES), lambda i: (0, 0)),
            pl.BlockSpec((length, LANES), lambda i: (0, 0)),
        ],
        out_specs=pl.BlockSpec((3, length, LANES), lambda i: (0, 0, i)),
        out_shape=jax.ShapeDtypeStruct((3, length, width), BF),
        scratch_shapes=[
            pltpu.VMEM((heads, length, HD), F32),
            pltpu.VMEM((heads, length, HD), F32),
        ],
        compiler_params=settings(),
        cost_estimate=cost(40 * live * width, 16 * length * width, live * width // HD),
        name="attend_back",
    )(qkv, qkv, qkv, attended, grad_attended, lse, bias, cosine, sine)


def rms_back(grad, x, gain):
    inverse = inverse_rms(x)
    unit = x * inverse
    scaled = grad * gain
    inner = jnp.mean(scaled * unit, axis=1, keepdims=True)
    return inverse * (scaled - unit * inner), jnp.sum(grad * unit, axis=0, keepdims=True)


def back_rows(acc_ref, x_ref, gain_ref, gain_part_ref, part_ref):
    chunk = 128

    @pl.loop(0, x_ref.shape[0] // chunk)
    def _(i):
        span = pl.ds(i * chunk, chunk)
        part, piece = rms_back(acc_ref[span, :], x_ref[span, :].astype(F32), gain_ref[...])
        part_ref[span, :] = part.astype(part_ref.dtype)
        gain_part_ref[...] += jnp.broadcast_to(piece, gain_part_ref.shape)


def ffn_kernel(
    x_own,
    x_other,
    cot_own,
    cot_other,
    gain_ref,
    wg_ref,
    wu_ref,
    wd_ref,
    grads_ref,
    normed_ref,
    part_ref,
    gain_part_ref,
    cot_ref,
    acc_ref,
):
    h, j = pl.program_id(0), pl.program_id(1)
    chunk = 256

    @pl.when((h == 0) & (j == 0))
    def _():
        gain_part_ref[...] = jnp.zeros_like(gain_part_ref)

    for side, (x_ref, c_ref) in enumerate(((x_own, cot_own), (x_other, cot_other))):

        @pl.when((h == side) & (j == 0))
        def _():
            norm_rows(x_ref, gain_ref, normed_ref)
            cot_ref[...] = c_ref[...]

    @pl.when(j == 0)
    def _():
        acc_ref[...] = jnp.zeros_like(acc_ref)

    for r in range(0, cot_ref.shape[0], chunk):
        span = slice(r, r + chunk)
        gate = nn(normed_ref[span, :], wg_ref[...])
        up = nn(normed_ref[span, :], wu_ref[...])
        grad_hidden = nn(cot_ref[span, :], wd_ref[...])
        sig = jax.nn.sigmoid(gate)
        silu = gate * sig
        grads_ref[2, span, :] = (silu * up).astype(BF)
        grad_gate = (grad_hidden * up * (sig + silu * (1.0 - sig))).astype(BF)
        grad_up = (grad_hidden * silu).astype(BF)
        grads_ref[0, span, :] = grad_gate
        grads_ref[1, span, :] = grad_up
        acc_ref[span, :] += nt(grad_gate, wg_ref[...]) + nt(grad_up, wu_ref[...])

    for side, x_ref in enumerate((x_own, x_other)):

        @pl.when((h == side) & (j == pl.num_programs(1) - 1))
        def _():
            back_rows(acc_ref, x_ref, gain_ref, gain_part_ref, part_ref)


def resident(shape):
    zeros = (0,) * len(shape)
    return pl.BlockSpec(shape, lambda *grid: zeros, pipeline_mode=pl.Buffered(1))


def ffn(xs, cots, gain, w, hidden_width, cols=512):
    rows, d = xs[0].shape
    steps = hidden_width // cols
    per_half = lambda h, j: (h, 0, 0)
    return pl.pallas_call(
        ffn_kernel,
        grid=(2, steps),
        in_specs=[resident((rows, d))] * 4
        + [
            resident((1, d)),
            pl.BlockSpec((d, cols), lambda h, j: (0, j)),
            pl.BlockSpec((d, cols), lambda h, j: (0, steps + j)),
            pl.BlockSpec((d, cols), lambda h, j: (0, 2 * steps + j)),
        ],
        out_specs=[
            pl.BlockSpec((None, 3, rows, cols), lambda h, j: (h, 0, 0, j)),
            pl.BlockSpec((None, rows, d), per_half),
            pl.BlockSpec((None, rows, d), per_half),
            pl.BlockSpec((8, d), lambda h, j: (0, 0)),
        ],
        out_shape=[
            jax.ShapeDtypeStruct((2, 3, rows, hidden_width), BF),
            jax.ShapeDtypeStruct((2, rows, d), BF),
            jax.ShapeDtypeStruct((2, rows, d), BF),
            jax.ShapeDtypeStruct((8, d), F32),
        ],
        scratch_shapes=[pltpu.VMEM((rows, d), BF), pltpu.VMEM((rows, d), F32)],
        compiler_params=pltpu.CompilerParams(
            dimension_semantics=("arbitrary", "arbitrary"), vmem_limit_bytes=56 * 1024 * 1024
        ),
        cost_estimate=cost(
            20 * rows * d * hidden_width,
            12 * d * hidden_width + 16 * rows * d + 12 * rows * hidden_width,
            2 * rows * hidden_width,
        ),
        name="ffn",
    )(*xs, *cots, gain, w, w, w)


MESH = pl.DeviceIdType.MESH
QUARTERS = 4


class Scatter:
    def __init__(self, devices, rows, count):
        self.devices, self.rows, self.count = devices, rows, count
        self.stages = devices.bit_length() - 1
        self.lags = [min(s + 1, 2) for s in range(self.stages)]
        self.slots = [2 * lag for lag in self.lags]
        if self.stages >= 3:
            self.slots[1] = self.slots[2] = 8
        self.starts = [sum(self.lags[:s]) for s in range(self.stages + 1)]
        self.steps = count + self.starts[-1]

    def scratch(self):
        shapes = []
        for s in range(self.stages):
            slots, left = self.slots[s], self.devices >> (s + 1)
            shapes.append(pltpu.VMEM((slots, 2, left, self.rows, COLS), BF))
            shapes.append(pltpu.VMEM((slots, left, self.rows, COLS), BF))
            shapes.append(pltpu.SemaphoreType.DMA((slots,)))
            shapes.append(pltpu.SemaphoreType.DMA((slots,)))
        return shapes

    def bind(self, refs):
        self.held, self.got = refs[0::4], refs[1::4]
        self.sent_sem, self.got_sem = refs[2::4], refs[3::4]
        self.me, self.side = lax.axis_index("dp"), lax.axis_index("tensor")

    def late(self, block):
        return (block % 4) // 3

    def own_bit(self, b):
        return (self.me // (1 << b)) % 2

    def partner(self, b):
        return self.me + (1 - 2 * self.own_bit(b)) * (1 << b)

    def turned(self, s, block):
        if s not in (1, 2) or self.stages < 3:
            return self.own_bit(s), self.partner(s)
        late = self.late(block)
        return (
            self.own_bit(s) * (1 - late) + self.own_bit(3 - s) * late,
            self.partner(s) * (1 - late) + self.partner(3 - s) * late,
        )

    def barrier(self):
        arrived = pltpu.get_barrier_semaphore()
        for b in range(self.stages):
            pl.semaphore_signal(
                arrived, inc=1, device_id=(self.partner(b), self.side), device_id_type=MESH
            )
        pl.semaphore_signal(
            arrived, inc=1, device_id=(self.me, 1 - self.side), device_id_type=MESH
        )
        pl.semaphore_wait(arrived, self.stages + 1)

    def copy(self, s, block):
        slot = block % self.slots[s]
        bit, partner = self.turned(s, block)
        return pltpu.make_async_remote_copy(
            src_ref=self.held[s].at[slot, 1 - bit],
            dst_ref=self.got[s].at[slot],
            send_sem=self.sent_sem[s].at[slot],
            recv_sem=self.got_sem[s].at[slot],
            device_id=(partner, self.side),
            device_id_type=MESH,
        )

    def advance(self, step, emit):
        for s in range(self.stages, 0, -1):
            block = step - self.starts[s]

            @pl.when((block >= 0) & (block < self.count))
            def _():
                slot = block % self.slots[s - 1]
                self.copy(s - 1, block).wait()
                keep, _ = self.turned(s - 1, block)
                held, got = self.held[s - 1], self.got[s - 1]
                if s == self.stages:
                    emit(block, held[slot, keep, 0].astype(F32) + got[slot, 0].astype(F32))
                else:
                    later = block % self.slots[s]
                    late = self.late(block)

                    def add(k, carry):
                        total = held[slot, keep, k] + got[slot, k]
                        bit, rest = k % 2, k // 2
                        if s == 1 and self.stages >= 3:
                            bit = bit * (1 - late) + (k // 2) % 2 * late
                            rest = rest * (1 - late) + (k // 4 * 2 + k % 2) * late
                        self.held[s][later, bit, rest] = total
                        return carry

                    lax.fori_loop(0, self.devices >> s, add, 0)
                    self.copy(s, block).start()

    def multiply(self, block, turned_ref, rights):
        slot = block % self.slots[0]
        pieces = 4
        size = self.devices // pieces

        def piece(i, carry):
            span = pl.ds(i * size * self.rows, size * self.rows)
            total, start = None, 0
            for right in rights:
                part = nn(turned_ref[span, start : start + right.shape[0]], right[...])
                total = part if total is None else total + part
                start += right.shape[0]
            for r in range(size):
                block_rows = total[r * self.rows : (r + 1) * self.rows].astype(BF)
                self.held[0][slot, r % 2, i * (size // 2) + r // 2] = block_rows
            return carry

        lax.fori_loop(0, pieces, piece, 0)
        self.copy(0, block).start()

    def put_gain(self, block, mine, other):
        slot = block % self.slots[0]
        column = jnp.broadcast_to(mine + other, (LANES, mine.shape[1])).T.astype(BF)
        for k in range(self.devices):
            rows = column[k * self.rows : (k + 1) * self.rows, :]
            wide = jnp.concatenate([rows] * (COLS // LANES), axis=1)
            self.held[0][slot, k % 2, k // 2] = wide
        self.copy(0, block).start()


def turn_into(turned_ref, lefts):
    start = 0
    for left in lefts:
        for r in range(0, left.shape[0], 256):

            @pl.loop(0, left.shape[1] // 256)
            def _(i):
                span = pl.ds(pl.multiple_of(i * 256, 256), 256)
                turned_ref[span, start + r : start + r + 256] = left[r : r + 256, span].T

        start += left.shape[0]


def gain_copy(scatter, gain_ref, got_ref, sems):
    return pltpu.make_async_remote_copy(
        src_ref=gain_ref,
        dst_ref=got_ref,
        send_sem=sems.at[0],
        recv_sem=sems.at[1],
        device_id=(scatter.me, 1 - scatter.side),
        device_id_type=MESH,
    )


def emit_into(outs, per, block, value):
    for kind, out in enumerate(outs):

        @pl.when((block >= kind * per) & (block < (kind + 1) * per))
        def _():
            out[...] = value


def emit_specs(scatter, kinds, per, width):
    lead = scatter.starts[-1]
    specs, shapes = [], []
    for kind in range(kinds + 1):
        most, size = (per - 1, width) if kind < kinds else (0, COLS)

        def where(j, first=lead + kind * per, most=most):
            return (0, jnp.clip(j - first, 0, most))

        specs.append(pl.BlockSpec((scatter.rows, COLS), where))
        shapes.append(jax.ShapeDtypeStruct((scatter.rows, size), F32))
    return specs, shapes


def remote(src, dst, sems, device):
    return pltpu.make_async_remote_copy(
        src_ref=src,
        dst_ref=dst,
        send_sem=sems.at[0],
        recv_sem=sems.at[1],
        device_id=device,
        device_id_type=MESH,
    )


def ffn_scatter_kernel(scatter, per, *refs):
    (
        norm_own, norm_other, cot_own, cot_other, right_own, right_other, gate_own, gate_other,
        part_own, part_other, gain_ref, middle_own, wd_ref,
    ) = refs[:13]
    outs = refs[13:16]
    gate_ref, gm_ref, block_own, block_send = refs[16:20]
    (
        cot_turned, norm_turned, got_part, gm_own, gain_got, acc_other,
        gain_sems, part_sems, gm_sems, local_sem,
    ) = refs[20:30]
    scatter.bind(refs[30:])
    step = pl.program_id(0)
    side = scatter.side
    across = (scatter.me, 1 - side)
    half = part_own.shape[0]
    quarter = half // QUARTERS
    row_chunk = 128

    def part_copy(r):
        span = pl.ds(r * quarter, quarter)
        return remote(part_other.at[1, span], got_part.at[span], part_sems.at[r], across)

    def gm_copy(r):
        span = pl.ds(r * quarter, quarter)
        return remote(gm_own.at[span], gm_ref.at[side, span], gm_sems.at[r], across)

    def gain_copy():
        return remote(gain_ref, gain_got, gain_sems, across)

    def gm_keep():
        return pltpu.make_async_copy(gm_own, gm_ref.at[side], local_sem)

    @pl.when(step == 0)
    def _():
        scatter.barrier()
        for r in range(QUARTERS):
            part_copy(r).start()
        gain_copy().start()
        turn_into(cot_turned, [cot_own, cot_other])
        block_own[...] = jnp.zeros_like(block_own)
        acc_other[...] = jnp.zeros_like(acc_other)

    @pl.when(step == 1)
    def _():
        turn_into(norm_turned, [norm_own, norm_other])

    scatter.advance(step, functools.partial(emit_into, outs, per))

    @pl.when(step < per)
    def _():
        scatter.multiply(step, cot_turned, (right_own, right_other))

        @pl.loop(0, half // 256)
        def _(i):
            span = pl.ds(i * 256, 256)
            block_own[span, :] += nt(right_own[span, :], wd_ref[...])
            acc_other[span, :] += nt(right_other[span, :], wd_ref[...])

    @pl.when((step >= per) & (step < 2 * per))
    def _():
        scatter.multiply(step, norm_turned, (right_own, right_other))

    @pl.when(step == 2 * per)
    def _():
        gain_copy().wait()
        scatter.put_gain(step, gain_ref[0:1, :], gain_got[0:1, :])

    @pl.when((step % 2 == 1) & (step < 2 * per))
    def _():
        rows = gate_ref.shape[0] // 4

        @pl.loop(0, 4)
        def _(i):
            span = pl.ds(i * rows, rows)
            total = nn(norm_turned[span, :half], gate_own[...])
            gate_ref[span, :] = (total + nn(norm_turned[span, half:], gate_other[...])).astype(BF)

    for r in range(QUARTERS):

        @pl.when(step == 3 + 2 * r)
        def _():
            part_copy(r).wait()

            @pl.loop(r * quarter // row_chunk, (r + 1) * quarter // row_chunk)
            def _(i):
                span = pl.ds(i * row_chunk, row_chunk)
                total = cot_own[span, :].astype(F32) + part_own[span, :].astype(F32)
                gm_own[span, :] = (total + got_part[span, :].astype(F32)).astype(BF)

            gm_copy(r).start()
            if r == QUARTERS - 1:
                gm_keep().start()

    @pl.when(step == per)
    def _():
        @pl.loop(0, half // row_chunk)
        def _(i):
            span = pl.ds(i * row_chunk, row_chunk)
            block_own[span, :] += middle_own[span, :].astype(F32)
            block_send[span, :] = acc_other[span, :].astype(BF)

    @pl.when(step == scatter.steps - 1)
    def _():
        for r in range(QUARTERS):
            gm_copy(r).wait()
        gm_keep().wait()


def remote_settings(identity, mib=60):
    return pltpu.CompilerParams(
        dimension_semantics=("arbitrary",),
        vmem_limit_bytes=mib * 1024 * 1024,
        collective_id=identity,
        has_side_effects=True,
    )


def ffn_scatter(devices, normed, cots, grads, parts, gain_part, middle, w):
    half, d = middle.shape
    width = grads.shape[3]
    per = width // COLS
    scatter = Scatter(devices, d // devices, 2 * per + 1)
    assert 2 * per > 3 + 2 * QUARTERS and scatter.rows * devices == d

    def right(side):
        def where(j):
            c = jnp.minimum(j, 2 * per - 1)
            return (side, 2 - c // per, 0, c % per)

        return pl.BlockSpec((None, None, half, COLS), where)

    def gate_block(j):
        return jnp.clip((j - 1) // 2, 0, per - 1)

    def gate(side):
        return pl.BlockSpec((None, None, half, COLS), lambda j: (side, 0, 0, gate_block(j)))

    def rows_of(side):
        return pl.BlockSpec(
            (None, half, d), lambda j: (side, 0, 0), pipeline_mode=pl.Buffered(1)
        )

    specs, shapes = emit_specs(scatter, 2, per, width)
    whole = lambda j: (0, 0)
    return pl.pallas_call(
        functools.partial(ffn_scatter_kernel, scatter, per),
        grid=(scatter.steps,),
        in_specs=[
            rows_of(0),
            rows_of(1),
            resident((half, d)),
            resident((half, d)),
            right(0),
            right(1),
            gate(0),
            gate(1),
            rows_of(0),
            pl.BlockSpec(memory_space=pl.ANY),
            resident((8, d)),
            resident((half, d)),
            pl.BlockSpec((d, COLS), lambda j: (0, 2 * per + jnp.minimum(j, per - 1))),
        ],
        out_specs=specs
        + [
            pl.BlockSpec((d, COLS), lambda j: (0, gate_block(j))),
            pl.BlockSpec(memory_space=pl.ANY),
            pl.BlockSpec((half, d), whole),
            pl.BlockSpec((half, d), whole),
        ],
        out_shape=shapes
        + [
            jax.ShapeDtypeStruct((d, width), BF),
            jax.ShapeDtypeStruct((2, half, d), BF),
            jax.ShapeDtypeStruct((half, d), F32),
            jax.ShapeDtypeStruct((half, d), BF),
        ],
        scratch_shapes=[
            pltpu.VMEM((d, 2 * half), BF),
            pltpu.VMEM((d, 2 * half), BF),
            pltpu.VMEM((half, d), BF),
            pltpu.VMEM((half, d), BF),
            pltpu.VMEM((8, d), F32),
            pltpu.VMEM((half, d), F32),
            pltpu.SemaphoreType.DMA((2,)),
            pltpu.SemaphoreType.DMA((QUARTERS, 2)),
            pltpu.SemaphoreType.DMA((QUARTERS, 2)),
            pltpu.SemaphoreType.DMA,
        ]
        + scatter.scratch(),
        compiler_params=remote_settings(0),
        cost_estimate=cost(16 * half * d * per * COLS, 20 * half * d),
        name="ffn_scatter",
    )(
        normed, normed, *cots, grads, grads, grads, grads, parts, parts, gain_part, middle, w,
    )


def attention_scatter_kernel(scatter, per, *refs):
    (
        normed_ref, gm_ref, x_ref, gain_ref, right_ref, attended_ref, block_own, block_send,
        first_ref, second_ref, w_first, w_second,
    ) = refs[:12]
    outs = refs[12:17]
    token_grad_ref, block_out_ref = refs[17:19]
    (
        turned_ref, acc_ref, part_send, part_got, block_got, gain_part, gain_got,
        gain_sems, part_sems, block_sems,
    ) = refs[19:29]
    scatter.bind(refs[29:])
    step = pl.program_id(0)
    side = scatter.side
    across = (scatter.me, 1 - side)
    length = x_ref.shape[0]
    half = length // 2
    quarter = half // QUARTERS
    chunk = 128
    kinds = 3 * per
    ready = (kinds + 1) // 2
    own, other = side * half, (1 - side) * half

    def part_copy(r):
        span = pl.ds(r * quarter, quarter)
        return remote(part_send.at[span], part_got.at[span], part_sems.at[r], across)

    def block_copy():
        return remote(block_send, block_got, block_sems, across)

    def gain_copy():
        return remote(gain_part, gain_got, gain_sems, across)

    def back(row):
        span = pl.ds(row, chunk)
        part, piece = rms_back(acc_ref[span, :], x_ref[span, :].astype(F32), gain_ref[...])
        gain_part[...] += jnp.broadcast_to(piece, gain_part.shape)
        return part

    @pl.when(step == 0)
    def _():
        scatter.barrier()
        turn_into(turned_ref, [normed_ref])
        acc_ref[...] = jnp.zeros_like(acc_ref)
        gain_part[...] = jnp.zeros_like(gain_part)

    @pl.when(step == kinds)
    def _():
        turn_into(turned_ref, [gm_ref])

    scatter.advance(step, functools.partial(emit_into, outs, per))

    @pl.when(step < kinds)
    def _():
        scatter.multiply(step, turned_ref, (right_ref,))

    @pl.when((step >= kinds) & (step < 4 * per))
    def _():
        scatter.multiply(step, turned_ref, (attended_ref,))

    for nth, (g_ref, w_ref) in enumerate(((first_ref, w_first), (second_ref, w_second))):

        @pl.when(2 * step + nth < kinds)
        def _():
            @pl.loop(0, length // 256)
            def _(i):
                span = pl.ds(i * 256, 256)
                acc_ref[span, :] += nt(g_ref[span, :], w_ref[...])

    @pl.when(step == ready)
    def _():
        for r in range(QUARTERS):

            @pl.loop(r * quarter // chunk, (r + 1) * quarter // chunk)
            def _(i):
                part_send[pl.ds(i * chunk, chunk), :] = back(other + i * chunk).astype(BF)

            part_copy(r).start()

    @pl.when(step == ready + 1)
    def _():
        @pl.loop(0, half // chunk)
        def _(i):
            span = pl.ds(own + i * chunk, chunk)
            acc_ref[span, :] = back(own + i * chunk) + gm_ref[span, :].astype(F32)

        gain_copy().start()
        block_copy().start()

    @pl.when(step == 4 * per)
    def _():
        gain_copy().wait()
        scatter.put_gain(step, gain_part[0:1, :], gain_got[0:1, :])

    for r in range(QUARTERS):

        @pl.when(step == scatter.steps - 1 - QUARTERS + r)
        def _():
            part_copy(r).wait()

            @pl.loop(r * quarter // chunk, (r + 1) * quarter // chunk)
            def _(i):
                span = pl.ds(i * chunk, chunk)
                total = acc_ref[pl.ds(own + i * chunk, chunk), :]
                token_grad_ref[span, :] = (total + part_got[span, :].astype(F32)).astype(BF)

    @pl.when(step == scatter.steps - 1)
    def _():
        block_copy().wait()

        @pl.loop(0, half // chunk)
        def _(i):
            span = pl.ds(i * chunk, chunk)
            total = block_own[span, :] + block_got[span, :].astype(F32)
            block_out_ref[span, :] = total.astype(BF)


def attention_scatter(
    devices, normed, gm, x, gain, grads, attended, block_own, block_send, w
):
    length, d = normed.shape
    half = length // 2
    width = grads.shape[2]
    per = width // COLS
    kinds = 3 * per
    scatter = Scatter(devices, d // devices, 4 * per + 1)
    assert (kinds + 1) // 2 + 1 < 4 * per and scatter.rows * devices == d

    def grads_spec(pick):
        def where(j):
            c = jnp.minimum(pick(j), kinds - 1)
            return (c // per, 0, c % per)

        return pl.BlockSpec((None, length, COLS), where)

    def weight_spec(pick):
        return pl.BlockSpec((d, COLS), lambda j: (0, jnp.minimum(pick(j), kinds - 1)))

    def attended_map(j):
        return (0, jnp.clip(j - kinds, 0, per - 1))

    specs, shapes = emit_specs(scatter, 4, per, width)
    whole = lambda j: (0, 0)
    even, odd = (lambda j: 2 * j), (lambda j: 2 * j + 1)
    return pl.pallas_call(
        functools.partial(attention_scatter_kernel, scatter, per),
        grid=(scatter.steps,),
        in_specs=[resident((length, d))] * 3
        + [
            resident((1, d)),
            grads_spec(lambda j: j),
            pl.BlockSpec((length, COLS), attended_map),
            resident((half, d)),
            pl.BlockSpec(memory_space=pl.ANY),
            grads_spec(even),
            grads_spec(odd),
            weight_spec(even),
            weight_spec(odd),
        ],
        out_specs=specs + [pl.BlockSpec((half, d), whole), pl.BlockSpec((half, d), whole)],
        out_shape=shapes
        + [jax.ShapeDtypeStruct((half, d), BF), jax.ShapeDtypeStruct((half, d), BF)],
        scratch_shapes=[
            pltpu.VMEM((d, length), BF),
            pltpu.VMEM((length, d), F32),
            pltpu.VMEM((half, d), BF),
            pltpu.VMEM((half, d), BF),
            pltpu.VMEM((half, d), BF),
            pltpu.VMEM((8, d), F32),
            pltpu.VMEM((8, d), F32),
            pltpu.SemaphoreType.DMA((2,)),
            pltpu.SemaphoreType.DMA((QUARTERS, 2)),
            pltpu.SemaphoreType.DMA((2,)),
        ]
        + scatter.scratch(),
        compiler_params=remote_settings(1),
        cost_estimate=cost(14 * length * d * per * COLS, 20 * length * d),
        name="attention_scatter",
    )(normed, gm, x, gain, grads, attended, block_own, block_send, grads, grads, w, w)


def swap(x):
    return lax.ppermute(x, "tensor", [(0, 1), (1, 0)])


def body(
    tokens,
    parents,
    attn_gain,
    ffn_gain,
    query_weight,
    key_weight,
    value_weight,
    output_weight,
    gate_weight,
    up_weight,
    down_weight,
    cotangent,
):
    half, d = tokens.shape
    length = 2 * half
    width = query_weight.shape[1]
    hidden_width = gate_weight.shape[1]
    seg_rows = length // parents.shape[1]
    mine = lax.axis_index("tensor")
    own_start = mine * half
    other_start = (1 - mine) * half

    def place(own, other):
        full = jnp.zeros((length, own.shape[1]), own.dtype)
        full = lax.dynamic_update_slice(full, own, (own_start, 0))
        return lax.dynamic_update_slice(full, other, (other_start, 0))

    def own_rows(full):
        return lax.dynamic_slice_in_dim(full, own_start, half, 0)

    def other_rows(full):
        return lax.dynamic_slice_in_dim(full, other_start, half, 0)

    def gather(shard):
        return lax.all_gather(shard, "dp", axis=0, tiled=True)

    attn_row = attn_gain[None, :]
    ffn_row = ffn_gain[None, :]

    first = gather(
        jnp.concatenate([query_weight, key_weight, value_weight, output_weight.T], axis=1)
    )
    second = gather(jnp.concatenate([gate_weight, up_weight, down_weight.T], axis=1))
    devices = lax.axis_size("dp")

    bias, positions = tree_tables(parents[0], seg_rows)
    cosine, sine = turn_tables(positions, COLS)
    rows_all, cot_other = lax.optimization_barrier(
        (place(tokens, swap(tokens)), swap(cotangent))
    )

    qkv, normed_one = project(rows_all, attn_row, cosine, sine, first, width)
    attended, lse = attend(qkv, bias, width, seg_rows)
    out_turned = first[:, 3 * width :]
    send = nt(other_rows(attended), out_turned).astype(BF)
    received = swap(send)
    middle = (
        tokens.astype(F32) + nt(own_rows(attended), out_turned) + received.astype(F32)
    ).astype(BF)
    middle_other = swap(middle)

    ffn_grads, normed_two, parts, gain_part = ffn(
        (middle, middle_other), (cotangent, cot_other), ffn_row, second, hidden_width
    )
    down_grad, up_grad, ffn_gain_grad, gate_whole, grad_middle, block_own, block_send = ffn_scatter(
        devices,
        normed_two,
        (cotangent, cot_other),
        ffn_grads,
        parts,
        gain_part,
        middle,
        second,
    )
    gate_grad = lax.psum_scatter(gate_whole, "dp", scatter_dimension=0, tiled=True).astype(F32)
    grad_middle = grad_middle.reshape(length, d)

    grad_attended = nn(grad_middle, out_turned).astype(BF)
    grads = attend_back(
        qkv, attended, grad_attended, lse, bias, cosine[:, :LANES], sine[:, :LANES], seg_rows
    )
    (
        query_grad, key_grad, value_grad, output_grad, attn_gain_grad, token_grad, block_out,
    ) = attention_scatter(
        devices,
        normed_one,
        grad_middle,
        rows_all,
        attn_row,
        grads,
        attended,
        block_own,
        block_send,
        first,
    )
    gain_rows = d // devices // 2

    def gain_piece(columns):
        return lax.dynamic_slice_in_dim(columns[:, 0], mine * gain_rows, gain_rows, 0)

    return (
        block_out,
        token_grad,
        query_grad,
        key_grad,
        value_grad,
        output_grad.T,
        gate_grad,
        up_grad,
        down_grad.T,
        gain_piece(attn_gain_grad),
        gain_piece(ffn_gain_grad),
    )


def solution(mesh):
    rows = P(("dp", "tensor"), None)
    tall = P("dp", "tensor")
    wide = P("tensor", "dp")
    return jax.shard_map(
        body,
        mesh=mesh,
        in_specs=(
            rows, P("dp", None), P(), P(), tall, tall, tall, wide, tall, tall, wide, rows,
        ),
        out_specs=(
            rows, rows, tall, tall, tall, wide, tall, tall, wide,
            P(("dp", "tensor")), P(("dp", "tensor")),
        ),
        check_vma=False,
    )
```

```python
import functools
import math

import jax
import jax.numpy as jnp
from jax import lax
from jax.experimental import pallas as pl
from jax.experimental.pallas import tpu as pltpu
from jax.sharding import PartitionSpec as P

HD = 64
EPS = 1e-05
BF = jnp.bfloat16
F32 = jnp.float32
COLS = 256
LANES = 128
MASKED = -1e30


def settings(mib=48):
    return pltpu.CompilerParams(
        dimension_semantics=("arbitrary",), vmem_limit_bytes=mib * 1024 * 1024
    )


def cost(flops, bytes_accessed, transcendentals=0):
    return pl.CostEstimate(
        flops=int(flops), bytes_accessed=int(bytes_accessed), transcendentals=int(transcendentals)
    )


def nn(a, b):
    return jnp.dot(a, b, preferred_element_type=F32)


def nt(a, b):
    return lax.dot_general(a, b, (((1,), (1,)), ((), ())), preferred_element_type=F32)


def tree_tables(parent_row, seg_rows):
    segs = parent_row.shape[0]
    index = jnp.arange(segs, dtype=jnp.int32)
    step_up = (parent_row[:, None] == index[None, :]).astype(jnp.int32)
    eye = (index[:, None] == index[None, :]).astype(jnp.int32)
    reach = eye
    for _ in range(segs):
        up = jnp.sum(step_up[:, :, None] * reach[None, :, :], axis=1)
        reach = jnp.minimum(eye + up, 1)
    depths = jnp.sum(reach, axis=1) - 1
    bias = jnp.where(reach.T > 0, 0.0, MASKED).astype(F32)
    bias = jnp.repeat(bias, seg_rows, axis=1)
    rows = jnp.arange(segs * seg_rows, dtype=jnp.int32)
    positions = jnp.repeat(depths * seg_rows, seg_rows) + rows % seg_rows
    return bias, positions.astype(F32)


def turn_tables(positions, width):
    half = HD // 2
    rates = jnp.exp(jnp.arange(half, dtype=F32) * (-2.0 * math.log(10000.0) / HD))
    angles = positions[:, None] * rates[None, :]
    cosine, sine = jnp.cos(angles), jnp.sin(angles)
    heads = width // HD
    return (
        jnp.tile(jnp.concatenate([cosine, cosine], axis=1), (1, heads)),
        jnp.tile(jnp.concatenate([-sine, sine], axis=1), (1, heads)),
    )


def turn(x, cosine, sine):
    width = x.shape[1]
    lane = lax.broadcasted_iota(jnp.int32, x.shape, 1)
    first = (lane % HD) < HD // 2
    other = jnp.where(
        first, pltpu.roll(x, width - HD // 2, 1), pltpu.roll(x, HD // 2, 1)
    )
    return x * cosine + other * sine


def inverse_rms(x):
    return lax.rsqrt(jnp.mean(x * x, axis=1, keepdims=True) + EPS)


def norm_rows(x_ref, gain_ref, normed_ref):
    chunk = 128

    @pl.loop(0, x_ref.shape[0] // chunk)
    def _(i):
        span = pl.ds(i * chunk, chunk)
        x = x_ref[span, :].astype(F32)
        normed_ref[span, :] = (x * inverse_rms(x) * gain_ref[...]).astype(BF)


def project_kernel(parts, x_ref, gain_ref, cos_ref, sin_ref, w_ref, out_ref, normed_ref):
    j = pl.program_id(0)
    rows = x_ref.shape[0]
    chunk = 256

    @pl.when(j == 0)
    def _():
        norm_rows(x_ref, gain_ref, normed_ref)

    @pl.when(j < 2 * parts)
    def _():
        scale = jnp.where(j < parts, 1.0 / math.sqrt(HD), 1.0).astype(BF)
        for r in range(0, rows, chunk):
            pre = nn(normed_ref[r : r + chunk, :], w_ref[...])
            rotated = turn(pre, cos_ref[r : r + chunk, :], sin_ref[r : r + chunk, :])
            out_ref[r : r + chunk, :] = rotated.astype(BF) * scale

    @pl.when(j >= 2 * parts)
    def _():
        for r in range(0, rows, chunk):
            out_ref[r : r + chunk, :] = nn(normed_ref[r : r + chunk, :], w_ref[...]).astype(BF)


def project(x, gain, cosine, sine, w, width):
    rows, d = x.shape
    parts = width // COLS
    whole = lambda j: (0, 0)
    return pl.pallas_call(
        functools.partial(project_kernel, parts),
        grid=(3 * parts,),
        in_specs=[
            pl.BlockSpec((rows, d), whole),
            pl.BlockSpec((1, d), whole),
            pl.BlockSpec((rows, COLS), whole),
            pl.BlockSpec((rows, COLS), whole),
            pl.BlockSpec((d, COLS), lambda j: (0, j)),
        ],
        out_specs=[
            pl.BlockSpec((rows, COLS), lambda j: (0, j)),
            pl.BlockSpec((rows, d), whole),
        ],
        out_shape=[
            jax.ShapeDtypeStruct((rows, 3 * width), BF),
            jax.ShapeDtypeStruct((rows, d), BF),
        ],
        compiler_params=settings(),
        cost_estimate=cost(6 * rows * d * width, 2 * (2 * rows * d + 3 * d * width)),
        name="project",
    )(x, gain, cosine, sine, w)


def mask_block(block, seg_rows, bias_ref, m, u):
    cols = slice(m * block, (m + 1) * block)
    per = block // seg_rows
    return jnp.concatenate(
        [
            jnp.broadcast_to(bias_ref[u * per + i : u * per + i + 1, cols], (seg_rows, block))
            for i in range(per)
        ],
        axis=0,
    )


def causal(block):
    key = lax.broadcasted_iota(jnp.int32, (block, block), 0)
    query = lax.broadcasted_iota(jnp.int32, (block, block), 1)
    return key <= query


def attend_kernel(block, seg_rows, q_ref, k_ref, v_ref, bias_ref, out_ref, lse_ref):
    length = q_ref.shape[0]
    heads = q_ref.shape[1] // HD
    v_turned = v_ref[...].T
    for m in range(length // block):
        cols = slice(m * block, (m + 1) * block)
        outs = []
        for h in range(heads):
            lanes = slice(h * HD, (h + 1) * HD)
            q = q_ref[cols, lanes]
            scores = []
            for u in range(m + 1):
                s = nt(k_ref[u * block : (u + 1) * block, lanes], q)
                s = s + mask_block(block, seg_rows, bias_ref, m, u)
                if u == m:
                    s = jnp.where(causal(block), s, MASKED)
                scores.append(s)
            peak = scores[0].max(axis=0, keepdims=True)
            for s in scores[1:]:
                peak = jnp.maximum(peak, s.max(axis=0, keepdims=True))
            total = jnp.zeros_like(peak)
            acc = jnp.zeros((HD, block), F32)
            for u, s in enumerate(scores):
                e = jnp.exp(s - peak)
                total = total + e.sum(axis=0, keepdims=True)
                acc = acc + nn(v_turned[lanes, u * block : (u + 1) * block], e.astype(BF))
            outs.append(acc / total)
            lse_ref[0, h : h + 1, cols] = peak + jnp.log(total)
        out_ref[cols, :] = jnp.concatenate(outs, axis=0).T.astype(BF)


def attend(qkv, bias, width, seg_rows):
    length = qkv.shape[0]
    groups = width // LANES
    heads = LANES // HD
    block = 2 * seg_rows
    live = length * length // 2
    return pl.pallas_call(
        functools.partial(attend_kernel, block, seg_rows),
        grid=(groups,),
        in_specs=[
            pl.BlockSpec((length, LANES), lambda i: (0, i)),
            pl.BlockSpec((length, LANES), lambda i: (0, groups + i)),
            pl.BlockSpec((length, LANES), lambda i: (0, 2 * groups + i)),
            pl.BlockSpec(bias.shape, lambda i: (0, 0)),
        ],
        out_specs=[
            pl.BlockSpec((length, LANES), lambda i: (0, i)),
            pl.BlockSpec((1, heads, length), lambda i: (i, 0, 0)),
        ],
        out_shape=[
            jax.ShapeDtypeStruct((length, width), BF),
            jax.ShapeDtypeStruct((groups, heads, length), F32),
        ],
        compiler_params=settings(),
        cost_estimate=cost(16 * live * width, 8 * length * width, live * width // HD),
        name="attend",
    )(qkv, qkv, qkv, bias)


def attend_back_kernel(
    block,
    seg_rows,
    q_ref,
    k_ref,
    v_ref,
    o_ref,
    do_ref,
    lse_ref,
    bias_ref,
    cos_ref,
    sin_ref,
    out_ref,
    dk_ref,
    dv_ref,
):
    length = q_ref.shape[0]
    heads = q_ref.shape[1] // HD
    k_turned = k_ref[...].T
    product = (do_ref[...].astype(F32) * o_ref[...].astype(F32)).T
    deltas = [product[h * HD : (h + 1) * HD].sum(axis=0, keepdims=True) for h in range(heads)]
    for m in range(length // block):
        cols = slice(m * block, (m + 1) * block)
        grads = []
        for h in range(heads):
            lanes = slice(h * HD, (h + 1) * HD)
            q, do = q_ref[cols, lanes], do_ref[cols, lanes]
            lse = lse_ref[0, h : h + 1, cols]
            delta = deltas[h][:, cols]
            acc = jnp.zeros((HD, block), F32)
            for u in range(m + 1):
                keys = slice(u * block, (u + 1) * block)
                s = nt(k_ref[keys, lanes], q)
                p = jnp.exp(s + (mask_block(block, seg_rows, bias_ref, m, u) - lse))
                if u == m:
                    p = jnp.where(causal(block), p, 0.0)
                dp = nt(v_ref[keys, lanes], do)
                ds = (p * (dp - delta)).astype(BF)
                dv = nn(p.astype(BF), do)
                dk = nn(ds, q)
                if u == m:
                    dv_ref[h, keys, :] = dv
                    dk_ref[h, keys, :] = dk
                else:
                    dv_ref[h, keys, :] += dv
                    dk_ref[h, keys, :] += dk
                acc = acc + nn(k_turned[lanes, keys], ds)
            grads.append(acc)
        dq = jnp.concatenate(grads, axis=0).T * (1.0 / math.sqrt(HD))
        out_ref[0, cols, :] = turn(dq, cos_ref[cols, :], -sin_ref[cols, :]).astype(BF)
    for m in range(length // block):
        cols = slice(m * block, (m + 1) * block)
        dk = jnp.concatenate([dk_ref[h, cols, :] for h in range(heads)], axis=1)
        out_ref[1, cols, :] = turn(dk, cos_ref[cols, :], -sin_ref[cols, :]).astype(BF)
        out_ref[2, cols, :] = jnp.concatenate(
            [dv_ref[h, cols, :] for h in range(heads)], axis=1
        ).astype(BF)


def attend_back(qkv, attended, grad_attended, lse, bias, cosine, sine, seg_rows):
    length, width = attended.shape
    groups = width // LANES
    heads = LANES // HD
    block = 2 * seg_rows
    live = length * length // 2
    return pl.pallas_call(
        functools.partial(attend_back_kernel, block, seg_rows),
        grid=(groups,),
        in_specs=[
            pl.BlockSpec((length, LANES), lambda i: (0, i)),
            pl.BlockSpec((length, LANES), lambda i: (0, groups + i)),
            pl.BlockSpec((length, LANES), lambda i: (0, 2 * groups + i)),
            pl.BlockSpec((length, LANES), lambda i: (0, i)),
            pl.BlockSpec((length, LANES), lambda i: (0, i)),
            pl.BlockSpec((1, heads, length), lambda i: (i, 0, 0)),
            pl.BlockSpec(bias.shape, lambda i: (0, 0)),
            pl.BlockSpec((length, LANES), lambda i: (0, 0)),
            pl.BlockSpec((length, LANES), lambda i: (0, 0)),
        ],
        out_specs=pl.BlockSpec((3, length, LANES), lambda i: (0, 0, i)),
        out_shape=jax.ShapeDtypeStruct((3, length, width), BF),
        scratch_shapes=[
            pltpu.VMEM((heads, length, HD), F32),
            pltpu.VMEM((heads, length, HD), F32),
        ],
        compiler_params=settings(),
        cost_estimate=cost(40 * live * width, 16 * length * width, live * width // HD),
        name="attend_back",
    )(qkv, qkv, qkv, attended, grad_attended, lse, bias, cosine, sine)


def rms_back(grad, x, gain):
    inverse = inverse_rms(x)
    unit = x * inverse
    scaled = grad * gain
    inner = jnp.mean(scaled * unit, axis=1, keepdims=True)
    return inverse * (scaled - unit * inner), jnp.sum(grad * unit, axis=0, keepdims=True)


def back_rows(acc_ref, x_ref, gain_ref, gain_part_ref, part_ref):
    chunk = 128

    @pl.loop(0, x_ref.shape[0] // chunk)
    def _(i):
        span = pl.ds(i * chunk, chunk)
        part, piece = rms_back(acc_ref[span, :], x_ref[span, :].astype(F32), gain_ref[...])
        part_ref[span, :] = part.astype(part_ref.dtype)
        gain_part_ref[...] += jnp.broadcast_to(piece, gain_part_ref.shape)


def ffn_kernel(
    x_own,
    x_other,
    cot_own,
    cot_other,
    gain_ref,
    wg_ref,
    wu_ref,
    wd_ref,
    grads_ref,
    normed_ref,
    part_ref,
    gain_part_ref,
    cot_ref,
    acc_ref,
):
    h, j = pl.program_id(0), pl.program_id(1)
    chunk = 256

    @pl.when((h == 0) & (j == 0))
    def _():
        gain_part_ref[...] = jnp.zeros_like(gain_part_ref)

    for side, (x_ref, c_ref) in enumerate(((x_own, cot_own), (x_other, cot_other))):

        @pl.when((h == side) & (j == 0))
        def _():
            norm_rows(x_ref, gain_ref, normed_ref)
            cot_ref[...] = c_ref[...]

    @pl.when(j == 0)
    def _():
        acc_ref[...] = jnp.zeros_like(acc_ref)

    for r in range(0, cot_ref.shape[0], chunk):
        span = slice(r, r + chunk)
        gate = nn(normed_ref[span, :], wg_ref[...])
        up = nn(normed_ref[span, :], wu_ref[...])
        grad_hidden = nn(cot_ref[span, :], wd_ref[...])
        sig = jax.nn.sigmoid(gate)
        silu = gate * sig
        grads_ref[2, span, :] = (silu * up).astype(BF)
        grad_gate = (grad_hidden * up * (sig + silu * (1.0 - sig))).astype(BF)
        grad_up = (grad_hidden * silu).astype(BF)
        grads_ref[0, span, :] = grad_gate
        grads_ref[1, span, :] = grad_up
        acc_ref[span, :] += nt(grad_gate, wg_ref[...]) + nt(grad_up, wu_ref[...])

    for side, x_ref in enumerate((x_own, x_other)):

        @pl.when((h == side) & (j == pl.num_programs(1) - 1))
        def _():
            back_rows(acc_ref, x_ref, gain_ref, gain_part_ref, part_ref)


def resident(shape):
    zeros = (0,) * len(shape)
    return pl.BlockSpec(shape, lambda *grid: zeros, pipeline_mode=pl.Buffered(1))


def ffn(xs, cots, gain, w, hidden_width, cols=512):
    rows, d = xs[0].shape
    steps = hidden_width // cols
    per_half = lambda h, j: (h, 0, 0)
    return pl.pallas_call(
        ffn_kernel,
        grid=(2, steps),
        in_specs=[resident((rows, d))] * 4
        + [
            resident((1, d)),
            pl.BlockSpec((d, cols), lambda h, j: (0, j)),
            pl.BlockSpec((d, cols), lambda h, j: (0, steps + j)),
            pl.BlockSpec((d, cols), lambda h, j: (0, 2 * steps + j)),
        ],
        out_specs=[
            pl.BlockSpec((None, 3, rows, cols), lambda h, j: (h, 0, 0, j)),
            pl.BlockSpec((None, rows, d), per_half),
            pl.BlockSpec((None, rows, d), per_half),
            pl.BlockSpec((8, d), lambda h, j: (0, 0)),
        ],
        out_shape=[
            jax.ShapeDtypeStruct((2, 3, rows, hidden_width), BF),
            jax.ShapeDtypeStruct((2, rows, d), BF),
            jax.ShapeDtypeStruct((2, rows, d), BF),
            jax.ShapeDtypeStruct((8, d), F32),
        ],
        scratch_shapes=[pltpu.VMEM((rows, d), BF), pltpu.VMEM((rows, d), F32)],
        compiler_params=pltpu.CompilerParams(
            dimension_semantics=("arbitrary", "arbitrary"), vmem_limit_bytes=56 * 1024 * 1024
        ),
        cost_estimate=cost(
            20 * rows * d * hidden_width,
            12 * d * hidden_width + 16 * rows * d + 12 * rows * hidden_width,
            2 * rows * hidden_width,
        ),
        name="ffn",
    )(*xs, *cots, gain, w, w, w)


MESH = pl.DeviceIdType.MESH
QUARTERS = 4


class Scatter:
    def __init__(self, devices, rows, count):
        self.devices, self.rows, self.count = devices, rows, count
        self.stages = devices.bit_length() - 1
        self.lags = [min(s + 1, 2) for s in range(self.stages)]
        self.slots = [2 * lag for lag in self.lags]
        if self.stages >= 3:
            self.slots[1] = self.slots[2] = 8
        self.starts = [sum(self.lags[:s]) for s in range(self.stages + 1)]
        self.steps = count + self.starts[-1]

    def scratch(self):
        shapes = []
        for s in range(self.stages):
            slots, left = self.slots[s], self.devices >> (s + 1)
            shapes.append(pltpu.VMEM((slots, 2, left, self.rows, COLS), BF))
            shapes.append(pltpu.VMEM((slots, left, self.rows, COLS), BF))
            shapes.append(pltpu.SemaphoreType.DMA((slots,)))
            shapes.append(pltpu.SemaphoreType.DMA((slots,)))
        return shapes

    def bind(self, refs):
        self.held, self.got = refs[0::4], refs[1::4]
        self.sent_sem, self.got_sem = refs[2::4], refs[3::4]
        self.me, self.side = lax.axis_index("dp"), lax.axis_index("tensor")

    def late(self, block):
        return (block % 4) // 3

    def own_bit(self, b):
        return (self.me // (1 << b)) % 2

    def partner(self, b):
        return self.me + (1 - 2 * self.own_bit(b)) * (1 << b)

    def turned(self, s, block):
        if s not in (1, 2) or self.stages < 3:
            return self.own_bit(s), self.partner(s)
        late = self.late(block)
        return (
            self.own_bit(s) * (1 - late) + self.own_bit(3 - s) * late,
            self.partner(s) * (1 - late) + self.partner(3 - s) * late,
        )

    def barrier(self):
        arrived = pltpu.get_barrier_semaphore()
        for b in range(self.stages):
            pl.semaphore_signal(
                arrived, inc=1, device_id=(self.partner(b), self.side), device_id_type=MESH
            )
        pl.semaphore_signal(
            arrived, inc=1, device_id=(self.me, 1 - self.side), device_id_type=MESH
        )
        pl.semaphore_wait(arrived, self.stages + 1)

    def copy(self, s, block):
        slot = block % self.slots[s]
        bit, partner = self.turned(s, block)
        return pltpu.make_async_remote_copy(
            src_ref=self.held[s].at[slot, 1 - bit],
            dst_ref=self.got[s].at[slot],
            send_sem=self.sent_sem[s].at[slot],
            recv_sem=self.got_sem[s].at[slot],
            device_id=(partner, self.side),
            device_id_type=MESH,
        )

    def advance(self, step, emit):
        for s in range(self.stages, 0, -1):
            block = step - self.starts[s]

            @pl.when((block >= 0) & (block < self.count))
            def _():
                slot = block % self.slots[s - 1]
                self.copy(s - 1, block).wait()
                keep, _ = self.turned(s - 1, block)
                held, got = self.held[s - 1], self.got[s - 1]
                if s == self.stages:
                    emit(block, held[slot, keep, 0].astype(F32) + got[slot, 0].astype(F32))
                else:
                    later = block % self.slots[s]
                    late = self.late(block)

                    def add(k, carry):
                        total = held[slot, keep, k] + got[slot, k]
                        bit, rest = k % 2, k // 2
                        if s == 1 and self.stages >= 3:
                            bit = bit * (1 - late) + (k // 2) % 2 * late
                            rest = rest * (1 - late) + (k // 4 * 2 + k % 2) * late
                        self.held[s][later, bit, rest] = total
                        return carry

                    lax.fori_loop(0, self.devices >> s, add, 0)
                    self.copy(s, block).start()

    def multiply(self, block, turned_ref, rights):
        slot = block % self.slots[0]
        pieces = 4
        size = self.devices // pieces

        def piece(i, carry):
            span = pl.ds(i * size * self.rows, size * self.rows)
            total, start = None, 0
            for right in rights:
                part = nn(turned_ref[span, start : start + right.shape[0]], right[...])
                total = part if total is None else total + part
                start += right.shape[0]
            for r in range(size):
                block_rows = total[r * self.rows : (r + 1) * self.rows].astype(BF)
                self.held[0][slot, r % 2, i * (size // 2) + r // 2] = block_rows
            return carry

        lax.fori_loop(0, pieces, piece, 0)
        self.copy(0, block).start()

    def put_gain(self, block, row):
        slot = block % self.slots[0]
        column = jnp.broadcast_to(row, (LANES, row.shape[1])).T.astype(BF)
        for k in range(self.devices):
            rows = column[k * self.rows : (k + 1) * self.rows, :]
            wide = jnp.concatenate([rows] * (COLS // LANES), axis=1)
            self.held[0][slot, k % 2, k // 2] = wide
        self.copy(0, block).start()


def turn_piece(turned_ref, left, start, row):
    @pl.loop(0, left.shape[1] // 256)
    def _(i):
        span = pl.ds(pl.multiple_of(i * 256, 256), 256)
        turned_ref[span, start + row : start + row + 256] = left[row : row + 256, span].T


def emit_into(outs, per, block, value):
    for kind, out in enumerate(outs):

        @pl.when((block >= kind * per) & (block < (kind + 1) * per))
        def _():
            out[...] = value


def emit_specs(scatter, kinds, per, width):
    lead = scatter.starts[-1]
    specs, shapes = [], []
    for kind in range(kinds + 1):
        most, size = (per - 1, width) if kind < kinds else (0, COLS)

        def where(j, first=lead + kind * per, most=most):
            return (0, jnp.clip(j - first, 0, most))

        specs.append(pl.BlockSpec((scatter.rows, COLS), where))
        shapes.append(jax.ShapeDtypeStruct((scatter.rows, size), F32))
    return specs, shapes


def remote(src, dst, sems, device):
    return pltpu.make_async_remote_copy(
        src_ref=src,
        dst_ref=dst,
        send_sem=sems.at[0],
        recv_sem=sems.at[1],
        device_id=device,
        device_id_type=MESH,
    )


def ffn_scatter_kernel(scatter, per, *refs):
    (
        cot_turned, norm_own, norm_other, right_own, right_other, gate_own, gate_other,
        cot_hbm, middle_hbm, parts_hbm, gain_ref, wd_ref,
    ) = refs[:12]
    outs = refs[12:15]
    gate_ref, gm_ref, block_own, block_send = refs[15:19]
    (
        norm_turned, cot_own, middle_own, part_own, got_part, gm_own, gain_got, acc_other,
        gain_sems, part_sems, gm_sems, local_sems,
    ) = refs[19:31]
    scatter.bind(refs[31:])
    step = pl.program_id(0)
    side = scatter.side
    across = (scatter.me, 1 - side)
    half = part_own.shape[0]
    quarter = half // QUARTERS
    row_chunk = 128

    def part_copy(r):
        span = pl.ds(r * quarter, quarter)
        return remote(parts_hbm.at[1, span], got_part.at[span], part_sems.at[r], across)

    def gm_copy(r):
        span = pl.ds(r * quarter, quarter)
        return remote(gm_own.at[span], gm_ref.at[side, span], gm_sems.at[r], across)

    def gain_copy():
        return remote(gain_ref, gain_got, gain_sems, across)

    loads = [
        pltpu.make_async_copy(cot_hbm, cot_own, local_sems.at[0]),
        pltpu.make_async_copy(parts_hbm.at[0], part_own, local_sems.at[1]),
        pltpu.make_async_copy(middle_hbm, middle_own, local_sems.at[2]),
    ]

    def gm_keep():
        return pltpu.make_async_copy(gm_own, gm_ref.at[side], local_sems.at[3])

    @pl.when(step == 0)
    def _():
        for load in loads:
            load.start()
        scatter.barrier()
        for r in range(QUARTERS):
            part_copy(r).start()
        gain_copy().start()

    scatter.advance(step, functools.partial(emit_into, outs, per))

    @pl.when(step < per)
    def _():
        scatter.multiply(step, cot_turned, (right_own, right_other))

        @pl.when(step == 0)
        def _():
            block_own[...] = jnp.zeros_like(block_own)
            acc_other[...] = jnp.zeros_like(acc_other)

        @pl.loop(0, half // 256)
        def _(i):
            span = pl.ds(i * 256, 256)
            block_own[span, :] += nt(right_own[span, :], wd_ref[...])
            acc_other[span, :] += nt(right_other[span, :], wd_ref[...])

    pieces = [(norm_own, 0, r) for r in range(0, half, 256)]
    pieces += [(norm_other, half, r) for r in range(0, half, 256)]
    for nth, (left, start, row) in enumerate(pieces):

        @pl.when(step == per - len(pieces) + nth)
        def _():
            turn_piece(norm_turned, left, start, row)

    @pl.when((step >= per) & (step < 2 * per))
    def _():
        scatter.multiply(step, norm_turned, (right_own, right_other))
        rows = gate_ref.shape[0] // 4

        @pl.loop(0, 4)
        def _(i):
            span = pl.ds(i * rows, rows)
            total = nn(norm_turned[span, :half], gate_own[...])
            gate_ref[span, :] = (total + nn(norm_turned[span, half:], gate_other[...])).astype(BF)

    @pl.when(step == 2 * per)
    def _():
        gain_copy().wait()
        scatter.put_gain(step, gain_ref[0:1, :] + gain_got[0:1, :])

    for r in range(QUARTERS):

        @pl.when(step == 3 + 2 * r)
        def _():
            if r == 0:
                for load in loads:
                    load.wait()
            part_copy(r).wait()

            @pl.loop(r * quarter // row_chunk, (r + 1) * quarter // row_chunk)
            def _(i):
                span = pl.ds(i * row_chunk, row_chunk)
                total = cot_own[span, :].astype(F32) + part_own[span, :].astype(F32)
                gm_own[span, :] = (total + got_part[span, :].astype(F32)).astype(BF)

            gm_copy(r).start()
            if r == QUARTERS - 1:
                gm_keep().start()

    @pl.when(step == 2 * per + 1)
    def _():
        @pl.loop(0, half // row_chunk)
        def _(i):
            span = pl.ds(i * row_chunk, row_chunk)
            block_own[span, :] += middle_own[span, :].astype(F32)
            block_send[span, :] = acc_other[span, :].astype(BF)

    @pl.when(step == scatter.steps - 1)
    def _():
        for r in range(QUARTERS):
            gm_copy(r).wait()
        gm_keep().wait()


def remote_settings(identity, mib=60):
    return pltpu.CompilerParams(
        dimension_semantics=("arbitrary",),
        vmem_limit_bytes=mib * 1024 * 1024,
        collective_id=identity,
        has_side_effects=True,
    )


def ffn_scatter(devices, cot_turned, normed, grads, cot, middle, parts, gain_part, w):
    half, d = middle.shape
    width = grads.shape[3]
    per = width // COLS
    scatter = Scatter(devices, d // devices, 2 * per + 1)
    assert 2 * per > 3 + 2 * QUARTERS and scatter.rows * devices == d and per >= 2 * half // 256

    def right(side):
        def where(j):
            c = jnp.minimum(j, 2 * per - 1)
            return (side, 2 - c // per, 0, c % per)

        return pl.BlockSpec((None, None, half, COLS), where)

    def gate_block(j):
        return jnp.clip(j - per, 0, per - 1)

    def gate(side):
        return pl.BlockSpec((None, None, half, COLS), lambda j: (side, 0, 0, gate_block(j)))

    def rows_of(side):
        return pl.BlockSpec(
            (None, half, d), lambda j: (side, 0, 0), pipeline_mode=pl.Buffered(1)
        )

    specs, shapes = emit_specs(scatter, 2, per, width)
    whole = lambda j: (0, 0)
    left_there = pl.BlockSpec(memory_space=pl.ANY)
    return pl.pallas_call(
        functools.partial(ffn_scatter_kernel, scatter, per),
        grid=(scatter.steps,),
        in_specs=[
            resident((d, 2 * half)),
            rows_of(0),
            rows_of(1),
            right(0),
            right(1),
            gate(0),
            gate(1),
            left_there,
            left_there,
            left_there,
            resident((8, d)),
            pl.BlockSpec((d, COLS), lambda j: (0, 2 * per + jnp.minimum(j, per - 1))),
        ],
        out_specs=specs
        + [
            pl.BlockSpec((d, COLS), lambda j: (0, gate_block(j))),
            left_there,
            pl.BlockSpec((half, d), whole),
            pl.BlockSpec((half, d), whole),
        ],
        out_shape=shapes
        + [
            jax.ShapeDtypeStruct((d, width), BF),
            jax.ShapeDtypeStruct((2, half, d), BF),
            jax.ShapeDtypeStruct((half, d), F32),
            jax.ShapeDtypeStruct((half, d), BF),
        ],
        scratch_shapes=[
            pltpu.VMEM((d, 2 * half), BF),
            pltpu.VMEM((half, d), BF),
            pltpu.VMEM((half, d), BF),
            pltpu.VMEM((half, d), BF),
            pltpu.VMEM((half, d), BF),
            pltpu.VMEM((half, d), BF),
            pltpu.VMEM((8, d), F32),
            pltpu.VMEM((half, d), F32),
            pltpu.SemaphoreType.DMA((2,)),
            pltpu.SemaphoreType.DMA((QUARTERS, 2)),
            pltpu.SemaphoreType.DMA((QUARTERS, 2)),
            pltpu.SemaphoreType.DMA((4,)),
        ]
        + scatter.scratch(),
        compiler_params=remote_settings(0),
        cost_estimate=cost(16 * half * d * per * COLS, 20 * half * d),
        name="ffn_scatter",
    )(
        cot_turned, normed, normed, grads, grads, grads, grads, cot, middle, parts, gain_part, w,
    )


def attention_scatter_kernel(scatter, per, *refs):
    (
        norm_turned, gain_ref, right_ref, w_ref, attended_ref, gm_hbm, x_hbm, block_hbm, block_send,
    ) = refs[:9]
    outs = refs[9:14]
    token_grad_ref, block_out_ref = refs[14:16]
    (
        gm_turned, gm_ref, x_ref, block_own, acc_ref, part_send, part_got, block_got,
        gain_part, part_sems, block_sems, local_sems,
    ) = refs[16:28]
    scatter.bind(refs[28:])
    step = pl.program_id(0)
    side = scatter.side
    across = (scatter.me, 1 - side)
    length = x_ref.shape[0]
    half = length // 2
    quarter = half // QUARTERS
    chunk = 128
    kinds = 3 * per
    own, other = side * half, (1 - side) * half

    def part_copy(r):
        span = pl.ds(r * quarter, quarter)
        return remote(part_send.at[span], part_got.at[span], part_sems.at[r], across)

    def block_copy():
        return remote(block_send, block_got, block_sems, across)

    loads = [
        pltpu.make_async_copy(x_hbm, x_ref, local_sems.at[0]),
        pltpu.make_async_copy(gm_hbm, gm_ref, local_sems.at[1]),
        pltpu.make_async_copy(block_hbm, block_own, local_sems.at[2]),
    ]

    def back(row):
        span = pl.ds(row, chunk)
        part, piece = rms_back(acc_ref[span, :], x_ref[span, :].astype(F32), gain_ref[...])
        gain_part[...] += jnp.broadcast_to(piece, gain_part.shape)
        return part

    @pl.when(step == 0)
    def _():
        for load in loads:
            load.start()
        scatter.barrier()
        block_copy().start()

    scatter.advance(step, functools.partial(emit_into, outs, per))

    @pl.when(step == 0)
    def _():
        acc_ref[...] = jnp.zeros_like(acc_ref)
        gain_part[...] = jnp.zeros_like(gain_part)

    @pl.when(step < kinds)
    def _():
        scatter.multiply(step, norm_turned, (right_ref,))

        @pl.loop(0, length // 256)
        def _(i):
            span = pl.ds(i * 256, 256)
            acc_ref[span, :] += nt(right_ref[span, :], w_ref[...])

    @pl.when(step == 1)
    def _():
        for load in loads:
            load.wait()

    for nth, row in enumerate(range(0, length, 256)):

        @pl.when(step == kinds - length // 256 + nth)
        def _():
            turn_piece(gm_turned, gm_ref, 0, row)

    @pl.when((step >= kinds) & (step < 4 * per))
    def _():
        scatter.multiply(step, gm_turned, (attended_ref,))

    for r in range(QUARTERS):

        @pl.when(step == kinds + min(r, per - 1))
        def _():
            @pl.loop(r * quarter // chunk, (r + 1) * quarter // chunk)
            def _(i):
                part_send[pl.ds(i * chunk, chunk), :] = back(other + i * chunk).astype(BF)

            part_copy(r).start()

            @pl.loop(r * quarter // chunk, (r + 1) * quarter // chunk)
            def _(i):
                span = pl.ds(own + i * chunk, chunk)
                acc_ref[span, :] = back(own + i * chunk) + gm_ref[span, :].astype(F32)

    @pl.when(step == 4 * per)
    def _():
        scatter.put_gain(step, gain_part[0:1, :])

    @pl.when(step == 4 * per + 1)
    def _():
        block_copy().wait()

        @pl.loop(0, half // chunk)
        def _(i):
            span = pl.ds(i * chunk, chunk)
            total = block_own[span, :] + block_got[span, :].astype(F32)
            block_out_ref[span, :] = total.astype(BF)

    for r in range(QUARTERS):

        @pl.when(step == scatter.steps - QUARTERS + r)
        def _():
            part_copy(r).wait()

            @pl.loop(r * quarter // chunk, (r + 1) * quarter // chunk)
            def _(i):
                span = pl.ds(i * chunk, chunk)
                total = acc_ref[pl.ds(own + i * chunk, chunk), :]
                token_grad_ref[span, :] = (total + part_got[span, :].astype(F32)).astype(BF)


def attention_scatter(
    devices, norm_turned, gm, x, gain, grads, attended, block_own, block_send, w
):
    length, d = gm.shape
    half = length // 2
    width = grads.shape[2]
    per = width // COLS
    kinds = 3 * per
    scatter = Scatter(devices, d // devices, 4 * per + 1)
    assert kinds >= length // 256 and scatter.rows * devices == d
    assert scatter.starts[-1] > QUARTERS

    def grads_map(j):
        c = jnp.minimum(j, kinds - 1)
        return (c // per, 0, c % per)

    def attended_map(j):
        return (0, jnp.clip(j - kinds, 0, per - 1))

    specs, shapes = emit_specs(scatter, 4, per, width)
    whole = lambda j: (0, 0)
    left_there = pl.BlockSpec(memory_space=pl.ANY)
    return pl.pallas_call(
        functools.partial(attention_scatter_kernel, scatter, per),
        grid=(scatter.steps,),
        in_specs=[
            resident((d, length)),
            resident((1, d)),
            pl.BlockSpec((None, length, COLS), grads_map),
            pl.BlockSpec((d, COLS), lambda j: (0, jnp.minimum(j, kinds - 1))),
            pl.BlockSpec((length, COLS), attended_map),
            left_there,
            left_there,
            left_there,
            left_there,
        ],
        out_specs=specs + [pl.BlockSpec((half, d), whole), pl.BlockSpec((half, d), whole)],
        out_shape=shapes
        + [jax.ShapeDtypeStruct((half, d), BF), jax.ShapeDtypeStruct((half, d), BF)],
        scratch_shapes=[
            pltpu.VMEM((d, length), BF),
            pltpu.VMEM((length, d), BF),
            pltpu.VMEM((length, d), BF),
            pltpu.VMEM((half, d), F32),
            pltpu.VMEM((length, d), F32),
            pltpu.VMEM((half, d), BF),
            pltpu.VMEM((half, d), BF),
            pltpu.VMEM((half, d), BF),
            pltpu.VMEM((8, d), F32),
            pltpu.SemaphoreType.DMA((QUARTERS, 2)),
            pltpu.SemaphoreType.DMA((2,)),
            pltpu.SemaphoreType.DMA((3,)),
        ]
        + scatter.scratch(),
        compiler_params=remote_settings(1),
        cost_estimate=cost(14 * length * d * per * COLS, 20 * length * d),
        name="attention_scatter",
    )(norm_turned, gain, grads, w, attended, gm, x, block_own, block_send)


def swap(x):
    return lax.ppermute(x, "tensor", [(0, 1), (1, 0)])


def body(
    tokens,
    parents,
    attn_gain,
    ffn_gain,
    query_weight,
    key_weight,
    value_weight,
    output_weight,
    gate_weight,
    up_weight,
    down_weight,
    cotangent,
):
    half, d = tokens.shape
    length = 2 * half
    width = query_weight.shape[1]
    hidden_width = gate_weight.shape[1]
    seg_rows = length // parents.shape[1]
    mine = lax.axis_index("tensor")
    own_start = mine * half
    other_start = (1 - mine) * half

    def place(own, other):
        full = jnp.zeros((length, own.shape[1]), own.dtype)
        full = lax.dynamic_update_slice(full, own, (own_start, 0))
        return lax.dynamic_update_slice(full, other, (other_start, 0))

    def own_rows(full):
        return lax.dynamic_slice_in_dim(full, own_start, half, 0)

    def other_rows(full):
        return lax.dynamic_slice_in_dim(full, other_start, half, 0)

    def gather(shard):
        return lax.all_gather(shard, "dp", axis=0, tiled=True)

    attn_row = attn_gain[None, :]
    ffn_row = ffn_gain[None, :]

    first = gather(
        jnp.concatenate([query_weight, key_weight, value_weight, output_weight.T], axis=1)
    )
    second = gather(jnp.concatenate([gate_weight, up_weight, down_weight.T], axis=1))
    devices = lax.axis_size("dp")

    bias, positions = tree_tables(parents[0], seg_rows)
    cosine, sine = turn_tables(positions, COLS)
    cot_other = swap(cotangent)
    rows_all, cot_other, cot_turned = lax.optimization_barrier(
        (
            place(tokens, swap(tokens)),
            cot_other,
            jnp.concatenate([cotangent.T, cot_other.T], axis=1),
        )
    )

    qkv, normed_one = project(rows_all, attn_row, cosine, sine, first, width)
    attended, lse = attend(qkv, bias, width, seg_rows)
    out_turned = first[:, 3 * width :]
    send = nt(other_rows(attended), out_turned).astype(BF)
    send, norm_source = lax.optimization_barrier((send, normed_one))
    received = swap(send)
    received, norm_turned = lax.optimization_barrier((received, norm_source.T))
    middle = (
        tokens.astype(F32) + nt(own_rows(attended), out_turned) + received.astype(F32)
    ).astype(BF)
    middle_other = swap(middle)

    ffn_grads, normed_two, parts, gain_part = ffn(
        (middle, middle_other), (cotangent, cot_other), ffn_row, second, hidden_width
    )
    down_grad, up_grad, ffn_gain_grad, gate_whole, grad_middle, block_own, block_send = ffn_scatter(
        devices, cot_turned, normed_two, ffn_grads, cotangent, middle, parts, gain_part, second
    )
    gate_grad = lax.psum_scatter(gate_whole, "dp", scatter_dimension=0, tiled=True).astype(F32)
    grad_middle = grad_middle.reshape(length, d)

    grad_attended = nn(grad_middle, out_turned).astype(BF)
    grads = attend_back(
        qkv, attended, grad_attended, lse, bias, cosine[:, :LANES], sine[:, :LANES], seg_rows
    )
    (
        query_grad, key_grad, value_grad, output_grad, attn_gain_grad, token_grad, block_out,
    ) = attention_scatter(
        devices,
        norm_turned,
        grad_middle,
        rows_all,
        attn_row,
        grads,
        attended,
        block_own,
        block_send,
        first,
    )
    gain_rows = d // devices // 2

    def gain_piece(columns, side):
        return lax.dynamic_slice_in_dim(columns[:, 0], side * gain_rows, gain_rows, 0)

    return (
        block_out,
        token_grad,
        query_grad,
        key_grad,
        value_grad,
        output_grad.T,
        gate_grad,
        up_grad,
        down_grad.T,
        gain_piece(attn_gain_grad, mine) + swap(gain_piece(attn_gain_grad, 1 - mine)),
        gain_piece(ffn_gain_grad, mine),
    )


def solution(mesh):
    rows = P(("dp", "tensor"), None)
    tall = P("dp", "tensor")
    wide = P("tensor", "dp")
    return jax.shard_map(
        body,
        mesh=mesh,
        in_specs=(
            rows, P("dp", None), P(), P(), tall, tall, tall, wide, tall, tall, wide, rows,
        ),
        out_specs=(
            rows, rows, tall, tall, tall, wide, tall, tall, wide,
            P(("dp", "tensor")), P(("dp", "tensor")),
        ),
        check_vma=False,
    )
```

```python
import functools
import math

import jax
import jax.numpy as jnp
from jax import lax
from jax.experimental import pallas as pl
from jax.experimental.pallas import tpu as pltpu
from jax.sharding import PartitionSpec as P

HD = 64
EPS = 1e-05
BF = jnp.bfloat16
F32 = jnp.float32
COLS = 256
LANES = 128
MASKED = -1e30


def settings(mib=48):
    return pltpu.CompilerParams(
        dimension_semantics=("arbitrary",), vmem_limit_bytes=mib * 1024 * 1024
    )


def cost(flops, bytes_accessed, transcendentals=0):
    return pl.CostEstimate(
        flops=int(flops), bytes_accessed=int(bytes_accessed), transcendentals=int(transcendentals)
    )


def nn(a, b):
    return jnp.dot(a, b, preferred_element_type=F32)


def nt(a, b):
    return lax.dot_general(a, b, (((1,), (1,)), ((), ())), preferred_element_type=F32)


def tree_tables(parent_row, seg_rows):
    segs = parent_row.shape[0]
    index = jnp.arange(segs, dtype=jnp.int32)
    step_up = (parent_row[:, None] == index[None, :]).astype(jnp.int32)
    eye = (index[:, None] == index[None, :]).astype(jnp.int32)
    reach = eye
    for _ in range(segs):
        up = jnp.sum(step_up[:, :, None] * reach[None, :, :], axis=1)
        reach = jnp.minimum(eye + up, 1)
    depths = jnp.sum(reach, axis=1) - 1
    bias = jnp.where(reach.T > 0, 0.0, MASKED).astype(F32)
    return jnp.repeat(bias, seg_rows, axis=1), depths


def turn_tables(depths_ref, cos_ref, sin_ref):
    segs = depths_ref.shape[0]
    seg_rows = 2 * cos_ref.shape[1] // segs
    shape = (seg_rows, LANES)
    lane = lax.broadcasted_iota(jnp.int32, shape, 1) % HD
    row = lax.broadcasted_iota(jnp.int32, shape, 0)
    rates = jnp.exp((lane % (HD // 2)).astype(F32) * (-2.0 * math.log(10000.0) / HD))
    sign = jnp.where(lane < HD // 2, -1.0, 1.0).astype(F32)

    @pl.loop(0, segs)
    def _(seg):
        angles = (depths_ref[seg] * seg_rows + row).astype(F32) * rates
        span = pl.ds(seg % (segs // 2) * seg_rows, seg_rows)
        cos_ref[seg // (segs // 2), span, :] = jnp.cos(angles)
        sin_ref[seg // (segs // 2), span, :] = jnp.sin(angles) * sign


def turn(x, cosine, sine):
    width = x.shape[1]
    lane = lax.broadcasted_iota(jnp.int32, x.shape, 1)
    first = (lane % HD) < HD // 2
    other = jnp.where(
        first, pltpu.roll(x, width - HD // 2, 1), pltpu.roll(x, HD // 2, 1)
    )
    return x * cosine + other * sine


def inverse_rms(x):
    return lax.rsqrt(jnp.mean(x * x, axis=1, keepdims=True) + EPS)


def norm_rows(x_ref, gain_ref, normed_ref):
    chunk = 128

    @pl.loop(0, x_ref.shape[0] // chunk)
    def _(i):
        span = pl.ds(i * chunk, chunk)
        x = x_ref[span, :].astype(F32)
        normed_ref[span, :] = (x * inverse_rms(x) * gain_ref[...]).astype(BF)


def mask_block(block, seg_rows, bias_ref, m, u):
    cols = slice(m * block, (m + 1) * block)
    per = block // seg_rows
    return jnp.concatenate(
        [
            jnp.broadcast_to(bias_ref[u * per + i : u * per + i + 1, cols], (seg_rows, block))
            for i in range(per)
        ],
        axis=0,
    )


def causal(block):
    key = lax.broadcasted_iota(jnp.int32, (block, block), 0)
    query = lax.broadcasted_iota(jnp.int32, (block, block), 1)
    return key <= query


def attend_kernel(block, seg_rows, q_ref, k_ref, v_ref, bias_ref, out_ref, lse_ref):
    length = q_ref.shape[0]
    heads = q_ref.shape[1] // HD
    v_turned = v_ref[...].T
    for m in range(length // block):
        cols = slice(m * block, (m + 1) * block)
        outs = []
        for h in range(heads):
            lanes = slice(h * HD, (h + 1) * HD)
            q = q_ref[cols, lanes]
            scores = []
            for u in range(m + 1):
                s = nt(k_ref[u * block : (u + 1) * block, lanes], q)
                s = s + mask_block(block, seg_rows, bias_ref, m, u)
                if u == m:
                    s = jnp.where(causal(block), s, MASKED)
                scores.append(s)
            peak = scores[0].max(axis=0, keepdims=True)
            for s in scores[1:]:
                peak = jnp.maximum(peak, s.max(axis=0, keepdims=True))
            total = jnp.zeros_like(peak)
            acc = jnp.zeros((HD, block), F32)
            for u, s in enumerate(scores):
                e = jnp.exp(s - peak)
                total = total + e.sum(axis=0, keepdims=True)
                acc = acc + nn(v_turned[lanes, u * block : (u + 1) * block], e.astype(BF))
            outs.append(acc / total)
            lse_ref[0, h : h + 1, cols] = peak + jnp.log(total)
        out_ref[cols, :] = jnp.concatenate(outs, axis=0).T.astype(BF)


def attend(qkv, bias, width, seg_rows):
    length = qkv.shape[0]
    groups = width // LANES
    heads = LANES // HD
    block = 2 * seg_rows
    live = length * length // 2
    return pl.pallas_call(
        functools.partial(attend_kernel, block, seg_rows),
        grid=(groups,),
        in_specs=[
            pl.BlockSpec((length, LANES), lambda i: (0, i)),
            pl.BlockSpec((length, LANES), lambda i: (0, groups + i)),
            pl.BlockSpec((length, LANES), lambda i: (0, 2 * groups + i)),
            pl.BlockSpec(bias.shape, lambda i: (0, 0)),
        ],
        out_specs=[
            pl.BlockSpec((length, LANES), lambda i: (0, i)),
            pl.BlockSpec((1, heads, length), lambda i: (i, 0, 0)),
        ],
        out_shape=[
            jax.ShapeDtypeStruct((length, width), BF),
            jax.ShapeDtypeStruct((groups, heads, length), F32),
        ],
        compiler_params=settings(),
        cost_estimate=cost(16 * live * width, 8 * length * width, live * width // HD),
        name="attend",
    )(qkv, qkv, qkv, bias)


def attend_back_kernel(
    block,
    seg_rows,
    q_ref,
    k_ref,
    v_ref,
    o_ref,
    do_ref,
    lse_ref,
    bias_ref,
    cos_ref,
    sin_ref,
    out_ref,
    dk_ref,
    dv_ref,
):
    length = q_ref.shape[0]
    heads = q_ref.shape[1] // HD
    k_turned = k_ref[...].T
    product = (do_ref[...].astype(F32) * o_ref[...].astype(F32)).T
    deltas = [product[h * HD : (h + 1) * HD].sum(axis=0, keepdims=True) for h in range(heads)]
    for m in range(length // block):
        cols = slice(m * block, (m + 1) * block)
        grads = []
        for h in range(heads):
            lanes = slice(h * HD, (h + 1) * HD)
            q, do = q_ref[cols, lanes], do_ref[cols, lanes]
            lse = lse_ref[0, h : h + 1, cols]
            delta = deltas[h][:, cols]
            acc = jnp.zeros((HD, block), F32)
            for u in range(m + 1):
                keys = slice(u * block, (u + 1) * block)
                s = nt(k_ref[keys, lanes], q)
                p = jnp.exp(s + (mask_block(block, seg_rows, bias_ref, m, u) - lse))
                if u == m:
                    p = jnp.where(causal(block), p, 0.0)
                dp = nt(v_ref[keys, lanes], do)
                ds = (p * (dp - delta)).astype(BF)
                dv = nn(p.astype(BF), do)
                dk = nn(ds, q)
                if u == m:
                    dv_ref[h, keys, :] = dv
                    dk_ref[h, keys, :] = dk
                else:
                    dv_ref[h, keys, :] += dv
                    dk_ref[h, keys, :] += dk
                acc = acc + nn(k_turned[lanes, keys], ds)
            grads.append(acc)
        dq = jnp.concatenate(grads, axis=0).T * (1.0 / math.sqrt(HD))
        out_ref[0, cols, :] = turn(dq, cos_ref[cols, :], -sin_ref[cols, :]).astype(BF)
    for m in range(length // block):
        cols = slice(m * block, (m + 1) * block)
        dk = jnp.concatenate([dk_ref[h, cols, :] for h in range(heads)], axis=1)
        out_ref[1, cols, :] = turn(dk, cos_ref[cols, :], -sin_ref[cols, :]).astype(BF)
        out_ref[2, cols, :] = jnp.concatenate(
            [dv_ref[h, cols, :] for h in range(heads)], axis=1
        ).astype(BF)


def attend_back(qkv, attended, grad_attended, lse, bias, cosine, sine, seg_rows):
    length, width = attended.shape
    groups = width // LANES
    heads = LANES // HD
    block = 2 * seg_rows
    live = length * length // 2
    return pl.pallas_call(
        functools.partial(attend_back_kernel, block, seg_rows),
        grid=(groups,),
        in_specs=[
            pl.BlockSpec((length, LANES), lambda i: (0, i)),
            pl.BlockSpec((length, LANES), lambda i: (0, groups + i)),
            pl.BlockSpec((length, LANES), lambda i: (0, 2 * groups + i)),
            pl.BlockSpec((length, LANES), lambda i: (0, i)),
            pl.BlockSpec((length, LANES), lambda i: (0, i)),
            pl.BlockSpec((1, heads, length), lambda i: (i, 0, 0)),
            pl.BlockSpec(bias.shape, lambda i: (0, 0)),
            pl.BlockSpec((length, LANES), lambda i: (0, 0)),
            pl.BlockSpec((length, LANES), lambda i: (0, 0)),
        ],
        out_specs=pl.BlockSpec((3, length, LANES), lambda i: (0, 0, i)),
        out_shape=jax.ShapeDtypeStruct((3, length, width), BF),
        scratch_shapes=[
            pltpu.VMEM((heads, length, HD), F32),
            pltpu.VMEM((heads, length, HD), F32),
        ],
        compiler_params=settings(),
        cost_estimate=cost(40 * live * width, 16 * length * width, live * width // HD),
        name="attend_back",
    )(qkv, qkv, qkv, attended, grad_attended, lse, bias, cosine, sine)


def rms_back(grad, x, gain):
    inverse = inverse_rms(x)
    unit = x * inverse
    scaled = grad * gain
    inner = jnp.mean(scaled * unit, axis=1, keepdims=True)
    return inverse * (scaled - unit * inner), jnp.sum(grad * unit, axis=0, keepdims=True)


def back_rows(acc_ref, x_ref, gain_ref, gain_part_ref, part_ref):
    chunk = 128

    @pl.loop(0, x_ref.shape[0] // chunk)
    def _(i):
        span = pl.ds(i * chunk, chunk)
        part, piece = rms_back(acc_ref[span, :], x_ref[span, :].astype(F32), gain_ref[...])
        part_ref[span, :] = part.astype(part_ref.dtype)
        gain_part_ref[...] += jnp.broadcast_to(piece, gain_part_ref.shape)


def ffn_kernel(
    x_own,
    x_other,
    cot_own,
    cot_other,
    gain_ref,
    wg_ref,
    wu_ref,
    wd_ref,
    grads_ref,
    normed_ref,
    part_ref,
    gain_part_ref,
    cot_ref,
    acc_ref,
):
    h, j = pl.program_id(0), pl.program_id(1)
    chunk = 256

    @pl.when((h == 0) & (j == 0))
    def _():
        gain_part_ref[...] = jnp.zeros_like(gain_part_ref)

    for side, (x_ref, c_ref) in enumerate(((x_own, cot_own), (x_other, cot_other))):

        @pl.when((h == side) & (j == 0))
        def _():
            norm_rows(x_ref, gain_ref, normed_ref)
            cot_ref[...] = c_ref[...]

    @pl.when(j == 0)
    def _():
        acc_ref[...] = jnp.zeros_like(acc_ref)

    for r in range(0, cot_ref.shape[0], chunk):
        span = slice(r, r + chunk)
        gate = nn(normed_ref[span, :], wg_ref[...])
        up = nn(normed_ref[span, :], wu_ref[...])
        grad_hidden = nn(cot_ref[span, :], wd_ref[...])
        sig = jax.nn.sigmoid(gate)
        silu = gate * sig
        grads_ref[2, span, :] = (silu * up).astype(BF)
        grad_gate = (grad_hidden * up * (sig + silu * (1.0 - sig))).astype(BF)
        grad_up = (grad_hidden * silu).astype(BF)
        grads_ref[0, span, :] = grad_gate
        grads_ref[1, span, :] = grad_up
        acc_ref[span, :] += nt(grad_gate, wg_ref[...]) + nt(grad_up, wu_ref[...])

    for side, x_ref in enumerate((x_own, x_other)):

        @pl.when((h == side) & (j == pl.num_programs(1) - 1))
        def _():
            back_rows(acc_ref, x_ref, gain_ref, gain_part_ref, part_ref)


def resident(shape):
    zeros = (0,) * len(shape)
    return pl.BlockSpec(shape, lambda *grid: zeros, pipeline_mode=pl.Buffered(1))


def ffn(xs, cots, gain, w, hidden_width, cols=512):
    rows, d = xs[0].shape
    steps = hidden_width // cols
    per_half = lambda h, j: (h, 0, 0)
    return pl.pallas_call(
        ffn_kernel,
        grid=(2, steps),
        in_specs=[resident((rows, d))] * 4
        + [
            resident((1, d)),
            pl.BlockSpec((d, cols), lambda h, j: (0, j)),
            pl.BlockSpec((d, cols), lambda h, j: (0, steps + j)),
            pl.BlockSpec((d, cols), lambda h, j: (0, 2 * steps + j)),
        ],
        out_specs=[
            pl.BlockSpec((None, 3, rows, cols), lambda h, j: (h, 0, 0, j)),
            pl.BlockSpec((None, rows, d), per_half),
            pl.BlockSpec((None, rows, d), per_half),
            pl.BlockSpec((8, d), lambda h, j: (0, 0)),
        ],
        out_shape=[
            jax.ShapeDtypeStruct((2, 3, rows, hidden_width), BF),
            jax.ShapeDtypeStruct((2, rows, d), BF),
            jax.ShapeDtypeStruct((2, rows, d), BF),
            jax.ShapeDtypeStruct((8, d), F32),
        ],
        scratch_shapes=[pltpu.VMEM((rows, d), BF), pltpu.VMEM((rows, d), F32)],
        compiler_params=pltpu.CompilerParams(
            dimension_semantics=("arbitrary", "arbitrary"), vmem_limit_bytes=56 * 1024 * 1024
        ),
        cost_estimate=cost(
            20 * rows * d * hidden_width,
            12 * d * hidden_width + 16 * rows * d + 12 * rows * hidden_width,
            2 * rows * hidden_width,
        ),
        name="ffn",
    )(*xs, *cots, gain, w, w, w)


MESH = pl.DeviceIdType.MESH
QUARTERS = 4


class Scatter:
    def __init__(self, devices, rows, count):
        self.devices, self.rows, self.count = devices, rows, count
        self.stages = devices.bit_length() - 1
        self.lags = [min(s + 1, 2) for s in range(self.stages)]
        self.slots = [2 * lag for lag in self.lags]
        if self.stages >= 3:
            self.slots[1] = self.slots[2] = 8
        self.starts = [sum(self.lags[:s]) for s in range(self.stages + 1)]
        self.steps = count + self.starts[-1]

    def scratch(self):
        shapes = []
        for s in range(self.stages):
            slots, left = self.slots[s], self.devices >> (s + 1)
            shapes.append(pltpu.VMEM((slots, 2, left, self.rows, COLS), BF))
            shapes.append(pltpu.VMEM((slots, left, self.rows, COLS), BF))
            shapes.append(pltpu.SemaphoreType.DMA((slots,)))
            shapes.append(pltpu.SemaphoreType.DMA((slots,)))
        return shapes

    def bind(self, refs):
        self.held, self.got = refs[0::4], refs[1::4]
        self.sent_sem, self.got_sem = refs[2::4], refs[3::4]
        self.me, self.side = lax.axis_index("dp"), lax.axis_index("tensor")

    def late(self, block):
        return (block % 4) // 3

    def own_bit(self, b):
        return (self.me // (1 << b)) % 2

    def partner(self, b):
        return self.me + (1 - 2 * self.own_bit(b)) * (1 << b)

    def turned(self, s, block):
        if s not in (1, 2) or self.stages < 3:
            return self.own_bit(s), self.partner(s)
        late = self.late(block)
        return (
            self.own_bit(s) * (1 - late) + self.own_bit(3 - s) * late,
            self.partner(s) * (1 - late) + self.partner(3 - s) * late,
        )

    def barrier(self):
        arrived = pltpu.get_barrier_semaphore()
        for b in range(self.stages):
            pl.semaphore_signal(
                arrived, inc=1, device_id=(self.partner(b), self.side), device_id_type=MESH
            )
        pl.semaphore_signal(
            arrived, inc=1, device_id=(self.me, 1 - self.side), device_id_type=MESH
        )
        pl.semaphore_wait(arrived, self.stages + 1)

    def copy(self, s, block):
        slot = block % self.slots[s]
        bit, partner = self.turned(s, block)
        return pltpu.make_async_remote_copy(
            src_ref=self.held[s].at[slot, 1 - bit],
            dst_ref=self.got[s].at[slot],
            send_sem=self.sent_sem[s].at[slot],
            recv_sem=self.got_sem[s].at[slot],
            device_id=(partner, self.side),
            device_id_type=MESH,
        )

    def advance(self, step, emit):
        for s in range(self.stages, 0, -1):
            block = step - self.starts[s]

            @pl.when((block >= 0) & (block < self.count))
            def _():
                slot = block % self.slots[s - 1]
                self.copy(s - 1, block).wait()
                keep, _ = self.turned(s - 1, block)
                held, got = self.held[s - 1], self.got[s - 1]
                if s == self.stages:
                    emit(block, held[slot, keep, 0].astype(F32) + got[slot, 0].astype(F32))
                else:
                    later = block % self.slots[s]
                    late = self.late(block)

                    def add(k, carry):
                        total = held[slot, keep, k] + got[slot, k]
                        bit, rest = k % 2, k // 2
                        if s == 1 and self.stages >= 3:
                            bit = bit * (1 - late) + (k // 2) % 2 * late
                            rest = rest * (1 - late) + (k // 4 * 2 + k % 2) * late
                        self.held[s][later, bit, rest] = total
                        return carry

                    lax.fori_loop(0, self.devices >> s, add, 0)
                    self.copy(s, block).start()

    def multiply(self, block, turned_ref, rights):
        slot = block % self.slots[0]
        pieces = 4
        size = self.devices // pieces

        def piece(i, carry):
            span = pl.ds(i * size * self.rows, size * self.rows)
            total, start = None, 0
            for right in rights:
                part = nn(turned_ref[span, start : start + right.shape[0]], right[...])
                total = part if total is None else total + part
                start += right.shape[0]
            for r in range(size):
                block_rows = total[r * self.rows : (r + 1) * self.rows].astype(BF)
                self.held[0][slot, r % 2, i * (size // 2) + r // 2] = block_rows
            return carry

        lax.fori_loop(0, pieces, piece, 0)
        self.copy(0, block).start()

    def put_gain(self, block, row):
        slot = block % self.slots[0]
        column = jnp.broadcast_to(row, (LANES, row.shape[1])).T.astype(BF)
        for k in range(self.devices):
            rows = column[k * self.rows : (k + 1) * self.rows, :]
            wide = jnp.concatenate([rows] * (COLS // LANES), axis=1)
            self.held[0][slot, k % 2, k // 2] = wide
        self.copy(0, block).start()


def turn_piece(turned_ref, left, start, row):
    cols = pl.ds(pl.multiple_of(start + row, 256), 256)

    @pl.loop(0, left.shape[1] // 256)
    def _(i):
        span = pl.ds(pl.multiple_of(i * 256, 256), 256)
        turned_ref[span, cols] = left[row : row + 256, span].T


def turn_kernel(first_ref, second_ref, out_ref):
    start = 0
    for left in (first_ref, second_ref):
        for row in range(0, left.shape[0], 256):
            turn_piece(out_ref, left, start, row)
        start += left.shape[0]


def turn_pair(first, second):
    rows, d = first.shape
    return pl.pallas_call(
        turn_kernel,
        out_shape=jax.ShapeDtypeStruct((d, 2 * rows), first.dtype),
        compiler_params=pltpu.CompilerParams(vmem_limit_bytes=32 * 1024 * 1024),
        cost_estimate=cost(0, 8 * rows * d),
        name="turn_pair",
    )(first, second)


def emit_into(outs, per, block, value):
    for kind, out in enumerate(outs):

        @pl.when((block >= kind * per) & (block < (kind + 1) * per))
        def _():
            out[...] = value


def emit_specs(scatter, kinds, per, width):
    lead = scatter.starts[-1]
    specs, shapes = [], []
    for kind in range(kinds + 1):
        most, size = (per - 1, width) if kind < kinds else (0, COLS)

        def where(j, first=lead + kind * per, most=most):
            return (0, jnp.clip(j - first, 0, most))

        specs.append(pl.BlockSpec((scatter.rows, COLS), where))
        shapes.append(jax.ShapeDtypeStruct((scatter.rows, size), F32))
    return specs, shapes


def remote(src, dst, sems, device):
    return pltpu.make_async_remote_copy(
        src_ref=src,
        dst_ref=dst,
        send_sem=sems.at[0],
        recv_sem=sems.at[1],
        device_id=device,
        device_id_type=MESH,
    )


def ffn_scatter_kernel(scatter, per, *refs):
    (
        cot_turned, norm_own, norm_other, right_own, right_other, gate_own, gate_other,
        cot_hbm, middle_hbm, parts_hbm, gain_ref, wd_ref,
    ) = refs[:12]
    outs = refs[12:15]
    gate_ref, gm_ref, block_own, block_send = refs[15:19]
    (
        norm_turned, cot_own, middle_own, part_own, got_part, gm_own, gain_got, acc_other,
        gain_sems, part_sems, gm_sems, local_sems,
    ) = refs[19:31]
    scatter.bind(refs[31:])
    step = pl.program_id(0)
    side = scatter.side
    across = (scatter.me, 1 - side)
    half = part_own.shape[0]
    quarter = half // QUARTERS
    row_chunk = 128

    def part_copy(r):
        span = pl.ds(r * quarter, quarter)
        return remote(parts_hbm.at[1, span], got_part.at[span], part_sems.at[r], across)

    def gm_copy(r):
        span = pl.ds(r * quarter, quarter)
        return remote(gm_own.at[span], gm_ref.at[side, span], gm_sems.at[r], across)

    def gain_copy():
        return remote(gain_ref, gain_got, gain_sems, across)

    loads = [
        pltpu.make_async_copy(cot_hbm, cot_own, local_sems.at[0]),
        pltpu.make_async_copy(parts_hbm.at[0], part_own, local_sems.at[1]),
        pltpu.make_async_copy(middle_hbm, middle_own, local_sems.at[2]),
    ]

    def gm_keep():
        return pltpu.make_async_copy(gm_own, gm_ref.at[side], local_sems.at[3])

    @pl.when(step == 0)
    def _():
        for load in loads:
            load.start()
        scatter.barrier()
        for r in range(QUARTERS):
            part_copy(r).start()
        gain_copy().start()

    scatter.advance(step, functools.partial(emit_into, outs, per))

    @pl.when(step < per)
    def _():
        scatter.multiply(step, cot_turned, (right_own, right_other))

        @pl.when(step == 0)
        def _():
            block_own[...] = jnp.zeros_like(block_own)
            acc_other[...] = jnp.zeros_like(acc_other)

        @pl.loop(0, half // 256)
        def _(i):
            span = pl.ds(i * 256, 256)
            block_own[span, :] += nt(right_own[span, :], wd_ref[...])
            acc_other[span, :] += nt(right_other[span, :], wd_ref[...])

    pieces = [(norm_own, 0, r) for r in range(0, half, 256)]
    pieces += [(norm_other, half, r) for r in range(0, half, 256)]
    for nth, (left, start, row) in enumerate(pieces):

        @pl.when(step == per - len(pieces) + nth)
        def _():
            turn_piece(norm_turned, left, start, row)

    @pl.when((step >= per) & (step < 2 * per))
    def _():
        scatter.multiply(step, norm_turned, (right_own, right_other))
        rows = gate_ref.shape[0] // 4

        @pl.loop(0, 4)
        def _(i):
            span = pl.ds(i * rows, rows)
            total = nn(norm_turned[span, :half], gate_own[...])
            gate_ref[span, :] = (total + nn(norm_turned[span, half:], gate_other[...])).astype(BF)

    @pl.when(step == 2 * per)
    def _():
        gain_copy().wait()
        scatter.put_gain(step, gain_ref[0:1, :] + gain_got[0:1, :])

    for r in range(QUARTERS):

        @pl.when(step == 3 + 2 * r)
        def _():
            if r == 0:
                for load in loads:
                    load.wait()
            part_copy(r).wait()

            @pl.loop(r * quarter // row_chunk, (r + 1) * quarter // row_chunk)
            def _(i):
                span = pl.ds(i * row_chunk, row_chunk)
                total = cot_own[span, :].astype(F32) + part_own[span, :].astype(F32)
                gm_own[span, :] = (total + got_part[span, :].astype(F32)).astype(BF)

            gm_copy(r).start()
            if r == QUARTERS - 1:
                gm_keep().start()

    @pl.when(step == 2 * per + 1)
    def _():
        @pl.loop(0, half // row_chunk)
        def _(i):
            span = pl.ds(i * row_chunk, row_chunk)
            block_own[span, :] += middle_own[span, :].astype(F32)
            block_send[span, :] = acc_other[span, :].astype(BF)

    @pl.when(step == scatter.steps - 1)
    def _():
        for r in range(QUARTERS):
            gm_copy(r).wait()
        gm_keep().wait()


def remote_settings(identity, mib=60):
    return pltpu.CompilerParams(
        dimension_semantics=("arbitrary",),
        vmem_limit_bytes=mib * 1024 * 1024,
        collective_id=identity,
        has_side_effects=True,
    )


def ffn_scatter(devices, cot_turned, normed, grads, cot, middle, parts, gain_part, w):
    half, d = middle.shape
    width = grads.shape[3]
    per = width // COLS
    scatter = Scatter(devices, d // devices, 2 * per + 1)
    assert 2 * per > 3 + 2 * QUARTERS and scatter.rows * devices == d and per >= 2 * half // 256

    def right(side):
        def where(j):
            c = jnp.minimum(j, 2 * per - 1)
            return (side, 2 - c // per, 0, c % per)

        return pl.BlockSpec((None, None, half, COLS), where)

    def gate_block(j):
        return jnp.clip(j - per, 0, per - 1)

    def gate(side):
        return pl.BlockSpec((None, None, half, COLS), lambda j: (side, 0, 0, gate_block(j)))

    def rows_of(side):
        return pl.BlockSpec(
            (None, half, d), lambda j: (side, 0, 0), pipeline_mode=pl.Buffered(1)
        )

    specs, shapes = emit_specs(scatter, 2, per, width)
    whole = lambda j: (0, 0)
    left_there = pl.BlockSpec(memory_space=pl.ANY)
    return pl.pallas_call(
        functools.partial(ffn_scatter_kernel, scatter, per),
        grid=(scatter.steps,),
        in_specs=[
            resident((d, 2 * half)),
            rows_of(0),
            rows_of(1),
            right(0),
            right(1),
            gate(0),
            gate(1),
            left_there,
            left_there,
            left_there,
            resident((8, d)),
            pl.BlockSpec((d, COLS), lambda j: (0, 2 * per + jnp.minimum(j, per - 1))),
        ],
        out_specs=specs
        + [
            pl.BlockSpec((d, COLS), lambda j: (0, gate_block(j))),
            left_there,
            pl.BlockSpec((half, d), whole),
            pl.BlockSpec((half, d), whole),
        ],
        out_shape=shapes
        + [
            jax.ShapeDtypeStruct((d, width), BF),
            jax.ShapeDtypeStruct((2, half, d), BF),
            jax.ShapeDtypeStruct((half, d), F32),
            jax.ShapeDtypeStruct((half, d), BF),
        ],
        scratch_shapes=[
            pltpu.VMEM((d, 2 * half), BF),
            pltpu.VMEM((half, d), BF),
            pltpu.VMEM((half, d), BF),
            pltpu.VMEM((half, d), BF),
            pltpu.VMEM((half, d), BF),
            pltpu.VMEM((half, d), BF),
            pltpu.VMEM((8, d), F32),
            pltpu.VMEM((half, d), F32),
            pltpu.SemaphoreType.DMA((2,)),
            pltpu.SemaphoreType.DMA((QUARTERS, 2)),
            pltpu.SemaphoreType.DMA((QUARTERS, 2)),
            pltpu.SemaphoreType.DMA((4,)),
        ]
        + scatter.scratch(),
        compiler_params=remote_settings(0),
        cost_estimate=cost(16 * half * d * per * COLS, 20 * half * d),
        name="ffn_scatter",
    )(
        cot_turned, normed, normed, grads, grads, grads, grads, cot, middle, parts, gain_part, w,
    )


def attention_scatter_kernel(scatter, per, *refs):
    (
        norm_turned, gain_ref, right_ref, w_ref, attended_ref, gm_hbm, x_hbm, block_hbm, block_send,
    ) = refs[:9]
    outs = refs[9:14]
    token_grad_ref, block_out_ref = refs[14:16]
    (
        gm_turned, gm_ref, x_ref, block_own, acc_ref, part_send, part_got, block_got,
        gain_part, part_sems, block_sems, local_sems,
    ) = refs[16:28]
    scatter.bind(refs[28:])
    step = pl.program_id(0)
    side = scatter.side
    across = (scatter.me, 1 - side)
    length = x_ref.shape[0]
    half = length // 2
    quarter = half // QUARTERS
    chunk = 128
    kinds = 3 * per
    own, other = side * half, (1 - side) * half

    def part_copy(r):
        span = pl.ds(r * quarter, quarter)
        return remote(part_send.at[span], part_got.at[span], part_sems.at[r], across)

    def block_copy():
        return remote(block_send, block_got, block_sems, across)

    loads = [
        pltpu.make_async_copy(x_hbm, x_ref, local_sems.at[0]),
        pltpu.make_async_copy(gm_hbm, gm_ref, local_sems.at[1]),
        pltpu.make_async_copy(block_hbm, block_own, local_sems.at[2]),
    ]

    def back(row):
        span = pl.ds(row, chunk)
        part, piece = rms_back(acc_ref[span, :], x_ref[span, :].astype(F32), gain_ref[...])
        gain_part[...] += jnp.broadcast_to(piece, gain_part.shape)
        return part

    @pl.when(step == 0)
    def _():
        for load in loads:
            load.start()
        scatter.barrier()
        block_copy().start()

    scatter.advance(step, functools.partial(emit_into, outs, per))

    @pl.when(step == 0)
    def _():
        acc_ref[...] = jnp.zeros_like(acc_ref)
        gain_part[...] = jnp.zeros_like(gain_part)

    @pl.when(step < kinds)
    def _():
        scatter.multiply(step, norm_turned, (right_ref,))

        @pl.loop(0, length // 256)
        def _(i):
            span = pl.ds(i * 256, 256)
            acc_ref[span, :] += nt(right_ref[span, :], w_ref[...])

    @pl.when(step == 1)
    def _():
        for load in loads:
            load.wait()

    for nth, row in enumerate(range(0, length, 256)):

        @pl.when(step == kinds - length // 256 + nth)
        def _():
            turn_piece(gm_turned, gm_ref, 0, row)

    @pl.when((step >= kinds) & (step < 4 * per))
    def _():
        scatter.multiply(step, gm_turned, (attended_ref,))

    for r in range(QUARTERS):

        @pl.when(step == kinds + min(r, per - 1))
        def _():
            @pl.loop(r * quarter // chunk, (r + 1) * quarter // chunk)
            def _(i):
                part_send[pl.ds(i * chunk, chunk), :] = back(other + i * chunk).astype(BF)

            part_copy(r).start()

            @pl.loop(r * quarter // chunk, (r + 1) * quarter // chunk)
            def _(i):
                span = pl.ds(own + i * chunk, chunk)
                acc_ref[span, :] = back(own + i * chunk) + gm_ref[span, :].astype(F32)

    @pl.when(step == 4 * per)
    def _():
        scatter.put_gain(step, gain_part[0:1, :])

    @pl.when(step == 4 * per + 1)
    def _():
        block_copy().wait()

        @pl.loop(0, half // chunk)
        def _(i):
            span = pl.ds(i * chunk, chunk)
            total = block_own[span, :] + block_got[span, :].astype(F32)
            block_out_ref[span, :] = total.astype(BF)

    for r in range(QUARTERS):

        @pl.when(step == scatter.steps - QUARTERS + r)
        def _():
            part_copy(r).wait()

            @pl.loop(r * quarter // chunk, (r + 1) * quarter // chunk)
            def _(i):
                span = pl.ds(i * chunk, chunk)
                total = acc_ref[pl.ds(own + i * chunk, chunk), :]
                token_grad_ref[span, :] = (total + part_got[span, :].astype(F32)).astype(BF)


def attention_scatter(
    devices, norm_turned, gm, x, gain, grads, attended, block_own, block_send, w
):
    length, d = gm.shape
    half = length // 2
    width = grads.shape[2]
    per = width // COLS
    kinds = 3 * per
    scatter = Scatter(devices, d // devices, 4 * per + 1)
    assert kinds >= length // 256 and scatter.rows * devices == d
    assert scatter.starts[-1] > QUARTERS

    def grads_map(j):
        c = jnp.minimum(j, kinds - 1)
        return (c // per, 0, c % per)

    def attended_map(j):
        return (0, jnp.clip(j - kinds, 0, per - 1))

    specs, shapes = emit_specs(scatter, 4, per, width)
    whole = lambda j: (0, 0)
    left_there = pl.BlockSpec(memory_space=pl.ANY)
    return pl.pallas_call(
        functools.partial(attention_scatter_kernel, scatter, per),
        grid=(scatter.steps,),
        in_specs=[
            resident((d, length)),
            resident((1, d)),
            pl.BlockSpec((None, length, COLS), grads_map),
            pl.BlockSpec((d, COLS), lambda j: (0, jnp.minimum(j, kinds - 1))),
            pl.BlockSpec((length, COLS), attended_map),
            left_there,
            left_there,
            left_there,
            left_there,
        ],
        out_specs=specs + [pl.BlockSpec((half, d), whole), pl.BlockSpec((half, d), whole)],
        out_shape=shapes
        + [jax.ShapeDtypeStruct((half, d), BF), jax.ShapeDtypeStruct((half, d), BF)],
        scratch_shapes=[
            pltpu.VMEM((d, length), BF),
            pltpu.VMEM((length, d), BF),
            pltpu.VMEM((length, d), BF),
            pltpu.VMEM((half, d), F32),
            pltpu.VMEM((length, d), F32),
            pltpu.VMEM((half, d), BF),
            pltpu.VMEM((half, d), BF),
            pltpu.VMEM((half, d), BF),
            pltpu.VMEM((8, d), F32),
            pltpu.SemaphoreType.DMA((QUARTERS, 2)),
            pltpu.SemaphoreType.DMA((2,)),
            pltpu.SemaphoreType.DMA((3,)),
        ]
        + scatter.scratch(),
        compiler_params=remote_settings(1),
        cost_estimate=cost(14 * length * d * per * COLS, 20 * length * d),
        name="attention_scatter",
    )(norm_turned, gain, grads, w, attended, gm, x, block_own, block_send)


class Gather:
    def __init__(self, devices, rows, count):
        self.devices, self.rows, self.count = devices, rows, count
        self.stages = devices.bit_length() - 1
        self.lags = [2] * (self.stages - 1) + [1]
        self.starts = [sum(self.lags[:t]) for t in range(self.stages + 1)]
        self.steps = count + self.starts[-1]

    def scratch(self):
        return [
            pltpu.VMEM((self.count, self.devices, self.rows, COLS), BF),
            pltpu.SemaphoreType.DMA((self.stages, self.count, 2)),
            pltpu.SemaphoreType.DMA((self.count,)),
        ]

    def bind(self, refs):
        self.held, self.sems, self.load_sems = refs
        self.me, self.side = lax.axis_index("dp"), lax.axis_index("tensor")

    def late(self, block):
        return (block % 4) // 3 if self.stages >= 4 else 0 * block

    def place(self, device, block):
        late = self.late(block)
        total = 0
        for t in range(self.stages):
            bit = (device // (1 << (self.stages - 1 - t))) % 2
            if t in (1, 2) and self.stages >= 4:
                total = total + bit * ((1 << t) * (1 - late) + (1 << (3 - t)) * late)
            else:
                total = total + bit * (1 << t)
        return total

    def partner_at(self, t):
        weight = 1 << (self.stages - 1 - t)
        return self.me + (1 - 2 * ((self.me // weight) % 2)) * weight

    def partner(self, t, block):
        if t not in (1, 2) or self.stages < 4:
            return self.partner_at(t)
        late = self.late(block)
        return self.partner_at(t) * (1 - late) + self.partner_at(3 - t) * late

    def barrier(self):
        arrived = pltpu.get_barrier_semaphore()
        for t in range(self.stages):
            pl.semaphore_signal(
                arrived, inc=1, device_id=(self.partner_at(t), self.side), device_id_type=MESH
            )
        pl.semaphore_signal(
            arrived, inc=1, device_id=(self.me, 1 - self.side), device_id_type=MESH
        )
        pl.semaphore_wait(arrived, self.stages + 1)

    def load(self, shard, column, block):
        return pltpu.make_async_copy(
            shard.at[:, pl.ds(column, COLS)],
            self.held.at[block, self.place(self.me, block)],
            self.load_sems.at[block],
        )

    def load_all(self, shards):
        block = 0
        for shard in shards:
            for column in range(0, shard.shape[1], COLS):
                self.load(shard, column, jnp.int32(block)).start()
                block += 1

    def copy(self, t, block):
        size = 1 << t
        first = self.place(self.me, block) // size * size
        run = self.held.at[block, pl.ds(first, size)]
        return remote(run, run, self.sems.at[t, block], (self.partner(t, block), self.side))

    def advance(self, step, shards):
        for t in range(self.stages, -1, -1):
            block = step - self.starts[t]

            @pl.when((block >= 0) & (block < self.count))
            def _():
                if t > 0:
                    self.copy(t - 1, block).wait()
                else:
                    self.load(shards[0], 0, block).wait()
                if t < self.stages:
                    self.copy(t, block).start()


def gather_project_kernel(gather, per, *refs):
    shards, (tokens, cot, gain_ref, depths_ref) = refs[:4], refs[4:8]
    w_hbm, qkv_ref, turned_ref, rows_hbm, cot_other, cos_ref, sin_ref, done_ref = refs[8:16]
    w_ref, rows_ref, normed_ref, x_sems, row_sems, w_sems = refs[16:22]
    gather.bind(refs[22:])
    step = pl.program_id(0)
    side = gather.side
    across = (gather.me, 1 - side)
    lead = gather.starts[-1]
    others = lead + gather.count // 2 - 1
    kinds = 3 * per

    def token_copy():
        return remote(tokens, rows_ref.at[side], x_sems.at[0], across)

    def cot_copy():
        return remote(cot, cot_other, x_sems.at[1], across)

    def token_load():
        return pltpu.make_async_copy(tokens, rows_ref.at[side], row_sems.at[0])

    def rows_store():
        return pltpu.make_async_copy(rows_ref, rows_hbm, row_sems.at[1])

    def w_store(block):
        cols = pl.ds(pl.multiple_of(block * COLS, COLS), COLS)
        return pltpu.make_async_copy(w_ref.at[:, cols], w_hbm.at[:, cols], w_sems.at[block])

    @pl.when(step == 0)
    def _():
        token_load().start()
        gather.load_all(shards)
        gather.barrier()
        token_copy().start()
        cot_copy().start()

    gather.advance(step, shards)

    @pl.when(step == 1)
    def _():
        token_load().wait()
        norm_rows(rows_ref.at[side], gain_ref, normed_ref.at[side])
        turn_tables(depths_ref, cos_ref, sin_ref)

    for nth, row in enumerate(range(0, rows_ref.shape[1], 256)):

        @pl.when(step == 2 + nth)
        def _():
            turn_piece(turned_ref, normed_ref.at[side], side * rows_ref.shape[1], row)

        @pl.when(step == others + 1 + nth)
        def _():
            turn_piece(turned_ref, normed_ref.at[1 - side], (1 - side) * rows_ref.shape[1], row)

    @pl.when(step == others)
    def _():
        token_copy().wait()
        rows_store().start()
        norm_rows(rows_ref.at[1 - side], gain_ref, normed_ref.at[1 - side])

    @pl.when(step >= lead)
    def _():
        block = step - lead
        cols = pl.ds(pl.multiple_of(block * COLS, COLS), COLS)
        for device in range(gather.devices):
            rows = slice(device * gather.rows, (device + 1) * gather.rows)
            w_ref[rows, cols] = gather.held[block, gather.place(device, block)]
        w_store(block).start()

    @pl.loop(0, 3)
    def _(task):
        mine = jnp.where(task == 0, 1, 0)
        half = side * mine + (1 - side) * (1 - mine)
        block = (step - lead) * mine + (2 * (step - others) + task - 1) * (1 - mine)
        cols = pl.ds(pl.multiple_of(block * COLS, COLS), COLS)
        chunk = 256

        @pl.when((block >= 0) & (block < 2 * per))
        def _():
            scale = jnp.where(block < per, 1.0 / math.sqrt(HD), 1.0).astype(BF)
            for r in range(0, qkv_ref.shape[1], chunk):
                span = slice(r, r + chunk)
                pre = nn(normed_ref[half, span, :], w_ref[:, cols])
                cosine = jnp.concatenate([cos_ref[half, span, :]] * (COLS // LANES), axis=1)
                sine = jnp.concatenate([sin_ref[half, span, :]] * (COLS // LANES), axis=1)
                turned = turn(pre, cosine, sine)
                qkv_ref[half, span, cols] = turned.astype(BF) * scale

        @pl.when((block >= 2 * per) & (block < kinds))
        def _():
            for r in range(0, qkv_ref.shape[1], chunk):
                span = slice(r, r + chunk)
                qkv_ref[half, span, cols] = nn(normed_ref[half, span, :], w_ref[:, cols]).astype(BF)

    @pl.when(step == gather.steps - 1)
    def _():
        done_ref[...] = gain_ref[...]
        cot_copy().wait()
        rows_store().wait()

        @pl.loop(0, gather.count)
        def _(block):
            w_store(block).wait()


def gather_project(devices, shards, tokens, cot, gain, depths):
    half, d = tokens.shape
    rows, width = shards[0].shape
    total = len(shards) * width
    per = width // COLS
    gather = Gather(devices, rows, total // COLS)
    count = gather.count
    assert rows * devices == d and count // 2 - 1 + (3 * per + 1) // 2 <= count
    left_there = pl.BlockSpec(memory_space=pl.ANY)
    return pl.pallas_call(
        functools.partial(gather_project_kernel, gather, per),
        grid=(gather.steps,),
        in_specs=[left_there] * 6 + [resident((1, d)), pl.BlockSpec(memory_space=pltpu.SMEM)],
        out_specs=[
            left_there,
            resident((2, half, 3 * width)),
            resident((d, 2 * half)),
            left_there,
            left_there,
            resident((2, half, LANES)),
            resident((2, half, LANES)),
            resident((1, d)),
        ],
        out_shape=[
            jax.ShapeDtypeStruct((d, total), BF),
            jax.ShapeDtypeStruct((2, half, 3 * width), BF),
            jax.ShapeDtypeStruct((d, 2 * half), BF),
            jax.ShapeDtypeStruct((2, half, d), BF),
            jax.ShapeDtypeStruct((half, d), BF),
            jax.ShapeDtypeStruct((2, half, LANES), F32),
            jax.ShapeDtypeStruct((2, half, LANES), F32),
            jax.ShapeDtypeStruct((1, d), F32),
        ],
        scratch_shapes=[
            pltpu.VMEM((d, total), BF),
            pltpu.VMEM((2, half, d), BF),
            pltpu.VMEM((2, half, d), BF),
            pltpu.SemaphoreType.DMA((2, 2)),
            pltpu.SemaphoreType.DMA((2,)),
            pltpu.SemaphoreType.DMA((count,)),
        ]
        + gather.scratch(),
        compiler_params=remote_settings(2),
        cost_estimate=cost(12 * half * d * width, 2 * d * total),
        name="gather_project",
    )(*shards, tokens, cot, gain, depths)


def swap(x):
    return lax.ppermute(x, "tensor", [(0, 1), (1, 0)])


def body(
    tokens,
    parents,
    attn_gain,
    ffn_gain,
    query_weight,
    key_weight,
    value_weight,
    output_weight,
    gate_weight,
    up_weight,
    down_weight,
    cotangent,
):
    half, d = tokens.shape
    length = 2 * half
    width = query_weight.shape[1]
    hidden_width = gate_weight.shape[1]
    seg_rows = length // parents.shape[1]
    mine = lax.axis_index("tensor")
    own_start = mine * half
    other_start = (1 - mine) * half

    def own_rows(full):
        return lax.dynamic_slice_in_dim(full, own_start, half, 0)

    def other_rows(full):
        return lax.dynamic_slice_in_dim(full, other_start, half, 0)

    def gather(shard):
        return lax.all_gather(shard, "dp", axis=0, tiled=True)

    attn_row = attn_gain[None, :]
    ffn_row = ffn_gain[None, :]

    devices = lax.axis_size("dp")
    bias, depths = tree_tables(parents[0], seg_rows)

    first, qkv, norm_turned, rows_all, cot_other, cosine, sine, attn_row = gather_project(
        devices,
        (query_weight, key_weight, value_weight, output_weight.T),
        tokens,
        cotangent,
        attn_row,
        depths,
    )
    second_shard, attn_row = lax.optimization_barrier(
        (jnp.concatenate([gate_weight, up_weight, down_weight.T], axis=1), attn_row)
    )
    second = gather(second_shard)
    qkv = qkv.reshape(length, 3 * width)
    rows_all = rows_all.reshape(length, d)
    cosine, sine = cosine.reshape(length, LANES), sine.reshape(length, LANES)

    attended, lse = attend(qkv, bias, width, seg_rows)
    out_turned = first[:, 3 * width :]
    send = nt(other_rows(attended), out_turned).astype(BF)
    send, cot_source = lax.optimization_barrier((send, cot_other))
    received = swap(send)
    received, cot_turned = lax.optimization_barrier((received, turn_pair(cotangent, cot_source)))
    middle = (
        tokens.astype(F32) + nt(own_rows(attended), out_turned) + received.astype(F32)
    ).astype(BF)
    middle_other = swap(middle)

    ffn_grads, normed_two, parts, gain_part = ffn(
        (middle, middle_other), (cotangent, cot_other), ffn_row, second, hidden_width
    )
    down_grad, up_grad, ffn_gain_grad, gate_whole, grad_middle, block_own, block_send = ffn_scatter(
        devices, cot_turned, normed_two, ffn_grads, cotangent, middle, parts, gain_part, second
    )
    gate_grad = lax.psum_scatter(gate_whole, "dp", scatter_dimension=0, tiled=True).astype(F32)
    grad_middle = grad_middle.reshape(length, d)

    grad_attended = nn(grad_middle, out_turned).astype(BF)
    grads = attend_back(
        qkv, attended, grad_attended, lse, bias, cosine, sine, seg_rows
    )
    (
        query_grad, key_grad, value_grad, output_grad, attn_gain_grad, token_grad, block_out,
    ) = attention_scatter(
        devices,
        norm_turned,
        grad_middle,
        rows_all,
        attn_row,
        grads,
        attended,
        block_own,
        block_send,
        first,
    )
    gain_rows = d // devices // 2

    def gain_piece(columns, side):
        return lax.dynamic_slice_in_dim(columns[:, 0], side * gain_rows, gain_rows, 0)

    return (
        block_out,
        token_grad,
        query_grad,
        key_grad,
        value_grad,
        output_grad.T,
        gate_grad,
        up_grad,
        down_grad.T,
        gain_piece(attn_gain_grad, mine) + swap(gain_piece(attn_gain_grad, 1 - mine)),
        gain_piece(ffn_gain_grad, mine),
    )


def solution(mesh):
    rows = P(("dp", "tensor"), None)
    tall = P("dp", "tensor")
    wide = P("tensor", "dp")
    return jax.shard_map(
        body,
        mesh=mesh,
        in_specs=(
            rows, P("dp", None), P(), P(), tall, tall, tall, wide, tall, tall, wide, rows,
        ),
        out_specs=(
            rows, rows, tall, tall, tall, wide, tall, tall, wide,
            P(("dp", "tensor")), P(("dp", "tensor")),
        ),
        check_vma=False,
    )
```

```python
import functools
import math

import jax
import jax.numpy as jnp
from jax import lax
from jax.experimental import pallas as pl
from jax.experimental.pallas import tpu as pltpu
from jax.sharding import PartitionSpec as P

HD = 64
EPS = 1e-05
BF = jnp.bfloat16
F32 = jnp.float32
COLS = 256
LANES = 128
MASKED = -1e30


def settings(mib=48):
    return pltpu.CompilerParams(
        dimension_semantics=("arbitrary",), vmem_limit_bytes=mib * 1024 * 1024
    )


def cost(flops, bytes_accessed, transcendentals=0):
    return pl.CostEstimate(
        flops=int(flops), bytes_accessed=int(bytes_accessed), transcendentals=int(transcendentals)
    )


def nn(a, b):
    return jnp.dot(a, b, preferred_element_type=F32)


def nt(a, b):
    return lax.dot_general(a, b, (((1,), (1,)), ((), ())), preferred_element_type=F32)


def tree_tables(parent_row, seg_rows):
    segs = parent_row.shape[0]
    index = jnp.arange(segs, dtype=jnp.int32)
    step_up = (parent_row[:, None] == index[None, :]).astype(jnp.int32)
    eye = (index[:, None] == index[None, :]).astype(jnp.int32)
    reach = eye
    for _ in range(segs):
        up = jnp.sum(step_up[:, :, None] * reach[None, :, :], axis=1)
        reach = jnp.minimum(eye + up, 1)
    depths = jnp.sum(reach, axis=1) - 1
    bias = jnp.where(reach.T > 0, 0.0, MASKED).astype(F32)
    return jnp.repeat(bias, seg_rows, axis=1), depths


def turn_tables(depths_ref, cos_ref, sin_ref):
    segs = depths_ref.shape[0]
    seg_rows = 2 * cos_ref.shape[1] // segs
    shape = (seg_rows, LANES)
    lane = lax.broadcasted_iota(jnp.int32, shape, 1) % HD
    row = lax.broadcasted_iota(jnp.int32, shape, 0)
    rates = jnp.exp((lane % (HD // 2)).astype(F32) * (-2.0 * math.log(10000.0) / HD))
    sign = jnp.where(lane < HD // 2, -1.0, 1.0).astype(F32)

    @pl.loop(0, segs)
    def _(seg):
        angles = (depths_ref[seg] * seg_rows + row).astype(F32) * rates
        span = pl.ds(seg % (segs // 2) * seg_rows, seg_rows)
        cos_ref[seg // (segs // 2), span, :] = jnp.cos(angles)
        sin_ref[seg // (segs // 2), span, :] = jnp.sin(angles) * sign


def turn(x, cosine, sine):
    width = x.shape[1]
    lane = lax.broadcasted_iota(jnp.int32, x.shape, 1)
    first = (lane % HD) < HD // 2
    other = jnp.where(
        first, pltpu.roll(x, width - HD // 2, 1), pltpu.roll(x, HD // 2, 1)
    )
    return x * cosine + other * sine


def inverse_rms(x):
    return lax.rsqrt(jnp.mean(x * x, axis=1, keepdims=True) + EPS)


def norm_rows(x_ref, gain_ref, normed_ref):
    chunk = 128

    @pl.loop(0, x_ref.shape[0] // chunk)
    def _(i):
        span = pl.ds(i * chunk, chunk)
        x = x_ref[span, :].astype(F32)
        normed_ref[span, :] = (x * inverse_rms(x) * gain_ref[...]).astype(BF)


def mask_block(block, seg_rows, bias_ref, m, u):
    cols = slice(m * block, (m + 1) * block)
    per = block // seg_rows
    return jnp.concatenate(
        [
            jnp.broadcast_to(bias_ref[u * per + i : u * per + i + 1, cols], (seg_rows, block))
            for i in range(per)
        ],
        axis=0,
    )


def causal(block):
    key = lax.broadcasted_iota(jnp.int32, (block, block), 0)
    query = lax.broadcasted_iota(jnp.int32, (block, block), 1)
    return key <= query


def attend_kernel(block, seg_rows, q_ref, k_ref, v_ref, bias_ref, out_ref, lse_ref):
    length = q_ref.shape[0]
    heads = q_ref.shape[1] // HD
    v_turned = v_ref[...].T
    for m in range(length // block):
        cols = slice(m * block, (m + 1) * block)
        outs = []
        for h in range(heads):
            lanes = slice(h * HD, (h + 1) * HD)
            q = q_ref[cols, lanes]
            scores = []
            for u in range(m + 1):
                s = nt(k_ref[u * block : (u + 1) * block, lanes], q)
                s = s + mask_block(block, seg_rows, bias_ref, m, u)
                if u == m:
                    s = jnp.where(causal(block), s, MASKED)
                scores.append(s)
            peak = scores[0].max(axis=0, keepdims=True)
            for s in scores[1:]:
                peak = jnp.maximum(peak, s.max(axis=0, keepdims=True))
            total = jnp.zeros_like(peak)
            acc = jnp.zeros((HD, block), F32)
            for u, s in enumerate(scores):
                e = jnp.exp(s - peak)
                total = total + e.sum(axis=0, keepdims=True)
                acc = acc + nn(v_turned[lanes, u * block : (u + 1) * block], e.astype(BF))
            outs.append(acc / total)
            lse_ref[0, h : h + 1, cols] = peak + jnp.log(total)
        out_ref[cols, :] = jnp.concatenate(outs, axis=0).T.astype(BF)


def attend(qkv, bias, width, seg_rows):
    length = qkv.shape[0]
    groups = width // LANES
    heads = LANES // HD
    block = 2 * seg_rows
    live = length * length // 2
    return pl.pallas_call(
        functools.partial(attend_kernel, block, seg_rows),
        grid=(groups,),
        in_specs=[
            pl.BlockSpec((length, LANES), lambda i: (0, i)),
            pl.BlockSpec((length, LANES), lambda i: (0, groups + i)),
            pl.BlockSpec((length, LANES), lambda i: (0, 2 * groups + i)),
            pl.BlockSpec(bias.shape, lambda i: (0, 0)),
        ],
        out_specs=[
            pl.BlockSpec((length, LANES), lambda i: (0, i)),
            pl.BlockSpec((1, heads, length), lambda i: (i, 0, 0)),
        ],
        out_shape=[
            jax.ShapeDtypeStruct((length, width), BF),
            jax.ShapeDtypeStruct((groups, heads, length), F32),
        ],
        compiler_params=settings(),
        cost_estimate=cost(16 * live * width, 8 * length * width, live * width // HD),
        name="attend",
    )(qkv, qkv, qkv, bias)


def attend_back_kernel(
    block,
    seg_rows,
    q_ref,
    k_ref,
    v_ref,
    o_ref,
    do_ref,
    lse_ref,
    bias_ref,
    cos_ref,
    sin_ref,
    out_ref,
    dk_ref,
    dv_ref,
):
    length = q_ref.shape[0]
    heads = q_ref.shape[1] // HD
    k_turned = k_ref[...].T
    product = (do_ref[...].astype(F32) * o_ref[...].astype(F32)).T
    deltas = [product[h * HD : (h + 1) * HD].sum(axis=0, keepdims=True) for h in range(heads)]
    for m in range(length // block):
        cols = slice(m * block, (m + 1) * block)
        grads = []
        for h in range(heads):
            lanes = slice(h * HD, (h + 1) * HD)
            q, do = q_ref[cols, lanes], do_ref[cols, lanes]
            lse = lse_ref[0, h : h + 1, cols]
            delta = deltas[h][:, cols]
            acc = jnp.zeros((HD, block), F32)
            for u in range(m + 1):
                keys = slice(u * block, (u + 1) * block)
                s = nt(k_ref[keys, lanes], q)
                p = jnp.exp(s + (mask_block(block, seg_rows, bias_ref, m, u) - lse))
                if u == m:
                    p = jnp.where(causal(block), p, 0.0)
                dp = nt(v_ref[keys, lanes], do)
                ds = (p * (dp - delta)).astype(BF)
                dv = nn(p.astype(BF), do)
                dk = nn(ds, q)
                if u == m:
                    dv_ref[h, keys, :] = dv
                    dk_ref[h, keys, :] = dk
                else:
                    dv_ref[h, keys, :] += dv
                    dk_ref[h, keys, :] += dk
                acc = acc + nn(k_turned[lanes, keys], ds)
            grads.append(acc)
        dq = jnp.concatenate(grads, axis=0).T * (1.0 / math.sqrt(HD))
        out_ref[0, cols, :] = turn(dq, cos_ref[cols, :], -sin_ref[cols, :]).astype(BF)
    for m in range(length // block):
        cols = slice(m * block, (m + 1) * block)
        dk = jnp.concatenate([dk_ref[h, cols, :] for h in range(heads)], axis=1)
        out_ref[1, cols, :] = turn(dk, cos_ref[cols, :], -sin_ref[cols, :]).astype(BF)
        out_ref[2, cols, :] = jnp.concatenate(
            [dv_ref[h, cols, :] for h in range(heads)], axis=1
        ).astype(BF)


def attend_back(qkv, attended, grad_attended, lse, bias, cosine, sine, seg_rows):
    length, width = attended.shape
    groups = width // LANES
    heads = LANES // HD
    block = 2 * seg_rows
    live = length * length // 2
    return pl.pallas_call(
        functools.partial(attend_back_kernel, block, seg_rows),
        grid=(groups,),
        in_specs=[
            pl.BlockSpec((length, LANES), lambda i: (0, i)),
            pl.BlockSpec((length, LANES), lambda i: (0, groups + i)),
            pl.BlockSpec((length, LANES), lambda i: (0, 2 * groups + i)),
            pl.BlockSpec((length, LANES), lambda i: (0, i)),
            pl.BlockSpec((length, LANES), lambda i: (0, i)),
            pl.BlockSpec((1, heads, length), lambda i: (i, 0, 0)),
            pl.BlockSpec(bias.shape, lambda i: (0, 0)),
            pl.BlockSpec((length, LANES), lambda i: (0, 0)),
            pl.BlockSpec((length, LANES), lambda i: (0, 0)),
        ],
        out_specs=pl.BlockSpec((3, length, LANES), lambda i: (0, 0, i)),
        out_shape=jax.ShapeDtypeStruct((3, length, width), BF),
        scratch_shapes=[
            pltpu.VMEM((heads, length, HD), F32),
            pltpu.VMEM((heads, length, HD), F32),
        ],
        compiler_params=settings(),
        cost_estimate=cost(40 * live * width, 16 * length * width, live * width // HD),
        name="attend_back",
    )(qkv, qkv, qkv, attended, grad_attended, lse, bias, cosine, sine)


def rms_back(grad, x, gain):
    inverse = inverse_rms(x)
    unit = x * inverse
    scaled = grad * gain
    inner = jnp.mean(scaled * unit, axis=1, keepdims=True)
    return inverse * (scaled - unit * inner), jnp.sum(grad * unit, axis=0, keepdims=True)


def back_rows(acc_ref, x_ref, gain_ref, gain_part_ref, part_ref):
    chunk = 128

    @pl.loop(0, x_ref.shape[0] // chunk)
    def _(i):
        span = pl.ds(i * chunk, chunk)
        part, piece = rms_back(acc_ref[span, :], x_ref[span, :].astype(F32), gain_ref[...])
        part_ref[span, :] = part.astype(part_ref.dtype)
        gain_part_ref[...] += jnp.broadcast_to(piece, gain_part_ref.shape)


def ffn_kernel(
    x_own,
    x_other,
    cot_own,
    cot_other,
    gain_ref,
    wg_ref,
    wu_ref,
    wd_ref,
    grads_ref,
    normed_ref,
    part_ref,
    gain_part_ref,
    got_hbm,
    cot_ref,
    acc_ref,
    part_send,
    part_sems,
):
    h, j = pl.program_id(0), pl.program_id(1)
    chunk = 256
    across = (lax.axis_index("dp"), 1 - lax.axis_index("tensor"))
    quarter = part_send.shape[0] // QUARTERS

    def part_copy(r):
        span = pl.ds(r * quarter, quarter)
        return remote(part_send.at[span], got_hbm.at[span], part_sems.at[r], across)

    @pl.when((h == 0) & (j == 0))
    def _():
        arrived = pltpu.get_barrier_semaphore()
        pl.semaphore_signal(arrived, inc=1, device_id=across, device_id_type=MESH)
        pl.semaphore_wait(arrived, 1)
        gain_part_ref[...] = jnp.zeros_like(gain_part_ref)

    for turn_at, (x_ref, c_ref) in enumerate(((x_other, cot_other), (x_own, cot_own))):

        @pl.when((h == turn_at) & (j == 0))
        def _():
            norm_rows(x_ref, gain_ref, normed_ref)
            cot_ref[...] = c_ref[...]

    @pl.when(j == 0)
    def _():
        acc_ref[...] = jnp.zeros_like(acc_ref)

    for r in range(0, cot_ref.shape[0], chunk):
        span = slice(r, r + chunk)
        gate = nn(normed_ref[span, :], wg_ref[...])
        up = nn(normed_ref[span, :], wu_ref[...])
        grad_hidden = nn(cot_ref[span, :], wd_ref[...])
        sig = jax.nn.sigmoid(gate)
        silu = gate * sig
        grads_ref[2, span, :] = (silu * up).astype(BF)
        grad_gate = (grad_hidden * up * (sig + silu * (1.0 - sig))).astype(BF)
        grad_up = (grad_hidden * silu).astype(BF)
        grads_ref[0, span, :] = grad_gate
        grads_ref[1, span, :] = grad_up
        acc_ref[span, :] += nt(grad_gate, wg_ref[...]) + nt(grad_up, wu_ref[...])

    for turn_at, x_ref in enumerate((x_other, x_own)):

        @pl.when((h == turn_at) & (j == pl.num_programs(1) - 1))
        def _():
            back_rows(acc_ref, x_ref, gain_ref, gain_part_ref, part_ref)
            if turn_at == 0:
                part_send[...] = part_ref[...]
                for r in range(EARLY):
                    part_copy(r).start()
            else:
                for r in range(EARLY):
                    part_copy(r).wait()


def resident(shape):
    zeros = (0,) * len(shape)
    return pl.BlockSpec(shape, lambda *grid: zeros, pipeline_mode=pl.Buffered(1))


def ffn(xs, cots, gain, w, hidden_width, cols=512):
    rows, d = xs[0].shape
    steps = hidden_width // cols
    per_half = lambda h, j: (1 - h, 0, 0)
    return pl.pallas_call(
        ffn_kernel,
        grid=(2, steps),
        in_specs=[resident((rows, d))] * 4
        + [
            resident((1, d)),
            pl.BlockSpec((d, cols), lambda h, j: (0, j)),
            pl.BlockSpec((d, cols), lambda h, j: (0, steps + j)),
            pl.BlockSpec((d, cols), lambda h, j: (0, 2 * steps + j)),
        ],
        out_specs=[
            pl.BlockSpec((None, 3, rows, cols), lambda h, j: (1 - h, 0, 0, j)),
            pl.BlockSpec((None, rows, d), per_half),
            pl.BlockSpec((None, rows, d), per_half),
            pl.BlockSpec((8, d), lambda h, j: (0, 0)),
            pl.BlockSpec(memory_space=pl.ANY),
        ],
        out_shape=[
            jax.ShapeDtypeStruct((2, 3, rows, hidden_width), BF),
            jax.ShapeDtypeStruct((2, rows, d), BF),
            jax.ShapeDtypeStruct((2, rows, d), BF),
            jax.ShapeDtypeStruct((8, d), F32),
            jax.ShapeDtypeStruct((rows, d), BF),
        ],
        scratch_shapes=[
            pltpu.VMEM((rows, d), BF),
            pltpu.VMEM((rows, d), F32),
            pltpu.VMEM((rows, d), BF),
            pltpu.SemaphoreType.DMA((EARLY, 2)),
        ],
        compiler_params=remote_settings(3, axes=2),
        cost_estimate=cost(
            20 * rows * d * hidden_width,
            12 * d * hidden_width + 16 * rows * d + 12 * rows * hidden_width,
            2 * rows * hidden_width,
        ),
        name="ffn",
    )(*xs, *cots, gain, w, w, w)


MESH = pl.DeviceIdType.MESH
QUARTERS = 4
EARLY = 3
UP_SENT = 8
GAIN_ROWS = 16


class Scatter:
    def __init__(self, devices, rows, count):
        self.devices, self.rows, self.count = devices, rows, count
        self.stages = devices.bit_length() - 1
        self.lags = [1] + [3] * (self.stages - 1)
        self.slots = [2 * lag for lag in self.lags]
        if self.stages >= 3:
            self.slots[1] = self.slots[2] = 8
        self.starts = [sum(self.lags[:s]) for s in range(self.stages + 1)]
        self.steps = count + self.starts[-1]

    def scratch(self):
        shapes = []
        for s in range(self.stages):
            slots, left = self.slots[s], self.devices >> (s + 1)
            shapes.append(pltpu.VMEM((slots, 2, left, self.rows, COLS), BF))
            shapes.append(pltpu.VMEM((slots, left, self.rows, COLS), BF))
            shapes.append(pltpu.SemaphoreType.DMA((slots,)))
            shapes.append(pltpu.SemaphoreType.DMA((slots,)))
        return shapes

    def bind(self, refs):
        self.held, self.got = refs[0::4], refs[1::4]
        self.sent_sem, self.got_sem = refs[2::4], refs[3::4]
        self.me, self.side = lax.axis_index("dp"), lax.axis_index("tensor")

    def late(self, block):
        return (block % 4) // 3

    def own_bit(self, b):
        return (self.me // (1 << b)) % 2

    def partner(self, b):
        return self.me + (1 - 2 * self.own_bit(b)) * (1 << b)

    def turned(self, s, block):
        if s not in (1, 2) or self.stages < 3:
            return self.own_bit(s), self.partner(s)
        late = self.late(block)
        return (
            self.own_bit(s) * (1 - late) + self.own_bit(3 - s) * late,
            self.partner(s) * (1 - late) + self.partner(3 - s) * late,
        )

    def barrier(self):
        arrived = pltpu.get_barrier_semaphore()
        for b in range(self.stages):
            pl.semaphore_signal(
                arrived, inc=1, device_id=(self.partner(b), self.side), device_id_type=MESH
            )
        pl.semaphore_signal(
            arrived, inc=1, device_id=(self.me, 1 - self.side), device_id_type=MESH
        )
        pl.semaphore_wait(arrived, self.stages + 1)

    def copy(self, s, block, gain=False):
        slot = block % self.slots[s]
        bit, partner = self.turned(s, block)
        src, dst = self.held[s].at[slot, 1 - bit], self.got[s].at[slot]
        if gain:
            src, dst = src.at[:, pl.ds(0, GAIN_ROWS)], dst.at[:, pl.ds(0, GAIN_ROWS)]
        sems = self.sent_sem[s].at[slot], self.got_sem[s].at[slot]
        return pltpu.make_async_remote_copy(
            src_ref=src,
            dst_ref=dst,
            send_sem=sems[0],
            recv_sem=sems[1],
            device_id=(partner, self.side),
            device_id_type=MESH,
        )

    def advance(self, step, emit):
        for s in range(self.stages, 0, -1):
            block = step - self.starts[s]
            last = self.count - 1
            for gain in (False, True):

                @pl.when((block == last) if gain else (block >= 0) & (block < last))
                def _():
                    self.receive(s, block, gain, emit)

    def receive(self, s, block, gain, emit):
        slot = block % self.slots[s - 1]
        self.copy(s - 1, block, gain).wait()
        keep, _ = self.turned(s - 1, block)
        held, got = self.held[s - 1], self.got[s - 1]
        rows = slice(0, GAIN_ROWS if gain else self.rows)
        if s == self.stages:
            total = held[slot, keep, 0, rows].astype(F32) + got[slot, 0, rows].astype(F32)
            emit(block, total, gain)
            return
        later = block % self.slots[s]
        late = self.late(block)

        def add(k, carry):
            total = held[slot, keep, k, rows] + got[slot, k, rows]
            bit, rest = k % 2, k // 2
            if s == 1 and self.stages >= 3:
                bit = bit * (1 - late) + (k // 2) % 2 * late
                rest = rest * (1 - late) + (k // 4 * 2 + k % 2) * late
            self.held[s][later, bit, rest, rows] = total
            return carry

        lax.fori_loop(0, self.devices >> s, add, 0)
        self.copy(s, block, gain).start()

    def multiply(self, block, turned_ref, rights):
        slot = block % self.slots[0]
        pieces = 4
        size = self.devices // pieces

        def piece(i, carry):
            span = pl.ds(i * size * self.rows, size * self.rows)
            total, start = None, 0
            for right in rights:
                part = nn(turned_ref[span, start : start + right.shape[0]], right[...])
                total = part if total is None else total + part
                start += right.shape[0]
            for r in range(size):
                block_rows = total[r * self.rows : (r + 1) * self.rows].astype(BF)
                self.held[0][slot, r % 2, i * (size // 2) + r // 2] = block_rows
            return carry

        lax.fori_loop(0, pieces, piece, 0)
        self.copy(0, block).start()

    def put_gain(self, block, row):
        slot = block % self.slots[0]
        empty = jnp.zeros((1, COLS - self.rows), F32)
        for k in range(self.devices):
            piece = jnp.concatenate([row[:, k * self.rows : (k + 1) * self.rows], empty], axis=1)
            piece = jnp.broadcast_to(piece, (GAIN_ROWS, COLS)).astype(BF)
            self.held[0][slot, k % 2, k // 2, :GAIN_ROWS] = piece
        self.copy(0, block, True).start()


def turn_piece(turned_ref, left, start, row):
    cols = pl.ds(pl.multiple_of(start + row, 256), 256)

    @pl.loop(0, left.shape[1] // 256)
    def _(i):
        span = pl.ds(pl.multiple_of(i * 256, 256), 256)
        turned_ref[span, cols] = left[row : row + 256, span].T


def turn_kernel(first_ref, second_ref, out_ref):
    start = 0
    for left in (first_ref, second_ref):
        for row in range(0, left.shape[0], 256):
            turn_piece(out_ref, left, start, row)
        start += left.shape[0]


def turn_pair(first, second):
    rows, d = first.shape
    return pl.pallas_call(
        turn_kernel,
        out_shape=jax.ShapeDtypeStruct((d, 2 * rows), first.dtype),
        compiler_params=pltpu.CompilerParams(vmem_limit_bytes=32 * 1024 * 1024),
        cost_estimate=cost(0, 8 * rows * d),
        name="turn_pair",
    )(first, second)


def emit_into(outs, counts, block, value, gain):
    if gain:
        outs[-1][...] = value
        return
    first = 0
    for out, count in zip(outs, counts):

        @pl.when((block >= first) & (block < first + count))
        def _():
            out[...] = value

        first += count


def emit_specs(scatter, counts):
    first = scatter.starts[-1]
    specs, shapes = [], []
    for count in counts:

        def where(j, first=first, most=count - 1):
            return (0, jnp.clip(j - first, 0, most))

        specs.append(pl.BlockSpec((scatter.rows, COLS), where))
        shapes.append(jax.ShapeDtypeStruct((scatter.rows, count * COLS), F32))
        first += count
    specs.append(pl.BlockSpec((GAIN_ROWS, COLS), lambda j: (0, 0)))
    shapes.append(jax.ShapeDtypeStruct((GAIN_ROWS, COLS), F32))
    return specs, shapes


def remote(src, dst, sems, device):
    return pltpu.make_async_remote_copy(
        src_ref=src,
        dst_ref=dst,
        send_sem=sems.at[0],
        recv_sem=sems.at[1],
        device_id=device,
        device_id_type=MESH,
    )


def ffn_scatter_kernel(scatter, per, sent, unsent, *refs):
    (
        cot_turned, norm_own, norm_other, right_own, right_other, whole_own, whole_other,
        cot_hbm, middle_hbm, parts_hbm, got_hbm, gain_ref, wd_ref, wo_ref,
    ) = refs[:14]
    outs = refs[14:17]
    whole_ref, gm_ref, grad_attended, block_out_ref = refs[17:21]
    (
        norm_turned, cot_own, middle_own, part_own, got_part, gm_own, gm_got, gain_got, acc_own,
        acc_other, block_send, block_got, gain_sems, part_sems, gm_sems, block_sems, local_sems,
    ) = refs[21:38]
    scatter.bind(refs[38:])
    step = pl.program_id(0)
    side = scatter.side
    across = (scatter.me, 1 - side)
    half = part_own.shape[0]
    quarter = half // QUARTERS
    row_chunk = 128
    early = pl.ds(0, EARLY * quarter)
    rest = pl.ds(EARLY * quarter, half - EARLY * quarter)

    def part_copy():
        return remote(parts_hbm.at[1, rest], got_part.at[rest], part_sems, across)

    def gm_copy(r):
        span = pl.ds(r * quarter, quarter)
        return remote(gm_own.at[span], gm_got.at[span], gm_sems.at[r], across)

    def block_copy():
        return remote(block_send, block_got, block_sems, across)

    def gain_copy():
        return remote(gain_ref, gain_got, gain_sems, across)

    loads = [
        pltpu.make_async_copy(cot_hbm, cot_own, local_sems.at[0]),
        pltpu.make_async_copy(parts_hbm.at[0], part_own, local_sems.at[1]),
        pltpu.make_async_copy(middle_hbm, middle_own, local_sems.at[2]),
        pltpu.make_async_copy(got_hbm.at[early], got_part.at[early], local_sems.at[3]),
    ]

    keeps = [
        pltpu.make_async_copy(gm_own, gm_ref.at[side], local_sems.at[4]),
        pltpu.make_async_copy(gm_got, gm_ref.at[1 - side], local_sems.at[5]),
    ]

    @pl.when(step == 0)
    def _():
        for load in loads:
            load.start()
        scatter.barrier()
        part_copy().start()
        gain_copy().start()

    scatter.advance(step, functools.partial(emit_into, outs, (per, sent - per)))

    @pl.when(step < per)
    def _():
        scatter.multiply(step, cot_turned, (right_own, right_other))

        @pl.when(step == 0)
        def _():
            acc_own[...] = jnp.zeros_like(acc_own)
            acc_other[...] = jnp.zeros_like(acc_other)

        @pl.loop(0, half // 256)
        def _(i):
            span = pl.ds(i * 256, 256)
            acc_own[span, :] += nt(right_own[span, :], wd_ref[...])
            acc_other[span, :] += nt(right_other[span, :], wd_ref[...])

    @pl.when(step == per)
    def _():
        @pl.loop(0, half // row_chunk)
        def _(i):
            span = pl.ds(i * row_chunk, row_chunk)
            block_send[span, :] = acc_other[span, :].astype(BF)

        block_copy().start()

    pieces = [(norm_own, 0, r) for r in range(0, half, 256)]
    pieces += [(norm_other, half, r) for r in range(0, half, 256)]
    for nth, (left, start, row) in enumerate(pieces):

        @pl.when(step == per - len(pieces) + nth)
        def _():
            turn_piece(norm_turned, left, start, row)

    @pl.when((step >= per) & (step < sent))
    def _():
        scatter.multiply(step, norm_turned, (right_own, right_other))

    @pl.when(step == sent)
    def _():
        gain_copy().wait()
        scatter.put_gain(step, gain_ref[0:1, :] + gain_got[0:1, :])

    @pl.when((step >= per) & (step < per + unsent))
    def _():
        rows = whole_ref.shape[0] // 4

        @pl.loop(0, 4)
        def _(i):
            span = pl.ds(i * rows, rows)
            total = nn(norm_turned[span, :half], whole_own[...])
            whole_ref[span, :] = (total + nn(norm_turned[span, half:], whole_other[...])).astype(BF)

    for r in range(QUARTERS):

        @pl.when(step == 1 + r + (1 if r >= EARLY else 0))
        def _():
            if r == 0:
                for load in loads:
                    load.wait()
            if r == EARLY:
                part_copy().wait()

            @pl.loop(r * quarter // row_chunk, (r + 1) * quarter // row_chunk)
            def _(i):
                span = pl.ds(i * row_chunk, row_chunk)
                total = cot_own[span, :].astype(F32) + part_own[span, :].astype(F32)
                gm_own[span, :] = (total + got_part[span, :].astype(F32)).astype(BF)

            gm_copy(r).start()

    @pl.when(step == sent + 1)
    def _():
        for r in range(QUARTERS):
            gm_copy(r).wait()
        for keep in keeps:
            keep.start()

    width = grad_attended.shape[2]
    for nth in range(width // COLS):

        @pl.when(step == sent + 2 + nth)
        def _():
            cols = slice(nth * COLS, (nth + 1) * COLS)
            grad_attended[side, :, cols] = nn(gm_own[...], wo_ref[...]).astype(BF)
            grad_attended[1 - side, :, cols] = nn(gm_got[...], wo_ref[...]).astype(BF)

    @pl.when(step == scatter.steps - 1)
    def _():
        block_copy().wait()

        @pl.loop(0, half // row_chunk)
        def _(i):
            span = pl.ds(i * row_chunk, row_chunk)
            total = middle_own[span, :].astype(F32) + acc_own[span, :]
            block_out_ref[span, :] = (total + block_got[span, :].astype(F32)).astype(BF)

        for keep in keeps:
            keep.wait()


def remote_settings(identity, mib=60, axes=1):
    return pltpu.CompilerParams(
        dimension_semantics=("arbitrary",) * axes,
        vmem_limit_bytes=mib * 1024 * 1024,
        collective_id=identity,
        has_side_effects=True,
    )


def ffn_scatter(
    devices, cot_turned, normed, grads, cot, middle, parts, got, gain_part, w, w_attention, heads
):
    half, d = middle.shape
    width = grads.shape[3]
    per = width // COLS
    up_sent = per * UP_SENT // 8
    sent = per + up_sent
    left = 2 * per - up_sent
    head_blocks = heads // COLS
    scatter = Scatter(devices, d // devices, sent + 1)
    assert scatter.rows * devices == d and per >= 2 * half // 256 and per > QUARTERS + 1
    assert scatter.steps >= max(per + left, sent + 2 + head_blocks) and COLS >= scatter.rows >= GAIN_ROWS

    def right(side):
        def where(j):
            c = jnp.minimum(j, sent - 1)
            return (side, 2 - c // per, 0, c % per)

        return pl.BlockSpec((None, None, half, COLS), where)

    def whole_block(j):
        return jnp.clip(j - per, 0, left - 1)

    def left_whole(side):
        def where(j):
            c = whole_block(j)
            kind = c // per
            return (side, kind, 0, (c + kind * up_sent) % per)

        return pl.BlockSpec((None, None, half, COLS), where)

    def rows_of(side):
        return pl.BlockSpec(
            (None, half, d), lambda j: (side, 0, 0), pipeline_mode=pl.Buffered(1)
        )

    specs, shapes = emit_specs(scatter, (per, sent - per))
    left_there = pl.BlockSpec(memory_space=pl.ANY)
    return pl.pallas_call(
        functools.partial(ffn_scatter_kernel, scatter, per, sent, left),
        grid=(scatter.steps,),
        in_specs=[
            resident((d, 2 * half)),
            rows_of(0),
            rows_of(1),
            right(0),
            right(1),
            left_whole(0),
            left_whole(1),
            left_there,
            left_there,
            left_there,
            left_there,
            resident((8, d)),
            pl.BlockSpec((d, COLS), lambda j: (0, 2 * per + jnp.minimum(j, per - 1))),
            pl.BlockSpec(
                (d, COLS),
                lambda j: (0, 3 * head_blocks + jnp.clip(j - sent - 2, 0, head_blocks - 1)),
            ),
        ],
        out_specs=specs
        + [
            pl.BlockSpec((d, COLS), lambda j: (0, whole_block(j))),
            left_there,
            resident((2, half, heads)),
            resident((half, d)),
        ],
        out_shape=shapes
        + [
            jax.ShapeDtypeStruct((d, left * COLS), BF),
            jax.ShapeDtypeStruct((2, half, d), BF),
            jax.ShapeDtypeStruct((2, half, heads), BF),
            jax.ShapeDtypeStruct((half, d), BF),
        ],
        scratch_shapes=[
            pltpu.VMEM((d, 2 * half), BF),
            pltpu.VMEM((half, d), BF),
            pltpu.VMEM((half, d), BF),
            pltpu.VMEM((half, d), BF),
            pltpu.VMEM((half, d), BF),
            pltpu.VMEM((half, d), BF),
            pltpu.VMEM((half, d), BF),
            pltpu.VMEM((8, d), F32),
            pltpu.VMEM((half, d), F32),
            pltpu.VMEM((half, d), F32),
            pltpu.VMEM((half, d), BF),
            pltpu.VMEM((half, d), BF),
            pltpu.SemaphoreType.DMA((2,)),
            pltpu.SemaphoreType.DMA((2,)),
            pltpu.SemaphoreType.DMA((QUARTERS, 2)),
            pltpu.SemaphoreType.DMA((2,)),
            pltpu.SemaphoreType.DMA((6,)),
        ]
        + scatter.scratch(),
        compiler_params=remote_settings(0),
        cost_estimate=cost(16 * half * d * per * COLS, 20 * half * d),
        name="ffn_scatter",
    )(
        cot_turned, normed, normed, grads, grads, grads, grads, cot, middle, parts, got,
        gain_part, w, w_attention,
    )


def attention_scatter_kernel(scatter, per, *refs):
    (
        norm_turned, gain_ref, right_ref, kind_ref, w_ref, attended_ref, gm_hbm, x_hbm,
    ) = refs[:8]
    outs, token_grad_ref = refs[8:13], refs[13]
    (
        gm_turned, gm_ref, x_ref, acc_ref, part_send, part_got, gain_part, part_sems, local_sems,
    ) = refs[14:23]
    scatter.bind(refs[23:])
    step = pl.program_id(0)
    side = scatter.side
    across = (scatter.me, 1 - side)
    length = x_ref.shape[0]
    half = length // 2
    quarter = half // QUARTERS
    chunk = 128
    kinds = 3 * per
    own, other = side * half, (1 - side) * half

    def part_copy(r):
        span = pl.ds(r * quarter, quarter)
        return remote(part_send.at[span], part_got.at[span], part_sems.at[r], across)

    loads = [
        pltpu.make_async_copy(x_hbm, x_ref, local_sems.at[0]),
        pltpu.make_async_copy(gm_hbm, gm_ref, local_sems.at[1]),
    ]

    def back(row):
        span = pl.ds(row, chunk)
        part, piece = rms_back(acc_ref[span, :], x_ref[span, :].astype(F32), gain_ref[...])
        gain_part[...] += jnp.broadcast_to(piece, gain_part.shape)
        return part

    @pl.when(step == 0)
    def _():
        for load in loads:
            load.start()
        scatter.barrier()

    scatter.advance(step, functools.partial(emit_into, outs, (per,) * 4))

    @pl.when(step == 0)
    def _():
        acc_ref[...] = jnp.zeros_like(acc_ref)
        gain_part[...] = jnp.zeros_like(gain_part)

    @pl.when(step < kinds)
    def _():
        scatter.multiply(step, norm_turned, (right_ref,))

    @pl.when(step < 3)
    def _():
        @pl.loop(0, length // 256)
        def _(i):
            span = pl.ds(i * 256, 256)
            acc_ref[span, :] += nt(kind_ref[span, :], w_ref[...])

    @pl.when(step == 1)
    def _():
        for load in loads:
            load.wait()

    for nth, row in enumerate(range(0, length, 256)):

        @pl.when(step == kinds - length // 256 + nth)
        def _():
            turn_piece(gm_turned, gm_ref, 0, row)

    @pl.when((step >= kinds) & (step < 4 * per))
    def _():
        scatter.multiply(step, gm_turned, (attended_ref,))

    for r in range(QUARTERS):

        @pl.when(step == 3 + r)
        def _():
            @pl.loop(r * quarter // chunk, (r + 1) * quarter // chunk)
            def _(i):
                part_send[pl.ds(i * chunk, chunk), :] = back(other + i * chunk).astype(BF)

            part_copy(r).start()

            @pl.loop(r * quarter // chunk, (r + 1) * quarter // chunk)
            def _(i):
                span = pl.ds(own + i * chunk, chunk)
                acc_ref[span, :] = back(own + i * chunk) + gm_ref[span, :].astype(F32)

    @pl.when(step == 4 * per)
    def _():
        scatter.put_gain(step, gain_part[0:1, :])

    for r in range(QUARTERS):

        @pl.when(step == scatter.steps - QUARTERS + r)
        def _():
            part_copy(r).wait()

            @pl.loop(r * quarter // chunk, (r + 1) * quarter // chunk)
            def _(i):
                span = pl.ds(i * chunk, chunk)
                total = acc_ref[pl.ds(own + i * chunk, chunk), :]
                token_grad_ref[span, :] = (total + part_got[span, :].astype(F32)).astype(BF)


def attention_scatter(devices, norm_turned, gm, x, gain, grads, attended, w):
    length, d = gm.shape
    half = length // 2
    width = grads.shape[2]
    per = width // COLS
    kinds = 3 * per
    scatter = Scatter(devices, d // devices, 4 * per + 1)
    assert kinds >= length // 256 and scatter.rows * devices == d
    assert scatter.starts[-1] > QUARTERS

    def grads_map(j):
        c = jnp.minimum(j, kinds - 1)
        return (c // per, 0, c % per)

    def attended_map(j):
        return (0, jnp.clip(j - kinds, 0, per - 1))

    specs, shapes = emit_specs(scatter, (per,) * 4)
    left_there = pl.BlockSpec(memory_space=pl.ANY)
    return pl.pallas_call(
        functools.partial(attention_scatter_kernel, scatter, per),
        grid=(scatter.steps,),
        in_specs=[
            resident((d, length)),
            resident((1, d)),
            pl.BlockSpec((None, length, COLS), grads_map),
            pl.BlockSpec((None, length, width), lambda j: (jnp.minimum(j, 2), 0, 0)),
            pl.BlockSpec((d, width), lambda j: (0, jnp.minimum(j, 2))),
            pl.BlockSpec((length, COLS), attended_map),
            left_there,
            left_there,
        ],
        out_specs=specs + [resident((half, d))],
        out_shape=shapes + [jax.ShapeDtypeStruct((half, d), BF)],
        scratch_shapes=[
            pltpu.VMEM((d, length), BF),
            pltpu.VMEM((length, d), BF),
            pltpu.VMEM((length, d), BF),
            pltpu.VMEM((length, d), F32),
            pltpu.VMEM((half, d), BF),
            pltpu.VMEM((half, d), BF),
            pltpu.VMEM((8, d), F32),
            pltpu.SemaphoreType.DMA((QUARTERS, 2)),
            pltpu.SemaphoreType.DMA((2,)),
        ]
        + scatter.scratch(),
        compiler_params=remote_settings(1),
        cost_estimate=cost(14 * length * d * per * COLS, 20 * length * d),
        name="attention_scatter",
    )(norm_turned, gain, grads, grads, w, attended, gm, x)


class Gather:
    def __init__(self, devices, rows, count):
        self.devices, self.rows, self.count = devices, rows, count
        self.stages = devices.bit_length() - 1
        self.lags = [2] * (self.stages - 1) + [1]
        self.starts = [sum(self.lags[:t]) for t in range(self.stages + 1)]
        self.steps = count + self.starts[-1]

    def scratch(self):
        return [
            pltpu.VMEM((self.count, self.devices, self.rows, COLS), BF),
            pltpu.SemaphoreType.DMA((self.stages, self.count, 2)),
            pltpu.SemaphoreType.DMA((self.count,)),
        ]

    def bind(self, refs):
        self.held, self.sems, self.load_sems = refs
        self.me, self.side = lax.axis_index("dp"), lax.axis_index("tensor")

    def late(self, block):
        return (block % 4) // 3 if self.stages >= 4 else 0 * block

    def place(self, device, block):
        late = self.late(block)
        total = 0
        for t in range(self.stages):
            bit = (device // (1 << (self.stages - 1 - t))) % 2
            if t in (1, 2) and self.stages >= 4:
                total = total + bit * ((1 << t) * (1 - late) + (1 << (3 - t)) * late)
            else:
                total = total + bit * (1 << t)
        return total

    def partner_at(self, t):
        weight = 1 << (self.stages - 1 - t)
        return self.me + (1 - 2 * ((self.me // weight) % 2)) * weight

    def partner(self, t, block):
        if t not in (1, 2) or self.stages < 4:
            return self.partner_at(t)
        late = self.late(block)
        return self.partner_at(t) * (1 - late) + self.partner_at(3 - t) * late

    def barrier(self):
        arrived = pltpu.get_barrier_semaphore()
        for t in range(self.stages):
            pl.semaphore_signal(
                arrived, inc=1, device_id=(self.partner_at(t), self.side), device_id_type=MESH
            )
        pl.semaphore_signal(
            arrived, inc=1, device_id=(self.me, 1 - self.side), device_id_type=MESH
        )
        pl.semaphore_wait(arrived, self.stages + 1)

    def load(self, shard, column, block):
        return pltpu.make_async_copy(
            shard.at[:, pl.ds(column, COLS)],
            self.held.at[block, self.place(self.me, block)],
            self.load_sems.at[block],
        )

    def load_all(self, shards):
        block = 0
        for shard in shards:
            for column in range(0, shard.shape[1], COLS):
                self.load(shard, column, jnp.int32(block)).start()
                block += 1

    def copy(self, t, block):
        size = 1 << t
        first = self.place(self.me, block) // size * size
        run = self.held.at[block, pl.ds(first, size)]
        return remote(run, run, self.sems.at[t, block], (self.partner(t, block), self.side))

    def advance(self, step, shards):
        for t in range(self.stages, -1, -1):
            block = step - self.starts[t]

            @pl.when((block >= 0) & (block < self.count))
            def _():
                if t > 0:
                    self.copy(t - 1, block).wait()
                else:
                    self.load(shards[0], 0, block).wait()
                if t < self.stages:
                    self.copy(t, block).start()


def gather_project_kernel(gather, per, *refs):
    shards, (tokens, cot, gain_ref, depths_ref), later = refs[:4], refs[4:8], refs[8:11]
    w_hbm, qkv_ref, turned_ref, rows_hbm, cot_other, cos_ref, sin_ref, joined = refs[11:19]
    w_ref, rows_ref, normed_ref, x_sems, row_sems, w_sems, join_sems = refs[19:26]
    gather.bind(refs[26:])
    step = pl.program_id(0)
    side = gather.side
    across = (gather.me, 1 - side)
    lead = gather.starts[-1]
    others = lead + gather.count // 2 - 1
    kinds = 3 * per

    def token_copy():
        return remote(tokens, rows_ref.at[side], x_sems.at[0], across)

    def cot_copy():
        return remote(cot, cot_other, x_sems.at[1], across)

    def token_load():
        return pltpu.make_async_copy(tokens, rows_ref.at[side], row_sems.at[0])

    def rows_store():
        return pltpu.make_async_copy(rows_ref, rows_hbm, row_sems.at[1])

    def w_store(block):
        cols = pl.ds(pl.multiple_of(block * COLS, COLS), COLS)
        return pltpu.make_async_copy(w_ref.at[:, cols], w_hbm.at[:, cols], w_sems.at[block])

    def joins():
        column = 0
        for nth, shard in enumerate(later):
            span = pl.ds(column, shard.shape[1])
            yield pltpu.make_async_copy(shard, joined.at[:, span], join_sems.at[nth])
            column += shard.shape[1]

    @pl.when(step == 1)
    def _():
        for join in joins():
            join.start()

    @pl.when(step == 0)
    def _():
        token_load().start()
        gather.load_all(shards)
        gather.barrier()
        token_copy().start()
        cot_copy().start()

    gather.advance(step, shards)

    @pl.when(step == 1)
    def _():
        token_load().wait()
        norm_rows(rows_ref.at[side], gain_ref, normed_ref.at[side])
        turn_tables(depths_ref, cos_ref, sin_ref)

    for nth, row in enumerate(range(0, rows_ref.shape[1], 256)):

        @pl.when(step == 2 + nth)
        def _():
            turn_piece(turned_ref, normed_ref.at[side], side * rows_ref.shape[1], row)

        @pl.when(step == others + 1 + nth)
        def _():
            turn_piece(turned_ref, normed_ref.at[1 - side], (1 - side) * rows_ref.shape[1], row)

    @pl.when(step == others)
    def _():
        token_copy().wait()
        rows_store().start()
        norm_rows(rows_ref.at[1 - side], gain_ref, normed_ref.at[1 - side])

    @pl.when(step >= lead)
    def _():
        block = step - lead
        cols = pl.ds(pl.multiple_of(block * COLS, COLS), COLS)
        for device in range(gather.devices):
            rows = slice(device * gather.rows, (device + 1) * gather.rows)
            w_ref[rows, cols] = gather.held[block, gather.place(device, block)]
        w_store(block).start()

    @pl.loop(0, 3)
    def _(task):
        mine = jnp.where(task == 0, 1, 0)
        half = side * mine + (1 - side) * (1 - mine)
        block = (step - lead) * mine + (2 * (step - others) + task - 1) * (1 - mine)
        cols = pl.ds(pl.multiple_of(block * COLS, COLS), COLS)
        chunk = 256

        @pl.when((block >= 0) & (block < 2 * per))
        def _():
            scale = jnp.where(block < per, 1.0 / math.sqrt(HD), 1.0).astype(BF)
            for r in range(0, qkv_ref.shape[1], chunk):
                span = slice(r, r + chunk)
                pre = nn(normed_ref[half, span, :], w_ref[:, cols])
                cosine = jnp.concatenate([cos_ref[half, span, :]] * (COLS // LANES), axis=1)
                sine = jnp.concatenate([sin_ref[half, span, :]] * (COLS // LANES), axis=1)
                turned = turn(pre, cosine, sine)
                qkv_ref[half, span, cols] = turned.astype(BF) * scale

        @pl.when((block >= 2 * per) & (block < kinds))
        def _():
            for r in range(0, qkv_ref.shape[1], chunk):
                span = slice(r, r + chunk)
                qkv_ref[half, span, cols] = nn(normed_ref[half, span, :], w_ref[:, cols]).astype(BF)

    @pl.when(step == gather.steps - 1)
    def _():
        for join in joins():
            join.wait()
        cot_copy().wait()
        rows_store().wait()

        @pl.loop(0, gather.count)
        def _(block):
            w_store(block).wait()


def gather_project(devices, shards, tokens, cot, gain, depths, later):
    half, d = tokens.shape
    rows, width = shards[0].shape
    total = len(shards) * width
    per = width // COLS
    gather = Gather(devices, rows, total // COLS)
    count = gather.count
    assert rows * devices == d and count // 2 - 1 + (3 * per + 1) // 2 <= count
    left_there = pl.BlockSpec(memory_space=pl.ANY)
    return pl.pallas_call(
        functools.partial(gather_project_kernel, gather, per),
        grid=(gather.steps,),
        in_specs=[left_there] * 6
        + [resident((1, d)), pl.BlockSpec(memory_space=pltpu.SMEM)]
        + [left_there] * len(later),
        out_specs=[
            left_there,
            resident((2, half, 3 * width)),
            resident((d, 2 * half)),
            left_there,
            left_there,
            resident((2, half, LANES)),
            resident((2, half, LANES)),
            left_there,
        ],
        out_shape=[
            jax.ShapeDtypeStruct((d, total), BF),
            jax.ShapeDtypeStruct((2, half, 3 * width), BF),
            jax.ShapeDtypeStruct((d, 2 * half), BF),
            jax.ShapeDtypeStruct((2, half, d), BF),
            jax.ShapeDtypeStruct((half, d), BF),
            jax.ShapeDtypeStruct((2, half, LANES), F32),
            jax.ShapeDtypeStruct((2, half, LANES), F32),
            jax.ShapeDtypeStruct((rows, sum(shard.shape[1] for shard in later)), BF),
        ],
        scratch_shapes=[
            pltpu.VMEM((d, total), BF),
            pltpu.VMEM((2, half, d), BF),
            pltpu.VMEM((2, half, d), BF),
            pltpu.SemaphoreType.DMA((2, 2)),
            pltpu.SemaphoreType.DMA((2,)),
            pltpu.SemaphoreType.DMA((count,)),
            pltpu.SemaphoreType.DMA((len(later),)),
        ]
        + gather.scratch(),
        compiler_params=remote_settings(2),
        cost_estimate=cost(12 * half * d * width, 2 * d * total),
        name="gather_project",
    )(*shards, tokens, cot, gain, depths, *later)


def swap(x):
    return lax.ppermute(x, "tensor", [(0, 1), (1, 0)])


def body(
    tokens,
    parents,
    attn_gain,
    ffn_gain,
    query_weight,
    key_weight,
    value_weight,
    output_weight,
    gate_weight,
    up_weight,
    down_weight,
    cotangent,
):
    half, d = tokens.shape
    length = 2 * half
    width = query_weight.shape[1]
    hidden_width = gate_weight.shape[1]
    seg_rows = length // parents.shape[1]
    mine = lax.axis_index("tensor")
    own_start = mine * half
    other_start = (1 - mine) * half

    def own_rows(full):
        return lax.dynamic_slice_in_dim(full, own_start, half, 0)

    def other_rows(full):
        return lax.dynamic_slice_in_dim(full, other_start, half, 0)

    def gather(shard):
        return lax.all_gather(shard, "dp", axis=0, tiled=True)

    attn_row = attn_gain[None, :]
    ffn_row = ffn_gain[None, :]

    devices = lax.axis_size("dp")
    bias, depths = tree_tables(parents[0], seg_rows)

    first, qkv, norm_turned, rows_all, cot_other, cosine, sine, second_shard = gather_project(
        devices,
        (query_weight, key_weight, value_weight, output_weight.T),
        tokens,
        cotangent,
        attn_row,
        depths,
        (gate_weight, up_weight, down_weight.T),
    )
    second = gather(second_shard)
    qkv = qkv.reshape(length, 3 * width)
    rows_all = rows_all.reshape(length, d)
    cosine, sine = cosine.reshape(length, LANES), sine.reshape(length, LANES)

    attended, lse = attend(qkv, bias, width, seg_rows)
    out_turned = first[:, 3 * width :]
    send = nt(other_rows(attended), out_turned).astype(BF)
    send, cot_source = lax.optimization_barrier((send, cot_other))
    received = swap(send)
    received, cot_turned = lax.optimization_barrier((received, turn_pair(cotangent, cot_source)))
    middle = (
        tokens.astype(F32) + nt(own_rows(attended), out_turned) + received.astype(F32)
    ).astype(BF)
    middle_other = swap(middle)

    ffn_grads, normed_two, parts, gain_part, got_part = ffn(
        (middle, middle_other), (cotangent, cot_other), ffn_row, second, hidden_width
    )
    down_grad, up_first, ffn_gain_grad, whole, grad_middle, grad_attended, block_out = ffn_scatter(
        devices,
        cot_turned,
        normed_two,
        ffn_grads,
        cotangent,
        middle,
        parts,
        got_part,
        gain_part,
        second,
        first,
        width,
    )
    whole = lax.psum_scatter(whole, "dp", scatter_dimension=0, tiled=True).astype(F32)
    gate_grad = whole[:, :hidden_width]
    up_grad = jnp.concatenate([up_first, whole[:, hidden_width:]], axis=1)
    grad_middle = grad_middle.reshape(length, d)
    grad_attended = grad_attended.reshape(length, width)
    grads = attend_back(qkv, attended, grad_attended, lse, bias, cosine, sine, seg_rows)
    (
        query_grad, key_grad, value_grad, output_grad, attn_gain_grad, token_grad,
    ) = attention_scatter(
        devices, norm_turned, grad_middle, rows_all, attn_row, grads, attended, first
    )
    gain_rows = d // devices // 2

    def gain_piece(columns, side):
        return lax.dynamic_slice_in_dim(columns[0], side * gain_rows, gain_rows, 0)

    return (
        block_out,
        token_grad,
        query_grad,
        key_grad,
        value_grad,
        output_grad.T,
        gate_grad,
        up_grad,
        down_grad.T,
        gain_piece(attn_gain_grad, mine) + swap(gain_piece(attn_gain_grad, 1 - mine)),
        gain_piece(ffn_gain_grad, mine),
    )


def solution(mesh):
    rows = P(("dp", "tensor"), None)
    tall = P("dp", "tensor")
    wide = P("tensor", "dp")
    return jax.shard_map(
        body,
        mesh=mesh,
        in_specs=(
            rows, P("dp", None), P(), P(), tall, tall, tall, wide, tall, tall, wide, rows,
        ),
        out_specs=(
            rows, rows, tall, tall, tall, wide, tall, tall, wide,
            P(("dp", "tensor")), P(("dp", "tensor")),
        ),
        check_vma=False,
    )
```

```python
import functools
import math

import jax
import jax.numpy as jnp
from jax import lax
from jax.experimental import pallas as pl
from jax.experimental.pallas import tpu as pltpu
from jax.sharding import PartitionSpec as P

HD = 64
EPS = 1e-05
BF = jnp.bfloat16
F32 = jnp.float32
COLS = 256
LANES = 128
MASKED = -1e30


def settings(mib=48):
    return pltpu.CompilerParams(
        dimension_semantics=("arbitrary",), vmem_limit_bytes=mib * 1024 * 1024
    )


def cost(flops, bytes_accessed, transcendentals=0):
    return pl.CostEstimate(
        flops=int(flops), bytes_accessed=int(bytes_accessed), transcendentals=int(transcendentals)
    )


def nn(a, b):
    return jnp.dot(a, b, preferred_element_type=F32)


def nt(a, b):
    return lax.dot_general(a, b, (((1,), (1,)), ((), ())), preferred_element_type=F32)


def tree_tables(parent_row, seg_rows):
    segs = parent_row.shape[0]
    index = jnp.arange(segs, dtype=jnp.int32)
    step_up = (parent_row[:, None] == index[None, :]).astype(jnp.int32)
    eye = (index[:, None] == index[None, :]).astype(jnp.int32)
    reach = eye
    for _ in range(segs):
        up = jnp.sum(step_up[:, :, None] * reach[None, :, :], axis=1)
        reach = jnp.minimum(eye + up, 1)
    depths = jnp.sum(reach, axis=1) - 1
    bias = jnp.where(reach.T > 0, 0.0, MASKED).astype(F32)
    return jnp.repeat(bias, seg_rows, axis=1), depths


def turn_tables(depths_ref, cos_ref, sin_ref):
    segs = depths_ref.shape[0]
    seg_rows = 2 * cos_ref.shape[1] // segs
    shape = (seg_rows, LANES)
    lane = lax.broadcasted_iota(jnp.int32, shape, 1) % HD
    row = lax.broadcasted_iota(jnp.int32, shape, 0)
    rates = jnp.exp((lane % (HD // 2)).astype(F32) * (-2.0 * math.log(10000.0) / HD))
    sign = jnp.where(lane < HD // 2, -1.0, 1.0).astype(F32)

    @pl.loop(0, segs)
    def _(seg):
        angles = (depths_ref[seg] * seg_rows + row).astype(F32) * rates
        span = pl.ds(seg % (segs // 2) * seg_rows, seg_rows)
        cos_ref[seg // (segs // 2), span, :] = jnp.cos(angles)
        sin_ref[seg // (segs // 2), span, :] = jnp.sin(angles) * sign


def turn(x, cosine, sine):
    width = x.shape[1]
    lane = lax.broadcasted_iota(jnp.int32, x.shape, 1)
    first = (lane % HD) < HD // 2
    other = jnp.where(
        first, pltpu.roll(x, width - HD // 2, 1), pltpu.roll(x, HD // 2, 1)
    )
    return x * cosine + other * sine


def inverse_rms(x):
    return lax.rsqrt(jnp.mean(x * x, axis=1, keepdims=True) + EPS)


def norm_rows(x_ref, gain_ref, normed_ref):
    chunk = 128

    @pl.loop(0, x_ref.shape[0] // chunk)
    def _(i):
        span = pl.ds(i * chunk, chunk)
        x = x_ref[span, :].astype(F32)
        normed_ref[span, :] = (x * inverse_rms(x) * gain_ref[...]).astype(BF)


def mask_block(block, seg_rows, bias_ref, m, u):
    cols = slice(m * block, (m + 1) * block)
    per = block // seg_rows
    return jnp.concatenate(
        [
            jnp.broadcast_to(bias_ref[u * per + i : u * per + i + 1, cols], (seg_rows, block))
            for i in range(per)
        ],
        axis=0,
    )


def causal(block):
    key = lax.broadcasted_iota(jnp.int32, (block, block), 0)
    query = lax.broadcasted_iota(jnp.int32, (block, block), 1)
    return key <= query


def attend_kernel(block, seg_rows, q_ref, k_ref, v_ref, bias_ref, out_ref, lse_ref):
    length = q_ref.shape[0]
    heads = q_ref.shape[1] // HD
    v_turned = v_ref[...].T
    for m in range(length // block):
        cols = slice(m * block, (m + 1) * block)
        outs = []
        for h in range(heads):
            lanes = slice(h * HD, (h + 1) * HD)
            q = q_ref[cols, lanes]
            scores = []
            for u in range(m + 1):
                s = nt(k_ref[u * block : (u + 1) * block, lanes], q)
                s = s + mask_block(block, seg_rows, bias_ref, m, u)
                if u == m:
                    s = jnp.where(causal(block), s, MASKED)
                scores.append(s)
            peak = scores[0].max(axis=0, keepdims=True)
            for s in scores[1:]:
                peak = jnp.maximum(peak, s.max(axis=0, keepdims=True))
            total = jnp.zeros_like(peak)
            acc = jnp.zeros((HD, block), F32)
            for u, s in enumerate(scores):
                e = jnp.exp(s - peak)
                total = total + e.sum(axis=0, keepdims=True)
                acc = acc + nn(v_turned[lanes, u * block : (u + 1) * block], e.astype(BF))
            outs.append(acc / total)
            lse_ref[0, h : h + 1, cols] = peak + jnp.log(total)
        out_ref[cols, :] = jnp.concatenate(outs, axis=0).T.astype(BF)


def attend(qkv, bias, width, seg_rows):
    length = qkv.shape[0]
    groups = width // LANES
    heads = LANES // HD
    block = 2 * seg_rows
    live = length * length // 2
    return pl.pallas_call(
        functools.partial(attend_kernel, block, seg_rows),
        grid=(groups,),
        in_specs=[
            pl.BlockSpec((length, LANES), lambda i: (0, i)),
            pl.BlockSpec((length, LANES), lambda i: (0, groups + i)),
            pl.BlockSpec((length, LANES), lambda i: (0, 2 * groups + i)),
            pl.BlockSpec(bias.shape, lambda i: (0, 0)),
        ],
        out_specs=[
            pl.BlockSpec((length, LANES), lambda i: (0, i)),
            pl.BlockSpec((1, heads, length), lambda i: (i, 0, 0)),
        ],
        out_shape=[
            jax.ShapeDtypeStruct((length, width), BF),
            jax.ShapeDtypeStruct((groups, heads, length), F32),
        ],
        compiler_params=settings(),
        cost_estimate=cost(16 * live * width, 8 * length * width, live * width // HD),
        name="attend",
    )(qkv, qkv, qkv, bias)


def attend_back_pair(
    blocks, finish, block, seg_rows, lanes_out, q_ref, k_ref, v_ref, o_ref, do_ref, lse_ref, bias_ref, cos_ref,
    sin_ref, out_ref, dk_ref, dv_ref,
):
    length = q_ref.shape[0]
    heads = q_ref.shape[1] // HD
    k_turned = k_ref[...].T
    product = (do_ref[...].astype(F32) * o_ref[...].astype(F32)).T
    deltas = [product[h * HD : (h + 1) * HD].sum(axis=0, keepdims=True) for h in range(heads)]
    for m in blocks:
        cols = slice(m * block, (m + 1) * block)
        grads = []
        for h in range(heads):
            lanes = slice(h * HD, (h + 1) * HD)
            q, do = q_ref[cols, lanes], do_ref[cols, lanes]
            lse = lse_ref[0, h : h + 1, cols]
            delta = deltas[h][:, cols]
            acc = jnp.zeros((HD, block), F32)
            for u in range(m + 1):
                keys = slice(u * block, (u + 1) * block)
                s = nt(k_ref[keys, lanes], q)
                p = jnp.exp(s + (mask_block(block, seg_rows, bias_ref, m, u) - lse))
                if u == m:
                    p = jnp.where(causal(block), p, 0.0)
                dp = nt(v_ref[keys, lanes], do)
                ds = (p * (dp - delta)).astype(BF)
                dv = nn(p.astype(BF), do)
                dk = nn(ds, q)
                if u == m:
                    dv_ref[h, keys, :] = dv
                    dk_ref[h, keys, :] = dk
                else:
                    dv_ref[h, keys, :] += dv
                    dk_ref[h, keys, :] += dk
                acc = acc + nn(k_turned[lanes, keys], ds)
            grads.append(acc)
        dq = jnp.concatenate(grads, axis=0).T * (1.0 / math.sqrt(HD))
        out_ref[0, cols, lanes_out] = turn(dq, cos_ref[cols, :], -sin_ref[cols, :]).astype(BF)
    for m in range(length // block if finish else 0):
        cols = slice(m * block, (m + 1) * block)
        dk = jnp.concatenate([dk_ref[h, cols, :] for h in range(heads)], axis=1)
        out_ref[1, cols, lanes_out] = turn(dk, cos_ref[cols, :], -sin_ref[cols, :]).astype(BF)
        out_ref[2, cols, lanes_out] = jnp.concatenate(
            [dv_ref[h, cols, :] for h in range(heads)], axis=1
        ).astype(BF)


def rms_back(grad, x, gain):
    inverse = inverse_rms(x)
    unit = x * inverse
    scaled = grad * gain
    inner = jnp.mean(scaled * unit, axis=1, keepdims=True)
    return inverse * (scaled - unit * inner), jnp.sum(grad * unit, axis=0, keepdims=True)


def back_rows(acc_ref, x_ref, gain_ref, gain_part_ref, part_ref):
    chunk = 128

    @pl.loop(0, x_ref.shape[0] // chunk)
    def _(i):
        span = pl.ds(i * chunk, chunk)
        part, piece = rms_back(acc_ref[span, :], x_ref[span, :].astype(F32), gain_ref[...])
        part_ref[span, :] = part.astype(part_ref.dtype)
        gain_part_ref[...] += jnp.broadcast_to(piece, gain_part_ref.shape)


def ffn_kernel(
    x_own,
    x_other,
    cot_own,
    cot_other,
    gain_ref,
    wg_ref,
    wu_ref,
    wd_ref,
    grads_ref,
    normed_ref,
    part_ref,
    gain_part_ref,
    got_hbm,
    cot_ref,
    acc_ref,
    part_send,
    part_sems,
):
    h, j = pl.program_id(0), pl.program_id(1)
    chunk = 256
    across = (lax.axis_index("dp"), 1 - lax.axis_index("tensor"))
    quarter = part_send.shape[0] // QUARTERS

    def part_copy(r):
        span = pl.ds(r * quarter, quarter)
        return remote(part_send.at[span], got_hbm.at[span], part_sems.at[r], across)

    @pl.when((h == 0) & (j == 0))
    def _():
        arrived = pltpu.get_barrier_semaphore()
        pl.semaphore_signal(arrived, inc=1, device_id=across, device_id_type=MESH)
        pl.semaphore_wait(arrived, 1)
        gain_part_ref[...] = jnp.zeros_like(gain_part_ref)

    for turn_at, (x_ref, c_ref) in enumerate(((x_other, cot_other), (x_own, cot_own))):

        @pl.when((h == turn_at) & (j == 0))
        def _():
            norm_rows(x_ref, gain_ref, normed_ref)
            cot_ref[...] = c_ref[...]

    @pl.when(j == 0)
    def _():
        acc_ref[...] = jnp.zeros_like(acc_ref)

    for r in range(0, cot_ref.shape[0], chunk):
        span = slice(r, r + chunk)
        gate = nn(normed_ref[span, :], wg_ref[...])
        up = nn(normed_ref[span, :], wu_ref[...])
        grad_hidden = nn(cot_ref[span, :], wd_ref[...])
        sig = jax.nn.sigmoid(gate)
        silu = gate * sig
        grads_ref[2, span, :] = (silu * up).astype(BF)
        grad_gate = (grad_hidden * up * (sig + silu * (1.0 - sig))).astype(BF)
        grad_up = (grad_hidden * silu).astype(BF)
        grads_ref[0, span, :] = grad_gate
        grads_ref[1, span, :] = grad_up
        acc_ref[span, :] += nt(grad_gate, wg_ref[...]) + nt(grad_up, wu_ref[...])

    for turn_at, x_ref in enumerate((x_other, x_own)):

        @pl.when((h == turn_at) & (j == pl.num_programs(1) - 1))
        def _():
            back_rows(acc_ref, x_ref, gain_ref, gain_part_ref, part_ref)
            if turn_at == 0:
                part_send[...] = part_ref[...]
                for r in range(EARLY):
                    part_copy(r).start()
            else:
                for r in range(EARLY):
                    part_copy(r).wait()


def resident(shape):
    zeros = (0,) * len(shape)
    return pl.BlockSpec(shape, lambda *grid: zeros, pipeline_mode=pl.Buffered(1))


def ffn(xs, cots, gain, w, hidden_width, cols=512):
    rows, d = xs[0].shape
    steps = hidden_width // cols
    per_half = lambda h, j: (1 - h, 0, 0)
    return pl.pallas_call(
        ffn_kernel,
        grid=(2, steps),
        in_specs=[resident((rows, d))] * 4
        + [
            resident((1, d)),
            pl.BlockSpec((d, cols), lambda h, j: (0, j)),
            pl.BlockSpec((d, cols), lambda h, j: (0, steps + j)),
            pl.BlockSpec((d, cols), lambda h, j: (0, 2 * steps + j)),
        ],
        out_specs=[
            pl.BlockSpec((None, 3, rows, cols), lambda h, j: (1 - h, 0, 0, j)),
            pl.BlockSpec((None, rows, d), per_half),
            pl.BlockSpec((None, rows, d), per_half),
            pl.BlockSpec((8, d), lambda h, j: (0, 0)),
            pl.BlockSpec(memory_space=pl.ANY),
        ],
        out_shape=[
            jax.ShapeDtypeStruct((2, 3, rows, hidden_width), BF),
            jax.ShapeDtypeStruct((2, rows, d), BF),
            jax.ShapeDtypeStruct((2, rows, d), BF),
            jax.ShapeDtypeStruct((8, d), F32),
            jax.ShapeDtypeStruct((rows, d), BF),
        ],
        scratch_shapes=[
            pltpu.VMEM((rows, d), BF),
            pltpu.VMEM((rows, d), F32),
            pltpu.VMEM((rows, d), BF),
            pltpu.SemaphoreType.DMA((EARLY, 2)),
        ],
        compiler_params=remote_settings(3, axes=2),
        cost_estimate=cost(
            20 * rows * d * hidden_width,
            12 * d * hidden_width + 16 * rows * d + 12 * rows * hidden_width,
            2 * rows * hidden_width,
        ),
        name="ffn",
    )(*xs, *cots, gain, w, w, w)


MESH = pl.DeviceIdType.MESH
QUARTERS = 4
EARLY = 3
UP_SENT = 6
GAIN_ROWS = 16


class Scatter:
    def __init__(self, devices, rows, count):
        self.devices, self.rows, self.count = devices, rows, count
        self.stages = devices.bit_length() - 1
        self.lags = [1] + [3] * (self.stages - 1)
        self.slots = [2 * lag for lag in self.lags]
        if self.stages >= 3:
            self.slots[1] = self.slots[2] = 8
        self.starts = [sum(self.lags[:s]) for s in range(self.stages + 1)]
        self.steps = count + self.starts[-1]

    def scratch(self):
        shapes = []
        for s in range(self.stages):
            slots, left = self.slots[s], self.devices >> (s + 1)
            shapes.append(pltpu.VMEM((slots, 2, left, self.rows, COLS), BF))
            shapes.append(pltpu.VMEM((slots, left, self.rows, COLS), BF))
            shapes.append(pltpu.SemaphoreType.DMA((slots,)))
            shapes.append(pltpu.SemaphoreType.DMA((slots,)))
        return shapes

    def bind(self, refs):
        self.held, self.got = refs[0::4], refs[1::4]
        self.sent_sem, self.got_sem = refs[2::4], refs[3::4]
        self.me, self.side = lax.axis_index("dp"), lax.axis_index("tensor")

    def late(self, block):
        return (block % 4) // 3

    def own_bit(self, b):
        return (self.me // (1 << b)) % 2

    def partner(self, b):
        return self.me + (1 - 2 * self.own_bit(b)) * (1 << b)

    def turned(self, s, block):
        if s not in (1, 2) or self.stages < 3:
            return self.own_bit(s), self.partner(s)
        late = self.late(block)
        return (
            self.own_bit(s) * (1 - late) + self.own_bit(3 - s) * late,
            self.partner(s) * (1 - late) + self.partner(3 - s) * late,
        )

    def barrier(self):
        arrived = pltpu.get_barrier_semaphore()
        for b in range(self.stages):
            pl.semaphore_signal(
                arrived, inc=1, device_id=(self.partner(b), self.side), device_id_type=MESH
            )
        pl.semaphore_signal(
            arrived, inc=1, device_id=(self.me, 1 - self.side), device_id_type=MESH
        )
        pl.semaphore_wait(arrived, self.stages + 1)

    def copy(self, s, block, gain=False):
        slot = block % self.slots[s]
        bit, partner = self.turned(s, block)
        src, dst = self.held[s].at[slot, 1 - bit], self.got[s].at[slot]
        if gain:
            src, dst = src.at[:, pl.ds(0, GAIN_ROWS)], dst.at[:, pl.ds(0, GAIN_ROWS)]
        sems = self.sent_sem[s].at[slot], self.got_sem[s].at[slot]
        return pltpu.make_async_remote_copy(
            src_ref=src,
            dst_ref=dst,
            send_sem=sems[0],
            recv_sem=sems[1],
            device_id=(partner, self.side),
            device_id_type=MESH,
        )

    def advance(self, step, emit):
        for s in range(self.stages, 0, -1):
            block = step - self.starts[s]
            last = self.count - 1
            for gain in (False, True):

                @pl.when((block == last) if gain else (block >= 0) & (block < last))
                def _():
                    self.receive(s, block, gain, emit)

    def receive(self, s, block, gain, emit):
        slot = block % self.slots[s - 1]
        self.copy(s - 1, block, gain).wait()
        keep, _ = self.turned(s - 1, block)
        held, got = self.held[s - 1], self.got[s - 1]
        rows = slice(0, GAIN_ROWS if gain else self.rows)
        if s == self.stages:
            total = held[slot, keep, 0, rows].astype(F32) + got[slot, 0, rows].astype(F32)
            emit(block, total, gain)
            return
        later = block % self.slots[s]
        late = self.late(block)

        def add(k, carry):
            total = held[slot, keep, k, rows] + got[slot, k, rows]
            bit, rest = k % 2, k // 2
            if s == 1 and self.stages >= 3:
                bit = bit * (1 - late) + (k // 2) % 2 * late
                rest = rest * (1 - late) + (k // 4 * 2 + k % 2) * late
            self.held[s][later, bit, rest, rows] = total
            return carry

        lax.fori_loop(0, self.devices >> s, add, 0)
        self.copy(s, block, gain).start()

    def multiply(self, block, turned_ref, rights):
        slot = block % self.slots[0]
        pieces = 4
        size = self.devices // pieces

        def piece(i, carry):
            span = pl.ds(i * size * self.rows, size * self.rows)
            total, start = None, 0
            for right in rights:
                part = nn(turned_ref[span, start : start + right.shape[0]], right[...])
                total = part if total is None else total + part
                start += right.shape[0]
            for r in range(size):
                block_rows = total[r * self.rows : (r + 1) * self.rows].astype(BF)
                self.held[0][slot, r % 2, i * (size // 2) + r // 2] = block_rows
            return carry

        lax.fori_loop(0, pieces, piece, 0)
        self.copy(0, block).start()

    def enter(self, block, ref):
        slot = block % self.slots[0]
        pieces = 4
        size = self.devices // pieces

        def piece(i, carry):
            rows = ref[pl.ds(i * size * self.rows, size * self.rows), :]
            for r in range(size):
                self.held[0][slot, r % 2, i * (size // 2) + r // 2] = rows[
                    r * self.rows : (r + 1) * self.rows
                ]
            return carry

        lax.fori_loop(0, pieces, piece, 0)
        self.copy(0, block).start()

    def put_gain(self, block, row):
        slot = block % self.slots[0]
        empty = jnp.zeros((1, COLS - self.rows), F32)
        for k in range(self.devices):
            piece = jnp.concatenate([row[:, k * self.rows : (k + 1) * self.rows], empty], axis=1)
            piece = jnp.broadcast_to(piece, (GAIN_ROWS, COLS)).astype(BF)
            self.held[0][slot, k % 2, k // 2, :GAIN_ROWS] = piece
        self.copy(0, block, True).start()


def turn_piece(turned_ref, left, start, row):
    cols = pl.ds(pl.multiple_of(start + row, 256), 256)

    @pl.loop(0, left.shape[1] // 256)
    def _(i):
        span = pl.ds(pl.multiple_of(i * 256, 256), 256)
        turned_ref[span, cols] = left[row : row + 256, span].T


def turn_kernel(first_ref, second_ref, out_ref):
    start = 0
    for left in (first_ref, second_ref):
        for row in range(0, left.shape[0], 256):
            turn_piece(out_ref, left, start, row)
        start += left.shape[0]


def turn_pair(first, second):
    rows, d = first.shape
    return pl.pallas_call(
        turn_kernel,
        out_shape=jax.ShapeDtypeStruct((d, 2 * rows), first.dtype),
        compiler_params=pltpu.CompilerParams(vmem_limit_bytes=32 * 1024 * 1024),
        cost_estimate=cost(0, 8 * rows * d),
        name="turn_pair",
    )(first, second)


def emit_into(outs, counts, block, value, gain):
    if gain:
        outs[-1][...] = value
        return
    first = 0
    for out, count in zip(outs, counts):

        @pl.when((block >= first) & (block < first + count))
        def _():
            out[...] = value

        first += count


def emit_specs(scatter, counts):
    first = scatter.starts[-1]
    specs, shapes = [], []
    for count in counts:

        def where(j, first=first, most=count - 1):
            return (0, jnp.clip(j - first, 0, most))

        specs.append(pl.BlockSpec((scatter.rows, COLS), where))
        shapes.append(jax.ShapeDtypeStruct((scatter.rows, count * COLS), F32))
        first += count
    specs.append(pl.BlockSpec((GAIN_ROWS, COLS), lambda j: (0, 0)))
    shapes.append(jax.ShapeDtypeStruct((GAIN_ROWS, COLS), F32))
    return specs, shapes


def remote(src, dst, sems, device):
    return pltpu.make_async_remote_copy(
        src_ref=src,
        dst_ref=dst,
        send_sem=sems.at[0],
        recv_sem=sems.at[1],
        device_id=device,
        device_id_type=MESH,
    )


def ffn_scatter_kernel(scatter, per, sent, unsent, *refs):
    (
        cot_turned, norm_own, norm_other, right_own, right_other, whole_own, whole_other,
        cot_hbm, middle_hbm, parts_hbm, got_hbm, gain_ref, wd_ref, wo_ref,
    ) = refs[:14]
    outs = refs[14:17]
    whole_ref, gm_ref, grad_attended, block_out_ref, gm_turned = refs[17:22]
    (
        norm_turned, cot_own, middle_own, part_own, got_part, gm_own, gm_got, gain_got, acc_own,
        acc_other, block_send, block_got, gain_sems, part_sems, gm_sems, block_sems, local_sems,
    ) = refs[22:39]
    scatter.bind(refs[39:])
    step = pl.program_id(0)
    side = scatter.side
    across = (scatter.me, 1 - side)
    half = part_own.shape[0]
    quarter = half // QUARTERS
    row_chunk = 128
    early = pl.ds(0, EARLY * quarter)
    rest = pl.ds(EARLY * quarter, half - EARLY * quarter)

    def part_copy():
        return remote(parts_hbm.at[1, rest], got_part.at[rest], part_sems, across)

    def gm_copy(r):
        span = pl.ds(r * quarter, quarter)
        return remote(gm_own.at[span], gm_got.at[span], gm_sems.at[r], across)

    def block_copy():
        return remote(block_send, block_got, block_sems, across)

    def gain_copy():
        return remote(gain_ref, gain_got, gain_sems, across)

    loads = [
        pltpu.make_async_copy(cot_hbm, cot_own, local_sems.at[0]),
        pltpu.make_async_copy(parts_hbm.at[0], part_own, local_sems.at[1]),
        pltpu.make_async_copy(middle_hbm, middle_own, local_sems.at[2]),
        pltpu.make_async_copy(got_hbm.at[early], got_part.at[early], local_sems.at[3]),
    ]

    keeps = [
        pltpu.make_async_copy(gm_own, gm_ref.at[side], local_sems.at[4]),
        pltpu.make_async_copy(gm_got, gm_ref.at[1 - side], local_sems.at[5]),
    ]

    @pl.when(step == 0)
    def _():
        for load in loads:
            load.start()
        scatter.barrier()
        part_copy().start()
        gain_copy().start()

    scatter.advance(step, functools.partial(emit_into, outs, (per, sent - per)))

    @pl.when(step < per)
    def _():
        scatter.multiply(step, cot_turned, (right_own, right_other))

        @pl.when(step == 0)
        def _():
            acc_own[...] = jnp.zeros_like(acc_own)
            acc_other[...] = jnp.zeros_like(acc_other)

        @pl.loop(0, half // 256)
        def _(i):
            span = pl.ds(i * 256, 256)
            acc_own[span, :] += nt(right_own[span, :], wd_ref[...])
            acc_other[span, :] += nt(right_other[span, :], wd_ref[...])

    @pl.when(step == per)
    def _():
        @pl.loop(0, half // row_chunk)
        def _(i):
            span = pl.ds(i * row_chunk, row_chunk)
            block_send[span, :] = acc_other[span, :].astype(BF)

        block_copy().start()

    pieces = [(norm_own, 0, r) for r in range(0, half, 256)]
    pieces += [(norm_other, half, r) for r in range(0, half, 256)]
    for nth, (left, start, row) in enumerate(pieces):

        @pl.when(step == per - len(pieces) + nth)
        def _():
            turn_piece(norm_turned, left, start, row)

    @pl.when((step >= per) & (step < sent))
    def _():
        scatter.multiply(step, norm_turned, (right_own, right_other))

    @pl.when(step == sent)
    def _():
        gain_copy().wait()
        scatter.put_gain(step, gain_ref[0:1, :] + gain_got[0:1, :])

    @pl.when((step >= per) & (step < per + unsent))
    def _():
        rows = whole_ref.shape[0] // 4

        @pl.loop(0, 4)
        def _(i):
            span = pl.ds(i * rows, rows)
            total = nn(norm_turned[span, :half], whole_own[...])
            whole_ref[span, :] = (total + nn(norm_turned[span, half:], whole_other[...])).astype(BF)

    for r in range(QUARTERS):

        @pl.when(step == 1 + r + (1 if r >= EARLY else 0))
        def _():
            if r == 0:
                for load in loads:
                    load.wait()
            if r == EARLY:
                part_copy().wait()

            @pl.loop(r * quarter // row_chunk, (r + 1) * quarter // row_chunk)
            def _(i):
                span = pl.ds(i * row_chunk, row_chunk)
                total = cot_own[span, :].astype(F32) + part_own[span, :].astype(F32)
                gm_own[span, :] = (total + got_part[span, :].astype(F32)).astype(BF)

            gm_copy(r).start()

    @pl.when(step == sent + 1)
    def _():
        for r in range(QUARTERS):
            gm_copy(r).wait()
        for keep in keeps:
            keep.start()

    width = grad_attended.shape[2]
    for nth in range(width // COLS):

        @pl.when(step == sent + 2 + nth)
        def _():
            cols = slice(nth * COLS, (nth + 1) * COLS)
            grad_attended[side, :, cols] = nn(gm_own[...], wo_ref[...]).astype(BF)
            grad_attended[1 - side, :, cols] = nn(gm_got[...], wo_ref[...]).astype(BF)

    pieces = [(gm_own, side, r) for r in range(0, half, 256)]
    pieces += [(gm_got, 1 - side, r) for r in range(0, half, 256)]
    for nth, (left, at, row) in enumerate(pieces):

        @pl.when(step == sent + 2 + width // COLS + nth)
        def _():
            turn_piece(gm_turned, left, at * half, row)

    @pl.when(step == scatter.steps - 1)
    def _():
        block_copy().wait()

        @pl.loop(0, half // row_chunk)
        def _(i):
            span = pl.ds(i * row_chunk, row_chunk)
            total = middle_own[span, :].astype(F32) + acc_own[span, :]
            block_out_ref[span, :] = (total + block_got[span, :].astype(F32)).astype(BF)

        for keep in keeps:
            keep.wait()


def remote_settings(identity, mib=60, axes=1):
    return pltpu.CompilerParams(
        dimension_semantics=("arbitrary",) * axes,
        vmem_limit_bytes=mib * 1024 * 1024,
        collective_id=identity,
        has_side_effects=True,
    )


def ffn_scatter(
    devices, cot_turned, normed, grads, cot, middle, parts, got, gain_part, w, w_attention, heads
):
    half, d = middle.shape
    width = grads.shape[3]
    per = width // COLS
    up_sent = per * UP_SENT // 8
    sent = per + up_sent
    left = 2 * per - up_sent
    head_blocks = heads // COLS
    scatter = Scatter(devices, d // devices, sent + 1)
    assert scatter.rows * devices == d and per >= 2 * half // 256 and per > QUARTERS + 1
    assert scatter.steps >= max(per + left, sent + 2 + head_blocks + 2 * half // 256)
    assert COLS >= scatter.rows >= GAIN_ROWS

    def right(side):
        def where(j):
            c = jnp.minimum(j, sent - 1)
            return (side, 2 - c // per, 0, c % per)

        return pl.BlockSpec((None, None, half, COLS), where)

    def whole_block(j):
        return jnp.clip(j - per, 0, left - 1)

    def left_whole(side):
        def where(j):
            c = whole_block(j)
            kind = c // per
            return (side, kind, 0, (c + kind * up_sent) % per)

        return pl.BlockSpec((None, None, half, COLS), where)

    def rows_of(side):
        return pl.BlockSpec(
            (None, half, d), lambda j: (side, 0, 0), pipeline_mode=pl.Buffered(1)
        )

    specs, shapes = emit_specs(scatter, (per, sent - per))
    left_there = pl.BlockSpec(memory_space=pl.ANY)
    return pl.pallas_call(
        functools.partial(ffn_scatter_kernel, scatter, per, sent, left),
        grid=(scatter.steps,),
        in_specs=[
            resident((d, 2 * half)),
            rows_of(0),
            rows_of(1),
            right(0),
            right(1),
            left_whole(0),
            left_whole(1),
            left_there,
            left_there,
            left_there,
            left_there,
            resident((8, d)),
            pl.BlockSpec((d, COLS), lambda j: (0, 2 * per + jnp.minimum(j, per - 1))),
            pl.BlockSpec(
                (d, COLS),
                lambda j: (0, 3 * head_blocks + jnp.clip(j - sent - 2, 0, head_blocks - 1)),
            ),
        ],
        out_specs=specs
        + [
            pl.BlockSpec((d, COLS), lambda j: (0, whole_block(j))),
            left_there,
            resident((2, half, heads)),
            resident((half, d)),
            resident((d, 2 * half)),
        ],
        out_shape=shapes
        + [
            jax.ShapeDtypeStruct((d, left * COLS), BF),
            jax.ShapeDtypeStruct((2, half, d), BF),
            jax.ShapeDtypeStruct((2, half, heads), BF),
            jax.ShapeDtypeStruct((half, d), BF),
            jax.ShapeDtypeStruct((d, 2 * half), BF),
        ],
        scratch_shapes=[
            pltpu.VMEM((d, 2 * half), BF),
            pltpu.VMEM((half, d), BF),
            pltpu.VMEM((half, d), BF),
            pltpu.VMEM((half, d), BF),
            pltpu.VMEM((half, d), BF),
            pltpu.VMEM((half, d), BF),
            pltpu.VMEM((half, d), BF),
            pltpu.VMEM((8, d), F32),
            pltpu.VMEM((half, d), F32),
            pltpu.VMEM((half, d), F32),
            pltpu.VMEM((half, d), BF),
            pltpu.VMEM((half, d), BF),
            pltpu.SemaphoreType.DMA((2,)),
            pltpu.SemaphoreType.DMA((2,)),
            pltpu.SemaphoreType.DMA((QUARTERS, 2)),
            pltpu.SemaphoreType.DMA((2,)),
            pltpu.SemaphoreType.DMA((6,)),
        ]
        + scatter.scratch(),
        compiler_params=remote_settings(0),
        cost_estimate=cost(16 * half * d * per * COLS, 20 * half * d),
        name="ffn_scatter",
    )(
        cot_turned, normed, normed, grads, grads, grads, grads, cot, middle, parts, got,
        gain_part, w, w_attention,
    )


def attention_scatter_kernel(scatter, per, early, block, seg_rows, *refs):
    (
        norm_turned, gm_turned, gain_ref, q_ref, k_ref, v_ref, o_ref, do_ref, lse_ref, bias_ref,
        cos_ref, sin_ref, attended_ref, w_ref, whole_ref, gm_hbm, x_hbm,
    ) = refs[:17]
    outs, token_grad_ref = refs[17 : 22 + len(early)], refs[22 + len(early)]
    refs = refs[23 + len(early) :]
    (
        grads_ref, dk_ref, dv_ref, gm_own, x_ref, acc_ref, part_send, part_got, gain_part,
        part_sems, local_sems,
    ) = refs[:11]
    scatter.bind(refs[11:])
    step = pl.program_id(0)
    side = scatter.side
    across = (scatter.me, 1 - side)
    length = x_ref.shape[0]
    half = length // 2
    quarter = half // QUARTERS
    chunk = 128
    groups = grads_ref.shape[2] // LANES
    own, other = side * half, (1 - side) * half
    before = sum(early)
    turns = 2 * groups

    def part_copy(r):
        span = pl.ds(r * quarter, quarter)
        return remote(part_send.at[span], part_got.at[span], part_sems.at[r], across)

    loads = [
        pltpu.make_async_copy(x_hbm, x_ref, local_sems.at[0]),
        pltpu.make_async_copy(gm_hbm.at[side], gm_own, local_sems.at[1]),
    ]

    def back(row):
        span = pl.ds(row, chunk)
        part, piece = rms_back(acc_ref[span, :], x_ref[span, :].astype(F32), gain_ref[...])
        gain_part[...] += jnp.broadcast_to(piece, gain_part.shape)
        return part

    def emit(column, value, gain):
        if gain:
            outs[4][...] = value
            return
        first = 0
        for out, count in zip(outs[5:], early):

            @pl.when((column >= first) & (column < first + count))
            def _():
                out[...] = value

            first += count

        @pl.when((column >= before) & (column < before + per))
        def _():
            outs[3][...] = value

        for kind in range(3):

            @pl.when((column >= before + per) & ((column - before - per) % 3 == kind))
            def _():
                outs[kind][...] = value

    @pl.when(step == 0)
    def _():
        for load in loads:
            load.start()
        scatter.barrier()

    scatter.advance(step, emit)

    @pl.when(step < before)
    def _():
        scatter.enter(step, whole_ref)

    @pl.when((step >= before) & (step < before + per))
    def _():
        scatter.multiply(step, gm_turned, (attended_ref,))

    @pl.when((step >= before + per) & (step < before + 4 * per))
    def _():
        column = step - before - per
        cols = pl.ds(pl.multiple_of(column // 3 * COLS, COLS), COLS)
        scatter.multiply(step, norm_turned, (grads_ref.at[column % 3, :, cols],))

    count = length // block
    split = count - count // 4
    for odd in range(2):

        @pl.when((step < turns) & (step % 2 == odd))
        def _():
            lanes = pl.ds(pl.multiple_of(step // 2 * LANES, LANES), LANES)
            blocks = range(split, count) if odd else range(split)
            attend_back_pair(
                blocks, odd == 1, block, seg_rows, lanes, q_ref, k_ref, v_ref, o_ref, do_ref,
                lse_ref, bias_ref, cos_ref, sin_ref, grads_ref, dk_ref, dv_ref,
            )

    @pl.when(step == 1)
    def _():
        for load in loads:
            load.wait()
        acc_ref[...] = jnp.zeros_like(acc_ref)
        gain_part[...] = jnp.zeros_like(gain_part)

    @pl.when((step >= turns) & (step < turns + 3))
    def _():
        kind = step - turns

        @pl.loop(0, length // 256)
        def _(i):
            span = pl.ds(i * 256, 256)
            acc_ref[span, :] += nt(grads_ref[kind, span, :], w_ref[...])

    for r in range(QUARTERS):

        @pl.when(step == turns + 3 + r // 2)
        def _():
            @pl.loop(r * quarter // chunk, (r + 1) * quarter // chunk)
            def _(i):
                part_send[pl.ds(i * chunk, chunk), :] = back(other + i * chunk).astype(BF)

            part_copy(r).start()

        @pl.when(step == turns + 5 + r // 2)
        def _():
            @pl.loop(r * quarter // chunk, (r + 1) * quarter // chunk)
            def _(i):
                span = pl.ds(own + i * chunk, chunk)
                kept = gm_own[pl.ds(i * chunk, chunk), :].astype(F32)
                acc_ref[span, :] = back(own + i * chunk) + kept

    @pl.when(step == before + 4 * per)
    def _():
        scatter.put_gain(step, gain_part[0:1, :])

    for r in range(QUARTERS):

        @pl.when(step == scatter.steps - QUARTERS + r)
        def _():
            part_copy(r).wait()

            @pl.loop(r * quarter // chunk, (r + 1) * quarter // chunk)
            def _(i):
                span = pl.ds(i * chunk, chunk)
                total = acc_ref[pl.ds(own + i * chunk, chunk), :]
                token_grad_ref[span, :] = (total + part_got[span, :].astype(F32)).astype(BF)


def attention_scatter(
    devices, norm_turned, gm_turned, gm, x, gain, qkv, attended, grad_attended, lse, bias, cosine,
    sine, w, whole, early, seg_rows,
):
    length, width = attended.shape
    half, d = gm.shape[1:]
    per = width // COLS
    groups = width // LANES
    heads = LANES // HD
    before = sum(early)
    scatter = Scatter(devices, d // devices, before + 4 * per + 1)
    lead = scatter.starts[-1]
    assert groups == 2 * per and 2 * groups + 7 <= before + 4 * per and lead > QUARTERS
    assert scatter.rows * devices == d and whole.shape[1] == before * COLS

    def group(j):
        return jnp.minimum(j // 2, groups - 1)

    def lanes_of(kind):
        return pl.BlockSpec((length, LANES), lambda j: (0, kind * groups + group(j)))

    specs, shapes = [], []
    for kind in range(4):
        first = lead + before + (per + kind if kind < 3 else 0)
        stride = 3 if kind < 3 else 1

        def where(j, first=first, stride=stride):
            return (0, jnp.clip(jnp.maximum(j - first, 0) // stride, 0, per - 1))

        specs.append(pl.BlockSpec((scatter.rows, COLS), where))
        shapes.append(jax.ShapeDtypeStruct((scatter.rows, width), F32))
    more_specs, more_shapes = emit_specs(scatter, early)
    specs += more_specs[-1:] + more_specs[:-1]
    shapes += more_shapes[-1:] + more_shapes[:-1]
    left_there = pl.BlockSpec(memory_space=pl.ANY)
    return pl.pallas_call(
        functools.partial(attention_scatter_kernel, scatter, per, early, 2 * seg_rows, seg_rows),
        grid=(scatter.steps,),
        in_specs=[
            resident((d, length)),
            resident((d, length)),
            resident((1, d)),
            lanes_of(0),
            lanes_of(1),
            lanes_of(2),
            lanes_of(0),
            lanes_of(0),
            pl.BlockSpec((1, heads, length), lambda j: (group(j), 0, 0)),
            resident(bias.shape),
            resident((length, LANES)),
            resident((length, LANES)),
            pl.BlockSpec((length, COLS), lambda j: (0, jnp.clip(j - before, 0, per - 1))),
            pl.BlockSpec((d, width), lambda j: (0, jnp.clip(j - 2 * groups, 0, 2))),
            pl.BlockSpec((d, COLS), lambda j: (0, jnp.minimum(j, before - 1))),
            left_there,
            left_there,
        ],
        out_specs=specs + [resident((half, d))],
        out_shape=shapes + [jax.ShapeDtypeStruct((half, d), BF)],
        scratch_shapes=[
            pltpu.VMEM((3, length, width), BF),
            pltpu.VMEM((heads, length, HD), F32),
            pltpu.VMEM((heads, length, HD), F32),
            pltpu.VMEM((half, d), BF),
            pltpu.VMEM((length, d), BF),
            pltpu.VMEM((length, d), F32),
            pltpu.VMEM((half, d), BF),
            pltpu.VMEM((half, d), BF),
            pltpu.VMEM((8, d), F32),
            pltpu.SemaphoreType.DMA((QUARTERS, 2)),
            pltpu.SemaphoreType.DMA((2,)),
        ]
        + scatter.scratch(),
        compiler_params=remote_settings(1),
        cost_estimate=cost(
            14 * length * d * width + 20 * length * length * width,
            20 * length * d,
            length * length * width // HD,
        ),
        name="attention_scatter",
    )(
        norm_turned, gm_turned, gain, qkv, qkv, qkv, attended, grad_attended, lse, bias, cosine,
        sine, attended, w, whole, gm, x,
    )


class Gather:
    def __init__(self, devices, rows, count):
        self.devices, self.rows, self.count = devices, rows, count
        self.stages = devices.bit_length() - 1
        self.lags = [2] * (self.stages - 1) + [1]
        self.starts = [sum(self.lags[:t]) for t in range(self.stages + 1)]
        self.steps = count + self.starts[-1]

    def scratch(self):
        return [
            pltpu.VMEM((self.count, self.devices, self.rows, COLS), BF),
            pltpu.SemaphoreType.DMA((self.stages, self.count, 2)),
            pltpu.SemaphoreType.DMA((self.count,)),
        ]

    def bind(self, refs):
        self.held, self.sems, self.load_sems = refs
        self.me, self.side = lax.axis_index("dp"), lax.axis_index("tensor")

    def late(self, block):
        return (block % 4) // 3 if self.stages >= 4 else 0 * block

    def place(self, device, block):
        late = self.late(block)
        total = 0
        for t in range(self.stages):
            bit = (device // (1 << (self.stages - 1 - t))) % 2
            if t in (1, 2) and self.stages >= 4:
                total = total + bit * ((1 << t) * (1 - late) + (1 << (3 - t)) * late)
            else:
                total = total + bit * (1 << t)
        return total

    def partner_at(self, t):
        weight = 1 << (self.stages - 1 - t)
        return self.me + (1 - 2 * ((self.me // weight) % 2)) * weight

    def partner(self, t, block):
        if t not in (1, 2) or self.stages < 4:
            return self.partner_at(t)
        late = self.late(block)
        return self.partner_at(t) * (1 - late) + self.partner_at(3 - t) * late

    def barrier(self):
        arrived = pltpu.get_barrier_semaphore()
        for t in range(self.stages):
            pl.semaphore_signal(
                arrived, inc=1, device_id=(self.partner_at(t), self.side), device_id_type=MESH
            )
        pl.semaphore_signal(
            arrived, inc=1, device_id=(self.me, 1 - self.side), device_id_type=MESH
        )
        pl.semaphore_wait(arrived, self.stages + 1)

    def load(self, shard, column, block):
        return pltpu.make_async_copy(
            shard.at[:, pl.ds(column, COLS)],
            self.held.at[block, self.place(self.me, block)],
            self.load_sems.at[block],
        )

    def load_all(self, shards):
        block = 0
        for shard in shards:
            for column in range(0, shard.shape[1], COLS):
                self.load(shard, column, jnp.int32(block)).start()
                block += 1

    def copy(self, t, block):
        size = 1 << t
        first = self.place(self.me, block) // size * size
        run = self.held.at[block, pl.ds(first, size)]
        return remote(run, run, self.sems.at[t, block], (self.partner(t, block), self.side))

    def advance(self, step, shards):
        for t in range(self.stages, -1, -1):
            block = step - self.starts[t]

            @pl.when((block >= 0) & (block < self.count))
            def _():
                if t > 0:
                    self.copy(t - 1, block).wait()
                else:
                    self.load(shards[0], 0, block).wait()
                if t < self.stages:
                    self.copy(t, block).start()


def gather_project_kernel(gather, per, *refs):
    shards, (tokens, cot, gain_ref, depths_ref), later = refs[:4], refs[4:8], refs[8:11]
    w_hbm, qkv_ref, turned_ref, rows_hbm, cot_other, cos_ref, sin_ref, joined = refs[11:19]
    w_ref, rows_ref, normed_ref, x_sems, row_sems, w_sems, join_sems = refs[19:26]
    gather.bind(refs[26:])
    step = pl.program_id(0)
    side = gather.side
    across = (gather.me, 1 - side)
    lead = gather.starts[-1]
    others = lead + gather.count // 2 - 1
    kinds = 3 * per

    def token_copy():
        return remote(tokens, rows_ref.at[side], x_sems.at[0], across)

    def cot_copy():
        return remote(cot, cot_other, x_sems.at[1], across)

    def token_load():
        return pltpu.make_async_copy(tokens, rows_ref.at[side], row_sems.at[0])

    def rows_store():
        return pltpu.make_async_copy(rows_ref, rows_hbm, row_sems.at[1])

    def w_store(block):
        cols = pl.ds(pl.multiple_of(block * COLS, COLS), COLS)
        return pltpu.make_async_copy(w_ref.at[:, cols], w_hbm.at[:, cols], w_sems.at[block])

    def joins():
        column = 0
        for nth, shard in enumerate(later):
            span = pl.ds(column, shard.shape[1])
            yield pltpu.make_async_copy(shard, joined.at[:, span], join_sems.at[nth])
            column += shard.shape[1]

    @pl.when(step == 1)
    def _():
        for join in joins():
            join.start()

    @pl.when(step == 0)
    def _():
        token_load().start()
        gather.load_all(shards)
        gather.barrier()
        token_copy().start()
        cot_copy().start()

    gather.advance(step, shards)

    @pl.when(step == 1)
    def _():
        token_load().wait()
        norm_rows(rows_ref.at[side], gain_ref, normed_ref.at[side])
        turn_tables(depths_ref, cos_ref, sin_ref)

    for nth, row in enumerate(range(0, rows_ref.shape[1], 256)):

        @pl.when(step == 2 + nth)
        def _():
            turn_piece(turned_ref, normed_ref.at[side], side * rows_ref.shape[1], row)

        @pl.when(step == others + 1 + nth)
        def _():
            turn_piece(turned_ref, normed_ref.at[1 - side], (1 - side) * rows_ref.shape[1], row)

    @pl.when(step == others)
    def _():
        token_copy().wait()
        rows_store().start()
        norm_rows(rows_ref.at[1 - side], gain_ref, normed_ref.at[1 - side])

    @pl.when(step >= lead)
    def _():
        block = step - lead
        cols = pl.ds(pl.multiple_of(block * COLS, COLS), COLS)
        for device in range(gather.devices):
            rows = slice(device * gather.rows, (device + 1) * gather.rows)
            w_ref[rows, cols] = gather.held[block, gather.place(device, block)]
        w_store(block).start()

    @pl.loop(0, 3)
    def _(task):
        mine = jnp.where(task == 0, 1, 0)
        half = side * mine + (1 - side) * (1 - mine)
        block = (step - lead) * mine + (2 * (step - others) + task - 1) * (1 - mine)
        cols = pl.ds(pl.multiple_of(block * COLS, COLS), COLS)
        chunk = 256

        @pl.when((block >= 0) & (block < 2 * per))
        def _():
            scale = jnp.where(block < per, 1.0 / math.sqrt(HD), 1.0).astype(BF)
            for r in range(0, qkv_ref.shape[1], chunk):
                span = slice(r, r + chunk)
                pre = nn(normed_ref[half, span, :], w_ref[:, cols])
                cosine = jnp.concatenate([cos_ref[half, span, :]] * (COLS // LANES), axis=1)
                sine = jnp.concatenate([sin_ref[half, span, :]] * (COLS // LANES), axis=1)
                turned = turn(pre, cosine, sine)
                qkv_ref[half, span, cols] = turned.astype(BF) * scale

        @pl.when((block >= 2 * per) & (block < kinds))
        def _():
            for r in range(0, qkv_ref.shape[1], chunk):
                span = slice(r, r + chunk)
                qkv_ref[half, span, cols] = nn(normed_ref[half, span, :], w_ref[:, cols]).astype(BF)

    @pl.when(step == gather.steps - 1)
    def _():
        for join in joins():
            join.wait()
        cot_copy().wait()
        rows_store().wait()

        @pl.loop(0, gather.count)
        def _(block):
            w_store(block).wait()


def gather_project(devices, shards, tokens, cot, gain, depths, later):
    half, d = tokens.shape
    rows, width = shards[0].shape
    total = len(shards) * width
    per = width // COLS
    gather = Gather(devices, rows, total // COLS)
    count = gather.count
    assert rows * devices == d and count // 2 - 1 + (3 * per + 1) // 2 <= count
    left_there = pl.BlockSpec(memory_space=pl.ANY)
    return pl.pallas_call(
        functools.partial(gather_project_kernel, gather, per),
        grid=(gather.steps,),
        in_specs=[left_there] * 6
        + [resident((1, d)), pl.BlockSpec(memory_space=pltpu.SMEM)]
        + [left_there] * len(later),
        out_specs=[
            left_there,
            resident((2, half, 3 * width)),
            resident((d, 2 * half)),
            left_there,
            left_there,
            resident((2, half, LANES)),
            resident((2, half, LANES)),
            left_there,
        ],
        out_shape=[
            jax.ShapeDtypeStruct((d, total), BF),
            jax.ShapeDtypeStruct((2, half, 3 * width), BF),
            jax.ShapeDtypeStruct((d, 2 * half), BF),
            jax.ShapeDtypeStruct((2, half, d), BF),
            jax.ShapeDtypeStruct((half, d), BF),
            jax.ShapeDtypeStruct((2, half, LANES), F32),
            jax.ShapeDtypeStruct((2, half, LANES), F32),
            jax.ShapeDtypeStruct((rows, sum(shard.shape[1] for shard in later)), BF),
        ],
        scratch_shapes=[
            pltpu.VMEM((d, total), BF),
            pltpu.VMEM((2, half, d), BF),
            pltpu.VMEM((2, half, d), BF),
            pltpu.SemaphoreType.DMA((2, 2)),
            pltpu.SemaphoreType.DMA((2,)),
            pltpu.SemaphoreType.DMA((count,)),
            pltpu.SemaphoreType.DMA((len(later),)),
        ]
        + gather.scratch(),
        compiler_params=remote_settings(2),
        cost_estimate=cost(12 * half * d * width, 2 * d * total),
        name="gather_project",
    )(*shards, tokens, cot, gain, depths, *later)


def swap(x):
    return lax.ppermute(x, "tensor", [(0, 1), (1, 0)])


def body(
    tokens,
    parents,
    attn_gain,
    ffn_gain,
    query_weight,
    key_weight,
    value_weight,
    output_weight,
    gate_weight,
    up_weight,
    down_weight,
    cotangent,
):
    half, d = tokens.shape
    length = 2 * half
    width = query_weight.shape[1]
    hidden_width = gate_weight.shape[1]
    seg_rows = length // parents.shape[1]
    mine = lax.axis_index("tensor")
    own_start = mine * half
    other_start = (1 - mine) * half

    def own_rows(full):
        return lax.dynamic_slice_in_dim(full, own_start, half, 0)

    def other_rows(full):
        return lax.dynamic_slice_in_dim(full, other_start, half, 0)

    def gather(shard):
        return lax.all_gather(shard, "dp", axis=0, tiled=True)

    attn_row = attn_gain[None, :]
    ffn_row = ffn_gain[None, :]

    devices = lax.axis_size("dp")
    bias, depths = tree_tables(parents[0], seg_rows)

    first, qkv, norm_turned, rows_all, cot_other, cosine, sine, second_shard = gather_project(
        devices,
        (query_weight, key_weight, value_weight, output_weight.T),
        tokens,
        cotangent,
        attn_row,
        depths,
        (gate_weight, up_weight, down_weight.T),
    )
    second = gather(second_shard)
    qkv = qkv.reshape(length, 3 * width)
    rows_all = rows_all.reshape(length, d)
    cosine, sine = cosine.reshape(length, LANES), sine.reshape(length, LANES)

    attended, lse = attend(qkv, bias, width, seg_rows)
    out_turned = first[:, 3 * width :]
    send = nt(other_rows(attended), out_turned).astype(BF)
    send, cot_source = lax.optimization_barrier((send, cot_other))
    received = swap(send)
    received, cot_turned = lax.optimization_barrier((received, turn_pair(cotangent, cot_source)))
    middle = (
        tokens.astype(F32) + nt(own_rows(attended), out_turned) + received.astype(F32)
    ).astype(BF)
    middle_other = swap(middle)

    ffn_grads, normed_two, parts, gain_part, got_part = ffn(
        (middle, middle_other), (cotangent, cot_other), ffn_row, second, hidden_width
    )
    (
        down_grad, up_first, ffn_gain_grad, whole, grad_middle, grad_attended, block_out, gm_turned,
    ) = ffn_scatter(
        devices,
        cot_turned,
        normed_two,
        ffn_grads,
        cotangent,
        middle,
        parts,
        got_part,
        gain_part,
        second,
        first,
        width,
    )
    blocks = hidden_width // COLS
    rest = whole.shape[1] // COLS - blocks
    (
        query_grad, key_grad, value_grad, output_grad, attn_gain_grad, gate_grad, *up_rest,
        token_grad,
    ) = attention_scatter(
        devices,
        norm_turned,
        gm_turned,
        grad_middle,
        rows_all,
        attn_row,
        qkv,
        attended,
        grad_attended.reshape(length, width),
        lse,
        bias,
        cosine,
        sine,
        first,
        whole,
        (blocks, rest) if rest else (blocks,),
        seg_rows,
    )
    up_grad = jnp.concatenate([up_first, *up_rest], axis=1)
    gain_rows = d // devices // 2

    def gain_piece(columns, side):
        return lax.dynamic_slice_in_dim(columns[0], side * gain_rows, gain_rows, 0)

    return (
        block_out,
        token_grad,
        query_grad,
        key_grad,
        value_grad,
        output_grad.T,
        gate_grad,
        up_grad,
        down_grad.T,
        gain_piece(attn_gain_grad, mine) + swap(gain_piece(attn_gain_grad, 1 - mine)),
        gain_piece(ffn_gain_grad, mine),
    )


def solution(mesh):
    rows = P(("dp", "tensor"), None)
    tall = P("dp", "tensor")
    wide = P("tensor", "dp")
    return jax.shard_map(
        body,
        mesh=mesh,
        in_specs=(
            rows, P("dp", None), P(), P(), tall, tall, tall, wide, tall, tall, wide, rows,
        ),
        out_specs=(
            rows, rows, tall, tall, tall, wide, tall, tall, wide,
            P(("dp", "tensor")), P(("dp", "tensor")),
        ),
        check_vma=False,
    )
```

```python
import functools
import math

import jax
import jax.numpy as jnp
from jax import lax
from jax.experimental import pallas as pl
from jax.experimental.pallas import tpu as pltpu
from jax.sharding import PartitionSpec as P

HD = 64
EPS = 1e-05
BF = jnp.bfloat16
F32 = jnp.float32
COLS = 256
LANES = 128
MASKED = -1e30


def settings(mib=48):
    return pltpu.CompilerParams(
        dimension_semantics=("arbitrary",), vmem_limit_bytes=mib * 1024 * 1024
    )


def cost(flops, bytes_accessed, transcendentals=0):
    return pl.CostEstimate(
        flops=int(flops), bytes_accessed=int(bytes_accessed), transcendentals=int(transcendentals)
    )


def nn(a, b):
    return jnp.dot(a, b, preferred_element_type=F32)


def nt(a, b):
    return lax.dot_general(a, b, (((1,), (1,)), ((), ())), preferred_element_type=F32)


def tree_tables(parent_row, seg_rows):
    segs = parent_row.shape[0]
    index = jnp.arange(segs, dtype=jnp.int32)
    step_up = (parent_row[:, None] == index[None, :]).astype(jnp.int32)
    eye = (index[:, None] == index[None, :]).astype(jnp.int32)
    reach = eye
    for _ in range(segs):
        up = jnp.sum(step_up[:, :, None] * reach[None, :, :], axis=1)
        reach = jnp.minimum(eye + up, 1)
    depths = jnp.sum(reach, axis=1) - 1
    bias = jnp.where(reach.T > 0, 0.0, MASKED).astype(F32)
    return jnp.repeat(bias, seg_rows, axis=1), depths


def turn_tables(depths_ref, cos_ref, sin_ref):
    segs = depths_ref.shape[0]
    seg_rows = 2 * cos_ref.shape[1] // segs
    shape = (seg_rows, LANES)
    lane = lax.broadcasted_iota(jnp.int32, shape, 1) % HD
    row = lax.broadcasted_iota(jnp.int32, shape, 0)
    rates = jnp.exp((lane % (HD // 2)).astype(F32) * (-2.0 * math.log(10000.0) / HD))
    sign = jnp.where(lane < HD // 2, -1.0, 1.0).astype(F32)

    @pl.loop(0, segs)
    def _(seg):
        angles = (depths_ref[seg] * seg_rows + row).astype(F32) * rates
        span = pl.ds(seg % (segs // 2) * seg_rows, seg_rows)
        cos_ref[seg // (segs // 2), span, :] = jnp.cos(angles)
        sin_ref[seg // (segs // 2), span, :] = jnp.sin(angles) * sign


def turn(x, cosine, sine):
    width = x.shape[1]
    lane = lax.broadcasted_iota(jnp.int32, x.shape, 1)
    first = (lane % HD) < HD // 2
    other = jnp.where(
        first, pltpu.roll(x, width - HD // 2, 1), pltpu.roll(x, HD // 2, 1)
    )
    return x * cosine + other * sine


def inverse_rms(x):
    return lax.rsqrt(jnp.mean(x * x, axis=1, keepdims=True) + EPS)


def norm_rows(x_ref, gain_ref, normed_ref):
    chunk = 128

    @pl.loop(0, x_ref.shape[0] // chunk)
    def _(i):
        span = pl.ds(i * chunk, chunk)
        x = x_ref[span, :].astype(F32)
        normed_ref[span, :] = (x * inverse_rms(x) * gain_ref[...]).astype(BF)


def mask_block(block, seg_rows, bias_ref, m, u):
    cols = slice(m * block, (m + 1) * block)
    per = block // seg_rows
    return jnp.concatenate(
        [
            jnp.broadcast_to(bias_ref[u * per + i : u * per + i + 1, cols], (seg_rows, block))
            for i in range(per)
        ],
        axis=0,
    )


def causal(block):
    key = lax.broadcasted_iota(jnp.int32, (block, block), 0)
    query = lax.broadcasted_iota(jnp.int32, (block, block), 1)
    return key <= query


def attend_kernel(block, seg_rows, q_ref, k_ref, v_ref, bias_ref, out_ref, lse_ref):
    length = q_ref.shape[0]
    heads = q_ref.shape[1] // HD
    v_turned = v_ref[...].T
    for m in range(length // block):
        cols = slice(m * block, (m + 1) * block)
        outs = []
        for h in range(heads):
            lanes = slice(h * HD, (h + 1) * HD)
            q = q_ref[cols, lanes]
            scores = []
            for u in range(m + 1):
                s = nt(k_ref[u * block : (u + 1) * block, lanes], q)
                s = s + mask_block(block, seg_rows, bias_ref, m, u)
                if u == m:
                    s = jnp.where(causal(block), s, MASKED)
                scores.append(s)
            peak = scores[0].max(axis=0, keepdims=True)
            for s in scores[1:]:
                peak = jnp.maximum(peak, s.max(axis=0, keepdims=True))
            total = jnp.zeros_like(peak)
            acc = jnp.zeros((HD, block), F32)
            for u, s in enumerate(scores):
                e = jnp.exp(s - peak)
                total = total + e.sum(axis=0, keepdims=True)
                acc = acc + nn(v_turned[lanes, u * block : (u + 1) * block], e.astype(BF))
            outs.append(acc / total)
            lse_ref[0, h : h + 1, cols] = peak + jnp.log(total)
        out_ref[cols, :] = jnp.concatenate(outs, axis=0).T.astype(BF)


def attend(qkv, bias, width, seg_rows):
    length = qkv.shape[0]
    groups = width // LANES
    heads = LANES // HD
    block = 2 * seg_rows
    live = length * length // 2
    return pl.pallas_call(
        functools.partial(attend_kernel, block, seg_rows),
        grid=(groups,),
        in_specs=[
            pl.BlockSpec((length, LANES), lambda i: (0, i)),
            pl.BlockSpec((length, LANES), lambda i: (0, groups + i)),
            pl.BlockSpec((length, LANES), lambda i: (0, 2 * groups + i)),
            pl.BlockSpec(bias.shape, lambda i: (0, 0)),
        ],
        out_specs=[
            pl.BlockSpec((length, LANES), lambda i: (0, i)),
            pl.BlockSpec((1, heads, length), lambda i: (i, 0, 0)),
        ],
        out_shape=[
            jax.ShapeDtypeStruct((length, width), BF),
            jax.ShapeDtypeStruct((groups, heads, length), F32),
        ],
        compiler_params=settings(),
        cost_estimate=cost(16 * live * width, 8 * length * width, live * width // HD),
        name="attend",
    )(qkv, qkv, qkv, bias)


def attend_back_pair(
    blocks, finish, block, seg_rows, lanes_out, q_ref, k_ref, v_ref, o_ref, do_ref, lse_ref, bias_ref, cos_ref,
    sin_ref, out_ref, dk_ref, dv_ref,
):
    length = q_ref.shape[0]
    heads = q_ref.shape[1] // HD
    k_turned = k_ref[...].T
    product = (do_ref[...].astype(F32) * o_ref[...].astype(F32)).T
    deltas = [product[h * HD : (h + 1) * HD].sum(axis=0, keepdims=True) for h in range(heads)]
    for m in blocks:
        cols = slice(m * block, (m + 1) * block)
        grads = []
        for h in range(heads):
            lanes = slice(h * HD, (h + 1) * HD)
            q, do = q_ref[cols, lanes], do_ref[cols, lanes]
            lse = lse_ref[0, h : h + 1, cols]
            delta = deltas[h][:, cols]
            acc = jnp.zeros((HD, block), F32)
            for u in range(m + 1):
                keys = slice(u * block, (u + 1) * block)
                s = nt(k_ref[keys, lanes], q)
                p = jnp.exp(s + (mask_block(block, seg_rows, bias_ref, m, u) - lse))
                if u == m:
                    p = jnp.where(causal(block), p, 0.0)
                dp = nt(v_ref[keys, lanes], do)
                ds = (p * (dp - delta)).astype(BF)
                dv = nn(p.astype(BF), do)
                dk = nn(ds, q)
                if u == m:
                    dv_ref[h, keys, :] = dv
                    dk_ref[h, keys, :] = dk
                else:
                    dv_ref[h, keys, :] += dv
                    dk_ref[h, keys, :] += dk
                acc = acc + nn(k_turned[lanes, keys], ds)
            grads.append(acc)
        dq = jnp.concatenate(grads, axis=0).T * (1.0 / math.sqrt(HD))
        out_ref[0, cols, lanes_out] = turn(dq, cos_ref[cols, :], -sin_ref[cols, :]).astype(BF)
    for m in range(length // block if finish else 0):
        cols = slice(m * block, (m + 1) * block)
        dk = jnp.concatenate([dk_ref[h, cols, :] for h in range(heads)], axis=1)
        out_ref[1, cols, lanes_out] = turn(dk, cos_ref[cols, :], -sin_ref[cols, :]).astype(BF)
        out_ref[2, cols, lanes_out] = jnp.concatenate(
            [dv_ref[h, cols, :] for h in range(heads)], axis=1
        ).astype(BF)


def rms_back(grad, x, gain):
    inverse = inverse_rms(x)
    unit = x * inverse
    scaled = grad * gain
    inner = jnp.mean(scaled * unit, axis=1, keepdims=True)
    return inverse * (scaled - unit * inner), jnp.sum(grad * unit, axis=0, keepdims=True)


def back_rows(acc_ref, x_ref, gain_ref, gain_part_ref, part_ref):
    chunk = 128

    @pl.loop(0, x_ref.shape[0] // chunk)
    def _(i):
        span = pl.ds(i * chunk, chunk)
        part, piece = rms_back(acc_ref[span, :], x_ref[span, :].astype(F32), gain_ref[...])
        part_ref[span, :] = part.astype(part_ref.dtype)
        gain_part_ref[...] += jnp.broadcast_to(piece, gain_part_ref.shape)


def ffn_kernel(
    x_own,
    x_other,
    cot_own,
    cot_other,
    gain_ref,
    wg_ref,
    wu_ref,
    wd_ref,
    grads_ref,
    normed_ref,
    part_ref,
    gain_part_ref,
    got_hbm,
    cot_ref,
    acc_ref,
    part_send,
    part_sems,
):
    h, j = pl.program_id(0), pl.program_id(1)
    chunk = 256
    across = (lax.axis_index("dp"), 1 - lax.axis_index("tensor"))
    quarter = part_send.shape[0] // QUARTERS

    def part_copy(r):
        span = pl.ds(r * quarter, quarter)
        return remote(part_send.at[span], got_hbm.at[span], part_sems.at[r], across)

    @pl.when((h == 0) & (j == 0))
    def _():
        arrived = pltpu.get_barrier_semaphore()
        pl.semaphore_signal(arrived, inc=1, device_id=across, device_id_type=MESH)
        pl.semaphore_wait(arrived, 1)
        gain_part_ref[...] = jnp.zeros_like(gain_part_ref)

    for turn_at, (x_ref, c_ref) in enumerate(((x_other, cot_other), (x_own, cot_own))):

        @pl.when((h == turn_at) & (j == 0))
        def _():
            norm_rows(x_ref, gain_ref, normed_ref)
            cot_ref[...] = c_ref[...]

    @pl.when(j == 0)
    def _():
        acc_ref[...] = jnp.zeros_like(acc_ref)

    for r in range(0, cot_ref.shape[0], chunk):
        span = slice(r, r + chunk)
        gate = nn(normed_ref[span, :], wg_ref[...])
        up = nn(normed_ref[span, :], wu_ref[...])
        grad_hidden = nn(cot_ref[span, :], wd_ref[...])
        sig = jax.nn.sigmoid(gate)
        silu = gate * sig
        grads_ref[2, span, :] = (silu * up).astype(BF)
        grad_gate = (grad_hidden * up * (sig + silu * (1.0 - sig))).astype(BF)
        grad_up = (grad_hidden * silu).astype(BF)
        grads_ref[0, span, :] = grad_gate
        grads_ref[1, span, :] = grad_up
        acc_ref[span, :] += nt(grad_gate, wg_ref[...]) + nt(grad_up, wu_ref[...])

    for turn_at, x_ref in enumerate((x_other, x_own)):

        @pl.when((h == turn_at) & (j == pl.num_programs(1) - 1))
        def _():
            back_rows(acc_ref, x_ref, gain_ref, gain_part_ref, part_ref)
            if turn_at == 0:
                part_send[...] = part_ref[...]
                for r in range(EARLY):
                    part_copy(r).start()
            else:
                for r in range(EARLY):
                    part_copy(r).wait()


def resident(shape):
    zeros = (0,) * len(shape)
    return pl.BlockSpec(shape, lambda *grid: zeros, pipeline_mode=pl.Buffered(1))


def ffn(xs, cots, gain, w, hidden_width, cols=512):
    rows, d = xs[0].shape
    steps = hidden_width // cols
    per_half = lambda h, j: (1 - h, 0, 0)
    return pl.pallas_call(
        ffn_kernel,
        grid=(2, steps),
        in_specs=[resident((rows, d))] * 4
        + [
            resident((1, d)),
            pl.BlockSpec((d, cols), lambda h, j: (0, j)),
            pl.BlockSpec((d, cols), lambda h, j: (0, steps + j)),
            pl.BlockSpec((d, cols), lambda h, j: (0, 2 * steps + j)),
        ],
        out_specs=[
            pl.BlockSpec((None, 3, rows, cols), lambda h, j: (1 - h, 0, 0, j)),
            pl.BlockSpec((None, rows, d), per_half),
            pl.BlockSpec((None, rows, d), per_half),
            pl.BlockSpec((8, d), lambda h, j: (0, 0)),
            pl.BlockSpec(memory_space=pl.ANY),
        ],
        out_shape=[
            jax.ShapeDtypeStruct((2, 3, rows, hidden_width), BF),
            jax.ShapeDtypeStruct((2, rows, d), BF),
            jax.ShapeDtypeStruct((2, rows, d), BF),
            jax.ShapeDtypeStruct((8, d), F32),
            jax.ShapeDtypeStruct((rows, d), BF),
        ],
        scratch_shapes=[
            pltpu.VMEM((rows, d), BF),
            pltpu.VMEM((rows, d), F32),
            pltpu.VMEM((rows, d), BF),
            pltpu.SemaphoreType.DMA((EARLY, 2)),
        ],
        compiler_params=remote_settings(3, axes=2),
        cost_estimate=cost(
            20 * rows * d * hidden_width,
            12 * d * hidden_width + 16 * rows * d + 12 * rows * hidden_width,
            2 * rows * hidden_width,
        ),
        name="ffn",
    )(*xs, *cots, gain, w, w, w)


MESH = pl.DeviceIdType.MESH
QUARTERS = 4
EARLY = 3
UP_SENT = 6
GAIN_ROWS = 16


class Scatter:
    def __init__(self, devices, rows, count):
        self.devices, self.rows, self.count = devices, rows, count
        self.stages = devices.bit_length() - 1
        self.lags = [1] + [3] * (self.stages - 1)
        self.slots = [2 * lag for lag in self.lags]
        if self.stages >= 3:
            self.slots[1] = self.slots[2] = 8
        self.starts = [sum(self.lags[:s]) for s in range(self.stages + 1)]
        self.steps = count + self.starts[-1]

    def scratch(self):
        shapes = []
        for s in range(self.stages):
            slots, left = self.slots[s], self.devices >> (s + 1)
            shapes.append(pltpu.VMEM((slots, 2, left, self.rows, COLS), BF))
            shapes.append(pltpu.VMEM((slots, left, self.rows, COLS), BF))
            shapes.append(pltpu.SemaphoreType.DMA((slots,)))
            shapes.append(pltpu.SemaphoreType.DMA((slots,)))
        return shapes

    def bind(self, refs):
        self.held, self.got = refs[0::4], refs[1::4]
        self.sent_sem, self.got_sem = refs[2::4], refs[3::4]
        self.me, self.side = lax.axis_index("dp"), lax.axis_index("tensor")

    def late(self, block):
        return (block % 4) // 3

    def own_bit(self, b):
        return (self.me // (1 << b)) % 2

    def partner(self, b):
        return self.me + (1 - 2 * self.own_bit(b)) * (1 << b)

    def turned(self, s, block):
        if s not in (1, 2) or self.stages < 3:
            return self.own_bit(s), self.partner(s)
        late = self.late(block)
        return (
            self.own_bit(s) * (1 - late) + self.own_bit(3 - s) * late,
            self.partner(s) * (1 - late) + self.partner(3 - s) * late,
        )

    def barrier(self):
        arrived = pltpu.get_barrier_semaphore()
        for b in range(self.stages):
            pl.semaphore_signal(
                arrived, inc=1, device_id=(self.partner(b), self.side), device_id_type=MESH
            )
        pl.semaphore_signal(
            arrived, inc=1, device_id=(self.me, 1 - self.side), device_id_type=MESH
        )
        pl.semaphore_wait(arrived, self.stages + 1)

    def copy(self, s, block, gain=False):
        slot = block % self.slots[s]
        bit, partner = self.turned(s, block)
        src, dst = self.held[s].at[slot, 1 - bit], self.got[s].at[slot]
        if gain:
            src, dst = src.at[:, pl.ds(0, GAIN_ROWS)], dst.at[:, pl.ds(0, GAIN_ROWS)]
        sems = self.sent_sem[s].at[slot], self.got_sem[s].at[slot]
        return pltpu.make_async_remote_copy(
            src_ref=src,
            dst_ref=dst,
            send_sem=sems[0],
            recv_sem=sems[1],
            device_id=(partner, self.side),
            device_id_type=MESH,
        )

    def advance(self, step, emit):
        for s in range(self.stages, 0, -1):
            block = step - self.starts[s]
            last = self.count - 1
            for gain in (False, True):

                @pl.when((block == last) if gain else (block >= 0) & (block < last))
                def _():
                    self.receive(s, block, gain, emit)

    def receive(self, s, block, gain, emit):
        slot = block % self.slots[s - 1]
        self.copy(s - 1, block, gain).wait()
        keep, _ = self.turned(s - 1, block)
        held, got = self.held[s - 1], self.got[s - 1]
        rows = slice(0, GAIN_ROWS if gain else self.rows)
        if s == self.stages:
            total = held[slot, keep, 0, rows].astype(F32) + got[slot, 0, rows].astype(F32)
            emit(block, total, gain)
            return
        later = block % self.slots[s]
        late = self.late(block)

        def add(k, carry):
            total = held[slot, keep, k, rows] + got[slot, k, rows]
            bit, rest = k % 2, k // 2
            if s == 1 and self.stages >= 3:
                bit = bit * (1 - late) + (k // 2) % 2 * late
                rest = rest * (1 - late) + (k // 4 * 2 + k % 2) * late
            self.held[s][later, bit, rest, rows] = total
            return carry

        lax.fori_loop(0, self.devices >> s, add, 0)
        self.copy(s, block, gain).start()

    def multiply(self, block, turned_ref, rights):
        slot = block % self.slots[0]
        pieces = 4
        size = self.devices // pieces

        def piece(i, carry):
            span = pl.ds(i * size * self.rows, size * self.rows)
            total, start = None, 0
            for right in rights:
                part = nn(turned_ref[span, start : start + right.shape[0]], right[...])
                total = part if total is None else total + part
                start += right.shape[0]
            for r in range(size):
                block_rows = total[r * self.rows : (r + 1) * self.rows].astype(BF)
                self.held[0][slot, r % 2, i * (size // 2) + r // 2] = block_rows
            return carry

        lax.fori_loop(0, pieces, piece, 0)
        self.copy(0, block).start()

    def enter(self, block, ref):
        slot = block % self.slots[0]
        pieces = 4
        size = self.devices // pieces

        def piece(i, carry):
            rows = ref[pl.ds(i * size * self.rows, size * self.rows), :]
            for r in range(size):
                self.held[0][slot, r % 2, i * (size // 2) + r // 2] = rows[
                    r * self.rows : (r + 1) * self.rows
                ]
            return carry

        lax.fori_loop(0, pieces, piece, 0)
        self.copy(0, block).start()

    def put_gain(self, block, row):
        slot = block % self.slots[0]
        empty = jnp.zeros((1, COLS - self.rows), F32)
        for k in range(self.devices):
            piece = jnp.concatenate([row[:, k * self.rows : (k + 1) * self.rows], empty], axis=1)
            piece = jnp.broadcast_to(piece, (GAIN_ROWS, COLS)).astype(BF)
            self.held[0][slot, k % 2, k // 2, :GAIN_ROWS] = piece
        self.copy(0, block, True).start()


def turn_piece(turned_ref, left, start, row):
    cols = pl.ds(pl.multiple_of(start + row, 256), 256)

    @pl.loop(0, left.shape[1] // 256)
    def _(i):
        span = pl.ds(pl.multiple_of(i * 256, 256), 256)
        turned_ref[span, cols] = left[row : row + 256, span].T


def turn_kernel(first_ref, second_ref, out_ref):
    start = 0
    for left in (first_ref, second_ref):
        for row in range(0, left.shape[0], 256):
            turn_piece(out_ref, left, start, row)
        start += left.shape[0]


def turn_pair(first, second):
    rows, d = first.shape
    return pl.pallas_call(
        turn_kernel,
        out_shape=jax.ShapeDtypeStruct((d, 2 * rows), first.dtype),
        compiler_params=pltpu.CompilerParams(vmem_limit_bytes=32 * 1024 * 1024),
        cost_estimate=cost(0, 8 * rows * d),
        name="turn_pair",
    )(first, second)


def emit_into(outs, counts, block, value, gain):
    if gain:
        outs[-1][...] = value
        return
    first = 0
    for out, count in zip(outs, counts):

        @pl.when((block >= first) & (block < first + count))
        def _():
            out[...] = value

        first += count


def emit_specs(scatter, counts):
    first = scatter.starts[-1]
    specs, shapes = [], []
    for count in counts:

        def where(j, first=first, most=count - 1):
            return (0, jnp.clip(j - first, 0, most))

        specs.append(pl.BlockSpec((scatter.rows, COLS), where))
        shapes.append(jax.ShapeDtypeStruct((scatter.rows, count * COLS), F32))
        first += count
    specs.append(pl.BlockSpec((GAIN_ROWS, COLS), lambda j: (0, 0)))
    shapes.append(jax.ShapeDtypeStruct((GAIN_ROWS, COLS), F32))
    return specs, shapes


def remote(src, dst, sems, device):
    return pltpu.make_async_remote_copy(
        src_ref=src,
        dst_ref=dst,
        send_sem=sems.at[0],
        recv_sem=sems.at[1],
        device_id=device,
        device_id_type=MESH,
    )


def ffn_scatter_kernel(scatter, per, sent, unsent, *refs):
    (
        cot_turned, norm_own, norm_other, right_own, right_other, whole_own, whole_other,
        cot_hbm, middle_hbm, parts_hbm, got_hbm, gain_ref, wd_ref, wo_ref,
    ) = refs[:14]
    outs = refs[14:17]
    whole_ref, gm_ref, grad_attended, block_out_ref, gm_turned = refs[17:22]
    (
        norm_turned, cot_own, middle_own, part_own, got_part, gm_own, gm_got, gain_got, acc_own,
        acc_other, block_send, block_got, gain_sems, part_sems, gm_sems, block_sems, local_sems,
    ) = refs[22:39]
    scatter.bind(refs[39:])
    step = pl.program_id(0)
    side = scatter.side
    across = (scatter.me, 1 - side)
    half = part_own.shape[0]
    quarter = half // QUARTERS
    row_chunk = 128
    early = pl.ds(0, EARLY * quarter)
    rest = pl.ds(EARLY * quarter, half - EARLY * quarter)

    def part_copy():
        return remote(parts_hbm.at[1, rest], got_part.at[rest], part_sems, across)

    def gm_copy(r):
        span = pl.ds(r * quarter, quarter)
        return remote(gm_own.at[span], gm_got.at[span], gm_sems.at[r], across)

    def block_copy():
        return remote(block_send, block_got, block_sems, across)

    def gain_copy():
        return remote(gain_ref, gain_got, gain_sems, across)

    loads = [
        pltpu.make_async_copy(cot_hbm, cot_own, local_sems.at[0]),
        pltpu.make_async_copy(parts_hbm.at[0], part_own, local_sems.at[1]),
        pltpu.make_async_copy(middle_hbm, middle_own, local_sems.at[2]),
        pltpu.make_async_copy(got_hbm.at[early], got_part.at[early], local_sems.at[3]),
    ]

    keeps = [
        pltpu.make_async_copy(gm_own, gm_ref.at[side], local_sems.at[4]),
        pltpu.make_async_copy(gm_got, gm_ref.at[1 - side], local_sems.at[5]),
    ]

    @pl.when(step == 0)
    def _():
        for load in loads:
            load.start()
        scatter.barrier()
        part_copy().start()
        gain_copy().start()

    scatter.advance(step, functools.partial(emit_into, outs, (per, sent - per)))

    @pl.when(step < per)
    def _():
        scatter.multiply(step, cot_turned, (right_own, right_other))

        @pl.when(step == 0)
        def _():
            acc_own[...] = jnp.zeros_like(acc_own)
            acc_other[...] = jnp.zeros_like(acc_other)

        @pl.loop(0, half // 256)
        def _(i):
            span = pl.ds(i * 256, 256)
            acc_own[span, :] += nt(right_own[span, :], wd_ref[...])
            acc_other[span, :] += nt(right_other[span, :], wd_ref[...])

    @pl.when(step == per)
    def _():
        @pl.loop(0, half // row_chunk)
        def _(i):
            span = pl.ds(i * row_chunk, row_chunk)
            block_send[span, :] = acc_other[span, :].astype(BF)

        block_copy().start()

    pieces = [(norm_own, 0, r) for r in range(0, half, 256)]
    pieces += [(norm_other, half, r) for r in range(0, half, 256)]
    for nth, (left, start, row) in enumerate(pieces):

        @pl.when(step == per - len(pieces) + nth)
        def _():
            turn_piece(norm_turned, left, start, row)

    @pl.when((step >= per) & (step < sent))
    def _():
        scatter.multiply(step, norm_turned, (right_own, right_other))

    @pl.when(step == sent)
    def _():
        gain_copy().wait()
        scatter.put_gain(step, gain_ref[0:1, :] + gain_got[0:1, :])

    @pl.when((step >= per) & (step < per + unsent))
    def _():
        rows = whole_ref.shape[0] // 4

        @pl.loop(0, 4)
        def _(i):
            span = pl.ds(i * rows, rows)
            total = nn(norm_turned[span, :half], whole_own[...])
            whole_ref[span, :] = (total + nn(norm_turned[span, half:], whole_other[...])).astype(BF)

    for r in range(QUARTERS):

        @pl.when(step == 1 + r + (1 if r >= EARLY else 0))
        def _():
            if r == 0:
                for load in loads:
                    load.wait()
            if r == EARLY:
                part_copy().wait()

            @pl.loop(r * quarter // row_chunk, (r + 1) * quarter // row_chunk)
            def _(i):
                span = pl.ds(i * row_chunk, row_chunk)
                total = cot_own[span, :].astype(F32) + part_own[span, :].astype(F32)
                gm_own[span, :] = (total + got_part[span, :].astype(F32)).astype(BF)

            gm_copy(r).start()

    @pl.when(step == sent + 1)
    def _():
        for r in range(QUARTERS):
            gm_copy(r).wait()
        for keep in keeps:
            keep.start()

    width = grad_attended.shape[2]
    for nth in range(width // COLS):

        @pl.when(step == sent + 2 + nth)
        def _():
            cols = slice(nth * COLS, (nth + 1) * COLS)
            grad_attended[side, :, cols] = nn(gm_own[...], wo_ref[...]).astype(BF)
            grad_attended[1 - side, :, cols] = nn(gm_got[...], wo_ref[...]).astype(BF)

    pieces = [(gm_own, side, r) for r in range(0, half, 256)]
    pieces += [(gm_got, 1 - side, r) for r in range(0, half, 256)]
    for nth, (left, at, row) in enumerate(pieces):

        @pl.when(step == sent + 2 + width // COLS + nth)
        def _():
            turn_piece(gm_turned, left, at * half, row)

    @pl.when(step == scatter.steps - 1)
    def _():
        block_copy().wait()

        @pl.loop(0, half // row_chunk)
        def _(i):
            span = pl.ds(i * row_chunk, row_chunk)
            total = middle_own[span, :].astype(F32) + acc_own[span, :]
            block_out_ref[span, :] = (total + block_got[span, :].astype(F32)).astype(BF)

        for keep in keeps:
            keep.wait()


def remote_settings(identity, mib=60, axes=1):
    return pltpu.CompilerParams(
        dimension_semantics=("arbitrary",) * axes,
        vmem_limit_bytes=mib * 1024 * 1024,
        collective_id=identity,
        has_side_effects=True,
    )


def ffn_scatter(
    devices, cot_turned, normed, grads, cot, middle, parts, got, gain_part, w, w_attention, heads
):
    half, d = middle.shape
    width = grads.shape[3]
    per = width // COLS
    up_sent = per * UP_SENT // 8
    sent = per + up_sent
    left = 2 * per - up_sent
    head_blocks = heads // COLS
    scatter = Scatter(devices, d // devices, sent + 1)
    assert scatter.rows * devices == d and per >= 2 * half // 256 and per > QUARTERS + 1
    assert scatter.steps >= max(per + left, sent + 2 + head_blocks + 2 * half // 256)
    assert COLS >= scatter.rows >= GAIN_ROWS

    def right(side):
        def where(j):
            c = jnp.minimum(j, sent - 1)
            return (side, 2 - c // per, 0, c % per)

        return pl.BlockSpec((None, None, half, COLS), where)

    def whole_block(j):
        return jnp.clip(j - per, 0, left - 1)

    def left_whole(side):
        def where(j):
            c = whole_block(j)
            kind = c // per
            return (side, kind, 0, (c + kind * up_sent) % per)

        return pl.BlockSpec((None, None, half, COLS), where)

    def rows_of(side):
        return pl.BlockSpec(
            (None, half, d), lambda j: (side, 0, 0), pipeline_mode=pl.Buffered(1)
        )

    specs, shapes = emit_specs(scatter, (per, sent - per))
    left_there = pl.BlockSpec(memory_space=pl.ANY)
    return pl.pallas_call(
        functools.partial(ffn_scatter_kernel, scatter, per, sent, left),
        grid=(scatter.steps,),
        in_specs=[
            resident((d, 2 * half)),
            rows_of(0),
            rows_of(1),
            right(0),
            right(1),
            left_whole(0),
            left_whole(1),
            left_there,
            left_there,
            left_there,
            left_there,
            resident((8, d)),
            pl.BlockSpec((d, COLS), lambda j: (0, 2 * per + jnp.minimum(j, per - 1))),
            pl.BlockSpec(
                (d, COLS),
                lambda j: (0, 3 * head_blocks + jnp.clip(j - sent - 2, 0, head_blocks - 1)),
            ),
        ],
        out_specs=specs
        + [
            pl.BlockSpec((d, COLS), lambda j: (0, whole_block(j))),
            left_there,
            resident((2, half, heads)),
            resident((half, d)),
            resident((d, 2 * half)),
        ],
        out_shape=shapes
        + [
            jax.ShapeDtypeStruct((d, left * COLS), BF),
            jax.ShapeDtypeStruct((2, half, d), BF),
            jax.ShapeDtypeStruct((2, half, heads), BF),
            jax.ShapeDtypeStruct((half, d), BF),
            jax.ShapeDtypeStruct((d, 2 * half), BF),
        ],
        scratch_shapes=[
            pltpu.VMEM((d, 2 * half), BF),
            pltpu.VMEM((half, d), BF),
            pltpu.VMEM((half, d), BF),
            pltpu.VMEM((half, d), BF),
            pltpu.VMEM((half, d), BF),
            pltpu.VMEM((half, d), BF),
            pltpu.VMEM((half, d), BF),
            pltpu.VMEM((8, d), F32),
            pltpu.VMEM((half, d), F32),
            pltpu.VMEM((half, d), F32),
            pltpu.VMEM((half, d), BF),
            pltpu.VMEM((half, d), BF),
            pltpu.SemaphoreType.DMA((2,)),
            pltpu.SemaphoreType.DMA((2,)),
            pltpu.SemaphoreType.DMA((QUARTERS, 2)),
            pltpu.SemaphoreType.DMA((2,)),
            pltpu.SemaphoreType.DMA((6,)),
        ]
        + scatter.scratch(),
        compiler_params=remote_settings(0),
        cost_estimate=cost(16 * half * d * per * COLS, 20 * half * d),
        name="ffn_scatter",
    )(
        cot_turned, normed, normed, grads, grads, grads, grads, cot, middle, parts, got,
        gain_part, w, w_attention,
    )


def attention_scatter_kernel(scatter, per, early, block, seg_rows, *refs):
    (
        norm_turned, gm_turned, gain_ref, q_ref, k_ref, v_ref, o_ref, do_ref, lse_ref, bias_ref,
        cos_ref, sin_ref, attended_ref, w_ref, whole_ref, gm_hbm, x_hbm,
    ) = refs[:17]
    outs, token_grad_ref = refs[17 : 22 + len(early)], refs[22 + len(early)]
    refs = refs[23 + len(early) :]
    (
        grads_ref, dk_ref, dv_ref, gm_own, x_ref, acc_ref, part_send, part_got, gain_part,
        part_sems, local_sems,
    ) = refs[:11]
    scatter.bind(refs[11:])
    step = pl.program_id(0)
    side = scatter.side
    across = (scatter.me, 1 - side)
    length = x_ref.shape[0]
    half = length // 2
    quarter = half // QUARTERS
    chunk = 128
    groups = grads_ref.shape[2] // LANES
    own, other = side * half, (1 - side) * half
    before = sum(early)
    turns = 2 * groups

    def part_copy(r):
        span = pl.ds(r * quarter, quarter)
        return remote(part_send.at[span], part_got.at[span], part_sems.at[r], across)

    loads = [
        pltpu.make_async_copy(x_hbm, x_ref, local_sems.at[0]),
        pltpu.make_async_copy(gm_hbm.at[side], gm_own, local_sems.at[1]),
    ]

    def back(row):
        span = pl.ds(row, chunk)
        part, piece = rms_back(acc_ref[span, :], x_ref[span, :].astype(F32), gain_ref[...])
        gain_part[...] += jnp.broadcast_to(piece, gain_part.shape)
        return part

    def emit(column, value, gain):
        if gain:
            outs[4][...] = value
            return
        first = 0
        for out, count in zip(outs[5:], early):

            @pl.when((column >= first) & (column < first + count))
            def _():
                out[...] = value

            first += count

        @pl.when((column >= before) & (column < before + per))
        def _():
            outs[3][...] = value

        for kind in range(3):

            @pl.when((column >= before + per) & ((column - before - per) % 3 == kind))
            def _():
                outs[kind][...] = value

    @pl.when(step == 0)
    def _():
        for load in loads:
            load.start()
        scatter.barrier()

    scatter.advance(step, emit)

    @pl.when(step < before)
    def _():
        scatter.enter(step, whole_ref)

    @pl.when((step >= before) & (step < before + per))
    def _():
        scatter.multiply(step, gm_turned, (attended_ref,))

    @pl.when((step >= before + per) & (step < before + 4 * per))
    def _():
        column = step - before - per
        cols = pl.ds(pl.multiple_of(column // 3 * COLS, COLS), COLS)
        scatter.multiply(step, norm_turned, (grads_ref.at[column % 3, :, cols],))

    count = length // block
    split = count - count // 4
    for odd in range(2):

        @pl.when((step < turns) & (step % 2 == odd))
        def _():
            lanes = pl.ds(pl.multiple_of(step // 2 * LANES, LANES), LANES)
            blocks = range(split, count) if odd else range(split)
            attend_back_pair(
                blocks, odd == 1, block, seg_rows, lanes, q_ref, k_ref, v_ref, o_ref, do_ref,
                lse_ref, bias_ref, cos_ref, sin_ref, grads_ref, dk_ref, dv_ref,
            )

    @pl.when(step == 1)
    def _():
        for load in loads:
            load.wait()
        acc_ref[...] = jnp.zeros_like(acc_ref)
        gain_part[...] = jnp.zeros_like(gain_part)

    @pl.when((step >= turns) & (step < turns + 3))
    def _():
        kind = step - turns

        @pl.loop(0, length // 256)
        def _(i):
            span = pl.ds(i * 256, 256)
            acc_ref[span, :] += nt(grads_ref[kind, span, :], w_ref[...])

    for r in range(QUARTERS):

        @pl.when(step == turns + 3 + r // 2)
        def _():
            @pl.loop(r * quarter // chunk, (r + 1) * quarter // chunk)
            def _(i):
                part_send[pl.ds(i * chunk, chunk), :] = back(other + i * chunk).astype(BF)

            part_copy(r).start()

        @pl.when(step == turns + 5 + r // 2)
        def _():
            @pl.loop(r * quarter // chunk, (r + 1) * quarter // chunk)
            def _(i):
                span = pl.ds(own + i * chunk, chunk)
                kept = gm_own[pl.ds(i * chunk, chunk), :].astype(F32)
                acc_ref[span, :] = back(own + i * chunk) + kept

    @pl.when(step == before + 4 * per)
    def _():
        scatter.put_gain(step, gain_part[0:1, :])

    for r in range(QUARTERS):

        @pl.when(step == scatter.steps - QUARTERS + r)
        def _():
            part_copy(r).wait()

            @pl.loop(r * quarter // chunk, (r + 1) * quarter // chunk)
            def _(i):
                span = pl.ds(i * chunk, chunk)
                total = acc_ref[pl.ds(own + i * chunk, chunk), :]
                token_grad_ref[span, :] = (total + part_got[span, :].astype(F32)).astype(BF)


def attention_scatter(
    devices, norm_turned, gm_turned, gm, x, gain, qkv, attended, grad_attended, lse, bias, cosine,
    sine, w, whole, early, seg_rows,
):
    length, width = attended.shape
    half, d = gm.shape[1:]
    per = width // COLS
    groups = width // LANES
    heads = LANES // HD
    before = sum(early)
    scatter = Scatter(devices, d // devices, before + 4 * per + 1)
    lead = scatter.starts[-1]
    assert groups == 2 * per and 2 * groups + 7 <= before + 4 * per and lead > QUARTERS
    assert scatter.rows * devices == d and whole.shape[1] == before * COLS

    def group(j):
        return jnp.minimum(j // 2, groups - 1)

    def lanes_of(kind):
        return pl.BlockSpec((length, LANES), lambda j: (0, kind * groups + group(j)))

    specs, shapes = [], []
    for kind in range(4):
        first = lead + before + (per + kind if kind < 3 else 0)
        stride = 3 if kind < 3 else 1

        def where(j, first=first, stride=stride):
            return (0, jnp.clip(jnp.maximum(j - first, 0) // stride, 0, per - 1))

        specs.append(pl.BlockSpec((scatter.rows, COLS), where))
        shapes.append(jax.ShapeDtypeStruct((scatter.rows, width), F32))
    more_specs, more_shapes = emit_specs(scatter, early)
    specs += more_specs[-1:] + more_specs[:-1]
    shapes += more_shapes[-1:] + more_shapes[:-1]
    left_there = pl.BlockSpec(memory_space=pl.ANY)
    return pl.pallas_call(
        functools.partial(attention_scatter_kernel, scatter, per, early, 2 * seg_rows, seg_rows),
        grid=(scatter.steps,),
        in_specs=[
            resident((d, length)),
            resident((d, length)),
            resident((1, d)),
            lanes_of(0),
            lanes_of(1),
            lanes_of(2),
            lanes_of(0),
            lanes_of(0),
            pl.BlockSpec((1, heads, length), lambda j: (group(j), 0, 0)),
            resident(bias.shape),
            resident((length, LANES)),
            resident((length, LANES)),
            pl.BlockSpec((length, COLS), lambda j: (0, jnp.clip(j - before, 0, per - 1))),
            pl.BlockSpec((d, width), lambda j: (0, jnp.clip(j - 2 * groups, 0, 2))),
            pl.BlockSpec((d, COLS), lambda j: (0, jnp.minimum(j, before - 1))),
            left_there,
            left_there,
        ],
        out_specs=specs + [resident((half, d))],
        out_shape=shapes + [jax.ShapeDtypeStruct((half, d), BF)],
        scratch_shapes=[
            pltpu.VMEM((3, length, width), BF),
            pltpu.VMEM((heads, length, HD), F32),
            pltpu.VMEM((heads, length, HD), F32),
            pltpu.VMEM((half, d), BF),
            pltpu.VMEM((length, d), BF),
            pltpu.VMEM((length, d), F32),
            pltpu.VMEM((half, d), BF),
            pltpu.VMEM((half, d), BF),
            pltpu.VMEM((8, d), F32),
            pltpu.SemaphoreType.DMA((QUARTERS, 2)),
            pltpu.SemaphoreType.DMA((2,)),
        ]
        + scatter.scratch(),
        compiler_params=remote_settings(1),
        cost_estimate=cost(
            14 * length * d * width + 20 * length * length * width,
            20 * length * d,
            length * length * width // HD,
        ),
        name="attention_scatter",
    )(
        norm_turned, gm_turned, gain, qkv, qkv, qkv, attended, grad_attended, lse, bias, cosine,
        sine, attended, w, whole, gm, x,
    )


class Gather:
    def __init__(self, devices, rows, count):
        self.devices, self.rows, self.count = devices, rows, count
        self.stages = devices.bit_length() - 1
        self.lags = [2] * (self.stages - 1) + [1]
        self.starts = [sum(self.lags[:t]) for t in range(self.stages + 1)]
        self.steps = count + self.starts[-1]

    def scratch(self):
        return [
            pltpu.VMEM((self.count, self.devices, self.rows, COLS), BF),
            pltpu.SemaphoreType.DMA((self.stages, self.count, 2)),
            pltpu.SemaphoreType.DMA((self.count,)),
        ]

    def bind(self, refs):
        self.held, self.sems, self.load_sems = refs
        self.me, self.side = lax.axis_index("dp"), lax.axis_index("tensor")

    def late(self, block):
        return (block % 4) // 3 if self.stages >= 4 else 0 * block

    def place(self, device, block):
        late = self.late(block)
        total = 0
        for t in range(self.stages):
            bit = (device // (1 << (self.stages - 1 - t))) % 2
            if t in (1, 2) and self.stages >= 4:
                total = total + bit * ((1 << t) * (1 - late) + (1 << (3 - t)) * late)
            else:
                total = total + bit * (1 << t)
        return total

    def partner_at(self, t):
        weight = 1 << (self.stages - 1 - t)
        return self.me + (1 - 2 * ((self.me // weight) % 2)) * weight

    def partner(self, t, block):
        if t not in (1, 2) or self.stages < 4:
            return self.partner_at(t)
        late = self.late(block)
        return self.partner_at(t) * (1 - late) + self.partner_at(3 - t) * late

    def barrier(self):
        arrived = pltpu.get_barrier_semaphore()
        for t in range(self.stages):
            pl.semaphore_signal(
                arrived, inc=1, device_id=(self.partner_at(t), self.side), device_id_type=MESH
            )
        pl.semaphore_signal(
            arrived, inc=1, device_id=(self.me, 1 - self.side), device_id_type=MESH
        )
        pl.semaphore_wait(arrived, self.stages + 1)

    def load(self, shard, column, block):
        return pltpu.make_async_copy(
            shard.at[:, pl.ds(column, COLS)],
            self.held.at[block, self.place(self.me, block)],
            self.load_sems.at[block],
        )

    def load_all(self, shards):
        block = 0
        for shard in shards:
            for column in range(0, shard.shape[1], COLS):
                self.load(shard, column, jnp.int32(block)).start()
                block += 1

    def copy(self, t, block):
        size = 1 << t
        first = self.place(self.me, block) // size * size
        run = self.held.at[block, pl.ds(first, size)]
        return remote(run, run, self.sems.at[t, block], (self.partner(t, block), self.side))

    def advance(self, step, shards):
        for t in range(self.stages, -1, -1):
            block = step - self.starts[t]

            @pl.when((block >= 0) & (block < self.count))
            def _():
                if t > 0:
                    self.copy(t - 1, block).wait()
                else:
                    self.load(shards[0], 0, block).wait()
                if t < self.stages:
                    self.copy(t, block).start()


def gather_project_kernel(gather, per, *refs):
    shards, (tokens, cot, gain_ref, depths_ref), later = refs[:4], refs[4:8], refs[8:11]
    w_hbm, qkv_ref, turned_ref, rows_hbm, cot_other, cot_rest, cos_ref, sin_ref, joined = refs[11:20]
    w_ref, rows_ref, normed_ref, x_sems, row_sems, w_sems, join_sems = refs[20:27]
    gather.bind(refs[27:])
    step = pl.program_id(0)
    side = gather.side
    across = (gather.me, 1 - side)
    lead = gather.starts[-1]
    others = lead + gather.count // 2 - 1
    kinds = 3 * per

    def token_copy():
        return remote(tokens, rows_ref.at[side], x_sems.at[0], across)

    def cot_copy():
        rows = pl.ds(0, cot_other.shape[0])
        return remote(cot.at[rows], cot_other, x_sems.at[1], across)

    def token_load():
        return pltpu.make_async_copy(tokens, rows_ref.at[side], row_sems.at[0])

    def rows_store():
        return pltpu.make_async_copy(rows_ref, rows_hbm, row_sems.at[1])

    def w_store(block):
        cols = pl.ds(pl.multiple_of(block * COLS, COLS), COLS)
        return pltpu.make_async_copy(w_ref.at[:, cols], w_hbm.at[:, cols], w_sems.at[block])

    def joins():
        column = 0
        for nth, shard in enumerate(later):
            span = pl.ds(column, shard.shape[1])
            yield pltpu.make_async_copy(shard, joined.at[:, span], join_sems.at[nth])
            column += shard.shape[1]
        rows = pl.ds(cot_other.shape[0], cot_rest.shape[0])
        yield pltpu.make_async_copy(cot.at[rows], cot_rest, join_sems.at[len(later)])

    @pl.when(step == 1)
    def _():
        for join in joins():
            join.start()

    @pl.when(step == 0)
    def _():
        token_load().start()
        gather.load_all(shards)
        gather.barrier()
        token_copy().start()
        cot_copy().start()

    gather.advance(step, shards)

    @pl.when(step == 1)
    def _():
        token_load().wait()
        norm_rows(rows_ref.at[side], gain_ref, normed_ref.at[side])
        turn_tables(depths_ref, cos_ref, sin_ref)

    for nth, row in enumerate(range(0, rows_ref.shape[1], 256)):

        @pl.when(step == 2 + nth)
        def _():
            turn_piece(turned_ref, normed_ref.at[side], side * rows_ref.shape[1], row)

        @pl.when(step == others + 1 + nth)
        def _():
            turn_piece(turned_ref, normed_ref.at[1 - side], (1 - side) * rows_ref.shape[1], row)

    @pl.when(step == others)
    def _():
        token_copy().wait()
        rows_store().start()
        norm_rows(rows_ref.at[1 - side], gain_ref, normed_ref.at[1 - side])

    @pl.when(step >= lead)
    def _():
        block = step - lead
        cols = pl.ds(pl.multiple_of(block * COLS, COLS), COLS)
        for device in range(gather.devices):
            rows = slice(device * gather.rows, (device + 1) * gather.rows)
            w_ref[rows, cols] = gather.held[block, gather.place(device, block)]
        w_store(block).start()

    @pl.loop(0, 3)
    def _(task):
        mine = jnp.where(task == 0, 1, 0)
        half = side * mine + (1 - side) * (1 - mine)
        block = (step - lead) * mine + (2 * (step - others) + task - 1) * (1 - mine)
        cols = pl.ds(pl.multiple_of(block * COLS, COLS), COLS)
        chunk = 256

        @pl.when((block >= 0) & (block < 2 * per))
        def _():
            scale = jnp.where(block < per, 1.0 / math.sqrt(HD), 1.0).astype(BF)
            for r in range(0, qkv_ref.shape[1], chunk):
                span = slice(r, r + chunk)
                pre = nn(normed_ref[half, span, :], w_ref[:, cols])
                cosine = jnp.concatenate([cos_ref[half, span, :]] * (COLS // LANES), axis=1)
                sine = jnp.concatenate([sin_ref[half, span, :]] * (COLS // LANES), axis=1)
                turned = turn(pre, cosine, sine)
                qkv_ref[half, span, cols] = turned.astype(BF) * scale

        @pl.when((block >= 2 * per) & (block < kinds))
        def _():
            for r in range(0, qkv_ref.shape[1], chunk):
                span = slice(r, r + chunk)
                qkv_ref[half, span, cols] = nn(normed_ref[half, span, :], w_ref[:, cols]).astype(BF)

    @pl.when(step == gather.steps - 1)
    def _():
        for join in joins():
            join.wait()
        cot_copy().wait()
        rows_store().wait()

        @pl.loop(0, gather.count)
        def _(block):
            w_store(block).wait()


def gather_project(devices, shards, tokens, cot, cot_rows, gain, depths, later):
    half, d = tokens.shape
    rows, width = shards[0].shape
    total = len(shards) * width
    per = width // COLS
    gather = Gather(devices, rows, total // COLS)
    count = gather.count
    assert rows * devices == d and count // 2 - 1 + (3 * per + 1) // 2 <= count
    left_there = pl.BlockSpec(memory_space=pl.ANY)
    return pl.pallas_call(
        functools.partial(gather_project_kernel, gather, per),
        grid=(gather.steps,),
        in_specs=[left_there] * 6
        + [resident((1, d)), pl.BlockSpec(memory_space=pltpu.SMEM)]
        + [left_there] * len(later),
        out_specs=[
            left_there,
            resident((2, half, 3 * width)),
            resident((d, 2 * half)),
            left_there,
            left_there,
            left_there,
            resident((2, half, LANES)),
            resident((2, half, LANES)),
            left_there,
        ],
        out_shape=[
            jax.ShapeDtypeStruct((d, total), BF),
            jax.ShapeDtypeStruct((2, half, 3 * width), BF),
            jax.ShapeDtypeStruct((d, 2 * half), BF),
            jax.ShapeDtypeStruct((2, half, d), BF),
            jax.ShapeDtypeStruct((cot_rows, d), BF),
            jax.ShapeDtypeStruct((half - cot_rows, d), BF),
            jax.ShapeDtypeStruct((2, half, LANES), F32),
            jax.ShapeDtypeStruct((2, half, LANES), F32),
            jax.ShapeDtypeStruct((rows, sum(shard.shape[1] for shard in later)), BF),
        ],
        scratch_shapes=[
            pltpu.VMEM((d, total), BF),
            pltpu.VMEM((2, half, d), BF),
            pltpu.VMEM((2, half, d), BF),
            pltpu.SemaphoreType.DMA((2, 2)),
            pltpu.SemaphoreType.DMA((2,)),
            pltpu.SemaphoreType.DMA((count,)),
            pltpu.SemaphoreType.DMA((len(later) + 1,)),
        ]
        + gather.scratch(),
        compiler_params=remote_settings(2),
        cost_estimate=cost(12 * half * d * width, 2 * d * total),
        name="gather_project",
    )(*shards, tokens, cot, gain, depths, *later)


def project_out_kernel(half_ref, attended_ref, w_ref, out_ref):
    out_ref[...] = nt(attended_ref[...], w_ref[...]).astype(BF)


def project_out(attended, w, half, cols=512):
    _, rows, width = attended.shape
    d = w.shape[0]
    part = w.shape[1] // width - 1
    return pl.pallas_call(
        project_out_kernel,
        grid_spec=pltpu.PrefetchScalarGridSpec(
            num_scalar_prefetch=1,
            grid=(d // cols,),
            in_specs=[
                pl.BlockSpec((None, rows, width), lambda j, half_ref: (half_ref[0], 0, 0)),
                pl.BlockSpec((cols, width), lambda j, half_ref: (j, part)),
            ],
            out_specs=pl.BlockSpec((rows, cols), lambda j, half_ref: (0, j)),
        ),
        out_shape=jax.ShapeDtypeStruct((rows, d), BF),
        compiler_params=settings(32),
        cost_estimate=cost(2 * rows * d * width, 2 * d * (width + rows)),
        name="project_out",
    )(half.reshape(1), attended, w)


def swap(x):
    return lax.ppermute(x, "tensor", [(0, 1), (1, 0)])


def body(
    tokens,
    parents,
    attn_gain,
    ffn_gain,
    query_weight,
    key_weight,
    value_weight,
    output_weight,
    gate_weight,
    up_weight,
    down_weight,
    cotangent,
):
    half, d = tokens.shape
    length = 2 * half
    width = query_weight.shape[1]
    hidden_width = gate_weight.shape[1]
    seg_rows = length // parents.shape[1]
    mine = lax.axis_index("tensor")
    own_start = mine * half

    def own_rows(full):
        return lax.dynamic_slice_in_dim(full, own_start, half, 0)

    def gather(shard):
        return lax.all_gather(shard, "dp", axis=0, tiled=True)

    attn_row = attn_gain[None, :]
    ffn_row = ffn_gain[None, :]

    devices = lax.axis_size("dp")
    bias, depths = tree_tables(parents[0], seg_rows)

    cut = half // 2
    first, qkv, norm_turned, rows_all, cot_first, cot_rest, cosine, sine, second_shard = gather_project(
        devices,
        (query_weight, key_weight, value_weight, output_weight.T),
        tokens,
        cotangent,
        cut,
        attn_row,
        depths,
        (gate_weight, up_weight, down_weight.T),
    )
    second = gather(second_shard)
    cot_rest = swap(cot_rest)
    qkv = qkv.reshape(length, 3 * width)
    rows_all = rows_all.reshape(length, d)
    cosine, sine = cosine.reshape(length, LANES), sine.reshape(length, LANES)

    attended, lse = attend(qkv, bias, width, seg_rows)
    out_turned = first[:, 3 * width :]
    send = project_out(attended.reshape(2, half, width), first, 1 - mine)
    send, cot_first, cot_rest = lax.optimization_barrier((send, cot_first, cot_rest))
    cot_other = jnp.concatenate([cot_first, cot_rest], axis=0)
    received = swap(send)
    received, cot_turned = lax.optimization_barrier((received, turn_pair(cotangent, cot_other)))
    middle = (
        tokens.astype(F32) + nt(own_rows(attended), out_turned) + received.astype(F32)
    ).astype(BF)
    middle_other = swap(middle)

    ffn_grads, normed_two, parts, gain_part, got_part = ffn(
        (middle, middle_other), (cotangent, cot_other), ffn_row, second, hidden_width
    )
    (
        down_grad, up_first, ffn_gain_grad, whole, grad_middle, grad_attended, block_out, gm_turned,
    ) = ffn_scatter(
        devices,
        cot_turned,
        normed_two,
        ffn_grads,
        cotangent,
        middle,
        parts,
        got_part,
        gain_part,
        second,
        first,
        width,
    )
    blocks = hidden_width // COLS
    rest = whole.shape[1] // COLS - blocks
    (
        query_grad, key_grad, value_grad, output_grad, attn_gain_grad, gate_grad, *up_rest,
        token_grad,
    ) = attention_scatter(
        devices,
        norm_turned,
        gm_turned,
        grad_middle,
        rows_all,
        attn_row,
        qkv,
        attended,
        grad_attended.reshape(length, width),
        lse,
        bias,
        cosine,
        sine,
        first,
        whole,
        (blocks, rest) if rest else (blocks,),
        seg_rows,
    )
    up_grad = jnp.concatenate([up_first, *up_rest], axis=1)
    gain_rows = d // devices // 2

    def gain_piece(columns, side):
        return lax.dynamic_slice_in_dim(columns[0], side * gain_rows, gain_rows, 0)

    return (
        block_out,
        token_grad,
        query_grad,
        key_grad,
        value_grad,
        output_grad.T,
        gate_grad,
        up_grad,
        down_grad.T,
        gain_piece(attn_gain_grad, mine) + swap(gain_piece(attn_gain_grad, 1 - mine)),
        gain_piece(ffn_gain_grad, mine),
    )


def solution(mesh):
    rows = P(("dp", "tensor"), None)
    tall = P("dp", "tensor")
    wide = P("tensor", "dp")
    return jax.shard_map(
        body,
        mesh=mesh,
        in_specs=(
            rows, P("dp", None), P(), P(), tall, tall, tall, wide, tall, tall, wide, rows,
        ),
        out_specs=(
            rows, rows, tall, tall, tall, wide, tall, tall, wide,
            P(("dp", "tensor")), P(("dp", "tensor")),
        ),
        check_vma=False,
    )
```

```python
import functools
import math

import jax
import jax.numpy as jnp
from jax import lax
from jax.experimental import pallas as pl
from jax.experimental.pallas import tpu as pltpu
from jax.sharding import PartitionSpec as P

HD = 64
EPS = 1e-05
BF = jnp.bfloat16
F32 = jnp.float32
COLS = 256
LANES = 128
MASKED = -1e30


def settings(mib=48):
    return pltpu.CompilerParams(
        dimension_semantics=("arbitrary",), vmem_limit_bytes=mib * 1024 * 1024
    )


def cost(flops, bytes_accessed, transcendentals=0):
    return pl.CostEstimate(
        flops=int(flops), bytes_accessed=int(bytes_accessed), transcendentals=int(transcendentals)
    )


def nn(a, b):
    return jnp.dot(a, b, preferred_element_type=F32)


def nt(a, b):
    return lax.dot_general(a, b, (((1,), (1,)), ((), ())), preferred_element_type=F32)


def tree_tables(parent_row, seg_rows):
    segs = parent_row.shape[0]
    index = jnp.arange(segs, dtype=jnp.int32)
    step_up = (parent_row[:, None] == index[None, :]).astype(jnp.int32)
    eye = (index[:, None] == index[None, :]).astype(jnp.int32)
    reach = eye
    for _ in range(segs):
        up = jnp.sum(step_up[:, :, None] * reach[None, :, :], axis=1)
        reach = jnp.minimum(eye + up, 1)
    depths = jnp.sum(reach, axis=1) - 1
    bias = jnp.where(reach.T > 0, 0.0, MASKED).astype(F32)
    return jnp.repeat(bias, seg_rows, axis=1), depths


def turn_tables(depths_ref, cos_ref, sin_ref):
    segs = depths_ref.shape[0]
    seg_rows = 2 * cos_ref.shape[1] // segs
    shape = (seg_rows, LANES)
    lane = lax.broadcasted_iota(jnp.int32, shape, 1) % HD
    row = lax.broadcasted_iota(jnp.int32, shape, 0)
    rates = jnp.exp((lane % (HD // 2)).astype(F32) * (-2.0 * math.log(10000.0) / HD))
    sign = jnp.where(lane < HD // 2, -1.0, 1.0).astype(F32)

    @pl.loop(0, segs)
    def _(seg):
        angles = (depths_ref[seg] * seg_rows + row).astype(F32) * rates
        span = pl.ds(seg % (segs // 2) * seg_rows, seg_rows)
        cos_ref[seg // (segs // 2), span, :] = jnp.cos(angles)
        sin_ref[seg // (segs // 2), span, :] = jnp.sin(angles) * sign


def turn(x, cosine, sine):
    width = x.shape[1]
    lane = lax.broadcasted_iota(jnp.int32, x.shape, 1)
    first = (lane % HD) < HD // 2
    other = jnp.where(
        first, pltpu.roll(x, width - HD // 2, 1), pltpu.roll(x, HD // 2, 1)
    )
    return x * cosine + other * sine


def inverse_rms(x):
    return lax.rsqrt(jnp.mean(x * x, axis=1, keepdims=True) + EPS)


def norm_rows(x_ref, gain_ref, normed_ref):
    chunk = 128

    @pl.loop(0, x_ref.shape[0] // chunk)
    def _(i):
        span = pl.ds(i * chunk, chunk)
        x = x_ref[span, :].astype(F32)
        normed_ref[span, :] = (x * inverse_rms(x) * gain_ref[...]).astype(BF)


def mask_block(block, seg_rows, bias_ref, m, u):
    cols = slice(m * block, (m + 1) * block)
    per = block // seg_rows
    return jnp.concatenate(
        [
            jnp.broadcast_to(bias_ref[u * per + i : u * per + i + 1, cols], (seg_rows, block))
            for i in range(per)
        ],
        axis=0,
    )


def causal(block):
    key = lax.broadcasted_iota(jnp.int32, (block, block), 0)
    query = lax.broadcasted_iota(jnp.int32, (block, block), 1)
    return key <= query


def attend_kernel(block, seg_rows, q_ref, k_ref, v_ref, bias_ref, out_ref, lse_ref):
    length = q_ref.shape[0]
    heads = q_ref.shape[1] // HD
    v_turned = v_ref[...].T
    for m in range(length // block):
        cols = slice(m * block, (m + 1) * block)
        outs = []
        for h in range(heads):
            lanes = slice(h * HD, (h + 1) * HD)
            q = q_ref[cols, lanes]
            scores = []
            for u in range(m + 1):
                s = nt(k_ref[u * block : (u + 1) * block, lanes], q)
                s = s + mask_block(block, seg_rows, bias_ref, m, u)
                if u == m:
                    s = jnp.where(causal(block), s, MASKED)
                scores.append(s)
            peak = scores[0].max(axis=0, keepdims=True)
            for s in scores[1:]:
                peak = jnp.maximum(peak, s.max(axis=0, keepdims=True))
            total = jnp.zeros_like(peak)
            acc = jnp.zeros((HD, block), F32)
            for u, s in enumerate(scores):
                e = jnp.exp(s - peak)
                total = total + e.sum(axis=0, keepdims=True)
                acc = acc + nn(v_turned[lanes, u * block : (u + 1) * block], e.astype(BF))
            outs.append(acc / total)
            lse_ref[0, h : h + 1, cols] = peak + jnp.log(total)
        out_ref[cols, :] = jnp.concatenate(outs, axis=0).T.astype(BF)


def attend(qkv, bias, width, seg_rows):
    length = qkv.shape[0]
    groups = width // LANES
    heads = LANES // HD
    block = 2 * seg_rows
    live = length * length // 2
    return pl.pallas_call(
        functools.partial(attend_kernel, block, seg_rows),
        grid=(groups,),
        in_specs=[
            pl.BlockSpec((length, LANES), lambda i: (0, i)),
            pl.BlockSpec((length, LANES), lambda i: (0, groups + i)),
            pl.BlockSpec((length, LANES), lambda i: (0, 2 * groups + i)),
            pl.BlockSpec(bias.shape, lambda i: (0, 0)),
        ],
        out_specs=[
            pl.BlockSpec((length, LANES), lambda i: (0, i)),
            pl.BlockSpec((1, heads, length), lambda i: (i, 0, 0)),
        ],
        out_shape=[
            jax.ShapeDtypeStruct((length, width), BF),
            jax.ShapeDtypeStruct((groups, heads, length), F32),
        ],
        compiler_params=settings(),
        cost_estimate=cost(16 * live * width, 8 * length * width, live * width // HD),
        name="attend",
    )(qkv, qkv, qkv, bias)


def attend_back_pair(
    blocks, finish, block, seg_rows, lanes_out, q_ref, k_ref, v_ref, o_ref, do_ref, lse_ref, bias_ref, cos_ref,
    sin_ref, out_ref, dk_ref, dv_ref,
):
    length = q_ref.shape[0]
    heads = q_ref.shape[1] // HD
    k_turned = k_ref[...].T
    product = (do_ref[...].astype(F32) * o_ref[...].astype(F32)).T
    deltas = [product[h * HD : (h + 1) * HD].sum(axis=0, keepdims=True) for h in range(heads)]
    for m in blocks:
        cols = slice(m * block, (m + 1) * block)
        grads = []
        for h in range(heads):
            lanes = slice(h * HD, (h + 1) * HD)
            q, do = q_ref[cols, lanes], do_ref[cols, lanes]
            lse = lse_ref[0, h : h + 1, cols]
            delta = deltas[h][:, cols]
            acc = jnp.zeros((HD, block), F32)
            for u in range(m + 1):
                keys = slice(u * block, (u + 1) * block)
                s = nt(k_ref[keys, lanes], q)
                p = jnp.exp(s + (mask_block(block, seg_rows, bias_ref, m, u) - lse))
                if u == m:
                    p = jnp.where(causal(block), p, 0.0)
                dp = nt(v_ref[keys, lanes], do)
                ds = (p * (dp - delta)).astype(BF)
                dv = nn(p.astype(BF), do)
                dk = nn(ds, q)
                if u == m:
                    dv_ref[h, keys, :] = dv
                    dk_ref[h, keys, :] = dk
                else:
                    dv_ref[h, keys, :] += dv
                    dk_ref[h, keys, :] += dk
                acc = acc + nn(k_turned[lanes, keys], ds)
            grads.append(acc)
        dq = jnp.concatenate(grads, axis=0).T * (1.0 / math.sqrt(HD))
        out_ref[0, cols, lanes_out] = turn(dq, cos_ref[cols, :], -sin_ref[cols, :]).astype(BF)
    for m in range(length // block if finish else 0):
        cols = slice(m * block, (m + 1) * block)
        dk = jnp.concatenate([dk_ref[h, cols, :] for h in range(heads)], axis=1)
        out_ref[1, cols, lanes_out] = turn(dk, cos_ref[cols, :], -sin_ref[cols, :]).astype(BF)
        out_ref[2, cols, lanes_out] = jnp.concatenate(
            [dv_ref[h, cols, :] for h in range(heads)], axis=1
        ).astype(BF)


def rms_back(grad, x, gain):
    inverse = inverse_rms(x)
    unit = x * inverse
    scaled = grad * gain
    inner = jnp.mean(scaled * unit, axis=1, keepdims=True)
    return inverse * (scaled - unit * inner), jnp.sum(grad * unit, axis=0, keepdims=True)


def back_rows(acc_ref, x_ref, gain_ref, gain_part_ref, part_ref):
    chunk = 128

    @pl.loop(0, x_ref.shape[0] // chunk)
    def _(i):
        span = pl.ds(i * chunk, chunk)
        part, piece = rms_back(acc_ref[span, :], x_ref[span, :].astype(F32), gain_ref[...])
        part_ref[span, :] = part.astype(part_ref.dtype)
        gain_part_ref[...] += jnp.broadcast_to(piece, gain_part_ref.shape)


def ffn_kernel(
    x_own,
    x_other,
    cot_own,
    cot_other,
    gain_ref,
    wg_ref,
    wu_ref,
    wd_ref,
    grads_ref,
    normed_ref,
    part_ref,
    gain_part_ref,
    got_hbm,
    cot_ref,
    acc_ref,
    part_send,
    part_sems,
):
    h, j = pl.program_id(0), pl.program_id(1)
    chunk = 256
    across = (lax.axis_index("dp"), 1 - lax.axis_index("tensor"))
    quarter = part_send.shape[0] // QUARTERS

    def part_copy(r):
        span = pl.ds(r * quarter, quarter)
        return remote(part_send.at[span], got_hbm.at[span], part_sems.at[r], across)

    @pl.when((h == 0) & (j == 0))
    def _():
        arrived = pltpu.get_barrier_semaphore()
        pl.semaphore_signal(arrived, inc=1, device_id=across, device_id_type=MESH)
        pl.semaphore_wait(arrived, 1)
        gain_part_ref[...] = jnp.zeros_like(gain_part_ref)

    for turn_at, (x_ref, c_ref) in enumerate(((x_other, cot_other), (x_own, cot_own))):

        @pl.when((h == turn_at) & (j == 0))
        def _():
            norm_rows(x_ref, gain_ref, normed_ref)
            cot_ref[...] = c_ref[...]

    @pl.when(j == 0)
    def _():
        acc_ref[...] = jnp.zeros_like(acc_ref)

    for r in range(0, cot_ref.shape[0], chunk):
        span = slice(r, r + chunk)
        gate = nn(normed_ref[span, :], wg_ref[...])
        up = nn(normed_ref[span, :], wu_ref[...])
        grad_hidden = nn(cot_ref[span, :], wd_ref[...])
        sig = jax.nn.sigmoid(gate)
        silu = gate * sig
        grads_ref[2, span, :] = (silu * up).astype(BF)
        grad_gate = (grad_hidden * up * (sig + silu * (1.0 - sig))).astype(BF)
        grad_up = (grad_hidden * silu).astype(BF)
        grads_ref[0, span, :] = grad_gate
        grads_ref[1, span, :] = grad_up
        acc_ref[span, :] += nt(grad_gate, wg_ref[...]) + nt(grad_up, wu_ref[...])

    for turn_at, x_ref in enumerate((x_other, x_own)):

        @pl.when((h == turn_at) & (j == pl.num_programs(1) - 1))
        def _():
            back_rows(acc_ref, x_ref, gain_ref, gain_part_ref, part_ref)
            if turn_at == 0:
                part_send[...] = part_ref[...]
                for r in range(EARLY):
                    part_copy(r).start()
            else:
                for r in range(EARLY):
                    part_copy(r).wait()


def resident(shape):
    zeros = (0,) * len(shape)
    return pl.BlockSpec(shape, lambda *grid: zeros, pipeline_mode=pl.Buffered(1))


def ffn(xs, cots, gain, w, hidden_width, cols=512):
    rows, d = xs[0].shape
    steps = hidden_width // cols
    per_half = lambda h, j: (1 - h, 0, 0)
    return pl.pallas_call(
        ffn_kernel,
        grid=(2, steps),
        in_specs=[resident((rows, d))] * 4
        + [
            resident((1, d)),
            pl.BlockSpec((d, cols), lambda h, j: (0, j)),
            pl.BlockSpec((d, cols), lambda h, j: (0, steps + j)),
            pl.BlockSpec((d, cols), lambda h, j: (0, 2 * steps + j)),
        ],
        out_specs=[
            pl.BlockSpec((None, 3, rows, cols), lambda h, j: (1 - h, 0, 0, j)),
            pl.BlockSpec((None, rows, d), per_half),
            pl.BlockSpec((None, rows, d), per_half),
            pl.BlockSpec((8, d), lambda h, j: (0, 0)),
            pl.BlockSpec(memory_space=pl.ANY),
        ],
        out_shape=[
            jax.ShapeDtypeStruct((2, 3, rows, hidden_width), BF),
            jax.ShapeDtypeStruct((2, rows, d), BF),
            jax.ShapeDtypeStruct((2, rows, d), BF),
            jax.ShapeDtypeStruct((8, d), F32),
            jax.ShapeDtypeStruct((rows, d), BF),
        ],
        scratch_shapes=[
            pltpu.VMEM((rows, d), BF),
            pltpu.VMEM((rows, d), F32),
            pltpu.VMEM((rows, d), BF),
            pltpu.SemaphoreType.DMA((EARLY, 2)),
        ],
        compiler_params=remote_settings(3, axes=2),
        cost_estimate=cost(
            20 * rows * d * hidden_width,
            12 * d * hidden_width + 16 * rows * d + 12 * rows * hidden_width,
            2 * rows * hidden_width,
        ),
        name="ffn",
    )(*xs, *cots, gain, w, w, w)


MESH = pl.DeviceIdType.MESH
QUARTERS = 4
EARLY = 3
UP_SENT = 7
GAIN_ROWS = 16


class Scatter:
    def __init__(self, devices, rows, count):
        self.devices, self.rows, self.count = devices, rows, count
        self.stages = devices.bit_length() - 1
        self.lags = [1] + [3] * (self.stages - 1)
        self.slots = [2 * lag for lag in self.lags]
        if self.stages >= 3:
            self.slots[1] = self.slots[2] = 8
        self.starts = [sum(self.lags[:s]) for s in range(self.stages + 1)]
        self.steps = count + self.starts[-1]

    def scratch(self):
        shapes = []
        for s in range(self.stages):
            slots, left = self.slots[s], self.devices >> (s + 1)
            shapes.append(pltpu.VMEM((slots, 2, left, self.rows, COLS), BF))
            shapes.append(pltpu.VMEM((slots, left, self.rows, COLS), BF))
            shapes.append(pltpu.SemaphoreType.DMA((slots,)))
            shapes.append(pltpu.SemaphoreType.DMA((slots,)))
        return shapes

    def bind(self, refs):
        self.held, self.got = refs[0::4], refs[1::4]
        self.sent_sem, self.got_sem = refs[2::4], refs[3::4]
        self.me, self.side = lax.axis_index("dp"), lax.axis_index("tensor")

    def late(self, block):
        return (block % 4) // 3

    def own_bit(self, b):
        return (self.me // (1 << b)) % 2

    def partner(self, b):
        return self.me + (1 - 2 * self.own_bit(b)) * (1 << b)

    def turned(self, s, block):
        if s not in (1, 2) or self.stages < 3:
            return self.own_bit(s), self.partner(s)
        late = self.late(block)
        return (
            self.own_bit(s) * (1 - late) + self.own_bit(3 - s) * late,
            self.partner(s) * (1 - late) + self.partner(3 - s) * late,
        )

    def barrier(self):
        arrived = pltpu.get_barrier_semaphore()
        for b in range(self.stages):
            pl.semaphore_signal(
                arrived, inc=1, device_id=(self.partner(b), self.side), device_id_type=MESH
            )
        pl.semaphore_signal(
            arrived, inc=1, device_id=(self.me, 1 - self.side), device_id_type=MESH
        )
        pl.semaphore_wait(arrived, self.stages + 1)

    def copy(self, s, block, gain=False):
        slot = block % self.slots[s]
        bit, partner = self.turned(s, block)
        src, dst = self.held[s].at[slot, 1 - bit], self.got[s].at[slot]
        if gain:
            src, dst = src.at[:, pl.ds(0, GAIN_ROWS)], dst.at[:, pl.ds(0, GAIN_ROWS)]
        sems = self.sent_sem[s].at[slot], self.got_sem[s].at[slot]
        return pltpu.make_async_remote_copy(
            src_ref=src,
            dst_ref=dst,
            send_sem=sems[0],
            recv_sem=sems[1],
            device_id=(partner, self.side),
            device_id_type=MESH,
        )

    def advance(self, step, emit):
        for s in range(self.stages, 0, -1):
            block = step - self.starts[s]
            last = self.count - 1
            for gain in (False, True):

                @pl.when((block == last) if gain else (block >= 0) & (block < last))
                def _():
                    self.receive(s, block, gain, emit)

    def receive(self, s, block, gain, emit):
        slot = block % self.slots[s - 1]
        self.copy(s - 1, block, gain).wait()
        keep, _ = self.turned(s - 1, block)
        held, got = self.held[s - 1], self.got[s - 1]
        rows = slice(0, GAIN_ROWS if gain else self.rows)
        if s == self.stages:
            total = held[slot, keep, 0, rows].astype(F32) + got[slot, 0, rows].astype(F32)
            emit(block, total, gain)
            return
        later = block % self.slots[s]
        late = self.late(block)

        def add(k, carry):
            total = held[slot, keep, k, rows] + got[slot, k, rows]
            bit, rest = k % 2, k // 2
            if s == 1 and self.stages >= 3:
                bit = bit * (1 - late) + (k // 2) % 2 * late
                rest = rest * (1 - late) + (k // 4 * 2 + k % 2) * late
            self.held[s][later, bit, rest, rows] = total
            return carry

        lax.fori_loop(0, self.devices >> s, add, 0)
        self.copy(s, block, gain).start()

    def multiply(self, block, turned_ref, rights):
        slot = block % self.slots[0]
        pieces = 4
        size = self.devices // pieces

        def piece(i, carry):
            span = pl.ds(i * size * self.rows, size * self.rows)
            total, start = None, 0
            for right in rights:
                part = nn(turned_ref[span, start : start + right.shape[0]], right[...])
                total = part if total is None else total + part
                start += right.shape[0]
            for r in range(size):
                block_rows = total[r * self.rows : (r + 1) * self.rows].astype(BF)
                self.held[0][slot, r % 2, i * (size // 2) + r // 2] = block_rows
            return carry

        lax.fori_loop(0, pieces, piece, 0)
        self.copy(0, block).start()

    def enter(self, block, ref):
        slot = block % self.slots[0]
        pieces = 4
        size = self.devices // pieces

        def piece(i, carry):
            rows = ref[pl.ds(i * size * self.rows, size * self.rows), :]
            for r in range(size):
                self.held[0][slot, r % 2, i * (size // 2) + r // 2] = rows[
                    r * self.rows : (r + 1) * self.rows
                ]
            return carry

        lax.fori_loop(0, pieces, piece, 0)
        self.copy(0, block).start()

    def put_gain(self, block, row):
        slot = block % self.slots[0]
        empty = jnp.zeros((1, COLS - self.rows), F32)
        for k in range(self.devices):
            piece = jnp.concatenate([row[:, k * self.rows : (k + 1) * self.rows], empty], axis=1)
            piece = jnp.broadcast_to(piece, (GAIN_ROWS, COLS)).astype(BF)
            self.held[0][slot, k % 2, k // 2, :GAIN_ROWS] = piece
        self.copy(0, block, True).start()


def turn_piece(turned_ref, left, start, row):
    cols = pl.ds(pl.multiple_of(start + row, 256), 256)

    @pl.loop(0, left.shape[1] // 256)
    def _(i):
        span = pl.ds(pl.multiple_of(i * 256, 256), 256)
        turned_ref[span, cols] = left[row : row + 256, span].T


def turn_kernel(first_ref, second_ref, out_ref):
    start = 0
    for left in (first_ref, second_ref):
        for row in range(0, left.shape[0], 256):
            turn_piece(out_ref, left, start, row)
        start += left.shape[0]


def turn_pair(first, second):
    rows, d = first.shape
    return pl.pallas_call(
        turn_kernel,
        out_shape=jax.ShapeDtypeStruct((d, 2 * rows), first.dtype),
        compiler_params=pltpu.CompilerParams(vmem_limit_bytes=32 * 1024 * 1024),
        cost_estimate=cost(0, 8 * rows * d),
        name="turn_pair",
    )(first, second)


def emit_into(outs, counts, block, value, gain):
    if gain:
        outs[-1][...] = value
        return
    first = 0
    for out, count in zip(outs, counts):

        @pl.when((block >= first) & (block < first + count))
        def _():
            out[...] = value

        first += count


def emit_specs(scatter, counts):
    first = scatter.starts[-1]
    specs, shapes = [], []
    for count in counts:

        def where(j, first=first, most=count - 1):
            return (0, jnp.clip(j - first, 0, most))

        specs.append(pl.BlockSpec((scatter.rows, COLS), where))
        shapes.append(jax.ShapeDtypeStruct((scatter.rows, count * COLS), F32))
        first += count
    specs.append(pl.BlockSpec((GAIN_ROWS, COLS), lambda j: (0, 0)))
    shapes.append(jax.ShapeDtypeStruct((GAIN_ROWS, COLS), F32))
    return specs, shapes


def remote(src, dst, sems, device):
    return pltpu.make_async_remote_copy(
        src_ref=src,
        dst_ref=dst,
        send_sem=sems.at[0],
        recv_sem=sems.at[1],
        device_id=device,
        device_id_type=MESH,
    )


def ffn_scatter_kernel(scatter, per, sent, unsent, *refs):
    (
        cot_turned, norm_own, norm_other, right_own, right_other, whole_own, whole_other,
        cot_hbm, middle_hbm, parts_hbm, got_hbm, gain_ref, wd_ref, wo_ref,
    ) = refs[:14]
    outs = refs[14:17]
    whole_ref, gm_ref, grad_attended, block_out_ref, gm_turned = refs[17:22]
    (
        norm_turned, cot_own, middle_own, part_own, got_part, gm_own, gm_got, gain_got, acc_own,
        acc_other, block_send, block_got, gain_sems, part_sems, gm_sems, block_sems, local_sems,
    ) = refs[22:39]
    scatter.bind(refs[39:])
    step = pl.program_id(0)
    side = scatter.side
    across = (scatter.me, 1 - side)
    half = part_own.shape[0]
    quarter = half // QUARTERS
    row_chunk = 128
    early = pl.ds(0, EARLY * quarter)
    rest = pl.ds(EARLY * quarter, half - EARLY * quarter)

    def part_copy():
        return remote(parts_hbm.at[1, rest], got_part.at[rest], part_sems, across)

    def gm_copy(r):
        span = pl.ds(r * quarter, quarter)
        return remote(gm_own.at[span], gm_got.at[span], gm_sems.at[r], across)

    def block_copy():
        return remote(block_send, block_got, block_sems, across)

    def gain_copy():
        return remote(gain_ref, gain_got, gain_sems, across)

    loads = [
        pltpu.make_async_copy(cot_hbm, cot_own, local_sems.at[0]),
        pltpu.make_async_copy(parts_hbm.at[0], part_own, local_sems.at[1]),
        pltpu.make_async_copy(middle_hbm, middle_own, local_sems.at[2]),
        pltpu.make_async_copy(got_hbm.at[early], got_part.at[early], local_sems.at[3]),
    ]

    keeps = [
        pltpu.make_async_copy(gm_own, gm_ref.at[side], local_sems.at[4]),
        pltpu.make_async_copy(gm_got, gm_ref.at[1 - side], local_sems.at[5]),
    ]

    @pl.when(step == 0)
    def _():
        for load in loads:
            load.start()
        scatter.barrier()
        part_copy().start()
        gain_copy().start()

    scatter.advance(step, functools.partial(emit_into, outs, (per, sent - per)))

    @pl.when(step < per)
    def _():
        scatter.multiply(step, cot_turned, (right_own, right_other))

        @pl.when(step == 0)
        def _():
            acc_own[...] = jnp.zeros_like(acc_own)
            acc_other[...] = jnp.zeros_like(acc_other)

        @pl.loop(0, half // 256)
        def _(i):
            span = pl.ds(i * 256, 256)
            acc_own[span, :] += nt(right_own[span, :], wd_ref[...])
            acc_other[span, :] += nt(right_other[span, :], wd_ref[...])

    @pl.when(step == per)
    def _():
        @pl.loop(0, half // row_chunk)
        def _(i):
            span = pl.ds(i * row_chunk, row_chunk)
            block_send[span, :] = acc_other[span, :].astype(BF)

        block_copy().start()

    pieces = [(norm_own, 0, r) for r in range(0, half, 256)]
    pieces += [(norm_other, half, r) for r in range(0, half, 256)]
    for nth, (left, start, row) in enumerate(pieces):

        @pl.when(step == per - len(pieces) + nth)
        def _():
            turn_piece(norm_turned, left, start, row)

    @pl.when((step >= per) & (step < sent))
    def _():
        scatter.multiply(step, norm_turned, (right_own, right_other))

    @pl.when(step == sent)
    def _():
        gain_copy().wait()
        scatter.put_gain(step, gain_ref[0:1, :] + gain_got[0:1, :])

    @pl.when((step >= per) & (step < per + unsent))
    def _():
        rows = whole_ref.shape[0] // 4

        @pl.loop(0, 4)
        def _(i):
            span = pl.ds(i * rows, rows)
            total = nn(norm_turned[span, :half], whole_own[...])
            whole_ref[span, :] = (total + nn(norm_turned[span, half:], whole_other[...])).astype(BF)

    for r in range(QUARTERS):

        @pl.when(step == 1 + r + (1 if r >= EARLY else 0))
        def _():
            if r == 0:
                for load in loads:
                    load.wait()
            if r == EARLY:
                part_copy().wait()

            @pl.loop(r * quarter // row_chunk, (r + 1) * quarter // row_chunk)
            def _(i):
                span = pl.ds(i * row_chunk, row_chunk)
                total = cot_own[span, :].astype(F32) + part_own[span, :].astype(F32)
                gm_own[span, :] = (total + got_part[span, :].astype(F32)).astype(BF)

            gm_copy(r).start()

    @pl.when(step == sent + 1)
    def _():
        for r in range(QUARTERS):
            gm_copy(r).wait()
        for keep in keeps:
            keep.start()

    width = grad_attended.shape[2]
    for nth in range(width // COLS):

        @pl.when(step == sent + 2 + nth)
        def _():
            cols = slice(nth * COLS, (nth + 1) * COLS)
            grad_attended[side, :, cols] = nn(gm_own[...], wo_ref[...]).astype(BF)
            grad_attended[1 - side, :, cols] = nn(gm_got[...], wo_ref[...]).astype(BF)

    pieces = [(gm_own, side, r) for r in range(0, half, 256)]
    pieces += [(gm_got, 1 - side, r) for r in range(0, half, 256)]
    for nth, (left, at, row) in enumerate(pieces):

        @pl.when(step == sent + 2 + width // COLS + nth)
        def _():
            turn_piece(gm_turned, left, at * half, row)

    @pl.when(step == scatter.steps - 1)
    def _():
        block_copy().wait()

        @pl.loop(0, half // row_chunk)
        def _(i):
            span = pl.ds(i * row_chunk, row_chunk)
            total = middle_own[span, :].astype(F32) + acc_own[span, :]
            block_out_ref[span, :] = (total + block_got[span, :].astype(F32)).astype(BF)

        for keep in keeps:
            keep.wait()


def remote_settings(identity, mib=60, axes=1):
    return pltpu.CompilerParams(
        dimension_semantics=("arbitrary",) * axes,
        vmem_limit_bytes=mib * 1024 * 1024,
        collective_id=identity,
        has_side_effects=True,
    )


def ffn_scatter(
    devices, cot_turned, normed, grads, cot, middle, parts, got, gain_part, w, w_attention, heads
):
    half, d = middle.shape
    width = grads.shape[3]
    per = width // COLS
    up_sent = per * UP_SENT // 8
    sent = per + up_sent
    left = 2 * per - up_sent
    head_blocks = heads // COLS
    scatter = Scatter(devices, d // devices, sent + 1)
    assert scatter.rows * devices == d and per >= 2 * half // 256 and per > QUARTERS + 1
    assert scatter.steps >= max(per + left, sent + 2 + head_blocks + 2 * half // 256)
    assert COLS >= scatter.rows >= GAIN_ROWS

    def right(side):
        def where(j):
            c = jnp.minimum(j, sent - 1)
            return (side, 2 - c // per, 0, c % per)

        return pl.BlockSpec((None, None, half, COLS), where)

    def whole_block(j):
        return jnp.clip(j - per, 0, left - 1)

    def left_whole(side):
        def where(j):
            c = whole_block(j)
            kind = c // per
            return (side, kind, 0, (c + kind * up_sent) % per)

        return pl.BlockSpec((None, None, half, COLS), where)

    def rows_of(side):
        return pl.BlockSpec(
            (None, half, d), lambda j: (side, 0, 0), pipeline_mode=pl.Buffered(1)
        )

    specs, shapes = emit_specs(scatter, (per, sent - per))
    left_there = pl.BlockSpec(memory_space=pl.ANY)
    return pl.pallas_call(
        functools.partial(ffn_scatter_kernel, scatter, per, sent, left),
        grid=(scatter.steps,),
        in_specs=[
            resident((d, 2 * half)),
            rows_of(0),
            rows_of(1),
            right(0),
            right(1),
            left_whole(0),
            left_whole(1),
            left_there,
            left_there,
            left_there,
            left_there,
            resident((8, d)),
            pl.BlockSpec((d, COLS), lambda j: (0, 2 * per + jnp.minimum(j, per - 1))),
            pl.BlockSpec(
                (d, COLS),
                lambda j: (0, 3 * head_blocks + jnp.clip(j - sent - 2, 0, head_blocks - 1)),
            ),
        ],
        out_specs=specs
        + [
            pl.BlockSpec((d, COLS), lambda j: (0, whole_block(j))),
            left_there,
            resident((2, half, heads)),
            resident((half, d)),
            resident((d, 2 * half)),
        ],
        out_shape=shapes
        + [
            jax.ShapeDtypeStruct((d, left * COLS), BF),
            jax.ShapeDtypeStruct((2, half, d), BF),
            jax.ShapeDtypeStruct((2, half, heads), BF),
            jax.ShapeDtypeStruct((half, d), BF),
            jax.ShapeDtypeStruct((d, 2 * half), BF),
        ],
        scratch_shapes=[
            pltpu.VMEM((d, 2 * half), BF),
            pltpu.VMEM((half, d), BF),
            pltpu.VMEM((half, d), BF),
            pltpu.VMEM((half, d), BF),
            pltpu.VMEM((half, d), BF),
            pltpu.VMEM((half, d), BF),
            pltpu.VMEM((half, d), BF),
            pltpu.VMEM((8, d), F32),
            pltpu.VMEM((half, d), F32),
            pltpu.VMEM((half, d), F32),
            pltpu.VMEM((half, d), BF),
            pltpu.VMEM((half, d), BF),
            pltpu.SemaphoreType.DMA((2,)),
            pltpu.SemaphoreType.DMA((2,)),
            pltpu.SemaphoreType.DMA((QUARTERS, 2)),
            pltpu.SemaphoreType.DMA((2,)),
            pltpu.SemaphoreType.DMA((6,)),
        ]
        + scatter.scratch(),
        compiler_params=remote_settings(0),
        cost_estimate=cost(16 * half * d * per * COLS, 20 * half * d),
        name="ffn_scatter",
    )(
        cot_turned, normed, normed, grads, grads, grads, grads, cot, middle, parts, got,
        gain_part, w, w_attention,
    )


def attention_scatter_kernel(scatter, per, early, block, seg_rows, *refs):
    (
        norm_turned, gm_turned, gain_ref, q_ref, k_ref, v_ref, o_ref, do_ref, lse_ref, bias_ref,
        cos_ref, sin_ref, attended_ref, w_ref, whole_ref, gm_hbm, x_hbm,
    ) = refs[:17]
    outs, token_grad_ref = refs[17 : 22 + len(early)], refs[22 + len(early)]
    refs = refs[23 + len(early) :]
    (
        grads_ref, dk_ref, dv_ref, gm_own, x_ref, acc_ref, part_send, part_got, gain_part,
        part_sems, local_sems,
    ) = refs[:11]
    scatter.bind(refs[11:])
    step = pl.program_id(0)
    side = scatter.side
    across = (scatter.me, 1 - side)
    length = x_ref.shape[0]
    half = length // 2
    quarter = half // QUARTERS
    chunk = 128
    groups = grads_ref.shape[2] // LANES
    own, other = side * half, (1 - side) * half
    before = sum(early)
    turns = 2 * groups

    def part_copy(r):
        span = pl.ds(r * quarter, quarter)
        return remote(part_send.at[span], part_got.at[span], part_sems.at[r], across)

    loads = [
        pltpu.make_async_copy(x_hbm, x_ref, local_sems.at[0]),
        pltpu.make_async_copy(gm_hbm.at[side], gm_own, local_sems.at[1]),
    ]

    def back(row):
        span = pl.ds(row, chunk)
        part, piece = rms_back(acc_ref[span, :], x_ref[span, :].astype(F32), gain_ref[...])
        gain_part[...] += jnp.broadcast_to(piece, gain_part.shape)
        return part

    def emit(column, value, gain):
        if gain:
            outs[4][...] = value
            return
        first = 0
        for out, count in zip(outs[5:], early):

            @pl.when((column >= first) & (column < first + count))
            def _():
                out[...] = value

            first += count

        @pl.when((column >= before) & (column < before + per))
        def _():
            outs[3][...] = value

        for kind in range(3):

            @pl.when((column >= before + per) & ((column - before - per) % 3 == kind))
            def _():
                outs[kind][...] = value

    @pl.when(step == 0)
    def _():
        for load in loads:
            load.start()
        scatter.barrier()

    scatter.advance(step, emit)

    @pl.when(step < before)
    def _():
        scatter.enter(step, whole_ref)

    @pl.when((step >= before) & (step < before + per))
    def _():
        scatter.multiply(step, gm_turned, (attended_ref,))

    @pl.when((step >= before + per) & (step < before + 4 * per))
    def _():
        column = step - before - per
        cols = pl.ds(pl.multiple_of(column // 3 * COLS, COLS), COLS)
        scatter.multiply(step, norm_turned, (grads_ref.at[column % 3, :, cols],))

    count = length // block
    split = count - count // 4
    for odd in range(2):

        @pl.when((step < turns) & (step % 2 == odd))
        def _():
            lanes = pl.ds(pl.multiple_of(step // 2 * LANES, LANES), LANES)
            blocks = range(split, count) if odd else range(split)
            attend_back_pair(
                blocks, odd == 1, block, seg_rows, lanes, q_ref, k_ref, v_ref, o_ref, do_ref,
                lse_ref, bias_ref, cos_ref, sin_ref, grads_ref, dk_ref, dv_ref,
            )

    @pl.when(step == 1)
    def _():
        for load in loads:
            load.wait()
        acc_ref[...] = jnp.zeros_like(acc_ref)
        gain_part[...] = jnp.zeros_like(gain_part)

    @pl.when((step >= turns) & (step < turns + 3))
    def _():
        kind = step - turns

        @pl.loop(0, length // 256)
        def _(i):
            span = pl.ds(i * 256, 256)
            acc_ref[span, :] += nt(grads_ref[kind, span, :], w_ref[...])

    for r in range(QUARTERS):

        @pl.when(step == turns + 3 + r // 2)
        def _():
            @pl.loop(r * quarter // chunk, (r + 1) * quarter // chunk)
            def _(i):
                part_send[pl.ds(i * chunk, chunk), :] = back(other + i * chunk).astype(BF)

            part_copy(r).start()

        @pl.when(step == turns + 5 + r // 2)
        def _():
            @pl.loop(r * quarter // chunk, (r + 1) * quarter // chunk)
            def _(i):
                span = pl.ds(own + i * chunk, chunk)
                kept = gm_own[pl.ds(i * chunk, chunk), :].astype(F32)
                acc_ref[span, :] = back(own + i * chunk) + kept

    @pl.when(step == before + 4 * per)
    def _():
        scatter.put_gain(step, gain_part[0:1, :])

    for r in range(QUARTERS):

        @pl.when(step == scatter.steps - QUARTERS + r)
        def _():
            part_copy(r).wait()

            @pl.loop(r * quarter // chunk, (r + 1) * quarter // chunk)
            def _(i):
                span = pl.ds(i * chunk, chunk)
                total = acc_ref[pl.ds(own + i * chunk, chunk), :]
                token_grad_ref[span, :] = (total + part_got[span, :].astype(F32)).astype(BF)


def attention_scatter(
    devices, norm_turned, gm_turned, gm, x, gain, qkv, attended, grad_attended, lse, bias, cosine,
    sine, w, whole, early, seg_rows,
):
    length, width = attended.shape
    half, d = gm.shape[1:]
    per = width // COLS
    groups = width // LANES
    heads = LANES // HD
    before = sum(early)
    scatter = Scatter(devices, d // devices, before + 4 * per + 1)
    lead = scatter.starts[-1]
    assert groups == 2 * per and 2 * groups + 7 <= before + 4 * per and lead > QUARTERS
    assert scatter.rows * devices == d and whole.shape[1] == before * COLS

    def group(j):
        return jnp.minimum(j // 2, groups - 1)

    def lanes_of(kind):
        return pl.BlockSpec((length, LANES), lambda j: (0, kind * groups + group(j)))

    specs, shapes = [], []
    for kind in range(4):
        first = lead + before + (per + kind if kind < 3 else 0)
        stride = 3 if kind < 3 else 1

        def where(j, first=first, stride=stride):
            return (0, jnp.clip(jnp.maximum(j - first, 0) // stride, 0, per - 1))

        specs.append(pl.BlockSpec((scatter.rows, COLS), where))
        shapes.append(jax.ShapeDtypeStruct((scatter.rows, width), F32))
    more_specs, more_shapes = emit_specs(scatter, early)
    specs += more_specs[-1:] + more_specs[:-1]
    shapes += more_shapes[-1:] + more_shapes[:-1]
    left_there = pl.BlockSpec(memory_space=pl.ANY)
    return pl.pallas_call(
        functools.partial(attention_scatter_kernel, scatter, per, early, 2 * seg_rows, seg_rows),
        grid=(scatter.steps,),
        in_specs=[
            resident((d, length)),
            resident((d, length)),
            resident((1, d)),
            lanes_of(0),
            lanes_of(1),
            lanes_of(2),
            lanes_of(0),
            lanes_of(0),
            pl.BlockSpec((1, heads, length), lambda j: (group(j), 0, 0)),
            resident(bias.shape),
            resident((length, LANES)),
            resident((length, LANES)),
            pl.BlockSpec((length, COLS), lambda j: (0, jnp.clip(j - before, 0, per - 1))),
            pl.BlockSpec((d, width), lambda j: (0, jnp.clip(j - 2 * groups, 0, 2))),
            pl.BlockSpec((d, COLS), lambda j: (0, jnp.minimum(j, before - 1))),
            left_there,
            left_there,
        ],
        out_specs=specs + [resident((half, d))],
        out_shape=shapes + [jax.ShapeDtypeStruct((half, d), BF)],
        scratch_shapes=[
            pltpu.VMEM((3, length, width), BF),
            pltpu.VMEM((heads, length, HD), F32),
            pltpu.VMEM((heads, length, HD), F32),
            pltpu.VMEM((half, d), BF),
            pltpu.VMEM((length, d), BF),
            pltpu.VMEM((length, d), F32),
            pltpu.VMEM((half, d), BF),
            pltpu.VMEM((half, d), BF),
            pltpu.VMEM((8, d), F32),
            pltpu.SemaphoreType.DMA((QUARTERS, 2)),
            pltpu.SemaphoreType.DMA((2,)),
        ]
        + scatter.scratch(),
        compiler_params=remote_settings(1),
        cost_estimate=cost(
            14 * length * d * width + 20 * length * length * width,
            20 * length * d,
            length * length * width // HD,
        ),
        name="attention_scatter",
    )(
        norm_turned, gm_turned, gain, qkv, qkv, qkv, attended, grad_attended, lse, bias, cosine,
        sine, attended, w, whole, gm, x,
    )


class Gather:
    def __init__(self, devices, rows, count):
        self.devices, self.rows, self.count = devices, rows, count
        self.stages = devices.bit_length() - 1
        self.lags = [2] * (self.stages - 1) + [1]
        self.starts = [sum(self.lags[:t]) for t in range(self.stages + 1)]
        self.steps = count + self.starts[-1]

    def scratch(self):
        return [
            pltpu.VMEM((self.count, self.devices, self.rows, COLS), BF),
            pltpu.SemaphoreType.DMA((self.stages, self.count, 2)),
            pltpu.SemaphoreType.DMA((self.count,)),
        ]

    def bind(self, refs):
        self.held, self.sems, self.load_sems = refs
        self.me, self.side = lax.axis_index("dp"), lax.axis_index("tensor")

    def late(self, block):
        return (block % 4) // 3 if self.stages >= 4 else 0 * block

    def place(self, device, block):
        late = self.late(block)
        total = 0
        for t in range(self.stages):
            bit = (device // (1 << (self.stages - 1 - t))) % 2
            if t in (1, 2) and self.stages >= 4:
                total = total + bit * ((1 << t) * (1 - late) + (1 << (3 - t)) * late)
            else:
                total = total + bit * (1 << t)
        return total

    def partner_at(self, t):
        weight = 1 << (self.stages - 1 - t)
        return self.me + (1 - 2 * ((self.me // weight) % 2)) * weight

    def partner(self, t, block):
        if t not in (1, 2) or self.stages < 4:
            return self.partner_at(t)
        late = self.late(block)
        return self.partner_at(t) * (1 - late) + self.partner_at(3 - t) * late

    def barrier(self):
        arrived = pltpu.get_barrier_semaphore()
        for t in range(self.stages):
            pl.semaphore_signal(
                arrived, inc=1, device_id=(self.partner_at(t), self.side), device_id_type=MESH
            )
        pl.semaphore_signal(
            arrived, inc=1, device_id=(self.me, 1 - self.side), device_id_type=MESH
        )
        pl.semaphore_wait(arrived, self.stages + 1)

    def load(self, shard, column, block):
        return pltpu.make_async_copy(
            shard.at[:, pl.ds(column, COLS)],
            self.held.at[block, self.place(self.me, block)],
            self.load_sems.at[block],
        )

    def load_all(self, shards):
        block = 0
        for shard in shards:
            for column in range(0, shard.shape[1], COLS):
                self.load(shard, column, jnp.int32(block)).start()
                block += 1

    def copy(self, t, block):
        size = 1 << t
        first = self.place(self.me, block) // size * size
        run = self.held.at[block, pl.ds(first, size)]
        return remote(run, run, self.sems.at[t, block], (self.partner(t, block), self.side))

    def advance(self, step, shards):
        for t in range(self.stages, -1, -1):
            block = step - self.starts[t]

            @pl.when((block >= 0) & (block < self.count))
            def _():
                if t > 0:
                    self.copy(t - 1, block).wait()
                else:
                    self.load(shards[0], 0, block).wait()
                if t < self.stages:
                    self.copy(t, block).start()


def gather_project_kernel(gather, per, *refs):
    shards, (tokens, cot, gain_ref, depths_ref), later = refs[:4], refs[4:8], refs[8:11]
    w_hbm, qkv_ref, turned_ref, rows_hbm, cot_other, cot_rest, cos_ref, sin_ref, joined = refs[11:20]
    w_ref, rows_ref, normed_ref, x_sems, row_sems, w_sems, join_sems = refs[20:27]
    gather.bind(refs[27:])
    step = pl.program_id(0)
    side = gather.side
    across = (gather.me, 1 - side)
    lead = gather.starts[-1]
    others = lead + gather.count // 2 - 1
    kinds = 3 * per

    def token_copy():
        return remote(tokens, rows_ref.at[side], x_sems.at[0], across)

    def cot_copy():
        rows = pl.ds(0, cot_other.shape[0])
        return remote(cot.at[rows], cot_other, x_sems.at[1], across)

    def token_load():
        return pltpu.make_async_copy(tokens, rows_ref.at[side], row_sems.at[0])

    def rows_store():
        return pltpu.make_async_copy(rows_ref, rows_hbm, row_sems.at[1])

    def w_store(block):
        cols = pl.ds(pl.multiple_of(block * COLS, COLS), COLS)
        return pltpu.make_async_copy(w_ref.at[:, cols], w_hbm.at[:, cols], w_sems.at[block])

    def joins():
        column = 0
        for nth, shard in enumerate(later):
            span = pl.ds(column, shard.shape[1])
            yield pltpu.make_async_copy(shard, joined.at[:, span], join_sems.at[nth])
            column += shard.shape[1]
        rows = pl.ds(cot_other.shape[0], cot_rest.shape[0])
        yield pltpu.make_async_copy(cot.at[rows], cot_rest, join_sems.at[len(later)])

    @pl.when(step == 1)
    def _():
        for join in joins():
            join.start()

    @pl.when(step == 0)
    def _():
        token_load().start()
        gather.load_all(shards)
        gather.barrier()
        token_copy().start()
        cot_copy().start()

    gather.advance(step, shards)

    @pl.when(step == 1)
    def _():
        token_load().wait()
        norm_rows(rows_ref.at[side], gain_ref, normed_ref.at[side])
        turn_tables(depths_ref, cos_ref, sin_ref)

    for nth, row in enumerate(range(0, rows_ref.shape[1], 256)):

        @pl.when(step == 2 + nth)
        def _():
            turn_piece(turned_ref, normed_ref.at[side], side * rows_ref.shape[1], row)

        @pl.when(step == others + 1 + nth)
        def _():
            turn_piece(turned_ref, normed_ref.at[1 - side], (1 - side) * rows_ref.shape[1], row)

    @pl.when(step == others)
    def _():
        token_copy().wait()
        rows_store().start()
        norm_rows(rows_ref.at[1 - side], gain_ref, normed_ref.at[1 - side])

    @pl.when(step >= lead)
    def _():
        block = step - lead
        cols = pl.ds(pl.multiple_of(block * COLS, COLS), COLS)
        for device in range(gather.devices):
            rows = slice(device * gather.rows, (device + 1) * gather.rows)
            w_ref[rows, cols] = gather.held[block, gather.place(device, block)]
        w_store(block).start()

    @pl.loop(0, 3)
    def _(task):
        mine = jnp.where(task == 0, 1, 0)
        half = side * mine + (1 - side) * (1 - mine)
        block = (step - lead) * mine + (2 * (step - others) + task - 1) * (1 - mine)
        cols = pl.ds(pl.multiple_of(block * COLS, COLS), COLS)
        chunk = 256

        @pl.when((block >= 0) & (block < 2 * per))
        def _():
            scale = jnp.where(block < per, 1.0 / math.sqrt(HD), 1.0).astype(BF)
            for r in range(0, qkv_ref.shape[1], chunk):
                span = slice(r, r + chunk)
                pre = nn(normed_ref[half, span, :], w_ref[:, cols])
                cosine = jnp.concatenate([cos_ref[half, span, :]] * (COLS // LANES), axis=1)
                sine = jnp.concatenate([sin_ref[half, span, :]] * (COLS // LANES), axis=1)
                turned = turn(pre, cosine, sine)
                qkv_ref[half, span, cols] = turned.astype(BF) * scale

        @pl.when((block >= 2 * per) & (block < kinds))
        def _():
            for r in range(0, qkv_ref.shape[1], chunk):
                span = slice(r, r + chunk)
                qkv_ref[half, span, cols] = nn(normed_ref[half, span, :], w_ref[:, cols]).astype(BF)

    @pl.when(step == gather.steps - 1)
    def _():
        for join in joins():
            join.wait()
        cot_copy().wait()
        rows_store().wait()

        @pl.loop(0, gather.count)
        def _(block):
            w_store(block).wait()


def gather_project(devices, shards, tokens, cot, cot_rows, gain, depths, later):
    half, d = tokens.shape
    rows, width = shards[0].shape
    total = len(shards) * width
    per = width // COLS
    gather = Gather(devices, rows, total // COLS)
    count = gather.count
    assert rows * devices == d and count // 2 - 1 + (3 * per + 1) // 2 <= count
    left_there = pl.BlockSpec(memory_space=pl.ANY)
    return pl.pallas_call(
        functools.partial(gather_project_kernel, gather, per),
        grid=(gather.steps,),
        in_specs=[left_there] * 6
        + [resident((d,)), pl.BlockSpec(memory_space=pltpu.SMEM)]
        + [left_there] * len(later),
        out_specs=[
            left_there,
            resident((2, half, 3 * width)),
            resident((d, 2 * half)),
            left_there,
            left_there,
            left_there,
            resident((2, half, LANES)),
            resident((2, half, LANES)),
            left_there,
        ],
        out_shape=[
            jax.ShapeDtypeStruct((d, total), BF),
            jax.ShapeDtypeStruct((2, half, 3 * width), BF),
            jax.ShapeDtypeStruct((d, 2 * half), BF),
            jax.ShapeDtypeStruct((2, half, d), BF),
            jax.ShapeDtypeStruct((cot_rows, d), BF),
            jax.ShapeDtypeStruct((half - cot_rows, d), BF),
            jax.ShapeDtypeStruct((2, half, LANES), F32),
            jax.ShapeDtypeStruct((2, half, LANES), F32),
            jax.ShapeDtypeStruct((rows, sum(shard.shape[1] for shard in later)), BF),
        ],
        scratch_shapes=[
            pltpu.VMEM((d, total), BF),
            pltpu.VMEM((2, half, d), BF),
            pltpu.VMEM((2, half, d), BF),
            pltpu.SemaphoreType.DMA((2, 2)),
            pltpu.SemaphoreType.DMA((2,)),
            pltpu.SemaphoreType.DMA((count,)),
            pltpu.SemaphoreType.DMA((len(later) + 1,)),
        ]
        + gather.scratch(),
        compiler_params=remote_settings(2),
        cost_estimate=cost(12 * half * d * width, 2 * d * total),
        name="gather_project",
    )(*shards, tokens, cot, gain, depths, *later)


def project_out_kernel(half_ref, attended_ref, w_ref, out_ref):
    out_ref[...] = nt(attended_ref[...], w_ref[...]).astype(BF)


def project_out(attended, w, half, cols=512):
    _, rows, width = attended.shape
    d = w.shape[0]
    part = w.shape[1] // width - 1
    return pl.pallas_call(
        project_out_kernel,
        grid_spec=pltpu.PrefetchScalarGridSpec(
            num_scalar_prefetch=1,
            grid=(d // cols,),
            in_specs=[
                pl.BlockSpec((None, rows, width), lambda j, half_ref: (half_ref[0], 0, 0)),
                pl.BlockSpec((cols, width), lambda j, half_ref: (j, part)),
            ],
            out_specs=pl.BlockSpec((rows, cols), lambda j, half_ref: (0, j)),
        ),
        out_shape=jax.ShapeDtypeStruct((rows, d), BF),
        compiler_params=settings(32),
        cost_estimate=cost(2 * rows * d * width, 2 * d * (width + rows)),
        name="project_out",
    )(half.reshape(1), attended, w)


def swap(x):
    return lax.ppermute(x, "tensor", [(0, 1), (1, 0)])


def body(
    tokens,
    parents,
    attn_gain,
    ffn_gain,
    query_weight,
    key_weight,
    value_weight,
    output_weight,
    gate_weight,
    up_weight,
    down_weight,
    cotangent,
):
    half, d = tokens.shape
    length = 2 * half
    width = query_weight.shape[1]
    hidden_width = gate_weight.shape[1]
    seg_rows = length // parents.shape[1]
    mine = lax.axis_index("tensor")
    own_start = mine * half

    def own_rows(full):
        return lax.dynamic_slice_in_dim(full, own_start, half, 0)

    def gather(shard):
        return lax.all_gather(shard, "dp", axis=0, tiled=True)

    attn_row = attn_gain[None, :]
    ffn_row = ffn_gain[None, :]

    devices = lax.axis_size("dp")
    bias, depths = tree_tables(parents[0], seg_rows)

    cut = half // 2
    first, qkv, norm_turned, rows_all, cot_first, cot_rest, cosine, sine, second_shard = gather_project(
        devices,
        (query_weight, key_weight, value_weight, output_weight.T),
        tokens,
        cotangent,
        cut,
        attn_gain,
        depths,
        (gate_weight, up_weight, down_weight.T),
    )
    second = gather(second_shard)
    cot_rest = swap(cot_rest)
    qkv = qkv.reshape(length, 3 * width)
    rows_all = rows_all.reshape(length, d)
    cosine, sine = cosine.reshape(length, LANES), sine.reshape(length, LANES)

    attended, lse = attend(qkv, bias, width, seg_rows)
    out_turned = first[:, 3 * width :]
    send = project_out(attended.reshape(2, half, width), first, 1 - mine)
    send, cot_first, cot_rest = lax.optimization_barrier((send, cot_first, cot_rest))
    cot_other = jnp.concatenate([cot_first, cot_rest], axis=0)
    received = swap(send)
    received, cot_turned = lax.optimization_barrier((received, turn_pair(cotangent, cot_other)))
    middle = (
        tokens.astype(F32) + nt(own_rows(attended), out_turned) + received.astype(F32)
    ).astype(BF)
    middle_other = swap(middle)

    ffn_grads, normed_two, parts, gain_part, got_part = ffn(
        (middle, middle_other), (cotangent, cot_other), ffn_row, second, hidden_width
    )
    (
        down_grad, up_first, ffn_gain_grad, whole, grad_middle, grad_attended, block_out, gm_turned,
    ) = ffn_scatter(
        devices,
        cot_turned,
        normed_two,
        ffn_grads,
        cotangent,
        middle,
        parts,
        got_part,
        gain_part,
        second,
        first,
        width,
    )
    blocks = hidden_width // COLS
    rest = whole.shape[1] // COLS - blocks
    (
        query_grad, key_grad, value_grad, output_grad, attn_gain_grad, gate_grad, *up_rest,
        token_grad,
    ) = attention_scatter(
        devices,
        norm_turned,
        gm_turned,
        grad_middle,
        rows_all,
        attn_row,
        qkv,
        attended,
        grad_attended.reshape(length, width),
        lse,
        bias,
        cosine,
        sine,
        first,
        whole,
        (blocks, rest) if rest else (blocks,),
        seg_rows,
    )
    up_grad = jnp.concatenate([up_first, *up_rest], axis=1)
    gain_rows = d // devices // 2

    def gain_piece(columns, side):
        return lax.dynamic_slice_in_dim(columns[0], side * gain_rows, gain_rows, 0)

    return (
        block_out,
        token_grad,
        query_grad,
        key_grad,
        value_grad,
        output_grad.T,
        gate_grad,
        up_grad,
        down_grad.T,
        gain_piece(attn_gain_grad, mine) + swap(gain_piece(attn_gain_grad, 1 - mine)),
        gain_piece(ffn_gain_grad, mine),
    )


def solution(mesh):
    rows = P(("dp", "tensor"), None)
    tall = P("dp", "tensor")
    wide = P("tensor", "dp")
    return jax.shard_map(
        body,
        mesh=mesh,
        in_specs=(
            rows, P("dp", None), P(), P(), tall, tall, tall, wide, tall, tall, wide, rows,
        ),
        out_specs=(
            rows, rows, tall, tall, tall, wide, tall, tall, wide,
            P(("dp", "tensor")), P(("dp", "tensor")),
        ),
        check_vma=False,
    )
```

```python
import functools
import math

import jax
import jax.numpy as jnp
from jax import lax
from jax.experimental import pallas as pl
from jax.experimental.pallas import tpu as pltpu
from jax.sharding import PartitionSpec as P

HD = 64
EPS = 1e-05
BF = jnp.bfloat16
F32 = jnp.float32
COLS = 256
LANES = 128
MASKED = -1e30


def settings(mib=48):
    return pltpu.CompilerParams(
        dimension_semantics=("arbitrary",), vmem_limit_bytes=mib * 1024 * 1024
    )


def cost(flops, bytes_accessed, transcendentals=0):
    return pl.CostEstimate(
        flops=int(flops), bytes_accessed=int(bytes_accessed), transcendentals=int(transcendentals)
    )


def nn(a, b):
    return jnp.dot(a, b, preferred_element_type=F32)


def nt(a, b):
    return lax.dot_general(a, b, (((1,), (1,)), ((), ())), preferred_element_type=F32)


def tree_tables(parent_row, seg_rows):
    segs = parent_row.shape[0]
    index = jnp.arange(segs, dtype=jnp.int32)
    step_up = (parent_row[:, None] == index[None, :]).astype(jnp.int32)
    eye = (index[:, None] == index[None, :]).astype(jnp.int32)
    reach = eye
    for _ in range(segs):
        up = jnp.sum(step_up[:, :, None] * reach[None, :, :], axis=1)
        reach = jnp.minimum(eye + up, 1)
    depths = jnp.sum(reach, axis=1) - 1
    bias = jnp.where(reach.T > 0, 0.0, MASKED).astype(F32)
    return jnp.repeat(bias, seg_rows, axis=1), depths


def turn_tables(depths_ref, cos_ref, sin_ref):
    segs = depths_ref.shape[0]
    seg_rows = 2 * cos_ref.shape[1] // segs
    shape = (seg_rows, LANES)
    lane = lax.broadcasted_iota(jnp.int32, shape, 1) % HD
    row = lax.broadcasted_iota(jnp.int32, shape, 0)
    rates = jnp.exp((lane % (HD // 2)).astype(F32) * (-2.0 * math.log(10000.0) / HD))
    sign = jnp.where(lane < HD // 2, -1.0, 1.0).astype(F32)

    @pl.loop(0, segs)
    def _(seg):
        angles = (depths_ref[seg] * seg_rows + row).astype(F32) * rates
        span = pl.ds(seg % (segs // 2) * seg_rows, seg_rows)
        cos_ref[seg // (segs // 2), span, :] = jnp.cos(angles)
        sin_ref[seg // (segs // 2), span, :] = jnp.sin(angles) * sign


def turn(x, cosine, sine):
    width = x.shape[1]
    lane = lax.broadcasted_iota(jnp.int32, x.shape, 1)
    first = (lane % HD) < HD // 2
    other = jnp.where(
        first, pltpu.roll(x, width - HD // 2, 1), pltpu.roll(x, HD // 2, 1)
    )
    return x * cosine + other * sine


def inverse_rms(x):
    return lax.rsqrt(jnp.mean(x * x, axis=1, keepdims=True) + EPS)


def norm_rows(x_ref, gain_ref, normed_ref):
    chunk = 128

    @pl.loop(0, x_ref.shape[0] // chunk)
    def _(i):
        span = pl.ds(i * chunk, chunk)
        x = x_ref[span, :].astype(F32)
        normed_ref[span, :] = (x * inverse_rms(x) * gain_ref[...]).astype(BF)


def mask_block(block, seg_rows, bias_ref, m, u):
    cols = slice(m * block, (m + 1) * block)
    per = block // seg_rows
    return jnp.concatenate(
        [
            jnp.broadcast_to(bias_ref[u * per + i : u * per + i + 1, cols], (seg_rows, block))
            for i in range(per)
        ],
        axis=0,
    )


def causal(block):
    key = lax.broadcasted_iota(jnp.int32, (block, block), 0)
    query = lax.broadcasted_iota(jnp.int32, (block, block), 1)
    return key <= query


def attend_kernel(block, seg_rows, q_ref, k_ref, v_ref, bias_ref, out_ref, lse_ref):
    length = q_ref.shape[0]
    heads = q_ref.shape[1] // HD
    v_turned = v_ref[...].T
    for m in range(length // block):
        cols = slice(m * block, (m + 1) * block)
        outs = []
        for h in range(heads):
            lanes = slice(h * HD, (h + 1) * HD)
            q = q_ref[cols, lanes]
            scores = []
            for u in range(m + 1):
                s = nt(k_ref[u * block : (u + 1) * block, lanes], q)
                s = s + mask_block(block, seg_rows, bias_ref, m, u)
                if u == m:
                    s = jnp.where(causal(block), s, MASKED)
                scores.append(s)
            peak = scores[0].max(axis=0, keepdims=True)
            for s in scores[1:]:
                peak = jnp.maximum(peak, s.max(axis=0, keepdims=True))
            total = jnp.zeros_like(peak)
            acc = jnp.zeros((HD, block), F32)
            for u, s in enumerate(scores):
                e = jnp.exp(s - peak)
                total = total + e.sum(axis=0, keepdims=True)
                acc = acc + nn(v_turned[lanes, u * block : (u + 1) * block], e.astype(BF))
            outs.append(acc / total)
            lse_ref[0, h : h + 1, cols] = peak + jnp.log(total)
        out_ref[cols, :] = jnp.concatenate(outs, axis=0).T.astype(BF)


def attend(qkv, bias, width, seg_rows):
    length = qkv.shape[0]
    groups = width // LANES
    heads = LANES // HD
    block = 2 * seg_rows
    live = length * length // 2
    return pl.pallas_call(
        functools.partial(attend_kernel, block, seg_rows),
        grid=(groups,),
        in_specs=[
            pl.BlockSpec((length, LANES), lambda i: (0, i)),
            pl.BlockSpec((length, LANES), lambda i: (0, groups + i)),
            pl.BlockSpec((length, LANES), lambda i: (0, 2 * groups + i)),
            pl.BlockSpec(bias.shape, lambda i: (0, 0)),
        ],
        out_specs=[
            pl.BlockSpec((length, LANES), lambda i: (0, i)),
            pl.BlockSpec((1, heads, length), lambda i: (i, 0, 0)),
        ],
        out_shape=[
            jax.ShapeDtypeStruct((length, width), BF),
            jax.ShapeDtypeStruct((groups, heads, length), F32),
        ],
        compiler_params=settings(),
        cost_estimate=cost(16 * live * width, 8 * length * width, live * width // HD),
        name="attend",
    )(qkv, qkv, qkv, bias)


def attend_back_pair(
    blocks, finish, block, seg_rows, lanes_out, q_ref, k_ref, v_ref, o_ref, do_ref, lse_ref, bias_ref, cos_ref,
    sin_ref, out_ref, dk_ref, dv_ref,
):
    length = q_ref.shape[0]
    heads = q_ref.shape[1] // HD
    k_turned = k_ref[...].T
    product = (do_ref[...].astype(F32) * o_ref[...].astype(F32)).T
    deltas = [product[h * HD : (h + 1) * HD].sum(axis=0, keepdims=True) for h in range(heads)]
    for m in blocks:
        cols = slice(m * block, (m + 1) * block)
        grads = []
        for h in range(heads):
            lanes = slice(h * HD, (h + 1) * HD)
            q, do = q_ref[cols, lanes], do_ref[cols, lanes]
            lse = lse_ref[0, h : h + 1, cols]
            delta = deltas[h][:, cols]
            acc = jnp.zeros((HD, block), F32)
            for u in range(m + 1):
                keys = slice(u * block, (u + 1) * block)
                s = nt(k_ref[keys, lanes], q)
                p = jnp.exp(s + (mask_block(block, seg_rows, bias_ref, m, u) - lse))
                if u == m:
                    p = jnp.where(causal(block), p, 0.0)
                dp = nt(v_ref[keys, lanes], do)
                ds = (p * (dp - delta)).astype(BF)
                dv = nn(p.astype(BF), do)
                dk = nn(ds, q)
                if u == m:
                    dv_ref[h, keys, :] = dv
                    dk_ref[h, keys, :] = dk
                else:
                    dv_ref[h, keys, :] += dv
                    dk_ref[h, keys, :] += dk
                acc = acc + nn(k_turned[lanes, keys], ds)
            grads.append(acc)
        dq = jnp.concatenate(grads, axis=0).T * (1.0 / math.sqrt(HD))
        out_ref[0, cols, lanes_out] = turn(dq, cos_ref[cols, :], -sin_ref[cols, :]).astype(BF)
    for m in range(length // block if finish else 0):
        cols = slice(m * block, (m + 1) * block)
        dk = jnp.concatenate([dk_ref[h, cols, :] for h in range(heads)], axis=1)
        out_ref[1, cols, lanes_out] = turn(dk, cos_ref[cols, :], -sin_ref[cols, :]).astype(BF)
        out_ref[2, cols, lanes_out] = jnp.concatenate(
            [dv_ref[h, cols, :] for h in range(heads)], axis=1
        ).astype(BF)


def rms_back(grad, x, gain):
    inverse = inverse_rms(x)
    unit = x * inverse
    scaled = grad * gain
    inner = jnp.mean(scaled * unit, axis=1, keepdims=True)
    return inverse * (scaled - unit * inner), jnp.sum(grad * unit, axis=0, keepdims=True)


def back_rows(acc_ref, x_ref, gain_ref, gain_part_ref, part_ref):
    chunk = 128

    @pl.loop(0, x_ref.shape[0] // chunk)
    def _(i):
        span = pl.ds(i * chunk, chunk)
        part, piece = rms_back(acc_ref[span, :], x_ref[span, :].astype(F32), gain_ref[...])
        part_ref[span, :] = part.astype(part_ref.dtype)
        gain_part_ref[...] += jnp.broadcast_to(piece, gain_part_ref.shape)


def ffn_kernel(
    x_own,
    x_other,
    cot_own,
    cot_other,
    gain_ref,
    wg_ref,
    wu_ref,
    wd_ref,
    grads_ref,
    normed_ref,
    part_ref,
    gain_part_ref,
    got_hbm,
    cot_ref,
    acc_ref,
    part_send,
    part_sems,
):
    h, j = pl.program_id(0), pl.program_id(1)
    chunk = 256
    across = (lax.axis_index("dp"), 1 - lax.axis_index("tensor"))
    quarter = part_send.shape[0] // QUARTERS

    def part_copy(r):
        span = pl.ds(r * quarter, quarter)
        return remote(part_send.at[span], got_hbm.at[span], part_sems.at[r], across)

    @pl.when((h == 0) & (j == 0))
    def _():
        arrived = pltpu.get_barrier_semaphore()
        pl.semaphore_signal(arrived, inc=1, device_id=across, device_id_type=MESH)
        pl.semaphore_wait(arrived, 1)
        gain_part_ref[...] = jnp.zeros_like(gain_part_ref)

    for turn_at, (x_ref, c_ref) in enumerate(((x_other, cot_other), (x_own, cot_own))):

        @pl.when((h == turn_at) & (j == 0))
        def _():
            norm_rows(x_ref, gain_ref, normed_ref)
            cot_ref[...] = c_ref[...]

    @pl.when(j == 0)
    def _():
        acc_ref[...] = jnp.zeros_like(acc_ref)

    for r in range(0, cot_ref.shape[0], chunk):
        span = slice(r, r + chunk)
        gate = nn(normed_ref[span, :], wg_ref[...])
        up = nn(normed_ref[span, :], wu_ref[...])
        grad_hidden = nn(cot_ref[span, :], wd_ref[...])
        sig = jax.nn.sigmoid(gate)
        silu = gate * sig
        grads_ref[2, span, :] = (silu * up).astype(BF)
        grad_gate = (grad_hidden * up * (sig + silu * (1.0 - sig))).astype(BF)
        grad_up = (grad_hidden * silu).astype(BF)
        grads_ref[0, span, :] = grad_gate
        grads_ref[1, span, :] = grad_up
        acc_ref[span, :] += nt(grad_gate, wg_ref[...]) + nt(grad_up, wu_ref[...])

    for turn_at, x_ref in enumerate((x_other, x_own)):

        @pl.when((h == turn_at) & (j == pl.num_programs(1) - 1))
        def _():
            back_rows(acc_ref, x_ref, gain_ref, gain_part_ref, part_ref)
            if turn_at == 0:
                part_send[...] = part_ref[...]
                for r in range(EARLY):
                    part_copy(r).start()
            else:
                for r in range(EARLY):
                    part_copy(r).wait()


def resident(shape):
    zeros = (0,) * len(shape)
    return pl.BlockSpec(shape, lambda *grid: zeros, pipeline_mode=pl.Buffered(1))


def ffn(xs, cots, gain, w, hidden_width, cols=512):
    rows, d = xs[0].shape
    steps = hidden_width // cols
    per_half = lambda h, j: (1 - h, 0, 0)
    return pl.pallas_call(
        ffn_kernel,
        grid=(2, steps),
        in_specs=[resident((rows, d))] * 4
        + [
            resident((1, d)),
            pl.BlockSpec((d, cols), lambda h, j: (0, j)),
            pl.BlockSpec((d, cols), lambda h, j: (0, steps + j)),
            pl.BlockSpec((d, cols), lambda h, j: (0, 2 * steps + j)),
        ],
        out_specs=[
            pl.BlockSpec((None, 3, rows, cols), lambda h, j: (1 - h, 0, 0, j)),
            pl.BlockSpec((None, rows, d), per_half),
            pl.BlockSpec((None, rows, d), per_half),
            pl.BlockSpec((8, d), lambda h, j: (0, 0)),
            pl.BlockSpec(memory_space=pl.ANY),
        ],
        out_shape=[
            jax.ShapeDtypeStruct((2, 3, rows, hidden_width), BF),
            jax.ShapeDtypeStruct((2, rows, d), BF),
            jax.ShapeDtypeStruct((2, rows, d), BF),
            jax.ShapeDtypeStruct((8, d), F32),
            jax.ShapeDtypeStruct((rows, d), BF),
        ],
        scratch_shapes=[
            pltpu.VMEM((rows, d), BF),
            pltpu.VMEM((rows, d), F32),
            pltpu.VMEM((rows, d), BF),
            pltpu.SemaphoreType.DMA((EARLY, 2)),
        ],
        compiler_params=remote_settings(3, axes=2),
        cost_estimate=cost(
            20 * rows * d * hidden_width,
            12 * d * hidden_width + 16 * rows * d + 12 * rows * hidden_width,
            2 * rows * hidden_width,
        ),
        name="ffn",
    )(*xs, *cots, gain, w, w, w)


MESH = pl.DeviceIdType.MESH
QUARTERS = 4
EARLY = 3
UP_SENT = 7
GAIN_ROWS = 16


class Scatter:
    def __init__(self, devices, rows, count):
        self.devices, self.rows, self.count = devices, rows, count
        self.stages = devices.bit_length() - 1
        self.lags = [1] + [3] * (self.stages - 1)
        self.slots = [2 * lag for lag in self.lags]
        if self.stages >= 3:
            self.slots[1] = self.slots[2] = 8
        self.starts = [sum(self.lags[:s]) for s in range(self.stages + 1)]
        self.steps = count + self.starts[-1]

    def scratch(self):
        shapes = []
        for s in range(self.stages):
            slots, left = self.slots[s], self.devices >> (s + 1)
            shapes.append(pltpu.VMEM((slots, 2, left, self.rows, COLS), BF))
            shapes.append(pltpu.VMEM((slots, left, self.rows, COLS), BF))
            shapes.append(pltpu.SemaphoreType.DMA((slots,)))
            shapes.append(pltpu.SemaphoreType.DMA((slots,)))
        return shapes

    def bind(self, refs):
        self.held, self.got = refs[0::4], refs[1::4]
        self.sent_sem, self.got_sem = refs[2::4], refs[3::4]
        self.me, self.side = lax.axis_index("dp"), lax.axis_index("tensor")

    def late(self, block):
        return (block % 4) // 3

    def own_bit(self, b):
        return (self.me // (1 << b)) % 2

    def partner(self, b):
        return self.me + (1 - 2 * self.own_bit(b)) * (1 << b)

    def turned(self, s, block):
        if s not in (1, 2) or self.stages < 3:
            return self.own_bit(s), self.partner(s)
        late = self.late(block)
        return (
            self.own_bit(s) * (1 - late) + self.own_bit(3 - s) * late,
            self.partner(s) * (1 - late) + self.partner(3 - s) * late,
        )

    def barrier(self):
        arrived = pltpu.get_barrier_semaphore()
        for b in range(self.stages):
            pl.semaphore_signal(
                arrived, inc=1, device_id=(self.partner(b), self.side), device_id_type=MESH
            )
        pl.semaphore_signal(
            arrived, inc=1, device_id=(self.me, 1 - self.side), device_id_type=MESH
        )
        pl.semaphore_wait(arrived, self.stages + 1)

    def copy(self, s, block, gain=False):
        slot = block % self.slots[s]
        bit, partner = self.turned(s, block)
        src, dst = self.held[s].at[slot, 1 - bit], self.got[s].at[slot]
        if gain:
            src, dst = src.at[:, pl.ds(0, GAIN_ROWS)], dst.at[:, pl.ds(0, GAIN_ROWS)]
        sems = self.sent_sem[s].at[slot], self.got_sem[s].at[slot]
        return pltpu.make_async_remote_copy(
            src_ref=src,
            dst_ref=dst,
            send_sem=sems[0],
            recv_sem=sems[1],
            device_id=(partner, self.side),
            device_id_type=MESH,
        )

    def advance(self, step, emit):
        for s in range(self.stages, 0, -1):
            block = step - self.starts[s]
            last = self.count - 1
            for gain in (False, True):

                @pl.when((block == last) if gain else (block >= 0) & (block < last))
                def _():
                    self.receive(s, block, gain, emit)

    def receive(self, s, block, gain, emit):
        slot = block % self.slots[s - 1]
        self.copy(s - 1, block, gain).wait()
        keep, _ = self.turned(s - 1, block)
        held, got = self.held[s - 1], self.got[s - 1]
        rows = slice(0, GAIN_ROWS if gain else self.rows)
        if s == self.stages:
            total = held[slot, keep, 0, rows].astype(F32) + got[slot, 0, rows].astype(F32)
            emit(block, total, gain)
            return
        later = block % self.slots[s]
        late = self.late(block)

        def add(k, carry):
            total = held[slot, keep, k, rows] + got[slot, k, rows]
            bit, rest = k % 2, k // 2
            if s == 1 and self.stages >= 3:
                bit = bit * (1 - late) + (k // 2) % 2 * late
                rest = rest * (1 - late) + (k // 4 * 2 + k % 2) * late
            self.held[s][later, bit, rest, rows] = total
            return carry

        lax.fori_loop(0, self.devices >> s, add, 0)
        self.copy(s, block, gain).start()

    def multiply(self, block, turned_ref, rights):
        slot = block % self.slots[0]
        pieces = 4
        size = self.devices // pieces

        def piece(i, carry):
            span = pl.ds(i * size * self.rows, size * self.rows)
            total, start = None, 0
            for right in rights:
                part = nn(turned_ref[span, start : start + right.shape[0]], right[...])
                total = part if total is None else total + part
                start += right.shape[0]
            for r in range(size):
                block_rows = total[r * self.rows : (r + 1) * self.rows].astype(BF)
                self.held[0][slot, r % 2, i * (size // 2) + r // 2] = block_rows
            return carry

        lax.fori_loop(0, pieces, piece, 0)
        self.copy(0, block).start()

    def enter(self, block, ref):
        slot = block % self.slots[0]
        pieces = 4
        size = self.devices // pieces

        def piece(i, carry):
            rows = ref[pl.ds(i * size * self.rows, size * self.rows), :]
            for r in range(size):
                self.held[0][slot, r % 2, i * (size // 2) + r // 2] = rows[
                    r * self.rows : (r + 1) * self.rows
                ]
            return carry

        lax.fori_loop(0, pieces, piece, 0)
        self.copy(0, block).start()

    def put_gain(self, block, row):
        slot = block % self.slots[0]
        empty = jnp.zeros((1, COLS - self.rows), F32)
        for k in range(self.devices):
            piece = jnp.concatenate([row[:, k * self.rows : (k + 1) * self.rows], empty], axis=1)
            piece = jnp.broadcast_to(piece, (GAIN_ROWS, COLS)).astype(BF)
            self.held[0][slot, k % 2, k // 2, :GAIN_ROWS] = piece
        self.copy(0, block, True).start()


def turn_piece(turned_ref, left, start, row):
    cols = pl.ds(pl.multiple_of(start + row, 256), 256)

    @pl.loop(0, left.shape[1] // 256)
    def _(i):
        span = pl.ds(pl.multiple_of(i * 256, 256), 256)
        turned_ref[span, cols] = left[row : row + 256, span].T


def turn_kernel(first_ref, second_ref, out_ref):
    start = 0
    for left in (first_ref, second_ref):
        for row in range(0, left.shape[0], 256):
            turn_piece(out_ref, left, start, row)
        start += left.shape[0]


def turn_pair(first, second):
    rows, d = first.shape
    return pl.pallas_call(
        turn_kernel,
        out_shape=jax.ShapeDtypeStruct((d, 2 * rows), first.dtype),
        compiler_params=pltpu.CompilerParams(vmem_limit_bytes=32 * 1024 * 1024),
        cost_estimate=cost(0, 8 * rows * d),
        name="turn_pair",
    )(first, second)


def emit_into(outs, counts, block, value, gain):
    if gain:
        outs[-1][...] = value
        return
    first = 0
    for out, count in zip(outs, counts):

        @pl.when((block >= first) & (block < first + count))
        def _():
            out[...] = value

        first += count


def emit_specs(scatter, counts):
    first = scatter.starts[-1]
    specs, shapes = [], []
    for count in counts:

        def where(j, first=first, most=count - 1):
            return (0, jnp.clip(j - first, 0, most))

        specs.append(pl.BlockSpec((scatter.rows, COLS), where))
        shapes.append(jax.ShapeDtypeStruct((scatter.rows, count * COLS), F32))
        first += count
    specs.append(pl.BlockSpec((GAIN_ROWS, COLS), lambda j: (0, 0)))
    shapes.append(jax.ShapeDtypeStruct((GAIN_ROWS, COLS), F32))
    return specs, shapes


def remote(src, dst, sems, device):
    return pltpu.make_async_remote_copy(
        src_ref=src,
        dst_ref=dst,
        send_sem=sems.at[0],
        recv_sem=sems.at[1],
        device_id=device,
        device_id_type=MESH,
    )


def ffn_scatter_kernel(scatter, per, sent, unsent, *refs):
    (
        cot_turned, norm_own, norm_other, right_own, right_other, whole_own, whole_other,
        cot_hbm, middle_hbm, parts_hbm, got_hbm, gain_ref, wd_ref, wo_ref,
    ) = refs[:14]
    outs = refs[14:17]
    whole_ref, gm_ref, grad_attended, block_out_ref, gm_turned = refs[17:22]
    (
        norm_turned, cot_own, middle_own, part_own, got_part, gm_own, gm_got, gain_got, acc_own,
        acc_other, block_send, block_got, gain_sems, part_sems, gm_sems, block_sems, local_sems,
    ) = refs[22:39]
    scatter.bind(refs[39:])
    step = pl.program_id(0)
    side = scatter.side
    across = (scatter.me, 1 - side)
    half = part_own.shape[0]
    quarter = half // QUARTERS
    row_chunk = 128
    early = pl.ds(0, EARLY * quarter)
    rest = pl.ds(EARLY * quarter, half - EARLY * quarter)

    def part_copy():
        return remote(parts_hbm.at[1, rest], got_part.at[rest], part_sems, across)

    def gm_copy(r):
        span = pl.ds(r * quarter, quarter)
        return remote(gm_own.at[span], gm_got.at[span], gm_sems.at[r], across)

    def block_copy():
        return remote(block_send, block_got, block_sems, across)

    def gain_copy():
        return remote(gain_ref, gain_got, gain_sems, across)

    loads = [
        pltpu.make_async_copy(cot_hbm, cot_own, local_sems.at[0]),
        pltpu.make_async_copy(parts_hbm.at[0], part_own, local_sems.at[1]),
        pltpu.make_async_copy(middle_hbm, middle_own, local_sems.at[2]),
        pltpu.make_async_copy(got_hbm.at[early], got_part.at[early], local_sems.at[3]),
    ]

    keeps = [
        pltpu.make_async_copy(gm_own, gm_ref.at[side], local_sems.at[4]),
        pltpu.make_async_copy(gm_got, gm_ref.at[1 - side], local_sems.at[5]),
    ]

    @pl.when(step == 0)
    def _():
        for load in loads:
            load.start()
        scatter.barrier()
        part_copy().start()
        gain_copy().start()

    scatter.advance(step, functools.partial(emit_into, outs, (per, sent - per)))

    @pl.when(step < per)
    def _():
        scatter.multiply(step, cot_turned, (right_own, right_other))

        @pl.when(step == 0)
        def _():
            acc_own[...] = jnp.zeros_like(acc_own)
            acc_other[...] = jnp.zeros_like(acc_other)

        @pl.loop(0, half // 256)
        def _(i):
            span = pl.ds(i * 256, 256)
            acc_own[span, :] += nt(right_own[span, :], wd_ref[...])
            acc_other[span, :] += nt(right_other[span, :], wd_ref[...])

    @pl.when(step == per)
    def _():
        @pl.loop(0, half // row_chunk)
        def _(i):
            span = pl.ds(i * row_chunk, row_chunk)
            block_send[span, :] = acc_other[span, :].astype(BF)

        block_copy().start()

    pieces = [(norm_own, 0, r) for r in range(0, half, 256)]
    pieces += [(norm_other, half, r) for r in range(0, half, 256)]
    for nth, (left, start, row) in enumerate(pieces):

        @pl.when(step == per - len(pieces) + nth)
        def _():
            turn_piece(norm_turned, left, start, row)

    @pl.when((step >= per) & (step < sent))
    def _():
        scatter.multiply(step, norm_turned, (right_own, right_other))

    @pl.when(step == sent)
    def _():
        gain_copy().wait()
        scatter.put_gain(step, gain_ref[0:1, :] + gain_got[0:1, :])

    @pl.when((step >= per) & (step < per + unsent))
    def _():
        rows = whole_ref.shape[0] // 4

        @pl.loop(0, 4)
        def _(i):
            span = pl.ds(i * rows, rows)
            total = nn(norm_turned[span, :half], whole_own[...])
            whole_ref[span, :] = (total + nn(norm_turned[span, half:], whole_other[...])).astype(BF)

    for r in range(QUARTERS):

        @pl.when(step == 1 + r + (1 if r >= EARLY else 0))
        def _():
            if r == 0:
                for load in loads:
                    load.wait()
            if r == EARLY:
                part_copy().wait()

            @pl.loop(r * quarter // row_chunk, (r + 1) * quarter // row_chunk)
            def _(i):
                span = pl.ds(i * row_chunk, row_chunk)
                total = cot_own[span, :].astype(F32) + part_own[span, :].astype(F32)
                gm_own[span, :] = (total + got_part[span, :].astype(F32)).astype(BF)

            gm_copy(r).start()

    @pl.when(step == sent + 1)
    def _():
        for r in range(QUARTERS):
            gm_copy(r).wait()
        for keep in keeps:
            keep.start()

    width = grad_attended.shape[2]
    for nth in range(width // COLS):

        @pl.when(step == sent + 2 + nth)
        def _():
            cols = slice(nth * COLS, (nth + 1) * COLS)
            grad_attended[side, :, cols] = nn(gm_own[...], wo_ref[...]).astype(BF)
            grad_attended[1 - side, :, cols] = nn(gm_got[...], wo_ref[...]).astype(BF)

    pieces = [(gm_own, side, r) for r in range(0, half, 256)]
    pieces += [(gm_got, 1 - side, r) for r in range(0, half, 256)]
    for nth, (left, at, row) in enumerate(pieces):

        @pl.when(step == sent + 2 + width // COLS + nth)
        def _():
            turn_piece(gm_turned, left, at * half, row)

    @pl.when(step == scatter.steps - 1)
    def _():
        block_copy().wait()

        @pl.loop(0, half // row_chunk)
        def _(i):
            span = pl.ds(i * row_chunk, row_chunk)
            total = middle_own[span, :].astype(F32) + acc_own[span, :]
            block_out_ref[span, :] = (total + block_got[span, :].astype(F32)).astype(BF)

        for keep in keeps:
            keep.wait()


def remote_settings(identity, mib=60, axes=1):
    return pltpu.CompilerParams(
        dimension_semantics=("arbitrary",) * axes,
        vmem_limit_bytes=mib * 1024 * 1024,
        collective_id=identity,
        has_side_effects=True,
    )


def ffn_scatter(
    devices, cot_turned, normed, grads, cot, middle, parts, got, gain_part, w, w_attention, heads
):
    half, d = middle.shape
    width = grads.shape[3]
    per = width // COLS
    up_sent = per * UP_SENT // 8
    sent = per + up_sent
    left = 2 * per - up_sent
    head_blocks = heads // COLS
    scatter = Scatter(devices, d // devices, sent + 1)
    assert scatter.rows * devices == d and per >= 2 * half // 256 and per > QUARTERS + 1
    assert scatter.steps >= max(per + left, sent + 2 + head_blocks + 2 * half // 256)
    assert COLS >= scatter.rows >= GAIN_ROWS

    def right(side):
        def where(j):
            c = jnp.minimum(j, sent - 1)
            return (side, 2 - c // per, 0, c % per)

        return pl.BlockSpec((None, None, half, COLS), where)

    def whole_block(j):
        return jnp.clip(j - per, 0, left - 1)

    def left_whole(side):
        def where(j):
            c = whole_block(j)
            kind = c // per
            return (side, kind, 0, (c + kind * up_sent) % per)

        return pl.BlockSpec((None, None, half, COLS), where)

    def rows_of(side):
        return pl.BlockSpec(
            (None, half, d), lambda j: (side, 0, 0), pipeline_mode=pl.Buffered(1)
        )

    specs, shapes = emit_specs(scatter, (per, sent - per))
    left_there = pl.BlockSpec(memory_space=pl.ANY)
    return pl.pallas_call(
        functools.partial(ffn_scatter_kernel, scatter, per, sent, left),
        grid=(scatter.steps,),
        in_specs=[
            resident((d, 2 * half)),
            rows_of(0),
            rows_of(1),
            right(0),
            right(1),
            left_whole(0),
            left_whole(1),
            left_there,
            left_there,
            left_there,
            left_there,
            resident((8, d)),
            pl.BlockSpec((d, COLS), lambda j: (0, 2 * per + jnp.minimum(j, per - 1))),
            pl.BlockSpec(
                (d, COLS),
                lambda j: (0, 3 * head_blocks + jnp.clip(j - sent - 2, 0, head_blocks - 1)),
            ),
        ],
        out_specs=specs
        + [
            pl.BlockSpec((d, COLS), lambda j: (0, whole_block(j))),
            left_there,
            resident((2, half, heads)),
            resident((half, d)),
            resident((d, 2 * half)),
        ],
        out_shape=shapes
        + [
            jax.ShapeDtypeStruct((d, left * COLS), BF),
            jax.ShapeDtypeStruct((2, half, d), BF),
            jax.ShapeDtypeStruct((2, half, heads), BF),
            jax.ShapeDtypeStruct((half, d), BF),
            jax.ShapeDtypeStruct((d, 2 * half), BF),
        ],
        scratch_shapes=[
            pltpu.VMEM((d, 2 * half), BF),
            pltpu.VMEM((half, d), BF),
            pltpu.VMEM((half, d), BF),
            pltpu.VMEM((half, d), BF),
            pltpu.VMEM((half, d), BF),
            pltpu.VMEM((half, d), BF),
            pltpu.VMEM((half, d), BF),
            pltpu.VMEM((8, d), F32),
            pltpu.VMEM((half, d), F32),
            pltpu.VMEM((half, d), F32),
            pltpu.VMEM((half, d), BF),
            pltpu.VMEM((half, d), BF),
            pltpu.SemaphoreType.DMA((2,)),
            pltpu.SemaphoreType.DMA((2,)),
            pltpu.SemaphoreType.DMA((QUARTERS, 2)),
            pltpu.SemaphoreType.DMA((2,)),
            pltpu.SemaphoreType.DMA((6,)),
        ]
        + scatter.scratch(),
        compiler_params=remote_settings(0),
        cost_estimate=cost(16 * half * d * per * COLS, 20 * half * d),
        name="ffn_scatter",
    )(
        cot_turned, normed, normed, grads, grads, grads, grads, cot, middle, parts, got,
        gain_part, w, w_attention,
    )


def attention_scatter_kernel(scatter, per, early, block, seg_rows, *refs):
    (
        norm_turned, gm_turned, gain_ref, q_ref, k_ref, v_ref, o_ref, do_ref, lse_ref, bias_ref,
        cos_ref, sin_ref, attended_ref, w_ref, whole_ref, gm_hbm, x_hbm,
    ) = refs[:17]
    outs, token_grad_ref = refs[17 : 22 + len(early)], refs[22 + len(early)]
    refs = refs[23 + len(early) :]
    (
        grads_ref, dk_ref, dv_ref, gm_own, x_ref, acc_ref, part_send, part_got, gain_part,
        part_sems, local_sems,
    ) = refs[:11]
    scatter.bind(refs[11:])
    step = pl.program_id(0)
    side = scatter.side
    across = (scatter.me, 1 - side)
    length = x_ref.shape[0]
    half = length // 2
    quarter = half // QUARTERS
    chunk = 128
    groups = grads_ref.shape[2] // LANES
    own, other = side * half, (1 - side) * half
    before = sum(early)
    turns = 2 * groups

    def part_copy(r):
        span = pl.ds(r * quarter, quarter)
        return remote(part_send.at[span], part_got.at[span], part_sems.at[r], across)

    loads = [
        pltpu.make_async_copy(x_hbm, x_ref, local_sems.at[0]),
        pltpu.make_async_copy(gm_hbm.at[side], gm_own, local_sems.at[1]),
    ]

    def back(row):
        span = pl.ds(row, chunk)
        part, piece = rms_back(acc_ref[span, :], x_ref[span, :].astype(F32), gain_ref[...])
        gain_part[...] += jnp.broadcast_to(piece, gain_part.shape)
        return part

    def emit(column, value, gain):
        if gain:
            outs[4][...] = value
            return
        first = 0
        for out, count in zip(outs[5:], early):

            @pl.when((column >= first) & (column < first + count))
            def _():
                out[...] = value

            first += count

        @pl.when((column >= before) & (column < before + per))
        def _():
            outs[3][...] = value

        for kind in range(3):

            @pl.when((column >= before + per) & ((column - before - per) % 3 == kind))
            def _():
                outs[kind][...] = value

    @pl.when(step == 0)
    def _():
        for load in loads:
            load.start()
        scatter.barrier()

    scatter.advance(step, emit)

    @pl.when(step < before)
    def _():
        scatter.enter(step, whole_ref)

    @pl.when((step >= before) & (step < before + per))
    def _():
        scatter.multiply(step, gm_turned, (attended_ref,))

    @pl.when((step >= before + per) & (step < before + 4 * per))
    def _():
        column = step - before - per
        cols = pl.ds(pl.multiple_of(column // 3 * COLS, COLS), COLS)
        scatter.multiply(step, norm_turned, (grads_ref.at[column % 3, :, cols],))

    count = length // block
    split = count - count // 4
    for odd in range(2):

        @pl.when((step < turns) & (step % 2 == odd))
        def _():
            lanes = pl.ds(pl.multiple_of(step // 2 * LANES, LANES), LANES)
            blocks = range(split, count) if odd else range(split)
            attend_back_pair(
                blocks, odd == 1, block, seg_rows, lanes, q_ref, k_ref, v_ref, o_ref, do_ref,
                lse_ref, bias_ref, cos_ref, sin_ref, grads_ref, dk_ref, dv_ref,
            )

    @pl.when(step == 1)
    def _():
        for load in loads:
            load.wait()
        acc_ref[...] = jnp.zeros_like(acc_ref)
        gain_part[...] = jnp.zeros_like(gain_part)

    @pl.when((step >= turns) & (step < turns + 3))
    def _():
        kind = step - turns

        @pl.loop(0, length // 256)
        def _(i):
            span = pl.ds(i * 256, 256)
            acc_ref[span, :] += nt(grads_ref[kind, span, :], w_ref[...])

    for r in range(QUARTERS):

        @pl.when(step == turns + 3 + r // 2)
        def _():
            @pl.loop(r * quarter // chunk, (r + 1) * quarter // chunk)
            def _(i):
                part_send[pl.ds(i * chunk, chunk), :] = back(other + i * chunk).astype(BF)

            part_copy(r).start()

        @pl.when(step == turns + 5 + r // 2)
        def _():
            @pl.loop(r * quarter // chunk, (r + 1) * quarter // chunk)
            def _(i):
                span = pl.ds(own + i * chunk, chunk)
                kept = gm_own[pl.ds(i * chunk, chunk), :].astype(F32)
                acc_ref[span, :] = back(own + i * chunk) + kept

    @pl.when(step == before + 4 * per)
    def _():
        scatter.put_gain(step, gain_part[0:1, :])

    for r in range(QUARTERS):

        @pl.when(step == scatter.steps - QUARTERS + r)
        def _():
            part_copy(r).wait()

            @pl.loop(r * quarter // chunk, (r + 1) * quarter // chunk)
            def _(i):
                span = pl.ds(i * chunk, chunk)
                total = acc_ref[pl.ds(own + i * chunk, chunk), :]
                token_grad_ref[span, :] = (total + part_got[span, :].astype(F32)).astype(BF)


def attention_scatter(
    devices, norm_turned, gm_turned, gm, x, gain, qkv, attended, grad_attended, lse, bias, cosine,
    sine, w, whole, early, seg_rows,
):
    length, width = attended.shape
    half, d = gm.shape[1:]
    per = width // COLS
    groups = width // LANES
    heads = LANES // HD
    before = sum(early)
    scatter = Scatter(devices, d // devices, before + 4 * per + 1)
    lead = scatter.starts[-1]
    assert groups == 2 * per and 2 * groups + 7 <= before + 4 * per and lead > QUARTERS
    assert scatter.rows * devices == d and whole.shape[1] == before * COLS

    def group(j):
        return jnp.minimum(j // 2, groups - 1)

    def lanes_of(kind):
        return pl.BlockSpec((length, LANES), lambda j: (0, kind * groups + group(j)))

    specs, shapes = [], []
    for kind in range(4):
        first = lead + before + (per + kind if kind < 3 else 0)
        stride = 3 if kind < 3 else 1

        def where(j, first=first, stride=stride):
            return (0, jnp.clip(jnp.maximum(j - first, 0) // stride, 0, per - 1))

        specs.append(pl.BlockSpec((scatter.rows, COLS), where))
        shapes.append(jax.ShapeDtypeStruct((scatter.rows, width), F32))
    more_specs, more_shapes = emit_specs(scatter, early)
    specs += more_specs[-1:] + more_specs[:-1]
    shapes += more_shapes[-1:] + more_shapes[:-1]
    left_there = pl.BlockSpec(memory_space=pl.ANY)
    return pl.pallas_call(
        functools.partial(attention_scatter_kernel, scatter, per, early, 2 * seg_rows, seg_rows),
        grid=(scatter.steps,),
        in_specs=[
            resident((d, length)),
            resident((d, length)),
            resident((1, d)),
            lanes_of(0),
            lanes_of(1),
            lanes_of(2),
            lanes_of(0),
            lanes_of(0),
            pl.BlockSpec((1, heads, length), lambda j: (group(j), 0, 0)),
            resident(bias.shape),
            resident((length, LANES)),
            resident((length, LANES)),
            pl.BlockSpec((length, COLS), lambda j: (0, jnp.clip(j - before, 0, per - 1))),
            pl.BlockSpec((d, width), lambda j: (0, jnp.clip(j - 2 * groups, 0, 2))),
            pl.BlockSpec((d, COLS), lambda j: (0, jnp.minimum(j, before - 1))),
            left_there,
            left_there,
        ],
        out_specs=specs + [resident((half, d))],
        out_shape=shapes + [jax.ShapeDtypeStruct((half, d), BF)],
        scratch_shapes=[
            pltpu.VMEM((3, length, width), BF),
            pltpu.VMEM((heads, length, HD), F32),
            pltpu.VMEM((heads, length, HD), F32),
            pltpu.VMEM((half, d), BF),
            pltpu.VMEM((length, d), BF),
            pltpu.VMEM((length, d), F32),
            pltpu.VMEM((half, d), BF),
            pltpu.VMEM((half, d), BF),
            pltpu.VMEM((8, d), F32),
            pltpu.SemaphoreType.DMA((QUARTERS, 2)),
            pltpu.SemaphoreType.DMA((2,)),
        ]
        + scatter.scratch(),
        compiler_params=remote_settings(1),
        cost_estimate=cost(
            14 * length * d * width + 20 * length * length * width,
            20 * length * d,
            length * length * width // HD,
        ),
        name="attention_scatter",
    )(
        norm_turned, gm_turned, gain, qkv, qkv, qkv, attended, grad_attended, lse, bias, cosine,
        sine, attended, w, whole, gm, x,
    )


class Gather:
    def __init__(self, devices, rows, count):
        self.devices, self.rows, self.count = devices, rows, count
        self.stages = devices.bit_length() - 1
        self.lags = [2] + [3] * (self.stages - 2) + [1]
        self.starts = [sum(self.lags[:t]) for t in range(self.stages + 1)]
        self.steps = count + self.starts[-1]

    def scratch(self):
        return [
            pltpu.VMEM((self.count, self.devices, self.rows, COLS), BF),
            pltpu.SemaphoreType.DMA((self.stages, self.count, 2)),
            pltpu.SemaphoreType.DMA((self.count,)),
        ]

    def bind(self, refs):
        self.held, self.sems, self.load_sems = refs
        self.me, self.side = lax.axis_index("dp"), lax.axis_index("tensor")

    def late(self, block):
        return (block % 4) // 3 if self.stages >= 4 else 0 * block

    def place(self, device, block):
        late = self.late(block)
        total = 0
        for t in range(self.stages):
            bit = (device // (1 << (self.stages - 1 - t))) % 2
            if t in (1, 2) and self.stages >= 4:
                total = total + bit * ((1 << t) * (1 - late) + (1 << (3 - t)) * late)
            else:
                total = total + bit * (1 << t)
        return total

    def partner_at(self, t):
        weight = 1 << (self.stages - 1 - t)
        return self.me + (1 - 2 * ((self.me // weight) % 2)) * weight

    def partner(self, t, block):
        if t not in (1, 2) or self.stages < 4:
            return self.partner_at(t)
        late = self.late(block)
        return self.partner_at(t) * (1 - late) + self.partner_at(3 - t) * late

    def barrier(self):
        arrived = pltpu.get_barrier_semaphore()
        for t in range(self.stages):
            pl.semaphore_signal(
                arrived, inc=1, device_id=(self.partner_at(t), self.side), device_id_type=MESH
            )
        pl.semaphore_signal(
            arrived, inc=1, device_id=(self.me, 1 - self.side), device_id_type=MESH
        )
        pl.semaphore_wait(arrived, self.stages + 1)

    def load(self, shard, column, block):
        return pltpu.make_async_copy(
            shard.at[:, pl.ds(column, COLS)],
            self.held.at[block, self.place(self.me, block)],
            self.load_sems.at[block],
        )

    def load_all(self, shards):
        block = 0
        for shard in shards:
            for column in range(0, shard.shape[1], COLS):
                self.load(shard, column, jnp.int32(block)).start()
                block += 1

    def copy(self, t, block):
        size = 1 << t
        first = self.place(self.me, block) // size * size
        run = self.held.at[block, pl.ds(first, size)]
        return remote(run, run, self.sems.at[t, block], (self.partner(t, block), self.side))

    def advance(self, step, shards):
        for t in range(self.stages, -1, -1):
            block = step - self.starts[t]

            @pl.when((block >= 0) & (block < self.count))
            def _():
                if t > 0:
                    self.copy(t - 1, block).wait()
                else:
                    self.load(shards[0], 0, block).wait()
                if t < self.stages:
                    self.copy(t, block).start()


def gather_project_kernel(gather, per, *refs):
    shards, (tokens, cot, gain_ref, depths_ref), later = refs[:4], refs[4:8], refs[8:11]
    w_hbm, qkv_ref, turned_ref, rows_hbm, cot_other, cot_rest, cos_ref, sin_ref, joined = refs[11:20]
    w_ref, rows_ref, normed_ref, x_sems, row_sems, w_sems, join_sems = refs[20:27]
    gather.bind(refs[27:])
    step = pl.program_id(0)
    side = gather.side
    across = (gather.me, 1 - side)
    lead = gather.starts[-1]
    others = lead + gather.count // 2 - 1
    kinds = 3 * per

    def token_copy():
        return remote(tokens, rows_ref.at[side], x_sems.at[0], across)

    def cot_copy():
        rows = pl.ds(0, cot_other.shape[0])
        return remote(cot.at[rows], cot_other, x_sems.at[1], across)

    def token_load():
        return pltpu.make_async_copy(tokens, rows_ref.at[side], row_sems.at[0])

    def rows_store():
        return pltpu.make_async_copy(rows_ref, rows_hbm, row_sems.at[1])

    def w_store(block):
        cols = pl.ds(pl.multiple_of(block * COLS, COLS), COLS)
        return pltpu.make_async_copy(w_ref.at[:, cols], w_hbm.at[:, cols], w_sems.at[block])

    def joins():
        column = 0
        for nth, shard in enumerate(later):
            span = pl.ds(column, shard.shape[1])
            yield pltpu.make_async_copy(shard, joined.at[:, span], join_sems.at[nth])
            column += shard.shape[1]
        rows = pl.ds(cot_other.shape[0], cot_rest.shape[0])
        yield pltpu.make_async_copy(cot.at[rows], cot_rest, join_sems.at[len(later)])

    @pl.when(step == 1)
    def _():
        for join in joins():
            join.start()

    @pl.when(step == 0)
    def _():
        token_load().start()
        gather.load_all(shards)
        gather.barrier()
        token_copy().start()
        cot_copy().start()

    gather.advance(step, shards)

    @pl.when(step == 1)
    def _():
        token_load().wait()
        norm_rows(rows_ref.at[side], gain_ref, normed_ref.at[side])
        turn_tables(depths_ref, cos_ref, sin_ref)

    for nth, row in enumerate(range(0, rows_ref.shape[1], 256)):

        @pl.when(step == 2 + nth)
        def _():
            turn_piece(turned_ref, normed_ref.at[side], side * rows_ref.shape[1], row)

        @pl.when(step == others + 1 + nth)
        def _():
            turn_piece(turned_ref, normed_ref.at[1 - side], (1 - side) * rows_ref.shape[1], row)

    @pl.when(step == others)
    def _():
        token_copy().wait()
        rows_store().start()
        norm_rows(rows_ref.at[1 - side], gain_ref, normed_ref.at[1 - side])

    @pl.when(step >= lead)
    def _():
        block = step - lead
        cols = pl.ds(pl.multiple_of(block * COLS, COLS), COLS)
        for device in range(gather.devices):
            rows = slice(device * gather.rows, (device + 1) * gather.rows)
            w_ref[rows, cols] = gather.held[block, gather.place(device, block)]
        w_store(block).start()

    @pl.loop(0, 3)
    def _(task):
        mine = jnp.where(task == 0, 1, 0)
        half = side * mine + (1 - side) * (1 - mine)
        block = (step - lead) * mine + (2 * (step - others) + task - 1) * (1 - mine)
        cols = pl.ds(pl.multiple_of(block * COLS, COLS), COLS)
        chunk = 256

        @pl.when((block >= 0) & (block < 2 * per))
        def _():
            scale = jnp.where(block < per, 1.0 / math.sqrt(HD), 1.0).astype(BF)
            for r in range(0, qkv_ref.shape[1], chunk):
                span = slice(r, r + chunk)
                pre = nn(normed_ref[half, span, :], w_ref[:, cols])
                cosine = jnp.concatenate([cos_ref[half, span, :]] * (COLS // LANES), axis=1)
                sine = jnp.concatenate([sin_ref[half, span, :]] * (COLS // LANES), axis=1)
                turned = turn(pre, cosine, sine)
                qkv_ref[half, span, cols] = turned.astype(BF) * scale

        @pl.when((block >= 2 * per) & (block < kinds))
        def _():
            for r in range(0, qkv_ref.shape[1], chunk):
                span = slice(r, r + chunk)
                qkv_ref[half, span, cols] = nn(normed_ref[half, span, :], w_ref[:, cols]).astype(BF)

    @pl.when(step == gather.steps - 1)
    def _():
        for join in joins():
            join.wait()
        cot_copy().wait()
        rows_store().wait()

        @pl.loop(0, gather.count)
        def _(block):
            w_store(block).wait()


def gather_project(devices, shards, tokens, cot, cot_rows, gain, depths, later):
    half, d = tokens.shape
    rows, width = shards[0].shape
    total = len(shards) * width
    per = width // COLS
    gather = Gather(devices, rows, total // COLS)
    count = gather.count
    assert rows * devices == d and count // 2 - 1 + (3 * per + 1) // 2 <= count
    left_there = pl.BlockSpec(memory_space=pl.ANY)
    return pl.pallas_call(
        functools.partial(gather_project_kernel, gather, per),
        grid=(gather.steps,),
        in_specs=[left_there] * 6
        + [resident((d,)), pl.BlockSpec(memory_space=pltpu.SMEM)]
        + [left_there] * len(later),
        out_specs=[
            left_there,
            resident((2, half, 3 * width)),
            resident((d, 2 * half)),
            left_there,
            left_there,
            left_there,
            resident((2, half, LANES)),
            resident((2, half, LANES)),
            left_there,
        ],
        out_shape=[
            jax.ShapeDtypeStruct((d, total), BF),
            jax.ShapeDtypeStruct((2, half, 3 * width), BF),
            jax.ShapeDtypeStruct((d, 2 * half), BF),
            jax.ShapeDtypeStruct((2, half, d), BF),
            jax.ShapeDtypeStruct((cot_rows, d), BF),
            jax.ShapeDtypeStruct((half - cot_rows, d), BF),
            jax.ShapeDtypeStruct((2, half, LANES), F32),
            jax.ShapeDtypeStruct((2, half, LANES), F32),
            jax.ShapeDtypeStruct((rows, sum(shard.shape[1] for shard in later)), BF),
        ],
        scratch_shapes=[
            pltpu.VMEM((d, total), BF),
            pltpu.VMEM((2, half, d), BF),
            pltpu.VMEM((2, half, d), BF),
            pltpu.SemaphoreType.DMA((2, 2)),
            pltpu.SemaphoreType.DMA((2,)),
            pltpu.SemaphoreType.DMA((count,)),
            pltpu.SemaphoreType.DMA((len(later) + 1,)),
        ]
        + gather.scratch(),
        compiler_params=remote_settings(2),
        cost_estimate=cost(12 * half * d * width, 2 * d * total),
        name="gather_project",
    )(*shards, tokens, cot, gain, depths, *later)


def project_out_kernel(half_ref, attended_ref, w_ref, out_ref):
    out_ref[...] = nt(attended_ref[...], w_ref[...]).astype(BF)


def project_out(attended, w, half, cols=512):
    _, rows, width = attended.shape
    d = w.shape[0]
    part = w.shape[1] // width - 1
    return pl.pallas_call(
        project_out_kernel,
        grid_spec=pltpu.PrefetchScalarGridSpec(
            num_scalar_prefetch=1,
            grid=(d // cols,),
            in_specs=[
                pl.BlockSpec((None, rows, width), lambda j, half_ref: (half_ref[0], 0, 0)),
                pl.BlockSpec((cols, width), lambda j, half_ref: (j, part)),
            ],
            out_specs=pl.BlockSpec((rows, cols), lambda j, half_ref: (0, j)),
        ),
        out_shape=jax.ShapeDtypeStruct((rows, d), BF),
        compiler_params=settings(32),
        cost_estimate=cost(2 * rows * d * width, 2 * d * (width + rows)),
        name="project_out",
    )(half.reshape(1), attended, w)


def swap(x):
    return lax.ppermute(x, "tensor", [(0, 1), (1, 0)])


def body(
    tokens,
    parents,
    attn_gain,
    ffn_gain,
    query_weight,
    key_weight,
    value_weight,
    output_weight,
    gate_weight,
    up_weight,
    down_weight,
    cotangent,
):
    half, d = tokens.shape
    length = 2 * half
    width = query_weight.shape[1]
    hidden_width = gate_weight.shape[1]
    seg_rows = length // parents.shape[1]
    mine = lax.axis_index("tensor")
    own_start = mine * half

    def own_rows(full):
        return lax.dynamic_slice_in_dim(full, own_start, half, 0)

    def gather(shard):
        return lax.all_gather(shard, "dp", axis=0, tiled=True)

    attn_row = attn_gain[None, :]
    ffn_row = ffn_gain[None, :]

    devices = lax.axis_size("dp")
    bias, depths = tree_tables(parents[0], seg_rows)

    cut = half // 2
    first, qkv, norm_turned, rows_all, cot_first, cot_rest, cosine, sine, second_shard = gather_project(
        devices,
        (query_weight, key_weight, value_weight, output_weight.T),
        tokens,
        cotangent,
        cut,
        attn_gain,
        depths,
        (gate_weight, up_weight, down_weight.T),
    )
    second = gather(second_shard)
    cot_rest = swap(cot_rest)
    qkv = qkv.reshape(length, 3 * width)
    rows_all = rows_all.reshape(length, d)
    cosine, sine = cosine.reshape(length, LANES), sine.reshape(length, LANES)

    attended, lse = attend(qkv, bias, width, seg_rows)
    out_turned = first[:, 3 * width :]
    send = project_out(attended.reshape(2, half, width), first, 1 - mine)
    send, cot_first, cot_rest = lax.optimization_barrier((send, cot_first, cot_rest))
    cot_other = jnp.concatenate([cot_first, cot_rest], axis=0)
    received = swap(send)
    received, cot_turned = lax.optimization_barrier((received, turn_pair(cotangent, cot_other)))
    middle = (
        tokens.astype(F32) + nt(own_rows(attended), out_turned) + received.astype(F32)
    ).astype(BF)
    middle_other = swap(middle)

    ffn_grads, normed_two, parts, gain_part, got_part = ffn(
        (middle, middle_other), (cotangent, cot_other), ffn_row, second, hidden_width
    )
    (
        down_grad, up_first, ffn_gain_grad, whole, grad_middle, grad_attended, block_out, gm_turned,
    ) = ffn_scatter(
        devices,
        cot_turned,
        normed_two,
        ffn_grads,
        cotangent,
        middle,
        parts,
        got_part,
        gain_part,
        second,
        first,
        width,
    )
    blocks = hidden_width // COLS
    rest = whole.shape[1] // COLS - blocks
    (
        query_grad, key_grad, value_grad, output_grad, attn_gain_grad, gate_grad, *up_rest,
        token_grad,
    ) = attention_scatter(
        devices,
        norm_turned,
        gm_turned,
        grad_middle,
        rows_all,
        attn_row,
        qkv,
        attended,
        grad_attended.reshape(length, width),
        lse,
        bias,
        cosine,
        sine,
        first,
        whole,
        (blocks, rest) if rest else (blocks,),
        seg_rows,
    )
    up_grad = jnp.concatenate([up_first, *up_rest], axis=1)
    gain_rows = d // devices // 2

    def gain_piece(columns, side):
        return lax.dynamic_slice_in_dim(columns[0], side * gain_rows, gain_rows, 0)

    return (
        block_out,
        token_grad,
        query_grad,
        key_grad,
        value_grad,
        output_grad.T,
        gate_grad,
        up_grad,
        down_grad.T,
        gain_piece(attn_gain_grad, mine) + swap(gain_piece(attn_gain_grad, 1 - mine)),
        gain_piece(ffn_gain_grad, mine),
    )


def solution(mesh):
    rows = P(("dp", "tensor"), None)
    tall = P("dp", "tensor")
    wide = P("tensor", "dp")
    return jax.shard_map(
        body,
        mesh=mesh,
        in_specs=(
            rows, P("dp", None), P(), P(), tall, tall, tall, wide, tall, tall, wide, rows,
        ),
        out_specs=(
            rows, rows, tall, tall, tall, wide, tall, tall, wide,
            P(("dp", "tensor")), P(("dp", "tensor")),
        ),
        check_vma=False,
    )
```
